32 devices in a mesh: tower: 2 (over core), batch: 16 (over z, y, x).
Axes of the slice: x: 2, y: 2, z: 4, core: 2. Of those that a mesh axis runs over, the one named last changes fastest.
Arguments:
- shard_ids: int32 [3, 1664, 10, 8], P(None, 'batch'), may hold values from 0 to 31, all different within a row; in each aligned block of 1040 rows (0 to 1039, 1040 to 2079, ..., all dimensions but the last counted through in order) at most 1040 rows name the same one
- local_rows: int32 [3, 1664, 10, 8], P(None, 'batch'), may hold values from 0 to 32767
- bag_counts: int32 [3, 1664, 39], P(None, 'batch'), may hold values from 1 to 24, 80 in all within a row
- click_labels: int32 [3, 1664], P(None, 'batch'), may hold values 0 or 1
- sample_weights: int32 [3, 1664], P(None, 'batch'), may hold values from 1 to 5
- embed_table: float32 [11, 1048576], P(None, ('tower', 'batch')), may hold values from -1 to 1
- table_first: float32 [11, 1048576], P(None, ('tower', 'batch')), may hold values from -1 to 1
- table_second: float32 [11, 1048576], P(None, ('tower', 'batch')), may hold values from 0 to 1
- dense_params: float32 [621632], P(('tower', 'batch')), may hold values from -1.5 to 1.5
- dense_first: float32 [621632], P(('tower', 'batch')), may hold values from -1 to 1
- dense_second: float32 [621632], P(('tower', 'batch')), may hold values from 0 to 1
Outputs:
- table_new: float32 [11, 1048576], P(None, ('tower', 'batch'))
- table_first_new: float32 [11, 1048576], P(None, ('tower', 'batch'))
- table_second_new: float32 [11, 1048576], P(None, ('tower', 'batch'))
- table_copy: bfloat16 [11, 1048576], P(None, ('tower', 'batch'))
- dense_new: float32 [621632], P(('tower', 'batch'))
- dense_first_new: float32 [621632], P(('tower', 'batch'))
- dense_second_new: float32 [621632], P(('tower', 'batch'))
- dense_copy: bfloat16 [621632], P(('tower', 'batch'))
- loss_value: float32 [], replicated
The draws below stay inside these ranges and needn't reach their ends.
Inputs may be any that keep to these rules, and one draw needn't show every extreme that they name: `shard_ids`: within each group of 8 the shards differ; over the ids of one device's samples in one micro-batch (aligned blocks of 104 samples) no shard is named more than 1040 times, a bound that some block reaches. `bag_counts`: the 39 counts of each sample add up to 80.
All inputs are finite; a program needn't handle non-finite values. No bound on the sum of `click_labels` on one device may be relied on, other than what follows from the above.
Results may differ from the reference program's by a relative error of at most 0.004.
The reference program's roundings to bfloat16 on the way count: a program that leaves them out, or rounds other values in their place, can miss the bound.
Values may be sent and summed in bfloat16 or wider, within the bound.
A program may use at most 192 MiB of HBM per device.

```python
import math
import jax
import jax.numpy as jnp
import numpy as np
from jax import lax

FIELDS = 39
EMB = 10
MAPS = 200
HID = 400
ROWS_DEV = 32768
SAMP_DEV = 104
MICRO = 3
IDS_SAMP = 80
BAG_MOST = 24
SAMPLES = 1664
VOCAB = 1048576
CAP = 1040
PARAMS = 621601
DENSE = 621632
DEVICES = 32


def draw_sample_weights(key, part):
    level_key, bit_key, pick_key = jax.random.split(key, 3)
    block_count = SAMPLES // SAMP_DEV
    levels = jax.random.randint(level_key, (block_count,), 0, 4).astype(jnp.int32)
    order = jax.random.permutation(pick_key, block_count).astype(jnp.int32)
    places = jnp.arange(block_count, dtype=jnp.int32)
    levels = jnp.where(places == order[0], 3, jnp.where(places == order[1], 0, levels)).astype(jnp.int32)
    owner = jnp.arange(SAMPLES, dtype=jnp.int32) // SAMP_DEV
    owner_level = jnp.sum((owner[:, None] == places[None, :]).astype(jnp.int32) * levels[None, :], axis=1)
    bits = jax.random.randint(bit_key, (MICRO, SAMPLES), 0, 2).astype(jnp.int32)
    return (1 + owner_level[None, :] + bits).astype(jnp.int32)


def column_scales(embed_factor, linear_factor):
    columns = jnp.arange(EMB + 1)
    return jnp.where(columns < EMB, embed_factor, linear_factor).astype(jnp.float32)


def table_gradient():
    hits = 1.0 + IDS_SAMP * MICRO * SAMPLES / VOCAB
    return 0.55 * math.sqrt(hits) / (MICRO * SAMPLES) * column_scales(0.077, 1.0)


def draw_embed_table(key, part):
    values = jax.random.truncated_normal(key, -3.5, 3.5, (EMB + 1, VOCAB), jnp.float32)
    return values * column_scales(0.25, 0.05)[:, None]


def draw_table_first(key, part):
    values = jax.random.truncated_normal(key, -2.5, 2.5, (EMB + 1, VOCAB), jnp.float32)
    return 0.1 / 0.9 * table_gradient()[:, None] * values


def draw_table_second(key, part):
    factor = jnp.exp2(jax.random.uniform(key, (EMB + 1, VOCAB), jnp.float32, 0.0, 2.0))
    scale = table_gradient()
    return 0.001 / 0.999 * (scale * scale)[:, None] * factor


def segment_values(factors):
    amounts = [MAPS * FIELDS * FIELDS, MAPS, FIELDS * EMB * HID, HID, HID * HID, HID, HID, 1, DENSE - PARAMS]
    return jnp.concatenate([jnp.full((amount,), factor, jnp.float32) for amount, factor in zip(amounts, factors)])


def dense_gradient():
    base = 0.55 / math.sqrt(MICRO * SAMPLES)
    factors = [0.029, 0.4, 0.018, 0.05, 0.018, 0.07, 0.19, 1.0, 0.02]
    return segment_values([base * factor for factor in factors])


def draw_dense_params(key, part):
    stds = [1.0 / FIELDS, MAPS ** (-0.5), (FIELDS * EMB) ** (-0.5), 0.1, HID ** (-0.5), 0.1, 2.0 * HID ** (-0.5), 0.5, 0.05]
    values = jax.random.truncated_normal(key, -3.0, 3.0, (DENSE,), jnp.float32)
    return values * segment_values(stds)


def draw_dense_first(key, part):
    values = jax.random.truncated_normal(key, -2.5, 2.5, (DENSE,), jnp.float32)
    return 0.1 / 0.9 * dense_gradient() * values


def draw_dense_second(key, part):
    factor = jnp.exp2(jax.random.uniform(key, (DENSE,), jnp.float32, 0.0, 2.0))
    scale = dense_gradient()
    return 0.001 / 0.999 * scale * scale * factor


def plant(drawn, own_key, smallest, top_value):
    dims = drawn.shape
    index_at = [jax.random.randint(jax.random.fold_in(own_key, axis), (), 0, dims[axis]) for axis in range(len(dims))]
    drawn = drawn.at[tuple(index_at)].set(smallest)
    longest = dims.index(max(dims))
    index_at[longest] = (index_at[longest] + 1) % dims[longest]
    return drawn.at[tuple(index_at)].set(top_value)


def length_profile(number_of, total, bound, skew):
    loads = [(1 << 20) // math.isqrt(standing ** skew) + 1 for standing in range(2, number_of + 1)]
    rest, given = total - bound - (number_of - 1), [1] * (number_of - 1)
    while rest > 0:
        candidates = [i for i in range(number_of - 1) if given[i] < bound]
        whole, budget = sum([loads[i] for i in candidates]), rest
        for i in candidates:
            addition = min(bound - given[i], max(1, budget * loads[i] // whole), rest)
            given[i] = given[i] + addition
            rest = rest - addition
    return np.array([bound] + given)


def ragged(stream_key, number_of, total, bound, lean):
    if number_of == 2:
        one = jax.random.randint(stream_key, (), max(1, total - bound), min(bound, total - 1) + 1)
        return jnp.stack([one, total - one])
    tallies = jnp.asarray(length_profile(number_of, total, bound, lean), jnp.int32)
    pairs = (number_of - 1) // 2
    giver, sink = tallies[1:1 + 2 * pairs:2], tallies[2:2 + 2 * pairs:2]
    slack = jnp.minimum(giver - 1, bound - sink)
    shifted = jax.random.randint(jax.random.fold_in(stream_key, 1), (pairs,), 0, 1 << 20) % (slack + 1)
    tallies = tallies.at[1:1 + 2 * pairs:2].set(giver - shifted).at[2:2 + 2 * pairs:2].set(sink + shifted)
    return tallies[jax.random.permutation(jax.random.fold_in(stream_key, 2), number_of)]


def assign_block(own_key, own, number, rows, count, top, bound, skew):
    ranking = jax.random.permutation(own_key, count)
    crowded, ordinary = portions_of(count, rows * top, bound, skew, True), portions_of(count, rows * top, bound, skew, False)
    places = jnp.arange(count)

    def named(tallies, offset_by):
        used = int((tallies > 0).sum())
        fixed = max(1, used // 4)
        shifted = fixed + (places - fixed + offset_by * (used - fixed)) % max(1, count - fixed)
        return jnp.zeros((count,), jnp.int32).at[ranking[jnp.where(places < fixed, places, shifted)]].set(jnp.asarray(tallies, jnp.int32))

    tallies = jnp.where(number % 4 == 0, named(crowded, number // 4), named(ordinary, number - number // 4 - 1))
    mixed = jax.random.permutation(jax.random.fold_in(own, 3), count)
    donor, receiver = mixed[0:count // 2 * 2:2], mixed[1:count // 2 * 2:2]
    margin = jnp.minimum(tallies[donor] - 1, bound - tallies[receiver]) // 2
    margin = jnp.where((donor == ranking[0]) | (receiver == ranking[0]) | (tallies[receiver] == 0), 0, jnp.maximum(margin, 0))
    shifted = jax.random.randint(jax.random.fold_in(own, 4), (count // 2,), 0, 1 << 20) % (margin + 1)
    tallies = tallies.at[donor].add(-shifted).at[receiver].add(shifted)
    items = jnp.searchsorted(jnp.cumsum(tallies), jnp.arange(rows * top), side="right").astype(jnp.int32)
    listing = items.reshape(top, rows).T
    listing = listing[jax.random.permutation(jax.random.fold_in(own, 1), rows)]
    offset_by = jax.random.randint(jax.random.fold_in(own, 2), (rows, 1), 0, top)
    return jnp.take_along_axis(listing, (jnp.arange(top)[None, :] + offset_by) % top, axis=1)


def portions_of(count, total, reach, slope, full):
    weights = [(1 << 20) // math.isqrt(standing ** slope) + 1 for standing in range(1, count + 1)]
    largest = reach if full else min(reach, max(-(-total // count), total * weights[0] // sum(weights)))
    least = 1 if total - largest >= count - 1 else 0
    given, surplus = [largest] + [least] * (count - 1), total - largest - least * (count - 1)
    while surplus > 0:
        movable = [i for i in range(1, count) if given[i] < largest] or [i for i in range(1, count) if given[i] < reach]
        mass, budget = sum([weights[i] for i in movable]), surplus
        for i in movable:
            extra = min(reach - given[i], max(1, budget * weights[i] // mass), surplus)
            given[i] = given[i] + extra
            surplus = surplus - extra
    return np.array(given)


def setup_inputs(seed: int = 0) -> dict:
    keys = jax.random.split(jax.random.key(seed), 12)
    shard_ids_keys = jax.random.split(jax.random.fold_in(keys[0], 1), MICRO * SAMPLES * (IDS_SAMP // 8) // (SAMP_DEV * IDS_SAMP // 8))
    shard_ids_turns = jax.random.permutation(jax.random.fold_in(keys[0], 3), MICRO * SAMPLES * (IDS_SAMP // 8) // (SAMP_DEV * IDS_SAMP // 8))
    shard_ids = jax.vmap(lambda own, number: assign_block(jax.random.fold_in(keys[0], 2), own, number, SAMP_DEV * IDS_SAMP // 8, DEVICES, 8, CAP, 2))(shard_ids_keys, shard_ids_turns).reshape((MICRO, SAMPLES, IDS_SAMP // 8, 8))
    local_rows = plant(jax.random.randint(keys[1], (MICRO, SAMPLES, IDS_SAMP // 8, 8), 0, ROWS_DEV), jax.random.fold_in(keys[1], 1), 0, ROWS_DEV - 1).astype(jnp.int32)
    bag_counts = jax.vmap(lambda own: ragged(own, FIELDS, IDS_SAMP, BAG_MOST, 2))(jax.random.split(keys[2], MICRO * SAMPLES)).reshape((MICRO, SAMPLES, FIELDS)).astype(jnp.int32)
    click_labels = plant((jax.random.randint(keys[3], (MICRO, SAMPLES), 0, 4) < 1).astype(jnp.int32), jax.random.fold_in(keys[3], 1), 0, 1)
    sample_weights = draw_sample_weights(jax.random.fold_in(keys[11], 71), 0)
    embed_table = draw_embed_table(jax.random.fold_in(keys[11], 71), 0)
    table_first = draw_table_first(jax.random.fold_in(keys[11], 71), 0)
    table_second = draw_table_second(jax.random.fold_in(keys[11], 71), 0)
    dense_params = draw_dense_params(jax.random.fold_in(keys[11], 71), 0)
    dense_first = draw_dense_first(jax.random.fold_in(keys[11], 71), 0)
    dense_second = draw_dense_second(jax.random.fold_in(keys[11], 71), 0)
    return dict(shard_ids=shard_ids, local_rows=local_rows, bag_counts=bag_counts, click_labels=click_labels, sample_weights=sample_weights, embed_table=embed_table, table_first=table_first, table_second=table_second, dense_params=dense_params, dense_first=dense_first, dense_second=dense_second)


@jax.custom_vjp
def low(v):
    return lax.optimization_barrier(v.astype(jnp.bfloat16)).astype(jnp.float32)

@jax.custom_vjp
def low_back(v):
    return v

def low_keep(v):
    return (low(v), None)

def low_pass(kept, grad):
    return (grad,)

def back_keep(v):
    return (v, None)

def back_low(kept, grad):
    return (low(grad),)
low.defvjp(low_keep, low_pass)
low_back.defvjp(back_keep, back_low)
highest = lax.Precision.HIGHEST
beta_one = 0.9
beta_two = 0.999
epsilon = 1e-08
decay_rate = 0.15
rate_table = 0.1
rate_dense = 0.05
step_count = 10

def adam_update(weight, first_old, second_old, gradient, step_rate):
    first_new = beta_one * first_old + (1.0 - beta_one) * gradient
    second_new = beta_two * second_old + (1.0 - beta_two) * gradient * gradient
    first_hat = first_new / (1.0 - beta_one ** step_count)
    second_hat = second_new / (1.0 - beta_two ** step_count)
    weight_new = weight - step_rate * (first_hat / (jnp.sqrt(second_hat) + epsilon) + decay_rate * weight)
    return (weight_new, first_new, second_new)

def field_table(counts_here):
    bag_ends = jnp.cumsum(counts_here, axis=-1)
    positions = jnp.arange(IDS_SAMP, dtype=jnp.int32)
    field_of = lax.optimization_barrier(jnp.sum((positions[None, :, None] >= bag_ends[:, None, :]).astype(jnp.int32), axis=-1))
    return (field_of[:, :, None] == jnp.arange(FIELDS, dtype=jnp.int32)[None, None, :]).astype(jnp.float32)

def cin_pairs(embedded):
    turned = jnp.swapaxes(embedded, 1, 2)
    pair_terms = turned[:, :, :, None] * turned[:, :, None, :]
    return pair_terms.reshape(turned.shape[0], EMB, FIELDS * FIELDS)

def unpack(flat_params):
    amounts = [MAPS * FIELDS * FIELDS, MAPS, FIELDS * EMB * HID, HID, HID * HID, HID, HID, 1]
    layouts = [(MAPS, FIELDS * FIELDS), (MAPS,), (FIELDS * EMB, HID), (HID,), (HID, HID), (HID,), (HID,), (1,)]
    pieces = []
    offset = 0
    for amount, layout in zip(amounts, layouts):
        pieces.append(flat_params[offset:offset + amount].reshape(layout))
        offset += amount
    return tuple(pieces)

def forward_logits(pooled, params):
    cin_w, cin_u, w_one, b_one, w_two, b_two, w_three, bias = params
    embedded = pooled[:, :, :EMB]
    pair_terms = low(cin_pairs(embedded))
    map_values = low_back(jnp.einsum('sdq,hq->sdh', pair_terms, cin_w, precision=highest))
    map_sum = lax.optimization_barrier(jnp.sum(map_values, axis=1))
    cin_logits = jnp.dot(map_sum, cin_u, precision=highest)
    flat_embed = low(embedded.reshape(embedded.shape[0], FIELDS * EMB))
    pre_one = low_back(jnp.dot(flat_embed, w_one, precision=highest) + b_one)
    hidden_one = low(jax.nn.relu(pre_one))
    pre_two = low_back(jnp.dot(hidden_one, w_two, precision=highest) + b_two)
    deep_logits = jnp.dot(jax.nn.relu(pre_two), w_three, precision=highest)
    linear_logits = lax.optimization_barrier(jnp.sum(pooled[:, :, EMB], axis=1))
    return cin_logits + deep_logits + linear_logits + bias[0]

def reference(shard_ids, local_rows, bag_counts, click_labels, sample_weights, embed_table, table_first, table_second, dense_params, dense_first, dense_second):
    blocks = MICRO * SAMPLES // SAMP_DEV
    row_ids = (shard_ids * ROWS_DEV + local_rows).reshape(blocks, SAMP_DEV, IDS_SAMP).astype(jnp.int32)
    counts_blocks = bag_counts.reshape(blocks, SAMP_DEV, FIELDS)
    labels_blocks = click_labels.reshape(blocks, SAMP_DEV).astype(jnp.float32)
    weights_blocks = sample_weights.reshape(blocks, SAMP_DEV).astype(jnp.float32)
    total_weight = jnp.sum(weights_blocks)

    def loss_fn(table_values, dense_values):
        gathered = low(jnp.moveaxis(table_values[:, row_ids], 0, -1))
        params = unpack(low(dense_values))

        def block_sum(pieces):
            rows_here, counts_here, labels_here, weights_here = pieces
            fields = field_table(counts_here)
            pooled = jnp.einsum('skf,skc->sfc', fields, rows_here, precision=highest)
            logits = forward_logits(pooled, params)
            return jnp.sum(weights_here * (jax.nn.softplus(logits) - labels_here * logits))
        block_sums = lax.map(jax.checkpoint(block_sum), (gathered, counts_blocks, labels_blocks, weights_blocks))
        return jnp.sum(block_sums) / total_weight
    loss_sum, pullback = jax.vjp(loss_fn, embed_table, dense_params)
    grad_table, grad_dense = pullback(jnp.ones_like(loss_sum))
    table_new, table_first_new, table_second_new = adam_update(embed_table, table_first, table_second, grad_table, rate_table)
    dense_new, dense_first_new, dense_second_new = adam_update(dense_params, dense_first, dense_second, grad_dense, rate_dense)
    return (table_new, table_first_new, table_second_new, table_new.astype(jnp.bfloat16), dense_new, dense_first_new, dense_second_new, dense_new.astype(jnp.bfloat16), loss_sum)
```

```python
from functools import partial

import jax
import jax.numpy as jnp
from jax import lax
from jax.experimental import pallas as pl
from jax.experimental.pallas import tpu as pltpu
from jax.sharding import PartitionSpec as P

FIELDS = 39
EMB = 10
MAPS = 200
HID = 400
IDS_SAMP = 80

beta_one = 0.9
beta_two = 0.999
epsilon = 1e-08
decay_rate = 0.15
rate_table = 0.1
rate_dense = 0.05
step_count = 10

LANES = 128
WIDE = 256
HALF = 24
BAG_ROWS = EMB * HALF + 8
FPAD = 40
PAIRS = FIELDS * FPAD
NT = (((1,), (1,)), ((), ()))
TN = (((0,), (0,)), ((), ()))
NN = (((1,), (0,)), ((), ()))


def adam_update(weight, first_old, second_old, gradient, step_rate):
    first_new = beta_one * first_old + (1.0 - beta_one) * gradient
    second_new = beta_two * second_old + (1.0 - beta_two) * gradient * gradient
    first_hat = first_new / (1.0 - beta_one**step_count)
    second_hat = second_new / (1.0 - beta_two**step_count)
    weight_new = weight - step_rate * (
        first_hat / (jnp.sqrt(second_hat) + epsilon) + decay_rate * weight
    )
    return (weight_new, first_new, second_new)


def dot(a, b, dims=NN):
    return lax.dot_general(a, b, dims, preferred_element_type=jnp.float32)


def iota(shape, dim):
    return lax.broadcasted_iota(jnp.int32, shape, dim)


def ones_at(mask):
    return jnp.where(mask, 1.0, 0.0).astype(jnp.bfloat16)


def layout_of(micro_count, capacity):
    first_rows = [m * capacity // WIDE for m in range(micro_count)]
    shifts = [m * capacity % WIDE for m in range(micro_count)]
    window = max(-(-(shift + capacity) // WIDE) for shift in shifts)
    return first_rows, shifts, window, max(first_rows) + window


def route_kernel(
    capacity, batch_count, micro_count, ids_ref, rows_ref, lanes_ref, field_ref,
    req_ref, code_ref, half_ref, slot_ref, left_ref, right_ref,
):
    first_rows, shifts, window, rows_msg = layout_of(micro_count, capacity)
    micro = pl.program_id(0)
    id_rows = ids_ref.shape[1]
    chunk = 16
    target = ids_ref[0]

    @pl.when(micro == 0)
    def _():
        req_ref[...] = jnp.zeros_like(req_ref)
        code_ref[...] = jnp.zeros_like(code_ref)
        half_ref[...] = jnp.zeros_like(half_ref)

    earlier_rows = ones_at(iota((id_rows, id_rows), 1) < iota((id_rows, id_rows), 0))
    upper = iota((2 * LANES, LANES), 0)
    mixing = ones_at((upper < iota((2 * LANES, LANES), 1)) | (upper >= LANES))
    rank = jnp.zeros((id_rows, LANES), jnp.float32)
    for begin in range(0, batch_count, chunk):
        hots = [ones_at(target == begin + d) for d in range(chunk)]
        above = dot(earlier_rows, jnp.concatenate(hots, axis=1)).astype(jnp.bfloat16)
        stacked = jnp.concatenate(
            [
                jnp.concatenate([hots[d], above[:, d * LANES : (d + 1) * LANES]], axis=1)
                for d in range(chunk)
            ],
            axis=0,
        )
        ranks = dot(stacked, mixing)
        for d in range(chunk):
            rank = rank + jnp.where(
                target == begin + d, ranks[d * id_rows : (d + 1) * id_rows], 0.0
            )
    shift = sum(jnp.where(micro == m, shifts[m], 0) for m in range(micro_count))
    place = rank.astype(jnp.int32) + shift
    slot_ref[0] = jnp.where(target < batch_count, (place // WIDE) * batch_count + target, -1)
    slot_ref[1] = place % WIDE
    places = window * batch_count

    def build(t, carry):
        here = pl.ds(t, 1)
        span = pl.ds(pl.multiple_of(t * LANES, LANES), LANES)
        mask = iota((places, LANES), 0) == slot_ref[0, here, :]
        row = rows_ref[0, here, :]
        values = [row // LANES, row % LANES, lanes_ref[0, here, :] + 1, field_ref[0, here, :]]
        for v in range(4):
            value = values[v].astype(jnp.float32)
            left_ref[v * places : (v + 1) * places, span] = jnp.where(mask, value, 0.0).astype(
                jnp.bfloat16
            )
        right_ref[:, span] = ones_at(iota((WIDE, LANES), 0) == slot_ref[1, here, :])
        return carry

    lax.fori_loop(0, id_rows, build, 0)
    placed = dot(left_ref[...], right_ref[...], NT)

    def part(v, r):
        return placed[(v * window + r) * batch_count : (v * window + r + 1) * batch_count].astype(
            jnp.int32
        )

    for m in range(micro_count):

        @pl.when(micro == m)
        def _():
            for r in range(window):
                code = part(2, r)
                at = first_rows[m] + r
                req_ref[at] += part(0, r) * LANES + part(1, r)
                code_ref[at] += jnp.where(code > 0, code + m * WIDE, 0)
                half_ref[at] += part(3, r)


def route(targets, rows, lane_codes, half_fields, capacity, batch_count):
    micro_count, id_rows, _ = targets.shape
    _, _, window, rows_msg = layout_of(micro_count, capacity)
    block = pl.BlockSpec((1, id_rows, LANES), lambda m: (m, 0, 0))
    whole = pl.BlockSpec((rows_msg, batch_count, WIDE), lambda m: (0, 0, 0))
    shape = jax.ShapeDtypeStruct((rows_msg, batch_count, WIDE), jnp.int32)
    return pl.pallas_call(
        partial(route_kernel, capacity, batch_count, micro_count),
        grid=(micro_count,),
        in_specs=[block] * 4,
        out_specs=[whole] * 3,
        out_shape=[shape] * 3,
        scratch_shapes=[
            pltpu.VMEM((2, id_rows, LANES), jnp.int32),
            pltpu.VMEM((4 * window * batch_count, id_rows * LANES), jnp.bfloat16),
            pltpu.VMEM((WIDE, id_rows * LANES), jnp.bfloat16),
        ],
        compiler_params=pltpu.CompilerParams(vmem_limit_bytes=60 << 20),
        name="route",
    )(targets, rows, lane_codes, half_fields)


def gather_columns(result, mask, depth, columns):
    width = result.shape[1]
    out = jnp.zeros((16, width), jnp.float32)
    for c in range(columns):
        row = jnp.sum(
            jnp.where(mask, result[c * depth : (c + 1) * depth], 0.0), axis=0, keepdims=True
        )
        out = jnp.where(iota((16, width), 0) == c, row, out)
    return out


def lookup_kernel(columns, req_ref, table_ref, out_ref):
    tiles = table_ref.shape[1]

    def step(r, carry):
        row = req_ref[0, pl.ds(r, 1), :]
        hot = ones_at(iota((tiles, WIDE), 0) == row // LANES)
        result = dot(table_ref[...], hot)
        mask = iota((LANES, WIDE), 0) == row % LANES
        span = pl.ds(pl.multiple_of(r * WIDE, WIDE), WIDE)
        out_ref[0, :, span] = gather_columns(result, mask, LANES, columns).astype(jnp.bfloat16)
        return carry

    lax.fori_loop(0, req_ref.shape[1], step, 0)


def lookup(requests, table_tiles):
    batch_count, rows_msg, _ = requests.shape
    columns = table_tiles.shape[0] // LANES
    return pl.pallas_call(
        partial(lookup_kernel, columns),
        grid=(batch_count,),
        in_specs=[
            pl.BlockSpec((1, rows_msg, WIDE), lambda d: (d, 0, 0)),
            pl.BlockSpec(table_tiles.shape, lambda d: (0, 0)),
        ],
        out_specs=pl.BlockSpec((1, 16, rows_msg * WIDE), lambda d: (d, 0, 0)),
        out_shape=jax.ShapeDtypeStruct((batch_count, 16, rows_msg * WIDE), jnp.bfloat16),
        compiler_params=pltpu.CompilerParams(vmem_limit_bytes=60 << 20),
        name="lookup",
    )(requests, table_tiles)


def pool_kernel(capacity, micro_count, ans_ref, code_ref, half_ref, out_ref, left_ref):
    first_rows, _, window, rows_msg = layout_of(micro_count, capacity)

    @pl.when(pl.program_id(0) == 0)
    def _():
        out_ref[...] = jnp.zeros_like(out_ref)

    for r in range(rows_msg):
        span = slice(r * WIDE, (r + 1) * WIDE)
        values = ans_ref[0, :, span].astype(jnp.float32)
        mask = iota((HALF, WIDE), 0) == half_ref[0, r : r + 1, :]
        pieces = [jnp.where(mask, values[c : c + 1], 0.0) for c in range(EMB)]
        pieces.append(jnp.where(iota((8, WIDE), 0) == 0, values[EMB : EMB + 1], 0.0))
        left_ref[:, span] = jnp.concatenate(pieces, axis=0).astype(jnp.bfloat16)
    for m in range(micro_count):
        rights = [
            ones_at(iota((WIDE, WIDE), 0) + (m * WIDE + 1) == code_ref[0, r : r + 1, :])
            for r in range(first_rows[m], first_rows[m] + window)
        ]
        span = slice(first_rows[m] * WIDE, (first_rows[m] + window) * WIDE)
        out_ref[m] += dot(left_ref[:, span], jnp.concatenate(rights, axis=1), NT)


def pool(answers, codes, halves, capacity, micro_count):
    batch_count, rows_msg, _ = codes.shape
    block = pl.BlockSpec((1, rows_msg, WIDE), lambda d: (d, 0, 0))
    return pl.pallas_call(
        partial(pool_kernel, capacity, micro_count),
        grid=(batch_count,),
        in_specs=[pl.BlockSpec((1, 16, rows_msg * WIDE), lambda d: (d, 0, 0)), block, block],
        out_specs=pl.BlockSpec((micro_count, BAG_ROWS, WIDE), lambda d: (0, 0, 0)),
        out_shape=jax.ShapeDtypeStruct((micro_count, BAG_ROWS, WIDE), jnp.float32),
        scratch_shapes=[pltpu.VMEM((BAG_ROWS, rows_msg * WIDE), jnp.bfloat16)],
        compiler_params=pltpu.CompilerParams(vmem_limit_bytes=60 << 20),
        name="pool",
    )(answers, codes, halves)


def spread_kernel(capacity, micro_count, grad_ref, code_ref, half_ref, out_ref):
    first_rows, _, window, rows_msg = layout_of(micro_count, capacity)
    for r in range(rows_msg):
        result = None
        for m in range(micro_count):
            if first_rows[m] <= r < first_rows[m] + window:
                hot = ones_at(iota((WIDE, WIDE), 0) + (m * WIDE + 1) == code_ref[0, r : r + 1, :])
                found = dot(grad_ref[m], hot)
                result = found if result is None else result + found
        mask = iota((HALF, WIDE), 0) == half_ref[0, r : r + 1, :]
        block = gather_columns(result, mask, HALF, EMB)
        linear = result[EMB * HALF : EMB * HALF + 1]
        block = jnp.where(iota((16, WIDE), 0) == EMB, linear, block)
        out_ref[0, :, r * WIDE : (r + 1) * WIDE] = block.astype(jnp.bfloat16)


def spread(grad_bags, codes, halves, capacity):
    batch_count, rows_msg, _ = codes.shape
    micro_count = grad_bags.shape[0]
    block = pl.BlockSpec((1, rows_msg, WIDE), lambda d: (d, 0, 0))
    return pl.pallas_call(
        partial(spread_kernel, capacity, micro_count),
        grid=(batch_count,),
        in_specs=[pl.BlockSpec(grad_bags.shape, lambda d: (0, 0, 0)), block, block],
        out_specs=pl.BlockSpec((1, 16, rows_msg * WIDE), lambda d: (d, 0, 0)),
        out_shape=jax.ShapeDtypeStruct((batch_count, 16, rows_msg * WIDE), jnp.bfloat16),
        compiler_params=pltpu.CompilerParams(vmem_limit_bytes=60 << 20),
        name="spread",
    )(grad_bags, codes, halves)


def scatter_kernel(columns, grads_ref, req_ref, out_ref, left_ref, right_ref, total_ref):
    rows_msg = req_ref.shape[1]
    tiles = right_ref.shape[0]

    @pl.when(pl.program_id(0) == 0)
    def _():
        total_ref[...] = jnp.zeros_like(total_ref)

    def build(r, carry):
        span = pl.ds(pl.multiple_of(r * WIDE, WIDE), WIDE)
        row = req_ref[0, pl.ds(r, 1), :]
        values = grads_ref[0, :, span].astype(jnp.float32)
        mask = iota((LANES, WIDE), 0) == row % LANES
        for c in range(columns):
            left_ref[c * LANES : (c + 1) * LANES, span] = jnp.where(
                mask, values[c : c + 1], 0.0
            ).astype(jnp.bfloat16)
        right_ref[:, span] = ones_at(iota((tiles, WIDE), 0) == row // LANES)
        return carry

    lax.fori_loop(0, rows_msg, build, 0)
    total_ref[...] += dot(left_ref[...], right_ref[...], NT)

    @pl.when(pl.program_id(0) == pl.num_programs(0) - 1)
    def _():
        for c in range(columns):
            out_ref[c] = total_ref[c * LANES : (c + 1) * LANES, :].T


def scatter_rows(delivered, served, columns, rows_dev):
    batch_count, rows_msg, _ = served.shape
    tiles = rows_dev // LANES
    slots = rows_msg * WIDE
    out = pl.pallas_call(
        partial(scatter_kernel, columns),
        grid=(batch_count,),
        in_specs=[
            pl.BlockSpec((1, 16, slots), lambda d: (d, 0, 0)),
            pl.BlockSpec((1, rows_msg, WIDE), lambda d: (d, 0, 0)),
        ],
        out_specs=pl.BlockSpec((columns, tiles, LANES), lambda d: (0, 0, 0)),
        out_shape=jax.ShapeDtypeStruct((columns, tiles, LANES), jnp.float32),
        scratch_shapes=[
            pltpu.VMEM((columns * LANES, slots), jnp.bfloat16),
            pltpu.VMEM((tiles, slots), jnp.bfloat16),
            pltpu.VMEM((columns * LANES, tiles), jnp.float32),
        ],
        compiler_params=pltpu.CompilerParams(vmem_limit_bytes=60 << 20),
        name="scatter",
    )(delivered, served)
    return out.reshape(columns, rows_dev)


def split_three(x):
    high = x.astype(jnp.bfloat16)
    rest = x - high.astype(jnp.float32)
    middle = rest.astype(jnp.bfloat16)
    low = (rest - middle.astype(jnp.float32)).astype(jnp.bfloat16)
    return high, middle, low


def dense_kernel(
    micro_count, tower_ref, scale_ref, pooled_ref, label_ref, weight_ref,
    cin_w_ref, cin_u_ref, w_one_ref, b_one_ref, w_two_ref, b_two_ref, w_three_ref, bias_ref,
    bags_ref, loss_ref, g_cin_w_ref, g_cin_u_ref, g_w_one_ref, g_b_one_ref, g_w_two_ref,
    g_b_two_ref, g_w_three_ref, g_bias_ref,
    embed_ref, total_ref, pairs_ref, sym_ref,
):
    f32 = jnp.float32
    width = micro_count * LANES

    def unpacked(row, count):
        pieces = []
        for m in range(micro_count):
            low = pooled_ref[m, row : row + HALF, :LANES]
            high = pooled_ref[m, row : row + HALF, LANES:]
            pieces.append(jnp.concatenate([low, high], axis=0)[:count])
        return jnp.concatenate(pieces, axis=1)

    for d in range(EMB):
        embed_ref[d * FPAD : (d + 1) * FPAD, :] = unpacked(d * HALF, FPAD)
    linear = jnp.concatenate(
        [
            pooled_ref[m, EMB * HALF : EMB * HALF + 1, :LANES]
            + pooled_ref[m, EMB * HALF : EMB * HALF + 1, LANES:]
            for m in range(micro_count)
        ],
        axis=1,
    )

    def pair_row(i, carry):
        total = jnp.zeros((FPAD, width), f32)
        for d in range(EMB):
            own = embed_ref[pl.ds(d * FPAD + i, 1), :]
            product = (embed_ref[d * FPAD : (d + 1) * FPAD, :] * own).astype(jnp.bfloat16)
            total = total + product.astype(f32)
        total_ref[pl.ds(pl.multiple_of(i * FPAD, 8), FPAD), :] = total
        return carry

    lax.fori_loop(0, FIELDS, pair_row, 0)
    thirds = split_three(total_ref[...])
    cin_w = cin_w_ref[...]
    cin_u = cin_u_ref[...].astype(f32)
    map_sum = sum(dot(cin_w, third) for third in thirds)
    cin_logits = jnp.sum(map_sum * cin_u, axis=0, keepdims=True)

    flat = embed_ref[...].astype(jnp.bfloat16)
    pre_one = dot(w_one_ref[...], flat, TN) + b_one_ref[...].astype(f32)
    hidden_one = jnp.maximum(pre_one, 0.0).astype(jnp.bfloat16)
    pre_two = dot(w_two_ref[...], hidden_one, TN) + b_two_ref[...].astype(f32)
    active_two = jnp.maximum(pre_two, 0.0)
    w_three = w_three_ref[...].astype(f32)
    deep_logits = jnp.sum(active_two * w_three, axis=0, keepdims=True)
    logits = cin_logits + deep_logits + linear + bias_ref[...].astype(f32)

    weight = weight_ref[...]
    label = label_ref[...]
    soft = jnp.maximum(logits, 0.0) + jnp.log1p(jnp.exp(-jnp.abs(logits)))
    loss_ref[...] = jnp.broadcast_to(
        jnp.sum(weight * (soft - label * logits), axis=1, keepdims=True), loss_ref.shape
    )
    grad_logits = weight * (jax.nn.sigmoid(logits) - label) / scale_ref[0]

    grad_maps = (grad_logits * cin_u).astype(jnp.bfloat16)
    grad_two = jnp.where(pre_two > 0, grad_logits * w_three, 0.0).astype(jnp.bfloat16)
    grad_hidden = dot(w_two_ref[...], grad_two)
    grad_one = jnp.where(pre_one > 0, grad_hidden, 0.0).astype(jnp.bfloat16)
    grad_flat = dot(w_one_ref[...], grad_one)

    grad_pairs = dot(cin_w, grad_maps, TN)
    for m in range(micro_count):
        pairs_ref[m, :PAIRS, :] = grad_pairs[:, m * LANES : (m + 1) * LANES]
        pairs_ref[m, PAIRS:, :] = jnp.zeros((FPAD * FPAD - PAIRS, LANES), f32)

    def mirror(j, carry):
        here = pl.ds(pl.multiple_of(j * FPAD, 8), FPAD)
        both = [
            pairs_ref[m, here, :] + pairs_ref[m, pl.ds(j, FPAD, stride=FPAD), :]
            for m in range(micro_count)
        ]
        sym_ref[here, :] = jnp.concatenate(both, axis=1)
        return carry

    lax.fori_loop(0, FIELDS, mirror, 0)
    empty = jnp.zeros((2 * HALF - FPAD, width), f32)

    for d in range(EMB):

        def add_row(j, total):
            here = pl.ds(pl.multiple_of(j * FPAD, 8), FPAD)
            return total + sym_ref[here, :] * embed_ref[pl.ds(d * FPAD + j, 1), :]

        grad_embed = lax.fori_loop(
            0, FIELDS, add_row, grad_flat[d * FPAD : (d + 1) * FPAD], unroll=3
        )
        grad_embed = jnp.concatenate([grad_embed, empty], axis=0)
        for m in range(micro_count):
            span = slice(m * LANES, (m + 1) * LANES)
            block = jnp.concatenate([grad_embed[:HALF, span], grad_embed[HALF:, span]], axis=1)
            bags_ref[m, d * HALF : (d + 1) * HALF, :] = block
    for m in range(micro_count):
        row = grad_logits[:, m * LANES : (m + 1) * LANES]
        row = jnp.concatenate([row, row], axis=1)
        bags_ref[m, EMB * HALF :, :] = jnp.broadcast_to(row, (8, WIDE))

    g_w_one_ref[...] = dot(flat, grad_one, NT)

    @pl.when(tower_ref[0] == 0)
    def _():
        g_cin_u_ref[...] = jnp.sum(map_sum * grad_logits, axis=1, keepdims=True)
        g_cin_w_ref[...] = sum(dot(grad_maps, third, NT) for third in thirds)

    @pl.when(tower_ref[0] != 0)
    def _():
        g_w_two_ref[...] = dot(hidden_one, grad_two, NT)
        g_b_one_ref[...] = jnp.sum(grad_one.astype(f32), axis=1, keepdims=True)
        g_b_two_ref[...] = jnp.sum(grad_two.astype(f32), axis=1, keepdims=True)
        g_w_three_ref[...] = jnp.sum(active_two * grad_logits, axis=1, keepdims=True)
        g_bias_ref[...] = jnp.broadcast_to(
            jnp.sum(grad_logits, axis=1, keepdims=True), g_bias_ref.shape
        )


def dense_step(tower_at, total_weight, pooled, labels, weights, params):
    micro_count = pooled.shape[0]
    width = micro_count * LANES
    cin_w, cin_u, w_one, b_one, w_two, b_two, w_three, bias = params
    in_vmem = pl.BlockSpec(memory_space=pltpu.VMEM)
    in_smem = pl.BlockSpec(memory_space=pltpu.SMEM)
    f32 = jnp.float32
    shapes = [
        ((micro_count, BAG_ROWS, WIDE), f32),
        ((1, LANES), f32),
        ((MAPS, PAIRS), f32),
        ((MAPS, 1), f32),
        ((EMB * FPAD, HID), f32),
        ((HID, 1), f32),
        ((HID, HID), f32),
        ((HID, 1), f32),
        ((HID, 1), f32),
        ((1, LANES), f32),
    ]
    return pl.pallas_call(
        partial(dense_kernel, micro_count),
        in_specs=[in_smem, in_smem] + [in_vmem] * 11,
        out_specs=[in_vmem] * len(shapes),
        out_shape=[jax.ShapeDtypeStruct(*shape) for shape in shapes],
        scratch_shapes=[
            pltpu.VMEM((EMB * FPAD, width), f32),
            pltpu.VMEM((PAIRS, width), f32),
            pltpu.VMEM((micro_count, FPAD * FPAD, LANES), f32),
            pltpu.VMEM((PAIRS, width), f32),
        ],
        compiler_params=pltpu.CompilerParams(vmem_limit_bytes=60 << 20),
        name="dense",
    )(
        tower_at.reshape(1), total_weight.reshape(1), pooled, labels, weights,
        cin_w, cin_u, w_one, b_one, w_two, b_two, w_three, bias,
    )


def unpack(flat):
    amounts = [MAPS * FIELDS * FIELDS, MAPS, FIELDS * EMB * HID, HID, HID * HID, HID, HID, 1]
    pieces = []
    offset = 0
    for amount in amounts:
        pieces.append(flat[offset : offset + amount])
        offset += amount
    cin_w = pieces[0].reshape(MAPS, FIELDS, FIELDS)
    cin_w = jnp.pad(cin_w, ((0, 0), (0, 0), (0, FPAD - FIELDS))).reshape(MAPS, PAIRS)
    w_one = jnp.swapaxes(pieces[2].reshape(FIELDS, EMB, HID), 0, 1)
    w_one = jnp.pad(w_one, ((0, 0), (0, FPAD - FIELDS), (0, 0))).reshape(EMB * FPAD, HID)
    return (
        cin_w,
        pieces[1].reshape(MAPS, 1),
        w_one,
        pieces[3].reshape(HID, 1),
        pieces[4].reshape(HID, HID),
        pieces[5].reshape(HID, 1),
        pieces[6].reshape(HID, 1),
        pieces[7].reshape(1, 1),
    )


def shards(
    shard_ids,
    local_rows,
    bag_counts,
    click_labels,
    sample_weights,
    embed_table,
    table_first,
    table_second,
    dense_params,
    dense_first,
    dense_second,
):
    tower_count = lax.axis_size("tower")
    batch_count = lax.axis_size("batch")
    tower_at = lax.axis_index("tower")
    micro_count, samples = shard_ids.shape[:2]
    columns, rows_dev = embed_table.shape
    capacity = 4 * samples * IDS_SAMP // (tower_count * batch_count)
    share = dense_params.shape[0]
    padded = -(-share // 1024) * 1024
    half_size = share * batch_count

    gathered = lax.all_gather(
        jnp.pad(dense_params.astype(jnp.bfloat16), (0, padded - share)),
        ("tower", "batch"),
        axis=0,
        tiled=True,
    )
    total_weight = lax.psum(jnp.sum(sample_weights.astype(jnp.float32)), "batch")

    id_count = samples * IDS_SAMP
    id_rows = -(-id_count // (8 * LANES)) * 8

    def arranged(values, filler):
        flat = values.reshape(micro_count, id_count)
        flat = jnp.pad(
            flat, ((0, 0), (0, id_rows * LANES - id_count)), constant_values=filler
        )
        return flat.reshape(micro_count, id_rows, LANES)

    bag_ends = jnp.cumsum(bag_counts, axis=-1)
    positions = jnp.arange(IDS_SAMP, dtype=jnp.int32)
    field_of = jnp.sum(
        (positions[None, None, :, None] >= bag_ends[:, :, None, :]).astype(jnp.int32), axis=-1
    )
    sample_of = jnp.arange(samples, dtype=jnp.int32)[None, :, None]
    is_late = (field_of >= HALF).astype(jnp.int32)
    lane_codes = arranged(sample_of + LANES * is_late, 0)
    half_fields = arranged(field_of - HALF * is_late, 0)
    targets = arranged(
        jnp.where(
            shard_ids // batch_count == tower_at, shard_ids % batch_count, batch_count
        ),
        batch_count,
    )
    requests, codes, halves = route(
        targets, arranged(local_rows, 0), lane_codes, half_fields, capacity, batch_count
    )
    requests, codes, halves = (jnp.swapaxes(x, 0, 1) for x in (requests, codes, halves))

    tiles = rows_dev // LANES
    table_tiles = jnp.swapaxes(
        embed_table.astype(jnp.bfloat16).reshape(columns, tiles, LANES), 1, 2
    ).reshape(columns * LANES, tiles)

    served = lax.all_to_all(requests, "batch", split_axis=0, concat_axis=0, tiled=True)
    answers = lax.all_to_all(
        lookup(served, table_tiles), "batch", split_axis=0, concat_axis=0, tiled=True
    )
    pooled = lax.psum(pool(answers, codes, halves, capacity, micro_count), "tower")

    def in_lanes(values):
        values = jnp.pad(values.astype(jnp.float32), ((0, 0), (0, LANES - samples)))
        return values.reshape(1, micro_count * LANES)

    flat = gathered.reshape(-1, padded)[:, :share].reshape(-1)
    (
        grad_bags, loss, g_cin_w, g_cin_u, g_w_one, g_b_one, g_w_two, g_b_two, g_w_three, g_bias,
    ) = dense_step(
        tower_at, total_weight, pooled, in_lanes(click_labels), in_lanes(sample_weights),
        unpack(flat),
    )
    sendable = spread(grad_bags.astype(jnp.bfloat16), codes, halves, capacity)
    delivered = lax.all_to_all(sendable, "batch", split_axis=0, concat_axis=0, tiled=True)
    table_grad = scatter_rows(delivered, served, columns, rows_dev)

    g_w_one = jnp.swapaxes(
        g_w_one.reshape(EMB, FPAD, HID)[:, :FIELDS], 0, 1
    ).reshape(-1)
    head = half_size - MAPS * FIELDS * FIELDS - MAPS
    rest = half_size - (FIELDS * EMB * HID - head) - HID - HID * HID - HID - HID - 1

    def pack_cin():
        flat_w = g_cin_w.reshape(MAPS, FIELDS, FPAD)[:, :, :FIELDS].reshape(-1)
        return jnp.concatenate([flat_w, g_cin_u.reshape(-1), g_w_one[:head]])

    def pack_deep():
        return jnp.concatenate(
            [
                g_w_one[head:], g_b_one.reshape(-1), g_w_two.reshape(-1), g_b_two.reshape(-1),
                g_w_three.reshape(-1), g_bias[0, :1], jnp.zeros((rest,), jnp.float32),
            ]
        )

    packed = lax.cond(tower_at == 0, pack_cin, pack_deep)
    packed = jnp.pad(packed.reshape(batch_count, share), ((0, 0), (0, padded - share)))
    own_grad = lax.psum_scatter(
        packed.reshape(-1, LANES), "batch", scatter_dimension=0, tiled=True
    ).reshape(-1)[:share]

    table_new, table_first_new, table_second_new = adam_update(
        embed_table, table_first, table_second, table_grad, rate_table
    )
    dense_new, dense_first_new, dense_second_new = adam_update(
        dense_params, dense_first, dense_second, own_grad, rate_dense
    )
    loss_sum = lax.psum(loss[0, 0], "batch") / total_weight
    return (
        table_new,
        table_first_new,
        table_second_new,
        table_new.astype(jnp.bfloat16),
        dense_new,
        dense_first_new,
        dense_second_new,
        dense_new.astype(jnp.bfloat16),
        loss_sum,
    )


def solution(mesh):
    rows = P(None, ("tower", "batch"))
    dense = P(("tower", "batch"))
    placed = (
        P(None, "batch", None, None),
        P(None, "batch", None, None),
        P(None, "batch", None),
        P(None, "batch"),
        P(None, "batch"),
        rows,
        rows,
        rows,
        dense,
        dense,
        dense,
    )
    return jax.shard_map(
        shards,
        mesh=mesh,
        in_specs=placed,
        out_specs=(rows, rows, rows, rows, dense, dense, dense, dense, P()),
        check_vma=False,
    )
```

```python
from functools import partial

import jax
import jax.numpy as jnp
from jax import lax
from jax.experimental import pallas as pl
from jax.experimental.pallas import tpu as pltpu
from jax.sharding import PartitionSpec as P

FIELDS = 39
EMB = 10
MAPS = 200
HID = 400
IDS_SAMP = 80

beta_one = 0.9
beta_two = 0.999
epsilon = 1e-08
decay_rate = 0.15
rate_table = 0.1
rate_dense = 0.05
step_count = 10

LANES = 128
WIDE = 256
BROAD = 512
TALL = 64
HALF = 24
BAG_ROWS = EMB * HALF + 8
FPAD = 40
PAIRS = FIELDS * FPAD
NT = (((1,), (1,)), ((), ()))
TN = (((0,), (0,)), ((), ()))
NN = (((1,), (0,)), ((), ()))


def adam_update(weight, first_old, second_old, gradient, step_rate):
    first_new = beta_one * first_old + (1.0 - beta_one) * gradient
    second_new = beta_two * second_old + (1.0 - beta_two) * gradient * gradient
    first_hat = first_new / (1.0 - beta_one**step_count)
    second_hat = second_new / (1.0 - beta_two**step_count)
    weight_new = weight - step_rate * (
        first_hat / (jnp.sqrt(second_hat) + epsilon) + decay_rate * weight
    )
    return (weight_new, first_new, second_new)


def dot(a, b, dims=NN):
    return lax.dot_general(a, b, dims, preferred_element_type=jnp.float32)


def iota(shape, dim):
    return lax.broadcasted_iota(jnp.int32, shape, dim)


def ones_at(mask):
    return jnp.where(mask, 1.0, 0.0).astype(jnp.bfloat16)


def layout_of(micro_count, capacity):
    first_rows = [m * capacity // WIDE for m in range(micro_count)]
    shifts = [m * capacity % WIDE for m in range(micro_count)]
    window = max(-(-(shift + capacity) // WIDE) for shift in shifts)
    return first_rows, shifts, window, max(first_rows) + window


def route_kernel(
    capacity, batch_count, micro_count, ids_ref, rows_ref, lanes_ref, field_ref,
    req_ref, code_ref, half_ref, slot_ref, left_ref, right_ref,
):
    first_rows, shifts, window, rows_msg = layout_of(micro_count, capacity)
    micro = pl.program_id(0)
    id_rows = ids_ref.shape[1]
    chunk = 16
    target = ids_ref[0]

    @pl.when(micro == 0)
    def _():
        req_ref[...] = jnp.zeros_like(req_ref)
        code_ref[...] = jnp.zeros_like(code_ref)
        half_ref[...] = jnp.zeros_like(half_ref)

    earlier_rows = ones_at(iota((id_rows, id_rows), 1) < iota((id_rows, id_rows), 0))
    upper = iota((2 * LANES, LANES), 0)
    mixing = ones_at((upper < iota((2 * LANES, LANES), 1)) | (upper >= LANES))
    rank = jnp.zeros((id_rows, LANES), jnp.float32)
    for begin in range(0, batch_count, chunk):
        hots = [ones_at(target == begin + d) for d in range(chunk)]
        above = dot(earlier_rows, jnp.concatenate(hots, axis=1)).astype(jnp.bfloat16)
        stacked = jnp.concatenate(
            [
                jnp.concatenate([hots[d], above[:, d * LANES : (d + 1) * LANES]], axis=1)
                for d in range(chunk)
            ],
            axis=0,
        )
        ranks = dot(stacked, mixing)
        for d in range(chunk):
            rank = rank + jnp.where(
                target == begin + d, ranks[d * id_rows : (d + 1) * id_rows], 0.0
            )
    shift = sum(jnp.where(micro == m, shifts[m], 0) for m in range(micro_count))
    place = rank.astype(jnp.int32) + shift
    slot_ref[0] = jnp.where(target < batch_count, (place // WIDE) * batch_count + target, -1)
    slot_ref[1] = place % WIDE
    places = window * batch_count

    def build(t, carry):
        here = pl.ds(t, 1)
        span = pl.ds(pl.multiple_of(t * LANES, LANES), LANES)
        mask = iota((places, LANES), 0) == slot_ref[0, here, :]
        row = rows_ref[0, here, :]
        values = [row // WIDE, row % WIDE, lanes_ref[0, here, :] + 1, field_ref[0, here, :]]
        for v in range(4):
            value = values[v].astype(jnp.float32)
            left_ref[v * places : (v + 1) * places, span] = jnp.where(mask, value, 0.0).astype(
                jnp.bfloat16
            )
        right_ref[:, span] = ones_at(iota((WIDE, LANES), 0) == slot_ref[1, here, :])
        return carry

    lax.fori_loop(0, id_rows, build, 0)
    placed = dot(left_ref[...], right_ref[...], NT)

    def part(v, r):
        return placed[(v * window + r) * batch_count : (v * window + r + 1) * batch_count].astype(
            jnp.int32
        )

    for m in range(micro_count):

        @pl.when(micro == m)
        def _():
            for r in range(window):
                code = part(2, r)
                at = first_rows[m] + r
                req_ref[at] += part(0, r) * WIDE + part(1, r)
                code_ref[at] += jnp.where(code > 0, code + m * WIDE, 0)
                half_ref[at] += part(3, r)


def route(targets, rows, lane_codes, half_fields, capacity, batch_count):
    micro_count, id_rows, _ = targets.shape
    _, _, window, rows_msg = layout_of(micro_count, capacity)
    block = pl.BlockSpec((1, id_rows, LANES), lambda m: (m, 0, 0))
    whole = pl.BlockSpec((rows_msg, batch_count, WIDE), lambda m: (0, 0, 0))
    shape = jax.ShapeDtypeStruct((rows_msg, batch_count, WIDE), jnp.int32)
    return pl.pallas_call(
        partial(route_kernel, capacity, batch_count, micro_count),
        grid=(micro_count,),
        in_specs=[block] * 4,
        out_specs=[whole] * 3,
        out_shape=[shape] * 3,
        scratch_shapes=[
            pltpu.VMEM((2, id_rows, LANES), jnp.int32),
            pltpu.VMEM((4 * window * batch_count, id_rows * LANES), jnp.bfloat16),
            pltpu.VMEM((WIDE, id_rows * LANES), jnp.bfloat16),
        ],
        compiler_params=pltpu.CompilerParams(vmem_limit_bytes=60 << 20),
        name="route",
    )(targets, rows, lane_codes, half_fields)


def peer_copy(src, dst, send_sem, recv_sem, peer):
    return pltpu.make_async_remote_copy(
        src_ref=src,
        dst_ref=dst,
        send_sem=send_sem,
        recv_sem=recv_sem,
        device_id={"batch": peer},
        device_id_type=pl.DeviceIdType.MESH,
    )


def greet(me, batch_count, other_tower=None):
    barrier = pltpu.get_barrier_semaphore()

    def signal(i, carry):
        pl.semaphore_signal(
            barrier,
            inc=1,
            device_id={"batch": lax.rem(me + i, batch_count)},
            device_id_type=pl.DeviceIdType.MESH,
        )
        return carry

    lax.fori_loop(1, batch_count, signal, 0)
    if other_tower is not None:
        pl.semaphore_signal(
            barrier,
            inc=1,
            device_id={"tower": other_tower},
            device_id_type=pl.DeviceIdType.MESH,
        )
    pl.semaphore_wait(barrier, batch_count - (1 if other_tower is None else 0))


def pick_rows(result, mask, depth, columns):
    width = result.shape[1]
    out = jnp.zeros((16, width), jnp.float32)
    for c in range(columns):
        row = jnp.sum(
            jnp.where(mask, result[c * depth : (c + 1) * depth], 0.0), axis=0, keepdims=True
        )
        out = jnp.where(iota((16, width), 0) == c, row, out)
    return out


def tile_table(table_ref, tiles_ref, stage_ref, columns):
    for c in range(columns):
        for q in range(TALL):
            stage_ref[q : q + 1, :] = table_ref[c : c + 1, q * BROAD : (q + 1) * BROAD]
        tiles_ref[c * TALL : (c + 1) * TALL, :] = stage_ref[...].astype(jnp.bfloat16)


def fetch_kernel(
    capacity, micro_count, batch_count, columns,
    req_ref, code_ref, half_ref, table_ref, stat_ref,
    out_ref, served_ref, stat_out_ref,
    tiles_ref, stage_ref, ans_out_ref, ans_in_ref, left_ref, pooled_ref, other_ref, stat_in_ref,
    req_send, req_recv, ans_send, ans_recv, stat_send, stat_recv, pair_send, pair_recv,
):
    first_rows, _, window, rows_msg = layout_of(micro_count, capacity)
    me = lax.axis_index("batch")
    other_tower = 1 - lax.axis_index("tower")
    greet(me, batch_count, other_tower)

    def request_copy(peer, slot):
        return peer_copy(
            req_ref.at[peer], served_ref.at[slot], req_send.at[peer], req_recv.at[slot], peer
        )

    def stat_copy(peer, slot):
        return peer_copy(stat_ref, stat_in_ref.at[slot], stat_send.at[peer], stat_recv.at[slot], peer)

    def answer_copy(peer, slot):
        return peer_copy(
            ans_out_ref.at[peer], ans_in_ref.at[slot], ans_send.at[peer], ans_recv.at[slot], peer
        )

    def own_copy():
        return pltpu.make_async_copy(ans_out_ref.at[me], ans_in_ref.at[me], ans_recv.at[me])

    def send_requests(i, carry):
        peer = lax.rem(me + i, batch_count)
        request_copy(peer, me).start()
        stat_copy(peer, me).start()
        return carry

    lax.fori_loop(1, batch_count, send_requests, 0)
    served_ref[me] = req_ref[me]
    stat_in_ref[me] = stat_ref[...]
    tile_table(table_ref, tiles_ref, stage_ref, columns)
    pooled_ref[...] = jnp.zeros_like(pooled_ref)

    def look_up(first, second):
        def step(r, carry):
            here = pl.ds(r, 1)
            row = jnp.concatenate([served_ref[first, here, :], served_ref[second, here, :]], axis=1)
            hot = ones_at(iota((BROAD, 2 * WIDE), 0) == row % BROAD)
            result = dot(tiles_ref[...], hot)
            mask = iota((TALL, 2 * WIDE), 0) == row // BROAD
            block = pick_rows(result, mask, TALL, columns).astype(jnp.bfloat16)
            span = pl.ds(pl.multiple_of(r * WIDE, WIDE), WIDE)
            ans_out_ref[first, :, span] = block[:, :WIDE]
            ans_out_ref[second, :, span] = block[:, WIDE:]
            return carry

        lax.fori_loop(0, rows_msg, step, 0)

    def pool(owner):
        for r in range(rows_msg):
            span = slice(r * WIDE, (r + 1) * WIDE)
            values = ans_in_ref[owner, :, span].astype(jnp.float32)
            mask = iota((HALF, WIDE), 0) == half_ref[owner, r : r + 1, :]
            pieces = [jnp.where(mask, values[c : c + 1], 0.0) for c in range(EMB)]
            pieces.append(jnp.where(iota((8, WIDE), 0) == 0, values[EMB : EMB + 1], 0.0))
            left_ref[:, span] = jnp.concatenate(pieces, axis=0).astype(jnp.bfloat16)
        for m in range(micro_count):
            rights = [
                ones_at(iota((WIDE, WIDE), 0) + (m * WIDE + 1) == code_ref[owner, r : r + 1, :])
                for r in range(first_rows[m], first_rows[m] + window)
            ]
            span = slice(first_rows[m] * WIDE, (first_rows[m] + window) * WIDE)
            pooled_ref[m] += dot(left_ref[:, span], jnp.concatenate(rights, axis=1), NT)

    pairs = batch_count // 2
    lag = 2

    def step(j, carry):
        @pl.when(j < pairs)
        def _():
            first = lax.rem(me + batch_count - (2 * j + 1), batch_count)
            second = lax.rem(me + 2 * batch_count - (2 * j + 2), batch_count)
            request_copy(first, first).wait_recv()

            @pl.when(j < pairs - 1)
            def _():
                request_copy(second, second).wait_recv()

            look_up(first, second)
            answer_copy(first, me).start()

            @pl.when(j < pairs - 1)
            def _():
                answer_copy(second, me).start()

            @pl.when(j == pairs - 1)
            def _():
                own_copy().start()

        @pl.when(j >= lag)
        def _():
            first = lax.rem(me + 2 * (j - lag) + 1, batch_count)
            answer_copy(first, first).wait_recv()
            pool(first)

        @pl.when((j >= lag) & (j < pairs - 1 + lag))
        def _():
            second = lax.rem(me + 2 * (j - lag) + 2, batch_count)
            answer_copy(second, second).wait_recv()
            pool(second)

        return carry

    lax.fori_loop(0, pairs + lag, step, 0)
    own_copy().wait()
    pool(me)

    pair = pltpu.make_async_remote_copy(
        src_ref=pooled_ref,
        dst_ref=other_ref,
        send_sem=pair_send,
        recv_sem=pair_recv,
        device_id={"tower": other_tower},
        device_id_type=pl.DeviceIdType.MESH,
    )
    pair.start()

    def finish(i, carry):
        peer = lax.rem(me + i, batch_count)
        request_copy(peer, me).wait_send()
        stat_copy(peer, me).wait_send()
        answer_copy(peer, me).wait_send()
        stat_copy(peer, peer).wait_recv()
        return carry

    lax.fori_loop(1, batch_count, finish, 0)
    stat_out_ref[...] = jnp.sum(stat_in_ref[...], axis=0)
    pair.wait()
    out_ref[...] = pooled_ref[...] + other_ref[...]


def fetch(requests, codes, halves, table, stat, capacity, micro_count):
    batch_count, rows_msg, _ = requests.shape
    columns, rows_dev = table.shape
    slots = rows_msg * WIDE
    in_vmem = pl.BlockSpec(memory_space=pltpu.VMEM)
    dma = pltpu.SemaphoreType.DMA
    bags = (micro_count, BAG_ROWS, WIDE)
    return pl.pallas_call(
        partial(fetch_kernel, capacity, micro_count, batch_count, columns),
        in_specs=[in_vmem] * 5,
        out_specs=[in_vmem] * 3,
        out_shape=[
            jax.ShapeDtypeStruct(bags, jnp.float32),
            jax.ShapeDtypeStruct(requests.shape, jnp.int32),
            jax.ShapeDtypeStruct(stat.shape, jnp.float32),
        ],
        scratch_shapes=[
            pltpu.VMEM((columns * TALL, BROAD), jnp.bfloat16),
            pltpu.VMEM((TALL, BROAD), jnp.float32),
            pltpu.VMEM((batch_count, 16, slots), jnp.bfloat16),
            pltpu.VMEM((batch_count, 16, slots), jnp.bfloat16),
            pltpu.VMEM((BAG_ROWS, slots), jnp.bfloat16),
            pltpu.VMEM(bags, jnp.float32),
            pltpu.VMEM(bags, jnp.float32),
            pltpu.VMEM((batch_count,) + stat.shape, jnp.float32),
        ]
        + [dma((batch_count,))] * 6
        + [dma, dma],
        compiler_params=pltpu.CompilerParams(
            vmem_limit_bytes=60 << 20, collective_id=0, has_side_effects=True
        ),
        name="fetch",
    )(requests, codes, halves, table, stat)


def return_kernel(
    capacity, micro_count, batch_count, columns,
    grad_ref, code_ref, half_ref, served_ref, stat_ref,
    out_ref, stat_out_ref,
    send_ref, recv_ref, left_ref, right_ref, total_ref, stat_in_ref,
    val_send, val_recv, stat_send, stat_recv,
):
    first_rows, _, window, rows_msg = layout_of(micro_count, capacity)
    me = lax.axis_index("batch")
    greet(me, batch_count)

    def value_copy(peer, slot):
        return peer_copy(
            send_ref.at[peer], recv_ref.at[slot], val_send.at[peer], val_recv.at[slot], peer
        )

    def own_copy():
        return pltpu.make_async_copy(send_ref.at[me], recv_ref.at[me], val_recv.at[me])

    def stat_copy(peer, slot):
        return peer_copy(stat_ref, stat_in_ref.at[slot], stat_send.at[peer], stat_recv.at[slot], peer)

    def send_stats(i, carry):
        stat_copy(lax.rem(me + i, batch_count), me).start()
        return carry

    lax.fori_loop(1, batch_count, send_stats, 0)
    stat_in_ref[me] = stat_ref[...]
    total_ref[...] = jnp.zeros_like(total_ref)

    def spread(first, second):
        for r in range(rows_msg):
            code = jnp.concatenate(
                [code_ref[first, r : r + 1, :], code_ref[second, r : r + 1, :]], axis=1
            )
            half = jnp.concatenate(
                [half_ref[first, r : r + 1, :], half_ref[second, r : r + 1, :]], axis=1
            )
            result = None
            for m in range(micro_count):
                if first_rows[m] <= r < first_rows[m] + window:
                    hot = ones_at(iota((WIDE, 2 * WIDE), 0) + (m * WIDE + 1) == code)
                    found = dot(grad_ref[m], hot)
                    result = found if result is None else result + found
            block = pick_rows(result, iota((HALF, 2 * WIDE), 0) == half, HALF, EMB)
            linear = result[EMB * HALF : EMB * HALF + 1]
            block = jnp.where(iota((16, 2 * WIDE), 0) == EMB, linear, block).astype(jnp.bfloat16)
            span = slice(r * WIDE, (r + 1) * WIDE)
            send_ref[first, :, span] = block[:, :WIDE]
            send_ref[second, :, span] = block[:, WIDE:]

    def scatter(source):
        for r in range(rows_msg):
            span = slice(r * WIDE, (r + 1) * WIDE)
            row = served_ref[source, r : r + 1, :]
            values = recv_ref[source, :, span].astype(jnp.float32)
            mask = iota((TALL, WIDE), 0) == row // BROAD
            for c in range(columns):
                left_ref[c * TALL : (c + 1) * TALL, span] = jnp.where(
                    mask, values[c : c + 1], 0.0
                ).astype(jnp.bfloat16)
            right_ref[:, span] = ones_at(iota((BROAD, WIDE), 0) == row % BROAD)
        total_ref[...] += dot(left_ref[...], right_ref[...], NT)

    pairs = batch_count // 2
    lag = 2

    def step(j, carry):
        @pl.when(j < pairs)
        def _():
            first = lax.rem(me + 2 * j + 1, batch_count)
            second = lax.rem(me + 2 * j + 2, batch_count)
            spread(first, second)
            value_copy(first, me).start()

            @pl.when(j < pairs - 1)
            def _():
                value_copy(second, me).start()

            @pl.when(j == pairs - 1)
            def _():
                own_copy().start()

        @pl.when(j >= lag)
        def _():
            first = lax.rem(me + batch_count - (2 * (j - lag) + 1), batch_count)
            value_copy(first, first).wait_recv()
            scatter(first)

        @pl.when((j >= lag) & (j < pairs - 1 + lag))
        def _():
            second = lax.rem(me + 2 * batch_count - (2 * (j - lag) + 2), batch_count)
            value_copy(second, second).wait_recv()
            scatter(second)

        return carry

    lax.fori_loop(0, pairs + lag, step, 0)
    own_copy().wait()
    scatter(me)

    def finish(i, carry):
        peer = lax.rem(me + i, batch_count)
        value_copy(peer, me).wait_send()
        stat_copy(peer, me).wait_send()
        stat_copy(peer, peer).wait_recv()
        return carry

    lax.fori_loop(1, batch_count, finish, 0)
    stat_out_ref[...] = jnp.sum(stat_in_ref[...], axis=0)
    for c in range(columns):
        for q in range(TALL):
            out_ref[c : c + 1, q * BROAD : (q + 1) * BROAD] = total_ref[
                c * TALL + q : c * TALL + q + 1, :
            ]


def return_grads(grad_bags, codes, halves, served, stat, capacity, columns):
    batch_count, rows_msg, _ = codes.shape
    micro_count = grad_bags.shape[0]
    slots = rows_msg * WIDE
    in_vmem = pl.BlockSpec(memory_space=pltpu.VMEM)
    dma = pltpu.SemaphoreType.DMA
    return pl.pallas_call(
        partial(return_kernel, capacity, micro_count, batch_count, columns),
        in_specs=[in_vmem] * 5,
        out_specs=[in_vmem] * 2,
        out_shape=[
            jax.ShapeDtypeStruct((columns, TALL * BROAD), jnp.float32),
            jax.ShapeDtypeStruct(stat.shape, jnp.float32),
        ],
        scratch_shapes=[
            pltpu.VMEM((batch_count, 16, slots), jnp.bfloat16),
            pltpu.VMEM((batch_count, 16, slots), jnp.bfloat16),
            pltpu.VMEM((columns * TALL, slots), jnp.bfloat16),
            pltpu.VMEM((BROAD, slots), jnp.bfloat16),
            pltpu.VMEM((columns * TALL, BROAD), jnp.float32),
            pltpu.VMEM((batch_count,) + stat.shape, jnp.float32),
        ]
        + [dma((batch_count,))] * 4,
        compiler_params=pltpu.CompilerParams(
            vmem_limit_bytes=60 << 20, collective_id=1, has_side_effects=True
        ),
        name="return_grads",
    )(grad_bags, codes, halves, served, stat)


def split_three(x):
    high = x.astype(jnp.bfloat16)
    rest = x - high.astype(jnp.float32)
    middle = rest.astype(jnp.bfloat16)
    low = (rest - middle.astype(jnp.float32)).astype(jnp.bfloat16)
    return high, middle, low


def dense_kernel(
    micro_count, tower_ref, scale_ref, pooled_ref, label_ref, weight_ref,
    cin_w_ref, cin_u_ref, w_one_ref, b_one_ref, w_two_ref, b_two_ref, w_three_ref, bias_ref,
    bags_ref, loss_ref, g_cin_w_ref, g_cin_u_ref, g_w_one_ref, g_b_one_ref, g_w_two_ref,
    g_b_two_ref, g_w_three_ref, g_bias_ref,
    embed_ref, total_ref, pairs_ref, sym_ref,
):
    f32 = jnp.float32
    width = micro_count * LANES

    def unpacked(row, count):
        pieces = []
        for m in range(micro_count):
            low = pooled_ref[m, row : row + HALF, :LANES]
            high = pooled_ref[m, row : row + HALF, LANES:]
            pieces.append(jnp.concatenate([low, high], axis=0)[:count])
        return jnp.concatenate(pieces, axis=1)

    for d in range(EMB):
        embed_ref[d * FPAD : (d + 1) * FPAD, :] = unpacked(d * HALF, FPAD)
    linear = jnp.concatenate(
        [
            pooled_ref[m, EMB * HALF : EMB * HALF + 1, :LANES]
            + pooled_ref[m, EMB * HALF : EMB * HALF + 1, LANES:]
            for m in range(micro_count)
        ],
        axis=1,
    )

    def pair_row(i, carry):
        total = jnp.zeros((FPAD, width), f32)
        for d in range(EMB):
            own = embed_ref[pl.ds(d * FPAD + i, 1), :]
            product = (embed_ref[d * FPAD : (d + 1) * FPAD, :] * own).astype(jnp.bfloat16)
            total = total + product.astype(f32)
        total_ref[pl.ds(pl.multiple_of(i * FPAD, 8), FPAD), :] = total
        return carry

    lax.fori_loop(0, FIELDS, pair_row, 0)
    thirds = split_three(total_ref[...])
    cin_w = cin_w_ref[...]
    cin_u = cin_u_ref[...].astype(f32)
    map_sum = sum(dot(cin_w, third) for third in thirds)
    cin_logits = jnp.sum(map_sum * cin_u, axis=0, keepdims=True)

    flat = embed_ref[...].astype(jnp.bfloat16)
    pre_one = dot(w_one_ref[...], flat, TN) + b_one_ref[...].astype(f32)
    hidden_one = jnp.maximum(pre_one, 0.0).astype(jnp.bfloat16)
    pre_two = dot(w_two_ref[...], hidden_one, TN) + b_two_ref[...].astype(f32)
    active_two = jnp.maximum(pre_two, 0.0)
    w_three = w_three_ref[...].astype(f32)
    deep_logits = jnp.sum(active_two * w_three, axis=0, keepdims=True)
    logits = cin_logits + deep_logits + linear + bias_ref[...].astype(f32)

    weight = weight_ref[...]
    label = label_ref[...]
    soft = jnp.maximum(logits, 0.0) + jnp.log1p(jnp.exp(-jnp.abs(logits)))
    loss_ref[...] = jnp.broadcast_to(
        jnp.sum(weight * (soft - label * logits), axis=1, keepdims=True), loss_ref.shape
    )
    grad_logits = weight * (jax.nn.sigmoid(logits) - label) / scale_ref[0]

    grad_maps = (grad_logits * cin_u).astype(jnp.bfloat16)
    grad_two = jnp.where(pre_two > 0, grad_logits * w_three, 0.0).astype(jnp.bfloat16)
    grad_hidden = dot(w_two_ref[...], grad_two)
    grad_one = jnp.where(pre_one > 0, grad_hidden, 0.0).astype(jnp.bfloat16)
    grad_flat = dot(w_one_ref[...], grad_one)

    grad_pairs = dot(cin_w, grad_maps, TN)
    for m in range(micro_count):
        pairs_ref[m, :PAIRS, :] = grad_pairs[:, m * LANES : (m + 1) * LANES]
        pairs_ref[m, PAIRS:, :] = jnp.zeros((FPAD * FPAD - PAIRS, LANES), f32)

    def mirror(j, carry):
        here = pl.ds(pl.multiple_of(j * FPAD, 8), FPAD)
        both = [
            pairs_ref[m, here, :] + pairs_ref[m, pl.ds(j, FPAD, stride=FPAD), :]
            for m in range(micro_count)
        ]
        sym_ref[here, :] = jnp.concatenate(both, axis=1)
        return carry

    lax.fori_loop(0, FIELDS, mirror, 0)
    empty = jnp.zeros((2 * HALF - FPAD, width), f32)

    for d in range(EMB):

        def add_row(j, total):
            here = pl.ds(pl.multiple_of(j * FPAD, 8), FPAD)
            return total + sym_ref[here, :] * embed_ref[pl.ds(d * FPAD + j, 1), :]

        grad_embed = lax.fori_loop(
            0, FIELDS, add_row, grad_flat[d * FPAD : (d + 1) * FPAD], unroll=3
        )
        grad_embed = jnp.concatenate([grad_embed, empty], axis=0)
        for m in range(micro_count):
            span = slice(m * LANES, (m + 1) * LANES)
            block = jnp.concatenate([grad_embed[:HALF, span], grad_embed[HALF:, span]], axis=1)
            bags_ref[m, d * HALF : (d + 1) * HALF, :] = block
    for m in range(micro_count):
        row = grad_logits[:, m * LANES : (m + 1) * LANES]
        row = jnp.concatenate([row, row], axis=1)
        bags_ref[m, EMB * HALF :, :] = jnp.broadcast_to(row, (8, WIDE))

    g_w_one_ref[...] = dot(flat, grad_one, NT)

    @pl.when(tower_ref[0] == 0)
    def _():
        g_cin_u_ref[...] = jnp.sum(map_sum * grad_logits, axis=1, keepdims=True)
        g_cin_w_ref[...] = sum(dot(grad_maps, third, NT) for third in thirds)

    @pl.when(tower_ref[0] != 0)
    def _():
        g_w_two_ref[...] = dot(hidden_one, grad_two, NT)
        g_b_one_ref[...] = jnp.sum(grad_one.astype(f32), axis=1, keepdims=True)
        g_b_two_ref[...] = jnp.sum(grad_two.astype(f32), axis=1, keepdims=True)
        g_w_three_ref[...] = jnp.sum(active_two * grad_logits, axis=1, keepdims=True)
        g_bias_ref[...] = jnp.broadcast_to(
            jnp.sum(grad_logits, axis=1, keepdims=True), g_bias_ref.shape
        )


def dense_step(tower_at, total_weight, pooled, labels, weights, params):
    micro_count = pooled.shape[0]
    width = micro_count * LANES
    cin_w, cin_u, w_one, b_one, w_two, b_two, w_three, bias = params
    in_vmem = pl.BlockSpec(memory_space=pltpu.VMEM)
    in_smem = pl.BlockSpec(memory_space=pltpu.SMEM)
    f32 = jnp.float32
    shapes = [
        ((micro_count, BAG_ROWS, WIDE), f32),
        ((1, LANES), f32),
        ((MAPS, PAIRS), f32),
        ((MAPS, 1), f32),
        ((EMB * FPAD, HID), f32),
        ((HID, 1), f32),
        ((HID, HID), f32),
        ((HID, 1), f32),
        ((HID, 1), f32),
        ((1, LANES), f32),
    ]
    return pl.pallas_call(
        partial(dense_kernel, micro_count),
        in_specs=[in_smem, in_smem] + [in_vmem] * 11,
        out_specs=[in_vmem] * len(shapes),
        out_shape=[jax.ShapeDtypeStruct(*shape) for shape in shapes],
        scratch_shapes=[
            pltpu.VMEM((EMB * FPAD, width), f32),
            pltpu.VMEM((PAIRS, width), f32),
            pltpu.VMEM((micro_count, FPAD * FPAD, LANES), f32),
            pltpu.VMEM((PAIRS, width), f32),
        ],
        compiler_params=pltpu.CompilerParams(vmem_limit_bytes=60 << 20),
        name="dense",
    )(
        tower_at.reshape(1), total_weight.reshape(1), pooled, labels, weights,
        cin_w, cin_u, w_one, b_one, w_two, b_two, w_three, bias,
    )


def unpack(flat):
    amounts = [MAPS * FIELDS * FIELDS, MAPS, FIELDS * EMB * HID, HID, HID * HID, HID, HID, 1]
    pieces = []
    offset = 0
    for amount in amounts:
        pieces.append(flat[offset : offset + amount])
        offset += amount
    cin_w = pieces[0].reshape(MAPS, FIELDS, FIELDS)
    cin_w = jnp.pad(cin_w, ((0, 0), (0, 0), (0, FPAD - FIELDS))).reshape(MAPS, PAIRS)
    w_one = jnp.swapaxes(pieces[2].reshape(FIELDS, EMB, HID), 0, 1)
    w_one = jnp.pad(w_one, ((0, 0), (0, FPAD - FIELDS), (0, 0))).reshape(EMB * FPAD, HID)
    return (
        cin_w,
        pieces[1].reshape(MAPS, 1),
        w_one,
        pieces[3].reshape(HID, 1),
        pieces[4].reshape(HID, HID),
        pieces[5].reshape(HID, 1),
        pieces[6].reshape(HID, 1),
        pieces[7].reshape(1, 1),
    )


def shards(
    shard_ids,
    local_rows,
    bag_counts,
    click_labels,
    sample_weights,
    embed_table,
    table_first,
    table_second,
    dense_params,
    dense_first,
    dense_second,
):
    tower_count = lax.axis_size("tower")
    batch_count = lax.axis_size("batch")
    tower_at = lax.axis_index("tower")
    micro_count, samples = shard_ids.shape[:2]
    columns, rows_dev = embed_table.shape
    capacity = 4 * samples * IDS_SAMP // (tower_count * batch_count)
    share = dense_params.shape[0]
    padded = -(-share // 1024) * 1024
    half_size = share * batch_count

    gathered = lax.all_gather(
        jnp.pad(dense_params.astype(jnp.bfloat16), (0, padded - share)),
        ("tower", "batch"),
        axis=0,
        tiled=True,
    )

    id_count = samples * IDS_SAMP
    id_rows = -(-id_count // (8 * LANES)) * 8

    def arranged(values, filler):
        flat = values.reshape(micro_count, id_count)
        flat = jnp.pad(
            flat, ((0, 0), (0, id_rows * LANES - id_count)), constant_values=filler
        )
        return flat.reshape(micro_count, id_rows, LANES)

    bag_ends = jnp.cumsum(bag_counts, axis=-1)
    positions = jnp.arange(IDS_SAMP, dtype=jnp.int32)
    field_of = jnp.sum(
        (positions[None, None, :, None] >= bag_ends[:, :, None, :]).astype(jnp.int32), axis=-1
    )
    sample_of = jnp.arange(samples, dtype=jnp.int32)[None, :, None]
    is_late = (field_of >= HALF).astype(jnp.int32)
    lane_codes = arranged(sample_of + LANES * is_late, 0)
    half_fields = arranged(field_of - HALF * is_late, 0)
    targets = arranged(
        jnp.where(
            shard_ids // batch_count == tower_at, shard_ids % batch_count, batch_count
        ),
        batch_count,
    )
    requests, codes, halves = route(
        targets, arranged(local_rows, 0), lane_codes, half_fields, capacity, batch_count
    )
    requests, codes, halves = (jnp.swapaxes(x, 0, 1) for x in (requests, codes, halves))

    weight_sum = jnp.sum(sample_weights.astype(jnp.float32))
    pooled, served, stats = fetch(
        requests, codes, halves, embed_table, jnp.full((8, LANES), weight_sum), capacity, micro_count
    )
    total_weight = stats[0, 0]

    def in_lanes(values):
        values = jnp.pad(values.astype(jnp.float32), ((0, 0), (0, LANES - samples)))
        return values.reshape(1, micro_count * LANES)

    flat = gathered.reshape(-1, padded)[:, :share].reshape(-1)
    (
        grad_bags, loss, g_cin_w, g_cin_u, g_w_one, g_b_one, g_w_two, g_b_two, g_w_three, g_bias,
    ) = dense_step(
        tower_at, total_weight, pooled, in_lanes(click_labels), in_lanes(sample_weights),
        unpack(flat),
    )
    table_grad, losses = return_grads(
        grad_bags.astype(jnp.bfloat16), codes, halves, served, jnp.broadcast_to(loss, (8, LANES)),
        capacity, columns,
    )

    g_w_one = jnp.swapaxes(
        g_w_one.reshape(EMB, FPAD, HID)[:, :FIELDS], 0, 1
    ).reshape(-1)
    head = half_size - MAPS * FIELDS * FIELDS - MAPS
    rest = half_size - (FIELDS * EMB * HID - head) - HID - HID * HID - HID - HID - 1

    def pack_cin():
        flat_w = g_cin_w.reshape(MAPS, FIELDS, FPAD)[:, :, :FIELDS].reshape(-1)
        return jnp.concatenate([flat_w, g_cin_u.reshape(-1), g_w_one[:head]])

    def pack_deep():
        return jnp.concatenate(
            [
                g_w_one[head:], g_b_one.reshape(-1), g_w_two.reshape(-1), g_b_two.reshape(-1),
                g_w_three.reshape(-1), g_bias[0, :1], jnp.zeros((rest,), jnp.float32),
            ]
        )

    packed = lax.cond(tower_at == 0, pack_cin, pack_deep)
    packed = jnp.pad(packed.reshape(batch_count, share), ((0, 0), (0, padded - share)))
    own_grad = lax.psum_scatter(
        packed.reshape(-1, LANES), "batch", scatter_dimension=0, tiled=True
    ).reshape(-1)[:share]

    table_new, table_first_new, table_second_new = adam_update(
        embed_table, table_first, table_second, table_grad, rate_table
    )
    dense_new, dense_first_new, dense_second_new = adam_update(
        dense_params, dense_first, dense_second, own_grad, rate_dense
    )
    loss_sum = losses[0, 0] / total_weight
    return (
        table_new,
        table_first_new,
        table_second_new,
        table_new.astype(jnp.bfloat16),
        dense_new,
        dense_first_new,
        dense_second_new,
        dense_new.astype(jnp.bfloat16),
        loss_sum,
    )


def solution(mesh):
    rows = P(None, ("tower", "batch"))
    dense = P(("tower", "batch"))
    placed = (
        P(None, "batch", None, None),
        P(None, "batch", None, None),
        P(None, "batch", None),
        P(None, "batch"),
        P(None, "batch"),
        rows,
        rows,
        rows,
        dense,
        dense,
        dense,
    )
    return jax.shard_map(
        shards,
        mesh=mesh,
        in_specs=placed,
        out_specs=(rows, rows, rows, rows, dense, dense, dense, dense, P()),
        check_vma=False,
    )
```

```python
from functools import partial

import jax
import jax.numpy as jnp
from jax import lax
from jax.experimental import pallas as pl
from jax.experimental.pallas import tpu as pltpu
from jax.sharding import PartitionSpec as P

FIELDS = 39
EMB = 10
MAPS = 200
HID = 400
IDS_SAMP = 80

beta_one = 0.9
beta_two = 0.999
epsilon = 1e-08
decay_rate = 0.15
rate_table = 0.1
rate_dense = 0.05
step_count = 10

LANES = 128
WIDE = 256
BROAD = 512
TALL = 64
HALF = 24
BAG_ROWS = EMB * HALF + 8
FPAD = 40
PAIRS = FIELDS * FPAD
SQUARE = FIELDS * FIELDS
CIN_SIZE = MAPS * SQUARE + MAPS
FLAT = EMB * FIELDS
B_ONE, W_TWO, B_TWO, W_THREE, BIAS = FLAT, FLAT + 1, FLAT + HID + 1, FLAT + HID + 2, FLAT + HID + 3
HPAD = 512
PLANE = 4
NT = (((1,), (1,)), ((), ()))
TN = (((0,), (0,)), ((), ()))
NN = (((1,), (0,)), ((), ()))


def adam_update(weight, first_old, second_old, gradient, step_rate):
    first_new = beta_one * first_old + (1.0 - beta_one) * gradient
    second_new = beta_two * second_old + (1.0 - beta_two) * gradient * gradient
    first_hat = first_new / (1.0 - beta_one**step_count)
    second_hat = second_new / (1.0 - beta_two**step_count)
    weight_new = weight - step_rate * (
        first_hat / (jnp.sqrt(second_hat) + epsilon) + decay_rate * weight
    )
    return (weight_new, first_new, second_new)


def dot(a, b, dims=NN):
    return lax.dot_general(a, b, dims, preferred_element_type=jnp.float32)


def iota(shape, dim):
    return lax.broadcasted_iota(jnp.int32, shape, dim)


def ones_at(mask):
    return jnp.where(mask, 1.0, 0.0).astype(jnp.bfloat16)


def layout_of(micro_count, capacity, size=WIDE):
    first_rows = [m * capacity // size for m in range(micro_count)]
    shifts = [m * capacity % size for m in range(micro_count)]
    window = max(-(-(shift + capacity) // WIDE) for shift in shifts)
    return first_rows, shifts, window, max(first_rows) + window


class Windows:
    def __init__(self, share, batch_count):
        self.share, self.batch_count = share, batch_count
        self.cin_rows = -(-(SQUARE - 1 + share) // SQUARE)
        self.rest_rows = -(-(HID - 1 + share) // HID)
        self.cin_pad = -(-self.cin_rows // 16) * 16
        self.rest_pad = -(-self.rest_rows // 16) * 16
        self.first_extra = CIN_SIZE // share
        self.extras = batch_count - self.first_extra
        self.cin_at = [b * share // SQUARE for b in range(batch_count)]
        self.rest_at = [
            ((batch_count + b) * share - CIN_SIZE) // HID for b in range(batch_count)
        ]
        self.extra_at = [
            (b * share - CIN_SIZE) // HID for b in range(self.first_extra, batch_count)
        ]
        depth = batch_count // PLANE
        self.slots = [b % PLANE * depth + b // PLANE for b in range(batch_count)]
        self.cin_total = -(-max(a + self.cin_rows for a in self.cin_at) // 8) * 8
        self.rest_total = -(-max(a + self.rest_rows for a in self.rest_at) // 8) * 8

    def phases(self, device):
        start = device * self.share
        return start % SQUARE, jnp.mod(start - CIN_SIZE, HID)


def bf16_iota(rows, width):
    return iota((rows, width), 0).astype(jnp.float32).astype(jnp.bfloat16)


def route_kernel(
    capacity, batch_count, micro_count, ids_ref, rows_ref, counts_ref,
    req_ref, code_ref, half_ref, part_ref, left_ref, right_ref,
):
    f32, bf16 = jnp.float32, jnp.bfloat16
    first_rows, shifts, window, _ = layout_of(micro_count, capacity, 2 * WIDE)
    rows_msg = req_ref.shape[1]
    micro = pl.program_id(0)
    id_rows, samples = ids_ref.shape[1:]
    chunk = 16
    tower = lax.axis_index("tower")

    @pl.when(micro == 0)
    def _():
        req_ref[...] = jnp.zeros_like(req_ref)
        code_ref[...] = jnp.zeros_like(code_ref)
        half_ref[...] = jnp.zeros_like(half_ref)
        part_ref[...] = jnp.zeros_like(part_ref)

    def widened(x, filler):
        part_ref[0, :, :samples] = x.astype(f32)
        inside = iota((id_rows, LANES), 1) < samples
        return jnp.where(inside, part_ref[0], filler)

    owner = ids_ref[0]
    target = widened(
        jnp.where(owner // batch_count == tower, owner % batch_count, batch_count), batch_count
    ).astype(jnp.int32)
    local = widened(rows_ref[0], 0.0).astype(jnp.int32)
    before = ones_at(iota((FIELDS, FIELDS), 1) <= iota((FIELDS, FIELDS), 0))
    ends = dot(before, counts_ref[0].astype(f32).astype(bf16)).astype(jnp.int32)
    field = jnp.zeros((id_rows, samples), jnp.int32)
    for f in range(FIELDS):
        field = field + jnp.where(iota((id_rows, samples), 0) >= ends[f : f + 1], 1, 0)
    field = widened(field, 0.0)
    late = jnp.where(field >= HALF, 1.0, 0.0)

    earlier_rows = ones_at(iota((id_rows, id_rows), 1) < iota((id_rows, id_rows), 0))
    upper = iota((2 * LANES, LANES), 0)
    mixing = ones_at((upper < iota((2 * LANES, LANES), 1)) | (upper >= LANES))
    rank = jnp.zeros((id_rows, LANES), f32)
    for begin in range(0, batch_count, chunk):
        hots = [ones_at(target == begin + d) for d in range(chunk)]
        above = dot(earlier_rows, jnp.concatenate(hots, axis=1)).astype(bf16)
        stacked = jnp.concatenate(
            [
                jnp.concatenate([hots[d], above[:, d * LANES : (d + 1) * LANES]], axis=1)
                for d in range(chunk)
            ],
            axis=0,
        )
        ranks = dot(stacked, mixing)
        for d in range(chunk):
            rank = rank + jnp.where(
                target == begin + d, ranks[d * id_rows : (d + 1) * id_rows], 0.0
            )
    shift = sum(jnp.where(micro == m, shifts[m], 0) for m in range(micro_count))
    slot = rank.astype(jnp.int32) + shift
    lane = slot % (2 * WIDE)
    place = jnp.where(target < batch_count, (slot // (2 * WIDE)) * batch_count + target, -1)
    part_ref[0] = place.astype(f32)
    part_ref[1] = jnp.where(lane < WIDE, lane, -1).astype(f32)
    part_ref[2] = jnp.where(lane < WIDE, -1, lane - WIDE).astype(f32)
    part_ref[3] = (local // WIDE).astype(f32)
    part_ref[4] = (local % WIDE).astype(f32)
    part_ref[5] = late * LANES + (iota((id_rows, LANES), 1) + 1).astype(f32)
    part_ref[6] = field - late * HALF
    places = window * batch_count
    one, zero = jnp.ones((), bf16), jnp.zeros((), bf16)

    def build(t, carry):
        span = pl.ds(pl.multiple_of(t * LANES, LANES), LANES)

        def row(k):
            return part_ref[k, pl.ds(t, 1), :].astype(bf16)

        mask = bf16_iota(places, LANES) == row(0)
        for v in range(4):
            left_ref[v * places : (v + 1) * places, span] = jnp.where(mask, row(3 + v), zero)
        for h in range(2):
            right_ref[h * WIDE : (h + 1) * WIDE, span] = jnp.where(
                bf16_iota(WIDE, LANES) == row(1 + h), one, zero
            )
        return carry

    lax.fori_loop(0, id_rows, build, 0, unroll=4)
    placed = dot(left_ref[...], right_ref[...], NT).astype(jnp.int32)

    def part(v, r, h):
        begin = (v * window + r) * batch_count
        return placed[begin : begin + batch_count, h * WIDE : (h + 1) * WIDE]

    for m in range(micro_count):

        @pl.when(micro == m)
        def _():
            for r in range(window):
                for h in range(2):
                    at = 2 * (first_rows[m] + r) + h
                    if at < rows_msg:
                        code = part(2, r, h)
                        req_ref[:, at, :] += part(0, r, h) * WIDE + part(1, r, h)
                        code_ref[:, at, :] += jnp.where(code > 0, code + m * WIDE, 0)
                        half_ref[:, at, :] += part(3, r, h)


def route(ids, rows, counts, capacity, batch_count):
    micro_count, id_rows, samples = ids.shape
    rows_msg = layout_of(micro_count, capacity)[3]
    places = layout_of(micro_count, capacity, 2 * WIDE)[2] * batch_count

    def block(x):
        return pl.BlockSpec((1,) + x.shape[1:], lambda m: (m, 0, 0))

    whole = pl.BlockSpec((batch_count, rows_msg, WIDE), lambda m: (0, 0, 0))
    shape = jax.ShapeDtypeStruct((batch_count, rows_msg, WIDE), jnp.int32)
    return pl.pallas_call(
        partial(route_kernel, capacity, batch_count, micro_count),
        grid=(micro_count,),
        in_specs=[block(ids), block(rows), block(counts)],
        out_specs=[whole] * 3,
        out_shape=[shape] * 3,
        scratch_shapes=[
            pltpu.VMEM((7, id_rows, LANES), jnp.float32),
            pltpu.VMEM((4 * places, id_rows * LANES), jnp.bfloat16),
            pltpu.VMEM((2 * WIDE, id_rows * LANES), jnp.bfloat16),
        ],
        compiler_params=pltpu.CompilerParams(vmem_limit_bytes=60 << 20),
        name="route",
    )(ids, rows, counts)


def peer_copy(src, dst, send_sem, recv_sem, peer):
    return pltpu.make_async_remote_copy(
        src_ref=src,
        dst_ref=dst,
        send_sem=send_sem,
        recv_sem=recv_sem,
        device_id={"batch": peer},
        device_id_type=pl.DeviceIdType.MESH,
    )


def greet(me, batch_count, other_tower=None):
    barrier = pltpu.get_barrier_semaphore()

    def signal(i, carry):
        pl.semaphore_signal(
            barrier,
            inc=1,
            device_id={"batch": lax.rem(me + i, batch_count)},
            device_id_type=pl.DeviceIdType.MESH,
        )
        return carry

    lax.fori_loop(1, batch_count, signal, 0)
    if other_tower is not None:
        pl.semaphore_signal(
            barrier,
            inc=1,
            device_id={"tower": other_tower},
            device_id_type=pl.DeviceIdType.MESH,
        )
    pl.semaphore_wait(barrier, batch_count - (1 if other_tower is None else 0))


def message_rows(rows_msg, columns):
    return -(-rows_msg * columns // 16) * 16


def each(count, action):
    def body(i, carry):
        action(i)
        return carry

    lax.fori_loop(1, count, body, 0)


def pick_rows(result, mask, depth, columns):
    width = result.shape[1]
    out = jnp.zeros((16, width), jnp.float32)
    for c in range(columns):
        row = jnp.sum(
            jnp.where(mask, result[c * depth : (c + 1) * depth], 0.0), axis=0, keepdims=True
        )
        out = jnp.where(iota((16, width), 0) == c, row, out)
    return out


def tile_table(table_ref, tiles_ref, stage_ref, columns):
    for c in range(columns):
        for q in range(TALL):
            stage_ref[q : q + 1, :] = table_ref[c : c + 1, q * BROAD : (q + 1) * BROAD]
        tiles_ref[c * TALL : (c + 1) * TALL, :] = stage_ref[...].astype(jnp.bfloat16)


def fetch_kernel(
    capacity, micro_count, windows, columns,
    req_ref, code_ref, half_ref, table_ref, weight_ref, cin_ref, rest_ref,
    out_ref, served_ref, stat_out_ref, cins_ref, rests_ref, extras_ref,
    tiles_ref, stage_ref, first_ref, second_ref, ans_out_ref, ans_in_ref, left_ref, pooled_ref,
    other_ref, stat_ref, stat_in_ref,
    req_send, req_recv, ans_send, ans_recv, stat_send, stat_recv, win_send, win_recv, plane_send,
    plane_recv, ext_send, ext_recv, pair_send, pair_recv,
):
    first_rows, _, window, rows_msg = layout_of(micro_count, capacity)
    batch_count = windows.batch_count
    first_extra = windows.first_extra
    me = lax.axis_index("batch")
    tower = lax.axis_index("tower")
    other_tower = 1 - tower
    greet(me, batch_count, other_tower)

    def request_copy(peer, slot):
        return peer_copy(
            req_ref.at[peer], served_ref.at[slot], req_send.at[peer], req_recv.at[slot], peer
        )

    stat_ref[...] = jnp.full(stat_ref.shape, jnp.sum(weight_ref[...].astype(jnp.float32)))

    def stat_copy(peer, slot):
        return peer_copy(stat_ref, stat_in_ref.at[slot], stat_send.at[peer], stat_recv.at[slot], peer)

    def answer_copy(peer, slot):
        return peer_copy(
            ans_out_ref.at[peer], ans_in_ref.at[slot], ans_send.at[peer], ans_recv.at[slot], peer
        )

    def own_copy():
        return pltpu.make_async_copy(ans_out_ref.at[me], ans_in_ref.at[me], ans_recv.at[me])

    def send_requests(i, carry):
        peer = lax.rem(me + i, batch_count)
        request_copy(peer, me).start()
        stat_copy(peer, me).start()
        return carry

    lax.fori_loop(1, batch_count, send_requests, 0)

    depth = batch_count // PLANE
    high, low = me // PLANE, lax.rem(me, PLANE)

    def others(action):
        each(batch_count, lambda i: action(lax.rem(me + i, batch_count)))

    def column(action):
        each(depth, lambda i: action(lax.rem(high + i, depth)))

    def plane(action):
        each(PLANE, lambda i: action(lax.rem(low + i, PLANE)))

    def column_copy(src, dst, to, source):
        return peer_copy(
            src, dst.at[low * depth + source], win_send.at[to], win_recv.at[source],
            to * PLANE + low,
        )

    def plane_copy(dst, to, source):
        block = dst.at[pl.ds(source * depth, depth)]
        return peer_copy(
            block, block, plane_send.at[to], plane_recv.at[source], high * PLANE + to
        )

    def extra_copy(peer, slot):
        return peer_copy(rest_ref, extras_ref.at[slot], ext_send.at[peer], ext_recv.at[slot], peer)

    def start_windows(src, dst):
        column(lambda to: column_copy(src, dst, to, high).start())
        dst[low * depth + high] = src[...]

    def pass_windows(src, dst):
        column(lambda source: column_copy(src, dst, source, source).wait_recv())
        plane(lambda to: plane_copy(dst, to, low).start())

    def sent_windows(src, dst):
        column(lambda to: column_copy(src, dst, to, high).wait_send())
        plane(lambda to: plane_copy(dst, to, low).wait_send())

    def split(action):
        @pl.when(tower == 0)
        def _():
            action(cin_ref, cins_ref)

        @pl.when(tower == 1)
        def _():
            action(rest_ref, rests_ref)

    served_ref[me] = req_ref[me]
    stat_in_ref[me] = stat_ref[...]
    tile_table(table_ref, tiles_ref, stage_ref, columns)
    pooled_ref[...] = jnp.zeros_like(pooled_ref)

    sizes = ans_out_ref.shape[1]

    def look_up(first, second):
        for r in range(rows_msg):
            row = jnp.concatenate(
                [served_ref[first, r : r + 1, :], served_ref[second, r : r + 1, :]], axis=1
            )
            hot = ones_at(iota((BROAD, 2 * WIDE), 0) == row % BROAD)
            result = dot(tiles_ref[...], hot)
            mask = iota((TALL, 2 * WIDE), 0) == row // BROAD
            block = pick_rows(result, mask, TALL, columns)
            first_ref[r * columns : r * columns + 16, :] = block[:, :WIDE]
            second_ref[r * columns : r * columns + 16, :] = block[:, WIDE:]
        ans_out_ref[first] = first_ref[:sizes, :].astype(jnp.bfloat16)
        ans_out_ref[second] = second_ref[:sizes, :].astype(jnp.bfloat16)

    def pool(owner):
        first_ref[:sizes, :] = ans_in_ref[owner].astype(jnp.float32)
        for r in range(rows_msg):
            span = slice(r * WIDE, (r + 1) * WIDE)
            values = [first_ref[r * columns + c : r * columns + c + 1, :] for c in range(columns)]
            mask = iota((HALF, WIDE), 0) == half_ref[owner, r : r + 1, :]
            pieces = [jnp.where(mask, values[c], 0.0) for c in range(EMB)]
            pieces.append(jnp.where(iota((8, WIDE), 0) == 0, values[EMB], 0.0))
            left_ref[:, span] = jnp.concatenate(pieces, axis=0).astype(jnp.bfloat16)
        for m in range(micro_count):
            rights = [
                ones_at(iota((WIDE, WIDE), 0) + (m * WIDE + 1) == code_ref[owner, r : r + 1, :])
                for r in range(first_rows[m], first_rows[m] + window)
            ]
            span = slice(first_rows[m] * WIDE, (first_rows[m] + window) * WIDE)
            pooled_ref[m] += dot(left_ref[:, span], jnp.concatenate(rights, axis=1), NT)

    pairs = batch_count // 2
    lag = 2

    def step(j, carry):
        @pl.when(j < pairs)
        def _():
            first = lax.rem(me + batch_count - (2 * j + 1), batch_count)
            second = lax.rem(me + 2 * batch_count - (2 * j + 2), batch_count)
            request_copy(first, first).wait_recv()

            @pl.when(j < pairs - 1)
            def _():
                request_copy(second, second).wait_recv()

            look_up(first, second)

            @pl.when(j == 0)
            def _():
                split(start_windows)

            @pl.when((j == 0) & (tower == 0) & (me >= first_extra))
            def _():
                others(lambda peer: extra_copy(peer, me - first_extra).start())
                extras_ref[me - first_extra] = rest_ref[...]

            @pl.when(j == 3)
            def _():
                split(pass_windows)

            answer_copy(first, me).start()

            @pl.when(j < pairs - 1)
            def _():
                answer_copy(second, me).start()

            @pl.when(j == pairs - 1)
            def _():
                own_copy().start()

        @pl.when(j >= lag)
        def _():
            first = lax.rem(me + 2 * (j - lag) + 1, batch_count)
            answer_copy(first, first).wait_recv()
            pool(first)

        @pl.when((j >= lag) & (j < pairs - 1 + lag))
        def _():
            second = lax.rem(me + 2 * (j - lag) + 2, batch_count)
            answer_copy(second, second).wait_recv()
            pool(second)

        return carry

    lax.fori_loop(0, pairs + lag, step, 0)

    def pair_copy(src, dst, k):
        return pltpu.make_async_remote_copy(
            src_ref=src,
            dst_ref=dst,
            send_sem=pair_send.at[k],
            recv_sem=pair_recv.at[k],
            device_id={"tower": other_tower},
            device_id_type=pl.DeviceIdType.MESH,
        )

    @pl.when(tower == 0)
    def _():
        plane(lambda source: plane_copy(cins_ref, source, source).wait_recv())
        for e in range(windows.extras):

            @pl.when(me != first_extra + e)
            def _():
                extra_copy(first_extra + e, e).wait_recv()

        pair_copy(cins_ref, cins_ref, 0).start()
        pair_copy(extras_ref, extras_ref, 1).start()

    @pl.when(tower == 1)
    def _():
        plane(lambda source: plane_copy(rests_ref, source, source).wait_recv())
        pair_copy(rests_ref, rests_ref, 0).start()

    own_copy().wait()
    pool(me)

    pooled_pair = pair_copy(pooled_ref, other_ref, 2)
    pooled_pair.start()

    def finish(i, carry):
        peer = lax.rem(me + i, batch_count)
        request_copy(peer, me).wait_send()
        stat_copy(peer, me).wait_send()
        answer_copy(peer, me).wait_send()
        stat_copy(peer, peer).wait_recv()
        return carry

    lax.fori_loop(1, batch_count, finish, 0)
    stat_out_ref[...] = jnp.sum(stat_in_ref[...], axis=0)

    split(sent_windows)

    @pl.when(tower == 0)
    def _():
        @pl.when(me >= first_extra)
        def _():
            others(lambda peer: extra_copy(peer, me - first_extra).wait_send())

        pair_copy(cins_ref, cins_ref, 0).wait_send()
        pair_copy(extras_ref, extras_ref, 1).wait_send()
        pair_copy(rests_ref, rests_ref, 0).wait_recv()

    @pl.when(tower == 1)
    def _():
        pair_copy(rests_ref, rests_ref, 0).wait_send()
        pair_copy(cins_ref, cins_ref, 0).wait_recv()
        pair_copy(extras_ref, extras_ref, 1).wait_recv()

    pooled_pair.wait()
    out_ref[...] = pooled_ref[...] + other_ref[...]


def fetch(
    requests, codes, halves, table, weights, cin_window, rest_window, windows, capacity, micro_count
):
    batch_count, rows_msg, _ = requests.shape
    columns, rows_dev = table.shape
    slots = rows_msg * WIDE
    sizes = message_rows(rows_msg, columns)
    in_vmem = pl.BlockSpec(memory_space=pltpu.VMEM)
    dma = pltpu.SemaphoreType.DMA
    bags = (micro_count, BAG_ROWS, WIDE)
    return pl.pallas_call(
        partial(fetch_kernel, capacity, micro_count, windows, columns),
        in_specs=[in_vmem] * 7,
        out_specs=[in_vmem] * 6,
        out_shape=[
            jax.ShapeDtypeStruct(bags, jnp.float32),
            jax.ShapeDtypeStruct(requests.shape, jnp.int32),
            jax.ShapeDtypeStruct((8, LANES), jnp.float32),
            jax.ShapeDtypeStruct((batch_count,) + cin_window.shape, jnp.bfloat16),
            jax.ShapeDtypeStruct((batch_count,) + rest_window.shape, jnp.bfloat16),
            jax.ShapeDtypeStruct((windows.extras,) + rest_window.shape, jnp.bfloat16),
        ],
        scratch_shapes=[
            pltpu.VMEM((columns * TALL, BROAD), jnp.bfloat16),
            pltpu.VMEM((TALL, BROAD), jnp.float32),
            pltpu.VMEM((sizes + 16, WIDE), jnp.float32),
            pltpu.VMEM((sizes + 16, WIDE), jnp.float32),
            pltpu.VMEM((batch_count, sizes, WIDE), jnp.bfloat16),
            pltpu.VMEM((batch_count, sizes, WIDE), jnp.bfloat16),
            pltpu.VMEM((BAG_ROWS, slots), jnp.bfloat16),
            pltpu.VMEM(bags, jnp.float32),
            pltpu.VMEM(bags, jnp.float32),
            pltpu.VMEM((8, LANES), jnp.float32),
            pltpu.VMEM((batch_count, 8, LANES), jnp.float32),
        ]
        + [dma((batch_count,))] * 11
        + [dma((windows.extras,)), dma((3,)), dma((3,))],
        compiler_params=pltpu.CompilerParams(
            vmem_limit_bytes=60 << 20, collective_id=0, has_side_effects=True
        ),
        name="fetch",
    )(requests, codes, halves, table, weights, cin_window, rest_window)


def return_kernel(
    capacity, micro_count, windows, columns,
    grad_ref, code_ref, half_ref, served_ref, stat_ref, cins_ref, rests_ref, extras_ref,
    out_ref, stat_out_ref, cin_ref, rest_ref,
    send_ref, recv_ref, first_ref, second_ref, left_ref, right_ref, total_ref, stat_in_ref,
    extra_in_ref, cin_near_ref, cin_sum_ref, cin_far_ref, rest_near_ref, rest_sum_ref, rest_far_ref,
    val_send, val_recv, stat_send, stat_recv, win_send, win_recv, plane_send, plane_recv, ext_send,
    ext_recv,
):
    batch_count = windows.batch_count
    first_extra = windows.first_extra
    tower = lax.axis_index("tower")
    first_rows, _, window, rows_msg = layout_of(micro_count, capacity)
    me = lax.axis_index("batch")
    greet(me, batch_count)

    def value_copy(peer, slot):
        return peer_copy(
            send_ref.at[peer], recv_ref.at[slot], val_send.at[peer], val_recv.at[slot], peer
        )

    def own_copy():
        return pltpu.make_async_copy(send_ref.at[me], recv_ref.at[me], val_recv.at[me])

    def stat_copy(peer, slot):
        return peer_copy(stat_ref, stat_in_ref.at[slot], stat_send.at[peer], stat_recv.at[slot], peer)

    depth = batch_count // PLANE
    high, low = me // PLANE, lax.rem(me, PLANE)

    def others(action):
        each(batch_count, lambda i: action(lax.rem(me + i, batch_count)))

    def column(action):
        each(depth, lambda i: action(lax.rem(high + i, depth)))

    def plane(action):
        each(PLANE, lambda i: action(lax.rem(low + i, PLANE)))

    def plane_copy(src, near, to, source):
        return peer_copy(
            src.at[pl.ds(to * depth, depth)], near.at[source], plane_send.at[to],
            plane_recv.at[source], high * PLANE + to,
        )

    def column_copy(total, far, to, source):
        return peer_copy(
            total.at[to], far.at[source], win_send.at[to], win_recv.at[source], to * PLANE + low
        )

    def start_windows(src, near, total, far, out):
        plane(lambda to: plane_copy(src, near, to, low).start())
        near[low] = src[pl.ds(low * depth, depth)]

    def pass_windows(src, near, total, far, out):
        plane(lambda source: plane_copy(src, near, source, source).wait_recv())
        total[...] = jnp.sum(near[...], axis=0)
        column(lambda to: column_copy(total, far, to, high).start())
        far[high] = total[high]

    def end_windows(src, near, total, far, out):
        column(lambda source: column_copy(total, far, source, source).wait_recv())
        out[...] = jnp.sum(far[...], axis=0)
        plane(lambda to: plane_copy(src, near, to, low).wait_send())
        column(lambda to: column_copy(total, far, to, high).wait_send())

    def split(action):
        @pl.when(tower == 0)
        def _():
            action(cins_ref, cin_near_ref, cin_sum_ref, cin_far_ref, cin_ref)

        @pl.when(tower == 1)
        def _():
            action(rests_ref, rest_near_ref, rest_sum_ref, rest_far_ref, rest_ref)

    def extra_copy(peer, slot):
        return peer_copy(
            extras_ref.at[peer - first_extra],
            extra_in_ref.at[slot],
            ext_send.at[peer],
            ext_recv.at[slot],
            peer,
        )

    def send_stats(i, carry):
        stat_copy(lax.rem(me + i, batch_count), me).start()
        return carry

    lax.fori_loop(1, batch_count, send_stats, 0)
    stat_in_ref[me] = stat_ref[...]
    total_ref[...] = jnp.zeros_like(total_ref)

    sizes = send_ref.shape[1]

    def spread(first, second):
        for r in range(rows_msg):
            code = jnp.concatenate(
                [code_ref[first, r : r + 1, :], code_ref[second, r : r + 1, :]], axis=1
            )
            half = jnp.concatenate(
                [half_ref[first, r : r + 1, :], half_ref[second, r : r + 1, :]], axis=1
            )
            result = None
            for m in range(micro_count):
                if first_rows[m] <= r < first_rows[m] + window:
                    hot = ones_at(iota((WIDE, 2 * WIDE), 0) + (m * WIDE + 1) == code)
                    found = dot(grad_ref[m], hot)
                    result = found if result is None else result + found
            block = pick_rows(result, iota((HALF, 2 * WIDE), 0) == half, HALF, EMB)
            linear = result[EMB * HALF : EMB * HALF + 1]
            block = jnp.where(iota((16, 2 * WIDE), 0) == EMB, linear, block)
            first_ref[r * columns : r * columns + 16, :] = block[:, :WIDE]
            second_ref[r * columns : r * columns + 16, :] = block[:, WIDE:]
        send_ref[first] = first_ref[:sizes, :].astype(jnp.bfloat16)
        send_ref[second] = second_ref[:sizes, :].astype(jnp.bfloat16)

    def scatter(source):
        first_ref[:sizes, :] = recv_ref[source].astype(jnp.float32)
        for r in range(rows_msg):
            span = slice(r * WIDE, (r + 1) * WIDE)
            row = served_ref[source, r : r + 1, :]
            mask = iota((TALL, WIDE), 0) == row // BROAD
            for c in range(columns):
                left_ref[c * TALL : (c + 1) * TALL, span] = jnp.where(
                    mask, first_ref[r * columns + c : r * columns + c + 1, :], 0.0
                ).astype(jnp.bfloat16)
            right_ref[:, span] = ones_at(iota((BROAD, WIDE), 0) == row % BROAD)
        total_ref[...] += dot(left_ref[...], right_ref[...], NT)

    pairs = batch_count // 2
    lag = 2

    def step(j, carry):
        @pl.when(j < pairs)
        def _():
            first = lax.rem(me + 2 * j + 1, batch_count)
            second = lax.rem(me + 2 * j + 2, batch_count)
            spread(first, second)
            value_copy(first, me).start()

            @pl.when(j == 1)
            def _():
                split(start_windows)

            @pl.when((j == 1) & (tower == 0))
            def _():
                for e in range(windows.extras):

                    @pl.when(me != first_extra + e)
                    def _():
                        extra_copy(first_extra + e, me).start()

            @pl.when(j < pairs - 1)
            def _():
                value_copy(second, me).start()

            @pl.when(j == pairs - 1)
            def _():
                own_copy().start()

        @pl.when(j == pairs - 1)
        def _():
            split(pass_windows)

        @pl.when(j >= lag)
        def _():
            first = lax.rem(me + batch_count - (2 * (j - lag) + 1), batch_count)
            value_copy(first, first).wait_recv()
            scatter(first)

        @pl.when((j >= lag) & (j < pairs - 1 + lag))
        def _():
            second = lax.rem(me + 2 * batch_count - (2 * (j - lag) + 2), batch_count)
            value_copy(second, second).wait_recv()
            scatter(second)

        return carry

    lax.fori_loop(0, pairs + lag, step, 0)
    own_copy().wait()
    scatter(me)

    split(end_windows)

    @pl.when(tower == 0)
    def _():
        for e in range(windows.extras):

            @pl.when(me != first_extra + e)
            def _():
                extra_copy(first_extra + e, me).wait_send()

        @pl.when(me >= first_extra)
        def _():
            extra_in_ref[me] = extras_ref[me - first_extra]
            others(lambda peer: extra_copy(me, peer).wait_recv())
            rest_ref[...] = jnp.sum(extra_in_ref[...], axis=0)

        @pl.when(me < first_extra)
        def _():
            rest_ref[...] = jnp.zeros_like(rest_ref)

    @pl.when(tower == 1)
    def _():
        cin_ref[...] = jnp.zeros_like(cin_ref)

    def finish(i, carry):
        peer = lax.rem(me + i, batch_count)
        value_copy(peer, me).wait_send()
        stat_copy(peer, me).wait_send()
        stat_copy(peer, peer).wait_recv()
        return carry

    lax.fori_loop(1, batch_count, finish, 0)
    stat_out_ref[...] = jnp.sum(stat_in_ref[...], axis=0)
    for c in range(columns):
        for q in range(TALL):
            out_ref[c : c + 1, q * BROAD : (q + 1) * BROAD] = total_ref[
                c * TALL + q : c * TALL + q + 1, :
            ]


def return_grads(
    grad_bags, codes, halves, served, stat, cins, rests, extras, windows, capacity, columns
):
    batch_count, rows_msg, _ = codes.shape
    micro_count = grad_bags.shape[0]
    slots = rows_msg * WIDE
    sizes = message_rows(rows_msg, columns)
    depth = batch_count // PLANE
    in_vmem = pl.BlockSpec(memory_space=pltpu.VMEM)
    dma = pltpu.SemaphoreType.DMA
    return pl.pallas_call(
        partial(return_kernel, capacity, micro_count, windows, columns),
        in_specs=[in_vmem] * 8,
        out_specs=[in_vmem] * 4,
        out_shape=[
            jax.ShapeDtypeStruct((columns, TALL * BROAD), jnp.float32),
            jax.ShapeDtypeStruct(stat.shape, jnp.float32),
            jax.ShapeDtypeStruct(cins.shape[1:], jnp.float32),
            jax.ShapeDtypeStruct(rests.shape[1:], jnp.float32),
        ],
        scratch_shapes=[
            pltpu.VMEM((batch_count, sizes, WIDE), jnp.bfloat16),
            pltpu.VMEM((batch_count, sizes, WIDE), jnp.bfloat16),
            pltpu.VMEM((sizes + 16, WIDE), jnp.float32),
            pltpu.VMEM((sizes + 16, WIDE), jnp.float32),
            pltpu.VMEM((columns * TALL, slots), jnp.bfloat16),
            pltpu.VMEM((BROAD, slots), jnp.bfloat16),
            pltpu.VMEM((columns * TALL, BROAD), jnp.float32),
            pltpu.VMEM((batch_count,) + stat.shape, jnp.float32),
            pltpu.VMEM(rests.shape, jnp.float32),
        ]
        + [
            pltpu.VMEM(lead + x.shape[1:], jnp.float32)
            for x in (cins, rests)
            for lead in ((PLANE, depth), (depth,), (depth,))
        ]
        + [dma((batch_count,))] * 10,
        compiler_params=pltpu.CompilerParams(
            vmem_limit_bytes=60 << 20, collective_id=1, has_side_effects=True
        ),
        name="return_grads",
    )(grad_bags, codes, halves, served, stat, cins, rests, extras)


def split_three(x):
    high = x.astype(jnp.bfloat16)
    rest = x - high.astype(jnp.float32)
    middle = rest.astype(jnp.bfloat16)
    low = (rest - middle.astype(jnp.float32)).astype(jnp.bfloat16)
    return high, middle, low


def dense_kernel(
    micro_count, windows, tower_ref, stat_ref, pooled_ref, label_ref, weight_ref,
    cins_ref, rests_ref, extras_ref,
    bags_ref, loss_ref, g_cins_ref, g_rests_ref, g_extras_ref,
    embed_ref, total_ref, pairs_ref, sym_ref, cin_ref, rest_ref, lane_ref,
):
    f32 = jnp.float32
    bf16 = jnp.bfloat16
    width = micro_count * LANES
    groups = HPAD // LANES

    cin_ref[...] = jnp.zeros_like(cin_ref)
    for b, at in enumerate(windows.cin_at):
        block = cins_ref[windows.slots[b]].astype(f32)
        cin_ref[at : at + windows.cin_rows, :] += block[: windows.cin_rows]
    rest_ref[...] = jnp.zeros_like(rest_ref)
    pieces = [(rests_ref, windows.slots[b], at) for b, at in enumerate(windows.rest_at)]
    pieces += [(extras_ref, e, at) for e, at in enumerate(windows.extra_at)]
    for source, b, at in pieces:
        skip = max(0, -at)
        block = source[b].astype(f32)
        for l in range(groups):
            rest_ref[l, at + skip : at + windows.rest_rows, :] += block[
                skip : windows.rest_rows, l * LANES : (l + 1) * LANES
            ]

    def rest_rows(begin, count):
        return jnp.concatenate(
            [rest_ref[l, begin : begin + count, :] for l in range(groups)], axis=1
        )[:, :HID]

    cin_w = cin_ref[:MAPS, :].astype(bf16)
    place = iota((MAPS, PAIRS), 0)
    place = place // FIELDS * FPAD + place % FIELDS == iota((MAPS, PAIRS), 1)
    picks_u = ones_at(place)
    row_u = jnp.broadcast_to(cin_ref[MAPS : MAPS + 1, :], (8, PAIRS)).astype(bf16)
    cin_u = dot(picks_u, row_u, NT)[:, :1]
    w_one = jnp.concatenate(
        [
            jnp.concatenate(
                [rest_ref[l, pl.ds(d, FPAD, stride=EMB), :] for l in range(groups)], axis=1
            )[:, :HID]
            for d in range(EMB)
        ],
        axis=0,
    ).astype(bf16)
    w_two = rest_rows(W_TWO, HID).astype(bf16)
    rows = jnp.zeros((8, HID), f32)
    for k, at in enumerate((B_ONE, B_TWO, W_THREE)):
        rows = jnp.where(iota((8, HID), 0) == k, rest_rows(at, 1), rows)
    unit = ones_at(iota((HID, HID), 0) == iota((HID, HID), 1))
    turned = dot(unit, rows.astype(bf16), NT)
    b_one, b_two, w_three = turned[:, 0:1], turned[:, 1:2], turned[:, 2:3]
    bias = rest_ref[0, BIAS : BIAS + 1, 0:1]

    def unpacked(row, count):
        pieces = []
        for m in range(micro_count):
            low = pooled_ref[m, row : row + HALF, :LANES]
            high = pooled_ref[m, row : row + HALF, LANES:]
            pieces.append(jnp.concatenate([low, high], axis=0)[:count])
        return jnp.concatenate(pieces, axis=1)

    for d in range(EMB):
        embed_ref[d * FPAD : (d + 1) * FPAD, :] = unpacked(d * HALF, FPAD)
    linear = jnp.concatenate(
        [
            pooled_ref[m, EMB * HALF : EMB * HALF + 1, :LANES]
            + pooled_ref[m, EMB * HALF : EMB * HALF + 1, LANES:]
            for m in range(micro_count)
        ],
        axis=1,
    )

    def pair_row(i, carry):
        total = jnp.zeros((FPAD, width), f32)
        for d in range(EMB):
            own = embed_ref[pl.ds(d * FPAD + i, 1), :]
            product = (embed_ref[d * FPAD : (d + 1) * FPAD, :] * own).astype(jnp.bfloat16)
            total = total + product.astype(f32)
        total_ref[pl.ds(pl.multiple_of(i * FPAD, 8), FPAD), :] = total
        return carry

    lax.fori_loop(0, FIELDS, pair_row, 0)
    thirds = split_three(total_ref[...])
    map_sum = sum(dot(cin_w, third) for third in thirds)
    cin_logits = jnp.sum(map_sum * cin_u, axis=0, keepdims=True)

    flat = embed_ref[...].astype(jnp.bfloat16)
    pre_one = dot(w_one, flat, TN) + b_one
    hidden_one = jnp.maximum(pre_one, 0.0).astype(jnp.bfloat16)
    pre_two = dot(w_two, hidden_one, TN) + b_two
    active_two = jnp.maximum(pre_two, 0.0)
    deep_logits = jnp.sum(active_two * w_three, axis=0, keepdims=True)
    logits = cin_logits + deep_logits + linear + bias

    samples = weight_ref.shape[1]
    lane_ref[...] = jnp.zeros_like(lane_ref)
    for m in range(micro_count):
        span = slice(m * LANES, m * LANES + samples)
        lane_ref[0:1, span] = weight_ref[m : m + 1, :].astype(f32)
        lane_ref[1:2, span] = label_ref[m : m + 1, :].astype(f32)
    weight = lane_ref[0:1, :]
    label = lane_ref[1:2, :]
    soft = jnp.maximum(logits, 0.0) + jnp.log1p(jnp.exp(-jnp.abs(logits)))
    loss_ref[...] = jnp.broadcast_to(
        jnp.sum(weight * (soft - label * logits), axis=1, keepdims=True), loss_ref.shape
    )
    grad_logits = weight * (jax.nn.sigmoid(logits) - label) / stat_ref[0:1, 0:1]

    grad_maps = (grad_logits * cin_u).astype(jnp.bfloat16)
    grad_two = jnp.where(pre_two > 0, grad_logits * w_three, 0.0).astype(jnp.bfloat16)
    grad_hidden = dot(w_two, grad_two)
    grad_one = jnp.where(pre_one > 0, grad_hidden, 0.0).astype(jnp.bfloat16)
    grad_flat = dot(w_one, grad_one)

    grad_pairs = dot(cin_w, grad_maps, TN)
    for m in range(micro_count):
        pairs_ref[m, :PAIRS, :] = grad_pairs[:, m * LANES : (m + 1) * LANES]
        pairs_ref[m, PAIRS:, :] = jnp.zeros((FPAD * FPAD - PAIRS, LANES), f32)

    def mirror(j, carry):
        here = pl.ds(pl.multiple_of(j * FPAD, 8), FPAD)
        both = [
            pairs_ref[m, here, :] + pairs_ref[m, pl.ds(j, FPAD, stride=FPAD), :]
            for m in range(micro_count)
        ]
        sym_ref[here, :] = jnp.concatenate(both, axis=1)
        return carry

    lax.fori_loop(0, FIELDS, mirror, 0)
    empty = jnp.zeros((2 * HALF - FPAD, width), f32)

    for d in range(EMB):

        def add_row(j, total):
            here = pl.ds(pl.multiple_of(j * FPAD, 8), FPAD)
            return total + sym_ref[here, :] * embed_ref[pl.ds(d * FPAD + j, 1), :]

        grad_embed = lax.fori_loop(
            0, FIELDS, add_row, grad_flat[d * FPAD : (d + 1) * FPAD], unroll=3
        )
        grad_embed = jnp.concatenate([grad_embed, empty], axis=0)
        for m in range(micro_count):
            span = slice(m * LANES, (m + 1) * LANES)
            block = jnp.concatenate([grad_embed[:HALF, span], grad_embed[HALF:, span]], axis=1)
            bags_ref[m, d * HALF : (d + 1) * HALF, :] = block.astype(bf16)
    for m in range(micro_count):
        row = grad_logits[:, m * LANES : (m + 1) * LANES]
        row = jnp.concatenate([row, row], axis=1)
        bags_ref[m, EMB * HALF :, :] = jnp.broadcast_to(row, (8, WIDE)).astype(bf16)

    ones = jnp.ones((8, width), bf16)

    def row_sum(x):
        return sum(dot(ones, third, NT) for third in split_three(x))[:1]

    rest_ref[...] = jnp.zeros_like(rest_ref)

    def put(begin, count, value, stride=None):
        for l in range(groups):
            piece = value[:, l * LANES : min((l + 1) * LANES, HID)]
            lanes = slice(0, piece.shape[1])
            if stride is None:
                rest_ref[l, begin : begin + count, lanes] = piece
            else:
                piece = jnp.pad(piece, ((0, 0), (0, LANES - piece.shape[1])))
                rest_ref[l, pl.ds(begin, count, stride=stride), :] = piece

    g_w_one = dot(flat, grad_one, NT)
    for d in range(EMB):
        put(d, FIELDS, g_w_one[d * FPAD : d * FPAD + FIELDS], EMB)

    @pl.when(tower_ref[0] == 0)
    def _():
        cin_ref[...] = jnp.zeros_like(cin_ref)
        cin_ref[:MAPS, :] = sum(dot(grad_maps, third, NT) for third in thirds)
        g_cin_u = jnp.sum(map_sum * grad_logits, axis=1, keepdims=True)
        thirds_u = split_three(jnp.broadcast_to(g_cin_u, (MAPS, 8)))
        cin_ref[MAPS : MAPS + 1, :] = sum(dot(third, picks_u, TN) for third in thirds_u)[:1]
        for b, at in enumerate(windows.cin_at):
            g_cins_ref[windows.slots[b], : windows.cin_rows, :] = cin_ref[
                at : at + windows.cin_rows, :
            ]
        for e, at in enumerate(windows.extra_at):
            skip = max(0, -at)
            for l in range(groups):
                span = slice(l * LANES, (l + 1) * LANES)
                g_extras_ref[e, skip : windows.rest_rows, span] = rest_ref[
                    l, at + skip : at + windows.rest_rows, :
                ]

    @pl.when(tower_ref[0] != 0)
    def _():
        put(W_TWO, HID, dot(hidden_one, grad_two, NT))
        put(B_ONE, 1, dot(ones, grad_one, NT)[:1])
        put(B_TWO, 1, dot(ones, grad_two, NT)[:1])
        put(W_THREE, 1, row_sum(active_two * grad_logits))
        g_bias = jnp.sum(grad_logits, axis=1, keepdims=True)
        put(BIAS, 1, jnp.where(iota((1, HID), 1) == 0, g_bias, 0.0))
        for b, at in enumerate(windows.rest_at):
            for l in range(groups):
                span = slice(l * LANES, (l + 1) * LANES)
                g_rests_ref[windows.slots[b], : windows.rest_rows, span] = rest_ref[
                    l, at : at + windows.rest_rows, :
                ]


def dense_step(tower_at, stats, pooled, labels, weights, cins, rests, extras, windows):
    micro_count = pooled.shape[0]
    width = micro_count * LANES
    in_vmem = pl.BlockSpec(memory_space=pltpu.VMEM)
    in_smem = pl.BlockSpec(memory_space=pltpu.SMEM)
    f32 = jnp.float32
    shapes = [
        ((micro_count, BAG_ROWS, WIDE), jnp.bfloat16),
        ((8, LANES), f32),
        (cins.shape, f32),
        (rests.shape, f32),
        (extras.shape, f32),
    ]
    return pl.pallas_call(
        partial(dense_kernel, micro_count, windows),
        in_specs=[in_smem] + [in_vmem] * 7,
        out_specs=[in_vmem] * len(shapes),
        out_shape=[jax.ShapeDtypeStruct(*shape) for shape in shapes],
        scratch_shapes=[
            pltpu.VMEM((EMB * FPAD, width), f32),
            pltpu.VMEM((PAIRS, width), f32),
            pltpu.VMEM((micro_count, FPAD * FPAD, LANES), f32),
            pltpu.VMEM((PAIRS, width), f32),
            pltpu.VMEM((windows.cin_total, PAIRS), f32),
            pltpu.VMEM((HPAD // LANES, windows.rest_total, LANES), f32),
            pltpu.VMEM((8, width), f32),
        ],
        compiler_params=pltpu.CompilerParams(vmem_limit_bytes=60 << 20),
        name="dense",
    )(tower_at.reshape(1), stats, pooled, labels, weights, cins, rests, extras)


def shards(
    shard_ids,
    local_rows,
    bag_counts,
    click_labels,
    sample_weights,
    embed_table,
    table_first,
    table_second,
    dense_params,
    dense_first,
    dense_second,
):
    tower_count = lax.axis_size("tower")
    batch_count = lax.axis_size("batch")
    tower_at = lax.axis_index("tower")
    micro_count, samples = shard_ids.shape[:2]
    columns, rows_dev = embed_table.shape
    capacity = 4 * samples * IDS_SAMP // (tower_count * batch_count)
    share = dense_params.shape[0]
    windows = Windows(share, batch_count)

    device = tower_at * batch_count + lax.axis_index("batch")
    cin_phase, rest_phase = windows.phases(device)
    low = dense_params.astype(jnp.bfloat16)

    def window(rows, row_size, phase):
        return lax.dynamic_update_slice(
            jnp.zeros((rows * row_size,), jnp.bfloat16), low, (phase,)
        )

    cin_window = window(windows.cin_rows, SQUARE, cin_phase).reshape(-1, FIELDS, FIELDS)
    cin_window = jnp.pad(
        cin_window,
        ((0, windows.cin_pad - windows.cin_rows), (0, 0), (0, FPAD - FIELDS)),
    ).reshape(windows.cin_pad, PAIRS)
    rest_window = jnp.pad(
        window(windows.rest_rows, HID, rest_phase).reshape(-1, HID),
        ((0, windows.rest_pad - windows.rest_rows), (0, HPAD - HID)),
    )

    def lanes_of(values):
        return jnp.moveaxis(values, 1, -1).reshape(micro_count, -1, samples)

    requests, codes, halves = route(
        lanes_of(shard_ids), lanes_of(local_rows), lanes_of(bag_counts), capacity, batch_count
    )
    pooled, served, stats, cins, rests, extras = fetch(
        requests, codes, halves, embed_table, sample_weights, cin_window, rest_window, windows,
        capacity, micro_count,
    )
    grad_bags, loss, g_cins, g_rests, g_extras = dense_step(
        tower_at, stats, pooled, click_labels, sample_weights, cins, rests, extras, windows
    )
    table_grad, losses, g_cin, g_rest = return_grads(
        grad_bags, codes, halves, served, loss, g_cins, g_rests, g_extras, windows, capacity, columns
    )
    g_cin = g_cin[: windows.cin_rows].reshape(-1, FIELDS, FPAD)[:, :, :FIELDS].reshape(-1)
    g_rest = g_rest[: windows.rest_rows, :HID].reshape(-1)
    is_cin = device * share + jnp.arange(share, dtype=jnp.int32) < CIN_SIZE
    own_grad = jnp.where(
        is_cin,
        lax.dynamic_slice(g_cin, (cin_phase,), (share,)),
        lax.dynamic_slice(g_rest, (rest_phase,), (share,)),
    )

    table_new, table_first_new, table_second_new = adam_update(
        embed_table, table_first, table_second, table_grad, rate_table
    )
    dense_new, dense_first_new, dense_second_new = adam_update(
        dense_params, dense_first, dense_second, own_grad, rate_dense
    )
    loss_sum = losses[0, 0] / stats[0, 0]
    return (
        table_new,
        table_first_new,
        table_second_new,
        table_new.astype(jnp.bfloat16),
        dense_new,
        dense_first_new,
        dense_second_new,
        dense_new.astype(jnp.bfloat16),
        loss_sum,
    )


def solution(mesh):
    rows = P(None, ("tower", "batch"))
    dense = P(("tower", "batch"))
    placed = (
        P(None, "batch", None, None),
        P(None, "batch", None, None),
        P(None, "batch", None),
        P(None, "batch"),
        P(None, "batch"),
        rows,
        rows,
        rows,
        dense,
        dense,
        dense,
    )
    return jax.shard_map(
        shards,
        mesh=mesh,
        in_specs=placed,
        out_specs=(rows, rows, rows, rows, dense, dense, dense, dense, P()),
        check_vma=False,
    )
```

```python
from functools import partial

import jax
import jax.numpy as jnp
from jax import lax
from jax.experimental import pallas as pl
from jax.experimental.pallas import tpu as pltpu
from jax.sharding import PartitionSpec as P

FIELDS = 39
EMB = 10
MAPS = 200
HID = 400
IDS_SAMP = 80

beta_one = 0.9
beta_two = 0.999
epsilon = 1e-08
decay_rate = 0.15
rate_table = 0.1
rate_dense = 0.05
step_count = 10

LANES = 128
WIDE = 256
BROAD = 512
TALL = 64
HALF = 24
BAG_ROWS = EMB * HALF + 8
FPAD = 40
PAIRS = FIELDS * FPAD
SQUARE = FIELDS * FIELDS
CIN_SIZE = MAPS * SQUARE + MAPS
FLAT = EMB * FIELDS
B_ONE, W_TWO, B_TWO, W_THREE, BIAS = FLAT, FLAT + 1, FLAT + HID + 1, FLAT + HID + 2, FLAT + HID + 3
HPAD = 512
PLANE = 4
NT = (((1,), (1,)), ((), ()))
TN = (((0,), (0,)), ((), ()))
NN = (((1,), (0,)), ((), ()))


def adam_update(weight, first_old, second_old, gradient, step_rate):
    first_new = beta_one * first_old + (1.0 - beta_one) * gradient
    second_new = beta_two * second_old + (1.0 - beta_two) * gradient * gradient
    first_hat = first_new / (1.0 - beta_one**step_count)
    second_hat = second_new / (1.0 - beta_two**step_count)
    weight_new = weight - step_rate * (
        first_hat / (jnp.sqrt(second_hat) + epsilon) + decay_rate * weight
    )
    return (weight_new, first_new, second_new)


def dot(a, b, dims=NN):
    return lax.dot_general(a, b, dims, preferred_element_type=jnp.float32)


def vmem_limit(batch_count):
    return (28 + batch_count // 4) << 20


def iota(shape, dim):
    return lax.broadcasted_iota(jnp.int32, shape, dim)


def ones_at(mask):
    return jnp.where(mask, 1.0, 0.0).astype(jnp.bfloat16)


def layout_of(micro_count, capacity):
    first_rows = [m * capacity // WIDE for m in range(micro_count)]
    shifts = [m * capacity % WIDE for m in range(micro_count)]
    window = max(-(-(shift + capacity) // WIDE) for shift in shifts)
    return first_rows, shifts, window, max(first_rows) + window


class Windows:
    def __init__(self, share, batch_count):
        self.share, self.batch_count = share, batch_count
        self.cin_rows = -(-(SQUARE - 1 + share) // SQUARE)
        self.rest_rows = -(-(HID - 1 + share) // HID)
        self.cin_pad = -(-self.cin_rows // 16) * 16
        self.rest_pad = -(-self.rest_rows // 16) * 16
        self.first_extra = CIN_SIZE // share
        self.extras = batch_count - self.first_extra
        self.cin_at = [b * share // SQUARE for b in range(batch_count)]
        self.rest_at = [
            ((batch_count + b) * share - CIN_SIZE) // HID for b in range(batch_count)
        ]
        self.extra_at = [
            (b * share - CIN_SIZE) // HID for b in range(self.first_extra, batch_count)
        ]
        depth = batch_count // PLANE
        self.slots = [b % PLANE * depth + b // PLANE for b in range(batch_count)]
        self.cin_total = -(-max(a + self.cin_rows for a in self.cin_at) // 8) * 8
        self.rest_total = -(-max(a + self.rest_rows for a in self.rest_at) // 8) * 8

    def phases(self, device):
        start = device * self.share
        return start % SQUARE, jnp.mod(start - CIN_SIZE, HID)


def route_kernel(
    capacity, batch_count, micro_count, ids_ref, rows_ref, counts_ref,
    req_ref, code_ref, half_ref, part_ref, left_ref, right_ref,
):
    f32, bf16 = jnp.float32, jnp.bfloat16
    first_rows, shifts, window, _ = layout_of(micro_count, capacity)
    micro = pl.program_id(0)
    id_rows, samples = ids_ref.shape[1:]
    chunk = 16
    tower = lax.axis_index("tower")

    @pl.when(micro == 0)
    def _():
        req_ref[...] = jnp.zeros_like(req_ref)
        code_ref[...] = jnp.zeros_like(code_ref)
        half_ref[...] = jnp.zeros_like(half_ref)
        part_ref[...] = jnp.zeros_like(part_ref)

    def widened(x, filler):
        part_ref[0, :, :samples] = x.astype(f32)
        inside = iota((id_rows, LANES), 1) < samples
        return jnp.where(inside, part_ref[0], filler)

    owner = ids_ref[0]
    target = widened(
        jnp.where(owner // batch_count == tower, owner % batch_count, batch_count), batch_count
    ).astype(jnp.int32)
    local = widened(rows_ref[0], 0.0).astype(jnp.int32)
    before = ones_at(iota((FIELDS, FIELDS), 1) <= iota((FIELDS, FIELDS), 0))
    ends = dot(before, counts_ref[0].astype(f32).astype(bf16)).astype(jnp.int32)
    field = jnp.zeros((id_rows, samples), jnp.int32)
    for f in range(FIELDS):
        field = field + jnp.where(iota((id_rows, samples), 0) >= ends[f : f + 1], 1, 0)
    field = widened(field, 0.0)
    late = jnp.where(field >= HALF, 1.0, 0.0)

    earlier_rows = ones_at(iota((id_rows, id_rows), 1) < iota((id_rows, id_rows), 0))
    upper = iota((2 * LANES, LANES), 0)
    mixing = ones_at((upper < iota((2 * LANES, LANES), 1)) | (upper >= LANES))
    rank = jnp.zeros((id_rows, LANES), f32)
    for begin in range(0, batch_count, chunk):
        hots = [ones_at(target == begin + d) for d in range(chunk)]
        above = dot(earlier_rows, jnp.concatenate(hots, axis=1)).astype(bf16)
        stacked = jnp.concatenate(
            [
                jnp.concatenate([hots[d], above[:, d * LANES : (d + 1) * LANES]], axis=1)
                for d in range(chunk)
            ],
            axis=0,
        )
        ranks = dot(stacked, mixing)
        for d in range(chunk):
            rank = rank + jnp.where(
                target == begin + d, ranks[d * id_rows : (d + 1) * id_rows], 0.0
            )
    shift = sum(jnp.where(micro == m, shifts[m], 0) for m in range(micro_count))
    slot = rank.astype(jnp.int32) + shift
    place = jnp.where(target < batch_count, (slot // WIDE) * batch_count + target, -1)
    part_ref[0] = place.astype(f32)
    part_ref[1] = (slot % WIDE).astype(f32)
    part_ref[2] = (local // WIDE).astype(f32)
    part_ref[3] = (local % WIDE).astype(f32)
    part_ref[4] = late * LANES + (iota((id_rows, LANES), 1) + 1).astype(f32)
    part_ref[5] = field - late * HALF
    places = window * batch_count

    def build(t, carry):
        span = pl.ds(pl.multiple_of(t * LANES, LANES), LANES)

        def row(k):
            return part_ref[k, pl.ds(t, 1), :]

        mask = iota((places, LANES), 0).astype(f32) == row(0)
        for v in range(4):
            left_ref[v * places : (v + 1) * places, span] = jnp.where(
                mask, row(2 + v), 0.0
            ).astype(bf16)
        right_ref[:, span] = ones_at(iota((WIDE, LANES), 0).astype(f32) == row(1))
        return carry

    lax.fori_loop(0, id_rows, build, 0, unroll=4)
    placed = dot(left_ref[...], right_ref[...], NT).astype(jnp.int32)

    def part(v, r):
        begin = (v * window + r) * batch_count
        return placed[begin : begin + batch_count]

    for m in range(micro_count):

        @pl.when(micro == m)
        def _():
            for r in range(window):
                at = first_rows[m] + r
                code = part(2, r)
                req_ref[:, at, :] += part(0, r) * WIDE + part(1, r)
                code_ref[:, at, :] += jnp.where(code > 0, code + m * WIDE, 0)
                half_ref[:, at, :] += part(3, r)


def route(ids, rows, counts, capacity, batch_count):
    micro_count, id_rows, samples = ids.shape
    _, _, window, rows_msg = layout_of(micro_count, capacity)
    places = window * batch_count

    def block(x):
        return pl.BlockSpec((1,) + x.shape[1:], lambda m: (m, 0, 0))

    whole = pl.BlockSpec((batch_count, rows_msg, WIDE), lambda m: (0, 0, 0))
    shape = jax.ShapeDtypeStruct((batch_count, rows_msg, WIDE), jnp.int32)
    return pl.pallas_call(
        partial(route_kernel, capacity, batch_count, micro_count),
        grid=(micro_count,),
        in_specs=[block(ids), block(rows), block(counts)],
        out_specs=[whole] * 3,
        out_shape=[shape] * 3,
        scratch_shapes=[
            pltpu.VMEM((6, id_rows, LANES), jnp.float32),
            pltpu.VMEM((4 * places, id_rows * LANES), jnp.bfloat16),
            pltpu.VMEM((WIDE, id_rows * LANES), jnp.bfloat16),
        ],
        compiler_params=pltpu.CompilerParams(vmem_limit_bytes=vmem_limit(batch_count)),
        name="route",
    )(ids, rows, counts)


def peer_copy(src, dst, send_sem, recv_sem, peer):
    return pltpu.make_async_remote_copy(
        src_ref=src,
        dst_ref=dst,
        send_sem=send_sem,
        recv_sem=recv_sem,
        device_id={"batch": peer},
        device_id_type=pl.DeviceIdType.MESH,
    )


def greet(me, batch_count, other_tower=None):
    barrier = pltpu.get_barrier_semaphore()

    def signal(i, carry):
        pl.semaphore_signal(
            barrier,
            inc=1,
            device_id={"batch": lax.rem(me + i, batch_count)},
            device_id_type=pl.DeviceIdType.MESH,
        )
        return carry

    lax.fori_loop(1, batch_count, signal, 0)
    if other_tower is not None:
        pl.semaphore_signal(
            barrier,
            inc=1,
            device_id={"tower": other_tower},
            device_id_type=pl.DeviceIdType.MESH,
        )
    pl.semaphore_wait(barrier, batch_count - (1 if other_tower is None else 0))


def message_rows(rows_msg, columns):
    return -(-rows_msg * columns // 16) * 16


def each(count, action):
    def body(i, carry):
        action(i)
        return carry

    lax.fori_loop(1, count, body, 0)


def pick_rows(result, mask, depth, columns):
    width = result.shape[1]
    out = jnp.zeros((16, width), jnp.float32)
    for c in range(columns):
        row = jnp.sum(
            jnp.where(mask, result[c * depth : (c + 1) * depth], 0.0), axis=0, keepdims=True
        )
        out = jnp.where(iota((16, width), 0) == c, row, out)
    return out


def tile_table(table_ref, tiles_ref, stage_ref, columns):
    for c in range(columns):
        for q in range(TALL):
            stage_ref[q : q + 1, :] = table_ref[c : c + 1, q * BROAD : (q + 1) * BROAD]
        tiles_ref[c * TALL : (c + 1) * TALL, :] = stage_ref[...].astype(jnp.bfloat16)


def fetch_kernel(
    capacity, micro_count, windows, columns,
    req_ref, code_ref, half_ref, table_ref, weight_ref, cin_ref, rest_ref,
    out_ref, served_ref, stat_out_ref, cins_ref, rests_ref, extras_ref,
    tiles_ref, stage_ref, first_ref, second_ref, ans_out_ref, ans_in_ref, left_ref, pooled_ref,
    other_ref, stat_ref, stat_in_ref,
    req_send, req_recv, ans_send, ans_recv, stat_send, stat_recv, win_send, win_recv, plane_send,
    plane_recv, ext_send, ext_recv, pair_send, pair_recv,
):
    first_rows, _, window, rows_msg = layout_of(micro_count, capacity)
    batch_count = windows.batch_count
    first_extra = windows.first_extra
    me = lax.axis_index("batch")
    tower = lax.axis_index("tower")
    other_tower = 1 - tower
    greet(me, batch_count, other_tower)

    def request_copy(peer, slot):
        return peer_copy(
            req_ref.at[peer], served_ref.at[slot], req_send.at[peer], req_recv.at[slot], peer
        )

    stat_ref[...] = jnp.full(stat_ref.shape, jnp.sum(weight_ref[...].astype(jnp.float32)))

    def stat_copy(peer, slot):
        return peer_copy(stat_ref, stat_in_ref.at[slot], stat_send.at[peer], stat_recv.at[slot], peer)

    def answer_copy(peer, slot):
        return peer_copy(
            ans_out_ref.at[peer], ans_in_ref.at[slot], ans_send.at[peer], ans_recv.at[slot], peer
        )

    def own_copy():
        return pltpu.make_async_copy(ans_out_ref.at[me], ans_in_ref.at[me], ans_recv.at[me])

    def send_requests(i, carry):
        peer = lax.rem(me + i, batch_count)
        request_copy(peer, me).start()
        stat_copy(peer, me).start()
        return carry

    lax.fori_loop(1, batch_count, send_requests, 0)

    depth = batch_count // PLANE
    high, low = me // PLANE, lax.rem(me, PLANE)

    def others(action):
        each(batch_count, lambda i: action(lax.rem(me + i, batch_count)))

    def column(action):
        each(depth, lambda i: action(lax.rem(high + i, depth)))

    def plane(action):
        each(PLANE, lambda i: action(lax.rem(low + i, PLANE)))

    def column_copy(src, dst, to, source):
        return peer_copy(
            src, dst.at[low * depth + source], win_send.at[to], win_recv.at[source],
            to * PLANE + low,
        )

    def plane_copy(dst, to, source):
        block = dst.at[pl.ds(source * depth, depth)]
        return peer_copy(
            block, block, plane_send.at[to], plane_recv.at[source], high * PLANE + to
        )

    def extra_copy(peer, slot):
        return peer_copy(rest_ref, extras_ref.at[slot], ext_send.at[peer], ext_recv.at[slot], peer)

    def start_windows(src, dst):
        column(lambda to: column_copy(src, dst, to, high).start())
        dst[low * depth + high] = src[...]

    def pass_windows(src, dst):
        column(lambda source: column_copy(src, dst, source, source).wait_recv())
        plane(lambda to: plane_copy(dst, to, low).start())

    def sent_windows(src, dst):
        column(lambda to: column_copy(src, dst, to, high).wait_send())
        plane(lambda to: plane_copy(dst, to, low).wait_send())

    def split(action):
        @pl.when(tower == 0)
        def _():
            action(cin_ref, cins_ref)

        @pl.when(tower == 1)
        def _():
            action(rest_ref, rests_ref)

    served_ref[me] = req_ref[me]
    stat_in_ref[me] = stat_ref[...]
    tile_table(table_ref, tiles_ref, stage_ref, columns)
    pooled_ref[...] = jnp.zeros_like(pooled_ref)

    sizes = ans_out_ref.shape[1]

    def look_up(first, second):
        for r in range(rows_msg):
            row = jnp.concatenate(
                [served_ref[first, r : r + 1, :], served_ref[second, r : r + 1, :]], axis=1
            )
            hot = ones_at(iota((BROAD, 2 * WIDE), 0) == row % BROAD)
            result = dot(tiles_ref[...], hot)
            mask = iota((TALL, 2 * WIDE), 0) == row // BROAD
            block = pick_rows(result, mask, TALL, columns)
            first_ref[r * columns : r * columns + 16, :] = block[:, :WIDE]
            second_ref[r * columns : r * columns + 16, :] = block[:, WIDE:]
        ans_out_ref[first] = first_ref[:sizes, :].astype(jnp.bfloat16)
        ans_out_ref[second] = second_ref[:sizes, :].astype(jnp.bfloat16)

    def pool(owner):
        first_ref[:sizes, :] = ans_in_ref[owner].astype(jnp.float32)
        for r in range(rows_msg):
            span = slice(r * WIDE, (r + 1) * WIDE)
            values = [first_ref[r * columns + c : r * columns + c + 1, :] for c in range(columns)]
            mask = iota((HALF, WIDE), 0) == half_ref[owner, r : r + 1, :]
            pieces = [jnp.where(mask, values[c], 0.0) for c in range(EMB)]
            pieces.append(jnp.where(iota((8, WIDE), 0) == 0, values[EMB], 0.0))
            left_ref[:, span] = jnp.concatenate(pieces, axis=0).astype(jnp.bfloat16)
        for m in range(micro_count):
            rights = [
                ones_at(iota((WIDE, WIDE), 0) + (m * WIDE + 1) == code_ref[owner, r : r + 1, :])
                for r in range(first_rows[m], first_rows[m] + window)
            ]
            span = slice(first_rows[m] * WIDE, (first_rows[m] + window) * WIDE)
            pooled_ref[m] += dot(left_ref[:, span], jnp.concatenate(rights, axis=1), NT)

    def pair_copy(src, dst, k):
        return pltpu.make_async_remote_copy(
            src_ref=src,
            dst_ref=dst,
            send_sem=pair_send.at[k],
            recv_sem=pair_recv.at[k],
            device_id={"tower": other_tower},
            device_id_type=pl.DeviceIdType.MESH,
        )

    def swap_windows():
        @pl.when(tower == 0)
        def _():
            plane(lambda source: plane_copy(cins_ref, source, source).wait_recv())
            for e in range(windows.extras):

                @pl.when(me != first_extra + e)
                def _():
                    extra_copy(first_extra + e, e).wait_recv()

            pair_copy(cins_ref, cins_ref, 0).start()
            pair_copy(extras_ref, extras_ref, 1).start()

        @pl.when(tower == 1)
        def _():
            plane(lambda source: plane_copy(rests_ref, source, source).wait_recv())
            pair_copy(rests_ref, rests_ref, 0).start()

    pairs = batch_count // 2
    lag = 2

    def step(j, carry):
        @pl.when(j < pairs)
        def _():
            first = lax.rem(me + batch_count - (2 * j + 1), batch_count)
            second = lax.rem(me + 2 * batch_count - (2 * j + 2), batch_count)
            request_copy(first, first).wait_recv()

            @pl.when(j < pairs - 1)
            def _():
                request_copy(second, second).wait_recv()

            look_up(first, second)

            @pl.when(j == 0)
            def _():
                split(start_windows)

            @pl.when((j == 0) & (tower == 0) & (me >= first_extra))
            def _():
                others(lambda peer: extra_copy(peer, me - first_extra).start())
                extras_ref[me - first_extra] = rest_ref[...]

            @pl.when(j == 3)
            def _():
                split(pass_windows)

            @pl.when(j == pairs - 2)
            def _():
                swap_windows()

            answer_copy(first, me).start()

            @pl.when(j < pairs - 1)
            def _():
                answer_copy(second, me).start()

            @pl.when(j == pairs - 1)
            def _():
                own_copy().start()

        @pl.when(j >= lag)
        def _():
            first = lax.rem(me + 2 * (j - lag) + 1, batch_count)
            answer_copy(first, first).wait_recv()
            pool(first)

        @pl.when((j >= lag) & (j < pairs - 1 + lag))
        def _():
            second = lax.rem(me + 2 * (j - lag) + 2, batch_count)
            answer_copy(second, second).wait_recv()
            pool(second)

        return carry

    lax.fori_loop(0, pairs + lag, step, 0)

    own_copy().wait()
    pool(me)

    pooled_pair = pair_copy(pooled_ref, other_ref, 2)
    pooled_pair.start()

    def finish(i, carry):
        peer = lax.rem(me + i, batch_count)
        request_copy(peer, me).wait_send()
        stat_copy(peer, me).wait_send()
        answer_copy(peer, me).wait_send()
        stat_copy(peer, peer).wait_recv()
        return carry

    lax.fori_loop(1, batch_count, finish, 0)
    stat_out_ref[...] = jnp.sum(stat_in_ref[...], axis=0)

    split(sent_windows)

    @pl.when(tower == 0)
    def _():
        @pl.when(me >= first_extra)
        def _():
            others(lambda peer: extra_copy(peer, me - first_extra).wait_send())

        pair_copy(cins_ref, cins_ref, 0).wait_send()
        pair_copy(extras_ref, extras_ref, 1).wait_send()
        pair_copy(rests_ref, rests_ref, 0).wait_recv()

    @pl.when(tower == 1)
    def _():
        pair_copy(rests_ref, rests_ref, 0).wait_send()
        pair_copy(cins_ref, cins_ref, 0).wait_recv()
        pair_copy(extras_ref, extras_ref, 1).wait_recv()

    pooled_pair.wait()
    out_ref[...] = pooled_ref[...] + other_ref[...]


def fetch(
    requests, codes, halves, table, weights, cin_window, rest_window, windows, capacity, micro_count
):
    batch_count, rows_msg, _ = requests.shape
    columns, rows_dev = table.shape
    slots = rows_msg * WIDE
    sizes = message_rows(rows_msg, columns)
    in_vmem = pl.BlockSpec(memory_space=pltpu.VMEM)
    dma = pltpu.SemaphoreType.DMA
    bags = (micro_count, BAG_ROWS, WIDE)
    return pl.pallas_call(
        partial(fetch_kernel, capacity, micro_count, windows, columns),
        in_specs=[in_vmem] * 7,
        out_specs=[in_vmem] * 6,
        out_shape=[
            jax.ShapeDtypeStruct(bags, jnp.float32),
            jax.ShapeDtypeStruct(requests.shape, jnp.int32),
            jax.ShapeDtypeStruct((8, LANES), jnp.float32),
            jax.ShapeDtypeStruct((batch_count,) + cin_window.shape, jnp.bfloat16),
            jax.ShapeDtypeStruct((batch_count,) + rest_window.shape, jnp.bfloat16),
            jax.ShapeDtypeStruct((windows.extras,) + rest_window.shape, jnp.bfloat16),
        ],
        scratch_shapes=[
            pltpu.VMEM((columns * TALL, BROAD), jnp.bfloat16),
            pltpu.VMEM((TALL, BROAD), jnp.float32),
            pltpu.VMEM((sizes + 16, WIDE), jnp.float32),
            pltpu.VMEM((sizes + 16, WIDE), jnp.float32),
            pltpu.VMEM((batch_count, sizes, WIDE), jnp.bfloat16),
            pltpu.VMEM((batch_count, sizes, WIDE), jnp.bfloat16),
            pltpu.VMEM((BAG_ROWS, slots), jnp.bfloat16),
            pltpu.VMEM(bags, jnp.float32),
            pltpu.VMEM(bags, jnp.float32),
            pltpu.VMEM((8, LANES), jnp.float32),
            pltpu.VMEM((batch_count, 8, LANES), jnp.float32),
        ]
        + [dma((batch_count,))] * 11
        + [dma((windows.extras,)), dma((3,)), dma((3,))],
        compiler_params=pltpu.CompilerParams(
            vmem_limit_bytes=vmem_limit(batch_count), collective_id=0, has_side_effects=True
        ),
        name="fetch",
    )(requests, codes, halves, table, weights, cin_window, rest_window)


def return_kernel(
    capacity, micro_count, windows, columns,
    grad_ref, code_ref, half_ref, served_ref, stat_ref, cins_ref, rests_ref, extras_ref,
    out_ref, stat_out_ref, cin_ref, rest_ref,
    send_ref, recv_ref, first_ref, second_ref, left_ref, right_ref, total_ref, stat_in_ref,
    extra_in_ref, cin_near_ref, cin_sum_ref, cin_far_ref, rest_near_ref, rest_sum_ref, rest_far_ref,
    val_send, val_recv, stat_send, stat_recv, win_send, win_recv, plane_send, plane_recv, ext_send,
    ext_recv,
):
    batch_count = windows.batch_count
    first_extra = windows.first_extra
    tower = lax.axis_index("tower")
    first_rows, _, window, rows_msg = layout_of(micro_count, capacity)
    me = lax.axis_index("batch")
    greet(me, batch_count)

    def value_copy(peer, slot):
        return peer_copy(
            send_ref.at[peer], recv_ref.at[slot], val_send.at[peer], val_recv.at[slot], peer
        )

    def own_copy():
        return pltpu.make_async_copy(send_ref.at[me], recv_ref.at[me], val_recv.at[me])

    def stat_copy(peer, slot):
        return peer_copy(stat_ref, stat_in_ref.at[slot], stat_send.at[peer], stat_recv.at[slot], peer)

    depth = batch_count // PLANE
    high, low = me // PLANE, lax.rem(me, PLANE)

    def others(action):
        each(batch_count, lambda i: action(lax.rem(me + i, batch_count)))

    def column(action):
        each(depth, lambda i: action(lax.rem(high + i, depth)))

    def plane(action):
        each(PLANE, lambda i: action(lax.rem(low + i, PLANE)))

    def plane_copy(src, near, to, source):
        return peer_copy(
            src.at[pl.ds(to * depth, depth)], near.at[source], plane_send.at[to],
            plane_recv.at[source], high * PLANE + to,
        )

    def column_copy(total, far, to, source):
        return peer_copy(
            total.at[to], far.at[source], win_send.at[to], win_recv.at[source], to * PLANE + low
        )

    def start_windows(src, near, total, far, out):
        plane(lambda to: plane_copy(src, near, to, low).start())
        near[low] = src[pl.ds(low * depth, depth)]

    def pass_windows(src, near, total, far, out):
        plane(lambda source: plane_copy(src, near, source, source).wait_recv())
        total[...] = jnp.sum(near[...], axis=0)
        column(lambda to: column_copy(total, far, to, high).start())
        far[high] = total[high]

    def end_windows(src, near, total, far, out):
        column(lambda source: column_copy(total, far, source, source).wait_recv())
        out[...] = jnp.sum(far[...], axis=0)
        plane(lambda to: plane_copy(src, near, to, low).wait_send())
        column(lambda to: column_copy(total, far, to, high).wait_send())

    def split(action):
        @pl.when(tower == 0)
        def _():
            action(cins_ref, cin_near_ref, cin_sum_ref, cin_far_ref, cin_ref)

        @pl.when(tower == 1)
        def _():
            action(rests_ref, rest_near_ref, rest_sum_ref, rest_far_ref, rest_ref)

    def extra_copy(peer, slot):
        return peer_copy(
            extras_ref.at[peer - first_extra],
            extra_in_ref.at[slot],
            ext_send.at[peer],
            ext_recv.at[slot],
            peer,
        )

    def send_stats(i, carry):
        stat_copy(lax.rem(me + i, batch_count), me).start()
        return carry

    lax.fori_loop(1, batch_count, send_stats, 0)
    stat_in_ref[me] = stat_ref[...]
    total_ref[...] = jnp.zeros_like(total_ref)

    sizes = send_ref.shape[1]

    def spread(first, second):
        for r in range(rows_msg):
            code = jnp.concatenate(
                [code_ref[first, r : r + 1, :], code_ref[second, r : r + 1, :]], axis=1
            )
            half = jnp.concatenate(
                [half_ref[first, r : r + 1, :], half_ref[second, r : r + 1, :]], axis=1
            )
            result = None
            for m in range(micro_count):
                if first_rows[m] <= r < first_rows[m] + window:
                    hot = ones_at(iota((WIDE, 2 * WIDE), 0) + (m * WIDE + 1) == code)
                    found = dot(grad_ref[m], hot)
                    result = found if result is None else result + found
            block = pick_rows(result, iota((HALF, 2 * WIDE), 0) == half, HALF, EMB)
            linear = result[EMB * HALF : EMB * HALF + 1]
            block = jnp.where(iota((16, 2 * WIDE), 0) == EMB, linear, block)
            first_ref[r * columns : r * columns + 16, :] = block[:, :WIDE]
            second_ref[r * columns : r * columns + 16, :] = block[:, WIDE:]
        send_ref[first] = first_ref[:sizes, :].astype(jnp.bfloat16)
        send_ref[second] = second_ref[:sizes, :].astype(jnp.bfloat16)

    def scatter(source):
        first_ref[:sizes, :] = recv_ref[source].astype(jnp.float32)
        for r in range(rows_msg):
            span = slice(r * WIDE, (r + 1) * WIDE)
            row = served_ref[source, r : r + 1, :]
            mask = iota((TALL, WIDE), 0) == row // BROAD
            for c in range(columns):
                left_ref[c * TALL : (c + 1) * TALL, span] = jnp.where(
                    mask, first_ref[r * columns + c : r * columns + c + 1, :], 0.0
                ).astype(jnp.bfloat16)
            right_ref[:, span] = ones_at(iota((BROAD, WIDE), 0) == row % BROAD)
        total_ref[...] += dot(left_ref[...], right_ref[...], NT)

    pairs = batch_count // 2
    lag = 2

    def step(j, carry):
        @pl.when(j < pairs)
        def _():
            first = lax.rem(me + 2 * j + 1, batch_count)
            second = lax.rem(me + 2 * j + 2, batch_count)
            spread(first, second)
            value_copy(first, me).start()

            @pl.when(j == 1)
            def _():
                split(start_windows)

            @pl.when((j == 1) & (tower == 0))
            def _():
                for e in range(windows.extras):

                    @pl.when(me != first_extra + e)
                    def _():
                        extra_copy(first_extra + e, me).start()

            @pl.when(j < pairs - 1)
            def _():
                value_copy(second, me).start()

            @pl.when(j == pairs - 1)
            def _():
                own_copy().start()

        @pl.when(j == pairs - 1)
        def _():
            split(pass_windows)

        @pl.when(j >= lag)
        def _():
            first = lax.rem(me + batch_count - (2 * (j - lag) + 1), batch_count)
            value_copy(first, first).wait_recv()
            scatter(first)

        @pl.when((j >= lag) & (j < pairs - 1 + lag))
        def _():
            second = lax.rem(me + 2 * batch_count - (2 * (j - lag) + 2), batch_count)
            value_copy(second, second).wait_recv()
            scatter(second)

        return carry

    lax.fori_loop(0, pairs + lag, step, 0)
    own_copy().wait()
    scatter(me)

    split(end_windows)

    @pl.when(tower == 0)
    def _():
        for e in range(windows.extras):

            @pl.when(me != first_extra + e)
            def _():
                extra_copy(first_extra + e, me).wait_send()

        @pl.when(me >= first_extra)
        def _():
            extra_in_ref[me] = extras_ref[me - first_extra]
            others(lambda peer: extra_copy(me, peer).wait_recv())
            rest_ref[...] = jnp.sum(extra_in_ref[...], axis=0)

        @pl.when(me < first_extra)
        def _():
            rest_ref[...] = jnp.zeros_like(rest_ref)

    @pl.when(tower == 1)
    def _():
        cin_ref[...] = jnp.zeros_like(cin_ref)

    def finish(i, carry):
        peer = lax.rem(me + i, batch_count)
        value_copy(peer, me).wait_send()
        stat_copy(peer, me).wait_send()
        stat_copy(peer, peer).wait_recv()
        return carry

    lax.fori_loop(1, batch_count, finish, 0)
    stat_out_ref[...] = jnp.sum(stat_in_ref[...], axis=0)
    for c in range(columns):
        for q in range(TALL):
            out_ref[c : c + 1, q * BROAD : (q + 1) * BROAD] = total_ref[
                c * TALL + q : c * TALL + q + 1, :
            ]


def return_grads(
    grad_bags, codes, halves, served, stat, cins, rests, extras, windows, capacity, columns
):
    batch_count, rows_msg, _ = codes.shape
    micro_count = grad_bags.shape[0]
    slots = rows_msg * WIDE
    sizes = message_rows(rows_msg, columns)
    depth = batch_count // PLANE
    in_vmem = pl.BlockSpec(memory_space=pltpu.VMEM)
    dma = pltpu.SemaphoreType.DMA
    return pl.pallas_call(
        partial(return_kernel, capacity, micro_count, windows, columns),
        in_specs=[in_vmem] * 8,
        out_specs=[in_vmem] * 4,
        out_shape=[
            jax.ShapeDtypeStruct((columns, TALL * BROAD), jnp.float32),
            jax.ShapeDtypeStruct(stat.shape, jnp.float32),
            jax.ShapeDtypeStruct(cins.shape[1:], jnp.float32),
            jax.ShapeDtypeStruct(rests.shape[1:], jnp.float32),
        ],
        scratch_shapes=[
            pltpu.VMEM((batch_count, sizes, WIDE), jnp.bfloat16),
            pltpu.VMEM((batch_count, sizes, WIDE), jnp.bfloat16),
            pltpu.VMEM((sizes + 16, WIDE), jnp.float32),
            pltpu.VMEM((sizes + 16, WIDE), jnp.float32),
            pltpu.VMEM((columns * TALL, slots), jnp.bfloat16),
            pltpu.VMEM((BROAD, slots), jnp.bfloat16),
            pltpu.VMEM((columns * TALL, BROAD), jnp.float32),
            pltpu.VMEM((batch_count,) + stat.shape, jnp.float32),
            pltpu.VMEM(rests.shape, jnp.float32),
        ]
        + [
            pltpu.VMEM(lead + x.shape[1:], jnp.float32)
            for x in (cins, rests)
            for lead in ((PLANE, depth), (depth,), (depth,))
        ]
        + [dma((batch_count,))] * 10,
        compiler_params=pltpu.CompilerParams(
            vmem_limit_bytes=vmem_limit(batch_count), collective_id=1, has_side_effects=True
        ),
        name="return_grads",
    )(grad_bags, codes, halves, served, stat, cins, rests, extras)


def split_three(x):
    high = x.astype(jnp.bfloat16)
    rest = x - high.astype(jnp.float32)
    middle = rest.astype(jnp.bfloat16)
    low = (rest - middle.astype(jnp.float32)).astype(jnp.bfloat16)
    return high, middle, low


def dense_kernel(
    micro_count, windows, tower_ref, stat_ref, pooled_ref, label_ref, weight_ref,
    cins_ref, rests_ref, extras_ref,
    bags_ref, loss_ref, g_cins_ref, g_rests_ref, g_extras_ref,
    embed_ref, total_ref, pairs_ref, sym_ref, cin_ref, rest_ref, lane_ref,
):
    f32 = jnp.float32
    bf16 = jnp.bfloat16
    width = micro_count * LANES
    groups = HPAD // LANES

    cin_ref[...] = jnp.zeros_like(cin_ref)
    for b, at in enumerate(windows.cin_at):
        block = cins_ref[windows.slots[b]].astype(f32)
        cin_ref[at : at + windows.cin_rows, :] += block[: windows.cin_rows]
    rest_ref[...] = jnp.zeros_like(rest_ref)
    pieces = [(rests_ref, windows.slots[b], at) for b, at in enumerate(windows.rest_at)]
    pieces += [(extras_ref, e, at) for e, at in enumerate(windows.extra_at)]
    for source, b, at in pieces:
        skip = max(0, -at)
        block = source[b].astype(f32)
        for l in range(groups):
            rest_ref[l, at + skip : at + windows.rest_rows, :] += block[
                skip : windows.rest_rows, l * LANES : (l + 1) * LANES
            ]

    def rest_rows(begin, count):
        return jnp.concatenate(
            [rest_ref[l, begin : begin + count, :] for l in range(groups)], axis=1
        )[:, :HID]

    cin_w = cin_ref[:MAPS, :].astype(bf16)
    place = iota((MAPS, PAIRS), 0)
    place = place // FIELDS * FPAD + place % FIELDS == iota((MAPS, PAIRS), 1)
    picks_u = ones_at(place)
    row_u = jnp.broadcast_to(cin_ref[MAPS : MAPS + 1, :], (8, PAIRS)).astype(bf16)
    cin_u = dot(picks_u, row_u, NT)[:, :1]
    w_one = jnp.concatenate(
        [
            jnp.concatenate(
                [rest_ref[l, pl.ds(d, FPAD, stride=EMB), :] for l in range(groups)], axis=1
            )[:, :HID]
            for d in range(EMB)
        ],
        axis=0,
    ).astype(bf16)
    w_two = rest_rows(W_TWO, HID).astype(bf16)
    rows = jnp.zeros((8, HID), f32)
    for k, at in enumerate((B_ONE, B_TWO, W_THREE)):
        rows = jnp.where(iota((8, HID), 0) == k, rest_rows(at, 1), rows)
    unit = ones_at(iota((HID, HID), 0) == iota((HID, HID), 1))
    turned = dot(unit, rows.astype(bf16), NT)
    b_one, b_two, w_three = turned[:, 0:1], turned[:, 1:2], turned[:, 2:3]
    bias = rest_ref[0, BIAS : BIAS + 1, 0:1]

    def unpacked(row, count):
        pieces = []
        for m in range(micro_count):
            low = pooled_ref[m, row : row + HALF, :LANES]
            high = pooled_ref[m, row : row + HALF, LANES:]
            pieces.append(jnp.concatenate([low, high], axis=0)[:count])
        return jnp.concatenate(pieces, axis=1)

    for d in range(EMB):
        embed_ref[d * FPAD : (d + 1) * FPAD, :] = unpacked(d * HALF, FPAD)
    linear = jnp.concatenate(
        [
            pooled_ref[m, EMB * HALF : EMB * HALF + 1, :LANES]
            + pooled_ref[m, EMB * HALF : EMB * HALF + 1, LANES:]
            for m in range(micro_count)
        ],
        axis=1,
    )

    def pair_row(i, carry):
        total = jnp.zeros((FPAD, width), f32)
        for d in range(EMB):
            own = embed_ref[pl.ds(d * FPAD + i, 1), :]
            product = (embed_ref[d * FPAD : (d + 1) * FPAD, :] * own).astype(jnp.bfloat16)
            total = total + product.astype(f32)
        total_ref[pl.ds(pl.multiple_of(i * FPAD, 8), FPAD), :] = total
        return carry

    lax.fori_loop(0, FIELDS, pair_row, 0, unroll=3)
    thirds = split_three(total_ref[...])
    map_sum = sum(dot(cin_w, third) for third in thirds)
    cin_logits = jnp.sum(map_sum * cin_u, axis=0, keepdims=True)

    flat = embed_ref[...].astype(jnp.bfloat16)
    pre_one = dot(w_one, flat, TN) + b_one
    hidden_one = jnp.maximum(pre_one, 0.0).astype(jnp.bfloat16)
    pre_two = dot(w_two, hidden_one, TN) + b_two
    active_two = jnp.maximum(pre_two, 0.0)
    deep_logits = jnp.sum(active_two * w_three, axis=0, keepdims=True)
    logits = cin_logits + deep_logits + linear + bias

    samples = weight_ref.shape[1]
    lane_ref[...] = jnp.zeros_like(lane_ref)
    for m in range(micro_count):
        span = slice(m * LANES, m * LANES + samples)
        lane_ref[0:1, span] = weight_ref[m : m + 1, :].astype(f32)
        lane_ref[1:2, span] = label_ref[m : m + 1, :].astype(f32)
    weight = lane_ref[0:1, :]
    label = lane_ref[1:2, :]
    soft = jnp.maximum(logits, 0.0) + jnp.log1p(jnp.exp(-jnp.abs(logits)))
    loss_ref[...] = jnp.broadcast_to(
        jnp.sum(weight * (soft - label * logits), axis=1, keepdims=True), loss_ref.shape
    )
    grad_logits = weight * (jax.nn.sigmoid(logits) - label) / stat_ref[0:1, 0:1]

    grad_maps = (grad_logits * cin_u).astype(jnp.bfloat16)
    grad_two = jnp.where(pre_two > 0, grad_logits * w_three, 0.0).astype(jnp.bfloat16)
    grad_hidden = dot(w_two, grad_two)
    grad_one = jnp.where(pre_one > 0, grad_hidden, 0.0).astype(jnp.bfloat16)
    grad_flat = dot(w_one, grad_one)

    grad_pairs = dot(cin_w, grad_maps, TN)
    for m in range(micro_count):
        pairs_ref[m, :PAIRS, :] = grad_pairs[:, m * LANES : (m + 1) * LANES]
        pairs_ref[m, PAIRS:, :] = jnp.zeros((FPAD * FPAD - PAIRS, LANES), f32)

    def mirror(j, carry):
        here = pl.ds(pl.multiple_of(j * FPAD, 8), FPAD)
        both = [
            pairs_ref[m, here, :] + pairs_ref[m, pl.ds(j, FPAD, stride=FPAD), :]
            for m in range(micro_count)
        ]
        sym_ref[here, :] = jnp.concatenate(both, axis=1)
        return carry

    lax.fori_loop(0, FIELDS, mirror, 0, unroll=3)
    empty = jnp.zeros((2 * HALF - FPAD, width), f32)

    for d in range(EMB):

        def add_row(j, total):
            here = pl.ds(pl.multiple_of(j * FPAD, 8), FPAD)
            return total + sym_ref[here, :] * embed_ref[pl.ds(d * FPAD + j, 1), :]

        grad_embed = lax.fori_loop(
            0, FIELDS, add_row, grad_flat[d * FPAD : (d + 1) * FPAD], unroll=13
        )
        grad_embed = jnp.concatenate([grad_embed, empty], axis=0)
        for m in range(micro_count):
            span = slice(m * LANES, (m + 1) * LANES)
            block = jnp.concatenate([grad_embed[:HALF, span], grad_embed[HALF:, span]], axis=1)
            bags_ref[m, d * HALF : (d + 1) * HALF, :] = block.astype(bf16)
    for m in range(micro_count):
        row = grad_logits[:, m * LANES : (m + 1) * LANES]
        row = jnp.concatenate([row, row], axis=1)
        bags_ref[m, EMB * HALF :, :] = jnp.broadcast_to(row, (8, WIDE)).astype(bf16)

    ones = jnp.ones((8, width), bf16)

    def row_sum(x):
        return sum(dot(ones, third, NT) for third in split_three(x))[:1]

    rest_ref[...] = jnp.zeros_like(rest_ref)

    def put(begin, count, value, stride=None):
        for l in range(groups):
            piece = value[:, l * LANES : min((l + 1) * LANES, HID)]
            lanes = slice(0, piece.shape[1])
            if stride is None:
                rest_ref[l, begin : begin + count, lanes] = piece
            else:
                piece = jnp.pad(piece, ((0, 0), (0, LANES - piece.shape[1])))
                rest_ref[l, pl.ds(begin, count, stride=stride), :] = piece

    g_w_one = dot(flat, grad_one, NT)
    for d in range(EMB):
        put(d, FIELDS, g_w_one[d * FPAD : d * FPAD + FIELDS], EMB)

    @pl.when(tower_ref[0] == 0)
    def _():
        cin_ref[...] = jnp.zeros_like(cin_ref)
        cin_ref[:MAPS, :] = sum(dot(grad_maps, third, NT) for third in thirds)
        g_cin_u = jnp.sum(map_sum * grad_logits, axis=1, keepdims=True)
        thirds_u = split_three(jnp.broadcast_to(g_cin_u, (MAPS, 8)))
        cin_ref[MAPS : MAPS + 1, :] = sum(dot(third, picks_u, TN) for third in thirds_u)[:1]
        for b, at in enumerate(windows.cin_at):
            g_cins_ref[windows.slots[b], : windows.cin_rows, :] = cin_ref[
                at : at + windows.cin_rows, :
            ]
        for e, at in enumerate(windows.extra_at):
            skip = max(0, -at)
            for l in range(groups):
                span = slice(l * LANES, (l + 1) * LANES)
                g_extras_ref[e, skip : windows.rest_rows, span] = rest_ref[
                    l, at + skip : at + windows.rest_rows, :
                ]

    @pl.when(tower_ref[0] != 0)
    def _():
        put(W_TWO, HID, dot(hidden_one, grad_two, NT))
        put(B_ONE, 1, dot(ones, grad_one, NT)[:1])
        put(B_TWO, 1, dot(ones, grad_two, NT)[:1])
        put(W_THREE, 1, row_sum(active_two * grad_logits))
        g_bias = jnp.sum(grad_logits, axis=1, keepdims=True)
        put(BIAS, 1, jnp.where(iota((1, HID), 1) == 0, g_bias, 0.0))
        for b, at in enumerate(windows.rest_at):
            for l in range(groups):
                span = slice(l * LANES, (l + 1) * LANES)
                g_rests_ref[windows.slots[b], : windows.rest_rows, span] = rest_ref[
                    l, at : at + windows.rest_rows, :
                ]


def dense_step(tower_at, stats, pooled, labels, weights, cins, rests, extras, windows):
    micro_count = pooled.shape[0]
    width = micro_count * LANES
    in_vmem = pl.BlockSpec(memory_space=pltpu.VMEM)
    in_smem = pl.BlockSpec(memory_space=pltpu.SMEM)
    f32 = jnp.float32
    shapes = [
        ((micro_count, BAG_ROWS, WIDE), jnp.bfloat16),
        ((8, LANES), f32),
        (cins.shape, f32),
        (rests.shape, f32),
        (extras.shape, f32),
    ]
    return pl.pallas_call(
        partial(dense_kernel, micro_count, windows),
        in_specs=[in_smem] + [in_vmem] * 7,
        out_specs=[in_vmem] * len(shapes),
        out_shape=[jax.ShapeDtypeStruct(*shape) for shape in shapes],
        scratch_shapes=[
            pltpu.VMEM((EMB * FPAD, width), f32),
            pltpu.VMEM((PAIRS, width), f32),
            pltpu.VMEM((micro_count, FPAD * FPAD, LANES), f32),
            pltpu.VMEM((PAIRS, width), f32),
            pltpu.VMEM((windows.cin_total, PAIRS), f32),
            pltpu.VMEM((HPAD // LANES, windows.rest_total, LANES), f32),
            pltpu.VMEM((8, width), f32),
        ],
        compiler_params=pltpu.CompilerParams(vmem_limit_bytes=vmem_limit(windows.batch_count)),
        name="dense",
    )(tower_at.reshape(1), stats, pooled, labels, weights, cins, rests, extras)


def shards(
    shard_ids,
    local_rows,
    bag_counts,
    click_labels,
    sample_weights,
    embed_table,
    table_first,
    table_second,
    dense_params,
    dense_first,
    dense_second,
):
    tower_count = lax.axis_size("tower")
    batch_count = lax.axis_size("batch")
    tower_at = lax.axis_index("tower")
    micro_count, samples = shard_ids.shape[:2]
    columns, rows_dev = embed_table.shape
    capacity = 4 * samples * IDS_SAMP // (tower_count * batch_count)
    share = dense_params.shape[0]
    windows = Windows(share, batch_count)

    device = tower_at * batch_count + lax.axis_index("batch")
    cin_phase, rest_phase = windows.phases(device)
    low = dense_params.astype(jnp.bfloat16)

    def window(rows, row_size, phase):
        return lax.dynamic_update_slice(
            jnp.zeros((rows * row_size,), jnp.bfloat16), low, (phase,)
        )

    cin_window = window(windows.cin_rows, SQUARE, cin_phase).reshape(-1, FIELDS, FIELDS)
    cin_window = jnp.pad(
        cin_window,
        ((0, windows.cin_pad - windows.cin_rows), (0, 0), (0, FPAD - FIELDS)),
    ).reshape(windows.cin_pad, PAIRS)
    rest_window = jnp.pad(
        window(windows.rest_rows, HID, rest_phase).reshape(-1, HID),
        ((0, windows.rest_pad - windows.rest_rows), (0, HPAD - HID)),
    )

    def lanes_of(values):
        return jnp.moveaxis(values, 1, -1).reshape(micro_count, -1, samples)

    requests, codes, halves = route(
        lanes_of(shard_ids), lanes_of(local_rows), lanes_of(bag_counts), capacity, batch_count
    )
    pooled, served, stats, cins, rests, extras = fetch(
        requests, codes, halves, embed_table, sample_weights, cin_window, rest_window, windows,
        capacity, micro_count,
    )
    grad_bags, loss, g_cins, g_rests, g_extras = dense_step(
        tower_at, stats, pooled, click_labels, sample_weights, cins, rests, extras, windows
    )
    table_grad, losses, g_cin, g_rest = return_grads(
        grad_bags, codes, halves, served, loss, g_cins, g_rests, g_extras, windows, capacity, columns
    )
    g_cin = g_cin[: windows.cin_rows].reshape(-1, FIELDS, FPAD)[:, :, :FIELDS].reshape(-1)
    g_rest = g_rest[: windows.rest_rows, :HID].reshape(-1)
    is_cin = device * share + jnp.arange(share, dtype=jnp.int32) < CIN_SIZE
    own_grad = jnp.where(
        is_cin,
        lax.dynamic_slice(g_cin, (cin_phase,), (share,)),
        lax.dynamic_slice(g_rest, (rest_phase,), (share,)),
    )

    table_new, table_first_new, table_second_new = adam_update(
        embed_table, table_first, table_second, table_grad, rate_table
    )
    dense_new, dense_first_new, dense_second_new = adam_update(
        dense_params, dense_first, dense_second, own_grad, rate_dense
    )
    loss_sum = losses[0, 0] / stats[0, 0]
    return (
        table_new,
        table_first_new,
        table_second_new,
        table_new.astype(jnp.bfloat16),
        dense_new,
        dense_first_new,
        dense_second_new,
        dense_new.astype(jnp.bfloat16),
        loss_sum,
    )


def solution(mesh):
    rows = P(None, ("tower", "batch"))
    dense = P(("tower", "batch"))
    placed = (
        P(None, "batch", None, None),
        P(None, "batch", None, None),
        P(None, "batch", None),
        P(None, "batch"),
        P(None, "batch"),
        rows,
        rows,
        rows,
        dense,
        dense,
        dense,
    )
    return jax.shard_map(
        shards,
        mesh=mesh,
        in_specs=placed,
        out_specs=(rows, rows, rows, rows, dense, dense, dense, dense, P()),
        check_vma=False,
    )
```

```python
from functools import partial

import jax
import jax.numpy as jnp
from jax import lax
from jax.experimental import pallas as pl
from jax.experimental.pallas import tpu as pltpu
from jax.sharding import PartitionSpec as P

FIELDS = 39
EMB = 10
MAPS = 200
HID = 400
IDS_SAMP = 80

beta_one = 0.9
beta_two = 0.999
epsilon = 1e-08
decay_rate = 0.15
rate_table = 0.1
rate_dense = 0.05
step_count = 10

LANES = 128
WIDE = 256
BROAD = 512
TALL = 64
HALF = 24
BAG_ROWS = EMB * HALF + 8
FPAD = 40
PAIRS = FIELDS * FPAD
SQUARE = FIELDS * FIELDS
CIN_SIZE = MAPS * SQUARE + MAPS
FLAT = EMB * FIELDS
B_ONE, W_TWO, B_TWO, W_THREE, BIAS = FLAT, FLAT + 1, FLAT + HID + 1, FLAT + HID + 2, FLAT + HID + 3
HPAD = 512
PLANE = 4
NT = (((1,), (1,)), ((), ()))
TN = (((0,), (0,)), ((), ()))
NN = (((1,), (0,)), ((), ()))


def adam_update(weight, first_old, second_old, gradient, step_rate):
    first_new = beta_one * first_old + (1.0 - beta_one) * gradient
    second_new = beta_two * second_old + (1.0 - beta_two) * gradient * gradient
    first_hat = first_new / (1.0 - beta_one**step_count)
    second_hat = second_new / (1.0 - beta_two**step_count)
    weight_new = weight - step_rate * (
        first_hat / (jnp.sqrt(second_hat) + epsilon) + decay_rate * weight
    )
    return (weight_new, first_new, second_new)


def dot(a, b, dims=NN):
    return lax.dot_general(a, b, dims, preferred_element_type=jnp.float32)


def vmem_limit(batch_count):
    return (28 + batch_count // 4) << 20


def iota(shape, dim):
    return lax.broadcasted_iota(jnp.int32, shape, dim)


def ones_at(mask):
    return jnp.where(mask, 1.0, 0.0).astype(jnp.bfloat16)


class Slots:
    def __init__(self, micro_count, capacity):
        self.micro_count = micro_count
        self.first_rows = [m * capacity // WIDE for m in range(micro_count)]
        self.shifts = [m * capacity % WIDE for m in range(micro_count)]
        self.spans = [-(-(shift + capacity) // LANES) * LANES for shift in self.shifts]
        self.length = max(
            first * WIDE + span for first, span in zip(self.first_rows, self.spans)
        )
        self.rows = -(-self.length // WIDE)
        self.window = max(-(-span // WIDE) for span in self.spans)

    def width(self, row):
        return min(WIDE, self.length - row * WIDE)

    def micro_width(self, micro, row):
        inside = row - self.first_rows[micro]
        return max(0, min(WIDE, self.spans[micro] - inside * WIDE)) if inside >= 0 else 0


class Windows:
    def __init__(self, share, batch_count):
        self.share, self.batch_count = share, batch_count
        self.cin_rows = -(-(SQUARE - 1 + share) // SQUARE)
        self.rest_rows = -(-(HID - 1 + share) // HID)
        self.cin_pad = -(-self.cin_rows // 16) * 16
        self.rest_pad = -(-self.rest_rows // 16) * 16
        self.cin_pad_wide = -(-self.cin_rows // 8) * 8
        self.rest_pad_wide = -(-self.rest_rows // 8) * 8
        self.first_extra = CIN_SIZE // share
        self.extras = batch_count - self.first_extra
        self.cin_at = [b * share // SQUARE for b in range(batch_count)]
        self.rest_at = [
            ((batch_count + b) * share - CIN_SIZE) // HID for b in range(batch_count)
        ]
        self.extra_at = [
            (b * share - CIN_SIZE) // HID for b in range(self.first_extra, batch_count)
        ]
        depth = batch_count // PLANE
        self.slots = [b % PLANE * depth + b // PLANE for b in range(batch_count)]
        self.cin_total = -(-max(a + self.cin_rows for a in self.cin_at) // 8) * 8
        self.rest_total = -(-max(a + self.rest_rows for a in self.rest_at) // 8) * 8

    def phases(self, device):
        start = device * self.share
        return start % SQUARE, jnp.mod(start - CIN_SIZE, HID)


def route_kernel(
    slots, batch_count, ids_ref, rows_ref, counts_ref,
    req_ref, code_ref, half_ref, part_ref, left_ref, right_ref,
):
    f32, bf16 = jnp.float32, jnp.bfloat16
    micro_count, window = slots.micro_count, slots.window
    micro = pl.program_id(0)
    id_rows, samples = ids_ref.shape[1:]
    chunk = 16
    tower = lax.axis_index("tower")

    @pl.when(micro == 0)
    def _():
        req_ref[...] = jnp.zeros_like(req_ref)
        code_ref[...] = jnp.zeros_like(code_ref)
        half_ref[...] = jnp.zeros_like(half_ref)
        part_ref[...] = jnp.zeros_like(part_ref)

    def widened(x, filler):
        part_ref[0, :, :samples] = x.astype(f32)
        inside = iota((id_rows, LANES), 1) < samples
        return jnp.where(inside, part_ref[0], filler)

    owner = ids_ref[0]
    target = widened(
        jnp.where(owner // batch_count == tower, owner % batch_count, batch_count), batch_count
    ).astype(jnp.int32)
    local = widened(rows_ref[0], 0.0).astype(jnp.int32)
    before = ones_at(iota((FIELDS, FIELDS), 1) <= iota((FIELDS, FIELDS), 0))
    ends = dot(before, counts_ref[0].astype(f32).astype(bf16)).astype(jnp.int32)
    field = jnp.zeros((id_rows, samples), jnp.int32)
    for f in range(FIELDS):
        field = field + jnp.where(iota((id_rows, samples), 0) >= ends[f : f + 1], 1, 0)
    field = widened(field, 0.0)
    late = jnp.where(field >= HALF, 1.0, 0.0)

    earlier_rows = ones_at(iota((id_rows, id_rows), 1) < iota((id_rows, id_rows), 0))
    upper = iota((2 * LANES, LANES), 0)
    mixing = ones_at((upper < iota((2 * LANES, LANES), 1)) | (upper >= LANES))
    rank = jnp.zeros((id_rows, LANES), f32)
    for begin in range(0, batch_count, chunk):
        hots = [ones_at(target == begin + d) for d in range(chunk)]
        above = dot(earlier_rows, jnp.concatenate(hots, axis=1)).astype(bf16)
        stacked = jnp.concatenate(
            [
                jnp.concatenate([hots[d], above[:, d * LANES : (d + 1) * LANES]], axis=1)
                for d in range(chunk)
            ],
            axis=0,
        )
        ranks = dot(stacked, mixing)
        for d in range(chunk):
            rank = rank + jnp.where(
                target == begin + d, ranks[d * id_rows : (d + 1) * id_rows], 0.0
            )
    shift = sum(jnp.where(micro == m, slots.shifts[m], 0) for m in range(micro_count))
    slot = rank.astype(jnp.int32) + shift
    place = jnp.where(target < batch_count, (slot // WIDE) * batch_count + target, -1)
    part_ref[0] = place.astype(f32)
    part_ref[1] = (slot % WIDE).astype(f32)
    part_ref[2] = (local // WIDE).astype(f32)
    part_ref[3] = (local % WIDE).astype(f32)
    part_ref[4] = late * LANES + (iota((id_rows, LANES), 1) + 1).astype(f32)
    part_ref[5] = field - late * HALF
    places = window * batch_count

    def build(t, carry):
        span = pl.ds(pl.multiple_of(t * LANES, LANES), LANES)

        def row(k):
            return part_ref[k, pl.ds(t, 1), :]

        mask = iota((places, LANES), 0).astype(f32) == row(0)
        for v in range(4):
            left_ref[v * places : (v + 1) * places, span] = jnp.where(
                mask, row(2 + v), 0.0
            ).astype(bf16)
        right_ref[:, span] = ones_at(iota((WIDE, LANES), 0).astype(f32) == row(1))
        return carry

    lax.fori_loop(0, id_rows, build, 0, unroll=4)
    placed = dot(left_ref[...], right_ref[...], NT).astype(jnp.int32)

    def part(v, r):
        begin = (v * window + r) * batch_count
        return placed[begin : begin + batch_count]

    for m in range(micro_count):

        @pl.when(micro == m)
        def _():
            for r in range(window):
                at = slots.first_rows[m] + r
                if slots.micro_width(m, at) == 0:
                    continue
                code = part(2, r)
                req_ref[:, at, :] += part(0, r) * WIDE + part(1, r)
                code_ref[:, at, :] += jnp.where(code > 0, code + m * WIDE, 0)
                half_ref[:, at, :] += part(3, r)


def in_hbm(x):
    return pltpu.with_memory_space_constraint(x, pltpu.HBM)


def route(ids, rows, counts, slots, batch_count):
    micro_count, id_rows, samples = ids.shape
    places = slots.window * batch_count

    def block(x):
        return pl.BlockSpec((1,) + x.shape[1:], lambda m: (m, 0, 0))

    whole = pl.BlockSpec((batch_count, slots.rows, WIDE), lambda m: (0, 0, 0))
    shape = jax.ShapeDtypeStruct((batch_count, slots.rows, WIDE), jnp.int32)
    return pl.pallas_call(
        partial(route_kernel, slots, batch_count),
        grid=(micro_count,),
        in_specs=[block(ids), block(rows), block(counts)],
        out_specs=[whole] * 3,
        out_shape=[shape] * 3,
        scratch_shapes=[
            pltpu.VMEM((6, id_rows, LANES), jnp.float32),
            pltpu.VMEM((4 * places, id_rows * LANES), jnp.bfloat16),
            pltpu.VMEM((WIDE, id_rows * LANES), jnp.bfloat16),
        ],
        compiler_params=pltpu.CompilerParams(vmem_limit_bytes=vmem_limit(batch_count)),
        name="route",
    )(in_hbm(ids), in_hbm(rows), in_hbm(counts))


def peer_copy(src, dst, send_sem, recv_sem, peer):
    return pltpu.make_async_remote_copy(
        src_ref=src,
        dst_ref=dst,
        send_sem=send_sem,
        recv_sem=recv_sem,
        device_id={"batch": peer},
        device_id_type=pl.DeviceIdType.MESH,
    )


def greet(me, batch_count, other_tower=None):
    barrier = pltpu.get_barrier_semaphore()

    def signal(i, carry):
        pl.semaphore_signal(
            barrier,
            inc=1,
            device_id={"batch": lax.rem(me + i, batch_count)},
            device_id_type=pl.DeviceIdType.MESH,
        )
        return carry

    lax.fori_loop(1, batch_count, signal, 0)
    if other_tower is not None:
        pl.semaphore_signal(
            barrier,
            inc=1,
            device_id={"tower": other_tower},
            device_id_type=pl.DeviceIdType.MESH,
        )


def all_greeted(batch_count, pair):
    pl.semaphore_wait(pltpu.get_barrier_semaphore(), batch_count - 1 + (1 if pair else 0))


def message_rows(rows_msg, columns):
    return -(-rows_msg * columns // 16) * 16


def each(count, action):
    def body(i, carry):
        action(i)
        return carry

    lax.fori_loop(1, count, body, 0)


def pick_rows(result, mask, depth, columns):
    width = result.shape[1]
    out = jnp.zeros((16, width), jnp.float32)
    for c in range(columns):
        row = jnp.sum(
            jnp.where(mask, result[c * depth : (c + 1) * depth], 0.0), axis=0, keepdims=True
        )
        out = jnp.where(iota((16, width), 0) == c, row, out)
    return out


def tile_table(table_ref, tiles_ref, stage_ref, columns):
    for c in range(columns):
        for q in range(TALL):
            stage_ref[q : q + 1, :] = table_ref[c : c + 1, q * BROAD : (q + 1) * BROAD]
        tiles_ref[c * TALL : (c + 1) * TALL, :] = stage_ref[...].astype(jnp.bfloat16)


def fetch_kernel(
    slots, windows, columns,
    req_ref, code_ref, half_ref, table_hbm_ref, weight_ref, cin_ref, rest_ref,
    out_ref, served_ref, stat_out_ref, cins_ref, rests_ref, extras_ref,
    table_ref, tiles_ref, stage_ref, first_ref, second_ref, ans_out_ref, ans_in_ref, left_ref, pooled_ref,
    other_ref, stat_ref, stat_in_ref,
    req_send, req_recv, ans_send, ans_recv, stat_send, stat_recv, win_send, win_recv, plane_send,
    plane_recv, ext_send, ext_recv, pair_send, pair_recv, table_sem,
):
    rows_msg = slots.rows
    batch_count = windows.batch_count
    first_extra = windows.first_extra
    me = lax.axis_index("batch")
    tower = lax.axis_index("tower")
    other_tower = 1 - tower
    greet(me, batch_count, other_tower)
    load_table = pltpu.make_async_copy(table_hbm_ref, table_ref, table_sem)
    load_table.start()
    pooled_ref[...] = jnp.zeros_like(pooled_ref)
    first_ref[...] = jnp.zeros_like(first_ref)
    second_ref[...] = jnp.zeros_like(second_ref)

    def request_copy(peer, slot):
        return peer_copy(
            req_ref.at[peer], served_ref.at[slot], req_send.at[peer], req_recv.at[slot], peer
        )

    stat_ref[...] = jnp.full(stat_ref.shape, jnp.sum(weight_ref[...].astype(jnp.float32)))

    def stat_copy(peer, slot):
        return peer_copy(stat_ref, stat_in_ref.at[slot], stat_send.at[peer], stat_recv.at[slot], peer)

    def answer_copy(peer, slot):
        return peer_copy(
            ans_out_ref.at[peer], ans_in_ref.at[slot], ans_send.at[peer], ans_recv.at[slot], peer
        )

    def own_copy():
        return pltpu.make_async_copy(ans_out_ref.at[me], ans_in_ref.at[me], ans_recv.at[me])

    all_greeted(batch_count, True)

    def send_requests(i, carry):
        peer = lax.rem(me + i, batch_count)
        request_copy(peer, me).start()
        stat_copy(peer, me).start()
        return carry

    lax.fori_loop(1, batch_count, send_requests, 0)

    depth = batch_count // PLANE
    high, low = me // PLANE, lax.rem(me, PLANE)

    def others(action):
        each(batch_count, lambda i: action(lax.rem(me + i, batch_count)))

    def column(action):
        each(depth, lambda i: action(lax.rem(high + i, depth)))

    def plane(action):
        each(PLANE, lambda i: action(lax.rem(low + i, PLANE)))

    def column_copy(src, dst, to, source):
        return peer_copy(
            src, dst.at[low * depth + source], win_send.at[to], win_recv.at[source],
            to * PLANE + low,
        )

    def plane_copy(dst, to, source):
        block = dst.at[pl.ds(source * depth, depth)]
        return peer_copy(
            block, block, plane_send.at[to], plane_recv.at[source], high * PLANE + to
        )

    def extra_copy(peer, slot):
        return peer_copy(rest_ref, extras_ref.at[slot], ext_send.at[peer], ext_recv.at[slot], peer)

    def start_windows(src, dst):
        column(lambda to: column_copy(src, dst, to, high).start())
        dst[low * depth + high] = src[...]

    def pass_windows(src, dst):
        column(lambda source: column_copy(src, dst, source, source).wait_recv())
        plane(lambda to: plane_copy(dst, to, low).start())

    def sent_windows(src, dst):
        column(lambda to: column_copy(src, dst, to, high).wait_send())
        plane(lambda to: plane_copy(dst, to, low).wait_send())

    def split(action):
        @pl.when(tower == 0)
        def _():
            action(cin_ref, cins_ref)

        @pl.when(tower == 1)
        def _():
            action(rest_ref, rests_ref)

    served_ref[me] = req_ref[me]
    stat_in_ref[me] = stat_ref[...]
    load_table.wait()
    tile_table(table_ref, tiles_ref, stage_ref, columns)

    sizes = ans_out_ref.shape[1]

    def look_up(first, second):
        for r in range(rows_msg):
            w = slots.width(r)
            row = jnp.concatenate(
                [served_ref[first, r : r + 1, :w], served_ref[second, r : r + 1, :w]], axis=1
            )
            hot = ones_at(iota((BROAD, 2 * w), 0) == row % BROAD)
            result = dot(tiles_ref[...], hot)
            mask = iota((TALL, 2 * w), 0) == row // BROAD
            block = pick_rows(result, mask, TALL, columns)
            first_ref[r * columns : r * columns + 16, :w] = block[:, :w]
            second_ref[r * columns : r * columns + 16, :w] = block[:, w:]
        ans_out_ref[first] = first_ref[:sizes, :].astype(jnp.bfloat16)
        ans_out_ref[second] = second_ref[:sizes, :].astype(jnp.bfloat16)

    def pool(owner):
        first_ref[:sizes, :] = ans_in_ref[owner].astype(jnp.float32)
        for r in range(rows_msg):
            w = slots.width(r)
            begin = r * columns
            values = [first_ref[begin + c : begin + c + 1, :w] for c in range(columns)]
            mask = iota((HALF, w), 0) == half_ref[owner, r : r + 1, :w]
            pieces = [jnp.where(mask, values[c], 0.0) for c in range(EMB)]
            pieces.append(jnp.where(iota((8, w), 0) == 0, values[EMB], 0.0))
            left_ref[:, r * WIDE : r * WIDE + w] = jnp.concatenate(pieces, axis=0).astype(
                jnp.bfloat16
            )
        for m in range(slots.micro_count):
            rights = []
            for r in range(slots.first_rows[m], rows_msg):
                w = slots.micro_width(m, r)
                if w:
                    lane = iota((WIDE, w), 0) + (m * WIDE + 1)
                    rights.append(ones_at(lane == code_ref[owner, r : r + 1, :w]))
            begin = slots.first_rows[m] * WIDE
            pooled_ref[m] += dot(
                left_ref[:, begin : begin + slots.spans[m]], jnp.concatenate(rights, axis=1), NT
            )

    def pair_copy(src, dst, k):
        return pltpu.make_async_remote_copy(
            src_ref=src,
            dst_ref=dst,
            send_sem=pair_send.at[k],
            recv_sem=pair_recv.at[k],
            device_id={"tower": other_tower},
            device_id_type=pl.DeviceIdType.MESH,
        )

    def swap_windows():
        @pl.when(tower == 0)
        def _():
            plane(lambda source: plane_copy(cins_ref, source, source).wait_recv())
            for e in range(windows.extras):

                @pl.when(me != first_extra + e)
                def _():
                    extra_copy(first_extra + e, e).wait_recv()

            pair_copy(cins_ref, cins_ref, 0).start()
            pair_copy(extras_ref, extras_ref, 1).start()

        @pl.when(tower == 1)
        def _():
            plane(lambda source: plane_copy(rests_ref, source, source).wait_recv())
            pair_copy(rests_ref, rests_ref, 0).start()

    pairs = batch_count // 2
    lag = 2

    def step(j, carry):
        @pl.when(j < pairs)
        def _():
            first = lax.rem(me + batch_count - (2 * j + 1), batch_count)
            second = lax.rem(me + 2 * batch_count - (2 * j + 2), batch_count)
            request_copy(first, first).wait_recv()

            @pl.when(j < pairs - 1)
            def _():
                request_copy(second, second).wait_recv()

            look_up(first, second)

            @pl.when(j == 0)
            def _():
                split(start_windows)

            @pl.when((j == 0) & (tower == 0) & (me >= first_extra))
            def _():
                others(lambda peer: extra_copy(peer, me - first_extra).start())
                extras_ref[me - first_extra] = rest_ref[...]

            @pl.when(j == 3)
            def _():
                split(pass_windows)

            @pl.when(j == pairs - 2)
            def _():
                swap_windows()

            answer_copy(first, me).start()

            @pl.when(j < pairs - 1)
            def _():
                answer_copy(second, me).start()

            @pl.when(j == pairs - 1)
            def _():
                own_copy().start()

        @pl.when(j >= lag)
        def _():
            first = lax.rem(me + 2 * (j - lag) + 1, batch_count)
            answer_copy(first, first).wait_recv()
            pool(first)

        @pl.when((j >= lag) & (j < pairs - 1 + lag))
        def _():
            second = lax.rem(me + 2 * (j - lag) + 2, batch_count)
            answer_copy(second, second).wait_recv()
            pool(second)

        return carry

    lax.fori_loop(0, pairs + lag, step, 0)

    own_copy().wait()
    pool(me)

    pooled_pair = pair_copy(pooled_ref, other_ref, 2)
    pooled_pair.start()

    def finish(i, carry):
        peer = lax.rem(me + i, batch_count)
        request_copy(peer, me).wait_send()
        stat_copy(peer, me).wait_send()
        answer_copy(peer, me).wait_send()
        stat_copy(peer, peer).wait_recv()
        return carry

    lax.fori_loop(1, batch_count, finish, 0)
    stat_out_ref[...] = jnp.sum(stat_in_ref[...], axis=0)

    split(sent_windows)

    @pl.when(tower == 0)
    def _():
        @pl.when(me >= first_extra)
        def _():
            others(lambda peer: extra_copy(peer, me - first_extra).wait_send())

        pair_copy(cins_ref, cins_ref, 0).wait_send()
        pair_copy(extras_ref, extras_ref, 1).wait_send()
        pair_copy(rests_ref, rests_ref, 0).wait_recv()

    @pl.when(tower == 1)
    def _():
        pair_copy(rests_ref, rests_ref, 0).wait_send()
        pair_copy(cins_ref, cins_ref, 0).wait_recv()
        pair_copy(extras_ref, extras_ref, 1).wait_recv()

    pooled_pair.wait()
    out_ref[...] = pooled_ref[...] + other_ref[...]


def fetch(
    requests, codes, halves, table, weights, cin_window, rest_window, windows, slots
):
    batch_count, rows_msg, _ = requests.shape
    columns, rows_dev = table.shape
    sizes = message_rows(rows_msg, columns)
    in_vmem = pl.BlockSpec(memory_space=pltpu.VMEM)
    dma = pltpu.SemaphoreType.DMA
    bags = (slots.micro_count, BAG_ROWS, WIDE)
    return pl.pallas_call(
        partial(fetch_kernel, slots, windows, columns),
        in_specs=[in_vmem] * 3 + [pl.BlockSpec(memory_space=pltpu.HBM)] + [in_vmem] * 3,
        out_specs=[in_vmem] * 6,
        out_shape=[
            jax.ShapeDtypeStruct(bags, jnp.float32),
            jax.ShapeDtypeStruct(requests.shape, jnp.int32),
            jax.ShapeDtypeStruct((8, LANES), jnp.float32),
            jax.ShapeDtypeStruct((batch_count,) + cin_window.shape, jnp.bfloat16),
            jax.ShapeDtypeStruct((batch_count,) + rest_window.shape, jnp.bfloat16),
            jax.ShapeDtypeStruct((windows.extras,) + rest_window.shape, jnp.bfloat16),
        ],
        scratch_shapes=[
            pltpu.VMEM(table.shape, jnp.float32),
            pltpu.VMEM((columns * TALL, BROAD), jnp.bfloat16),
            pltpu.VMEM((TALL, BROAD), jnp.float32),
            pltpu.VMEM((sizes + 16, WIDE), jnp.float32),
            pltpu.VMEM((sizes + 16, WIDE), jnp.float32),
            pltpu.VMEM((batch_count, sizes, WIDE), jnp.bfloat16),
            pltpu.VMEM((batch_count, sizes, WIDE), jnp.bfloat16),
            pltpu.VMEM((BAG_ROWS, rows_msg * WIDE), jnp.bfloat16),
            pltpu.VMEM(bags, jnp.float32),
            pltpu.VMEM(bags, jnp.float32),
            pltpu.VMEM((8, LANES), jnp.float32),
            pltpu.VMEM((batch_count, 8, LANES), jnp.float32),
        ]
        + [dma((batch_count,))] * 11
        + [dma((windows.extras,)), dma((3,)), dma((3,)), dma],
        compiler_params=pltpu.CompilerParams(
            vmem_limit_bytes=vmem_limit(batch_count), collective_id=0, has_side_effects=True
        ),
        name="fetch",
    )(requests, codes, halves, in_hbm(table), weights, cin_window, rest_window)


def return_kernel(
    slots, windows, columns,
    grad_ref, code_ref, half_ref, served_ref, stat_ref, cins_ref, rests_ref, extras_ref,
    out_ref, stat_out_ref, cin_ref, rest_ref,
    send_ref, recv_ref, first_ref, second_ref, left_ref, right_ref, total_ref, stat_in_ref,
    extra_in_ref, cin_near_ref, cin_sum_ref, cin_far_ref, rest_near_ref, rest_sum_ref, rest_far_ref,
    val_send, val_recv, stat_send, stat_recv, win_send, win_recv, plane_send, plane_recv, ext_send,
    ext_recv,
):
    batch_count = windows.batch_count
    first_extra = windows.first_extra
    tower = lax.axis_index("tower")
    rows_msg = slots.rows
    me = lax.axis_index("batch")
    greet(me, batch_count)

    def value_copy(peer, slot):
        return peer_copy(
            send_ref.at[peer], recv_ref.at[slot], val_send.at[peer], val_recv.at[slot], peer
        )

    def own_copy():
        return pltpu.make_async_copy(send_ref.at[me], recv_ref.at[me], val_recv.at[me])

    def stat_copy(peer, slot):
        return peer_copy(stat_ref, stat_in_ref.at[slot], stat_send.at[peer], stat_recv.at[slot], peer)

    depth = batch_count // PLANE
    high, low = me // PLANE, lax.rem(me, PLANE)

    def others(action):
        each(batch_count, lambda i: action(lax.rem(me + i, batch_count)))

    def column(action):
        each(depth, lambda i: action(lax.rem(high + i, depth)))

    def plane(action):
        each(PLANE, lambda i: action(lax.rem(low + i, PLANE)))

    def plane_copy(src, near, to, source):
        return peer_copy(
            src.at[pl.ds(to * depth, depth)], near.at[source], plane_send.at[to],
            plane_recv.at[source], high * PLANE + to,
        )

    def column_copy(total, far, to, source):
        return peer_copy(
            total.at[to], far.at[source], win_send.at[to], win_recv.at[source], to * PLANE + low
        )

    def start_windows(src, near, total, far, out):
        plane(lambda to: plane_copy(src, near, to, low).start())
        near[low] = src[pl.ds(low * depth, depth)]

    def pass_windows(src, near, total, far, out):
        plane(lambda source: plane_copy(src, near, source, source).wait_recv())
        total[...] = jnp.sum(near[...], axis=0)
        column(lambda to: column_copy(total, far, to, high).start())
        far[high] = total[high]

    def end_windows(src, near, total, far, out):
        column(lambda source: column_copy(total, far, source, source).wait_recv())
        out[...] = jnp.sum(far[...], axis=0)
        plane(lambda to: plane_copy(src, near, to, low).wait_send())
        column(lambda to: column_copy(total, far, to, high).wait_send())

    def split(action):
        @pl.when(tower == 0)
        def _():
            action(cins_ref, cin_near_ref, cin_sum_ref, cin_far_ref, cin_ref)

        @pl.when(tower == 1)
        def _():
            action(rests_ref, rest_near_ref, rest_sum_ref, rest_far_ref, rest_ref)

    def extra_copy(peer, slot):
        return peer_copy(
            extras_ref.at[peer - first_extra],
            extra_in_ref.at[slot],
            ext_send.at[peer],
            ext_recv.at[slot],
            peer,
        )

    def send_stats(i, carry):
        stat_copy(lax.rem(me + i, batch_count), me).start()
        return carry

    first_ref[...] = jnp.zeros_like(first_ref)
    second_ref[...] = jnp.zeros_like(second_ref)
    stat_in_ref[me] = stat_ref[...]
    total_ref[...] = jnp.zeros_like(total_ref)

    sizes = send_ref.shape[1]

    def spread(first, second):
        def both(ref, r, w):
            return jnp.concatenate([ref[first, r : r + 1, :w], ref[second, r : r + 1, :w]], axis=1)

        for r in range(rows_msg):
            w = slots.width(r)
            result = None
            for m in range(slots.micro_count):
                inner = slots.micro_width(m, r)
                if inner == 0:
                    continue
                hot = ones_at(iota((WIDE, 2 * inner), 0) + (m * WIDE + 1) == both(code_ref, r, inner))
                found = dot(grad_ref[m], hot)
                if inner < w:
                    blank = jnp.zeros((BAG_ROWS, w - inner), jnp.float32)
                    found = jnp.concatenate(
                        [found[:, :inner], blank, found[:, inner:], blank], axis=1
                    )
                result = found if result is None else result + found
            mask = iota((HALF, 2 * w), 0) == both(half_ref, r, w)
            block = pick_rows(result, mask, HALF, EMB)
            linear = result[EMB * HALF : EMB * HALF + 1]
            block = jnp.where(iota((16, 2 * w), 0) == EMB, linear, block)
            first_ref[r * columns : r * columns + 16, :w] = block[:, :w]
            second_ref[r * columns : r * columns + 16, :w] = block[:, w:]
        send_ref[first] = first_ref[:sizes, :].astype(jnp.bfloat16)
        send_ref[second] = second_ref[:sizes, :].astype(jnp.bfloat16)

    def scatter(source):
        first_ref[:sizes, :] = recv_ref[source].astype(jnp.float32)
        for r in range(rows_msg):
            w = slots.width(r)
            span = slice(r * WIDE, r * WIDE + w)
            row = served_ref[source, r : r + 1, :w]
            mask = iota((TALL, w), 0) == row // BROAD
            for c in range(columns):
                left_ref[c * TALL : (c + 1) * TALL, span] = jnp.where(
                    mask, first_ref[r * columns + c : r * columns + c + 1, :w], 0.0
                ).astype(jnp.bfloat16)
            right_ref[:, span] = ones_at(iota((BROAD, w), 0) == row % BROAD)
        total_ref[...] += dot(
            left_ref[:, : slots.length], right_ref[:, : slots.length], NT
        )

    pairs = batch_count // 2
    lag = 2

    def step(j, carry):
        @pl.when(j < pairs)
        def _():
            first = lax.rem(me + 2 * j + 1, batch_count)
            second = lax.rem(me + 2 * j + 2, batch_count)
            spread(first, second)

            @pl.when(j == 0)
            def _():
                all_greeted(batch_count, False)
                lax.fori_loop(1, batch_count, send_stats, 0)

            value_copy(first, me).start()

            @pl.when(j == 1)
            def _():
                split(start_windows)

            @pl.when((j == 1) & (tower == 0))
            def _():
                for e in range(windows.extras):

                    @pl.when(me != first_extra + e)
                    def _():
                        extra_copy(first_extra + e, me).start()

            @pl.when(j < pairs - 1)
            def _():
                value_copy(second, me).start()

            @pl.when(j == pairs - 1)
            def _():
                own_copy().start()

        @pl.when(j == pairs - 1)
        def _():
            split(pass_windows)

        @pl.when(j >= lag)
        def _():
            first = lax.rem(me + batch_count - (2 * (j - lag) + 1), batch_count)
            value_copy(first, first).wait_recv()
            scatter(first)

        @pl.when((j >= lag) & (j < pairs - 1 + lag))
        def _():
            second = lax.rem(me + 2 * batch_count - (2 * (j - lag) + 2), batch_count)
            value_copy(second, second).wait_recv()
            scatter(second)

        return carry

    lax.fori_loop(0, pairs + lag, step, 0)
    own_copy().wait()
    scatter(me)

    split(end_windows)

    @pl.when(tower == 0)
    def _():
        for e in range(windows.extras):

            @pl.when(me != first_extra + e)
            def _():
                extra_copy(first_extra + e, me).wait_send()

        @pl.when(me >= first_extra)
        def _():
            extra_in_ref[me] = extras_ref[me - first_extra]
            others(lambda peer: extra_copy(me, peer).wait_recv())
            rest_ref[...] = jnp.sum(extra_in_ref[...], axis=0)

        @pl.when(me < first_extra)
        def _():
            rest_ref[...] = jnp.zeros_like(rest_ref)

    @pl.when(tower == 1)
    def _():
        cin_ref[...] = jnp.zeros_like(cin_ref)

    def finish(i, carry):
        peer = lax.rem(me + i, batch_count)
        value_copy(peer, me).wait_send()
        stat_copy(peer, me).wait_send()
        stat_copy(peer, peer).wait_recv()
        return carry

    lax.fori_loop(1, batch_count, finish, 0)
    stat_out_ref[...] = jnp.sum(stat_in_ref[...], axis=0)
    for c in range(columns):
        for q in range(TALL):
            out_ref[c : c + 1, q * BROAD : (q + 1) * BROAD] = total_ref[
                c * TALL + q : c * TALL + q + 1, :
            ]


def return_grads(
    grad_bags, codes, halves, served, stat, cins, rests, extras, windows, slots, columns
):
    batch_count, rows_msg, _ = codes.shape
    long = rows_msg * WIDE
    sizes = message_rows(rows_msg, columns)
    depth = batch_count // PLANE
    in_vmem = pl.BlockSpec(memory_space=pltpu.VMEM)
    dma = pltpu.SemaphoreType.DMA
    return pl.pallas_call(
        partial(return_kernel, slots, windows, columns),
        in_specs=[in_vmem] * 8,
        out_specs=[in_vmem] * 4,
        out_shape=[
            jax.ShapeDtypeStruct((columns, TALL * BROAD), jnp.float32),
            jax.ShapeDtypeStruct(stat.shape, jnp.float32),
            jax.ShapeDtypeStruct(cins.shape[1:], jnp.float32),
            jax.ShapeDtypeStruct(rests.shape[1:], jnp.float32),
        ],
        scratch_shapes=[
            pltpu.VMEM((batch_count, sizes, WIDE), jnp.bfloat16),
            pltpu.VMEM((batch_count, sizes, WIDE), jnp.bfloat16),
            pltpu.VMEM((sizes + 16, WIDE), jnp.float32),
            pltpu.VMEM((sizes + 16, WIDE), jnp.float32),
            pltpu.VMEM((columns * TALL, long), jnp.bfloat16),
            pltpu.VMEM((BROAD, long), jnp.bfloat16),
            pltpu.VMEM((columns * TALL, BROAD), jnp.float32),
            pltpu.VMEM((batch_count,) + stat.shape, jnp.float32),
            pltpu.VMEM(rests.shape, jnp.float32),
        ]
        + [
            pltpu.VMEM(lead + x.shape[1:], jnp.float32)
            for x in (cins, rests)
            for lead in ((PLANE, depth), (depth,), (depth,))
        ]
        + [dma((batch_count,))] * 10,
        compiler_params=pltpu.CompilerParams(
            vmem_limit_bytes=vmem_limit(batch_count), collective_id=1, has_side_effects=True
        ),
        name="return_grads",
    )(grad_bags, codes, halves, served, stat, cins, rests, extras)


def split_three(x):
    high = x.astype(jnp.bfloat16)
    rest = x - high.astype(jnp.float32)
    middle = rest.astype(jnp.bfloat16)
    low = (rest - middle.astype(jnp.float32)).astype(jnp.bfloat16)
    return high, middle, low


def dense_kernel(
    micro_count, windows, tower_ref, stat_ref, pooled_ref, label_ref, weight_ref,
    cins_ref, rests_ref, extras_ref,
    bags_ref, loss_ref, g_cins_ref, g_rests_ref, g_extras_ref,
    embed_ref, total_ref, pairs_ref, sym_ref, cin_ref, rest_ref, lane_ref,
):
    f32 = jnp.float32
    bf16 = jnp.bfloat16
    width = micro_count * LANES
    groups = HPAD // LANES

    cin_ref[...] = jnp.zeros_like(cin_ref)
    for b, at in enumerate(windows.cin_at):
        block = cins_ref[windows.slots[b]].astype(f32)
        cin_ref[at : at + windows.cin_rows, :] += block[: windows.cin_rows]
    rest_ref[...] = jnp.zeros_like(rest_ref)
    pieces = [(rests_ref, windows.slots[b], at) for b, at in enumerate(windows.rest_at)]
    pieces += [(extras_ref, e, at) for e, at in enumerate(windows.extra_at)]
    for source, b, at in pieces:
        skip = max(0, -at)
        block = source[b].astype(f32)
        for l in range(groups):
            rest_ref[l, at + skip : at + windows.rest_rows, :] += block[
                skip : windows.rest_rows, l * LANES : (l + 1) * LANES
            ]

    def rest_rows(begin, count):
        return jnp.concatenate(
            [rest_ref[l, begin : begin + count, :] for l in range(groups)], axis=1
        )[:, :HID]

    cin_w = cin_ref[:MAPS, :].astype(bf16)
    place = iota((MAPS, PAIRS), 0)
    place = place // FIELDS * FPAD + place % FIELDS == iota((MAPS, PAIRS), 1)
    picks_u = ones_at(place)
    row_u = jnp.broadcast_to(cin_ref[MAPS : MAPS + 1, :], (8, PAIRS)).astype(bf16)
    cin_u = dot(picks_u, row_u, NT)[:, :1]
    w_one = jnp.concatenate(
        [
            jnp.concatenate(
                [rest_ref[l, pl.ds(d, FPAD, stride=EMB), :] for l in range(groups)], axis=1
            )[:, :HID]
            for d in range(EMB)
        ],
        axis=0,
    ).astype(bf16)
    w_two = rest_rows(W_TWO, HID).astype(bf16)
    rows = jnp.zeros((8, HID), f32)
    for k, at in enumerate((B_ONE, B_TWO, W_THREE)):
        rows = jnp.where(iota((8, HID), 0) == k, rest_rows(at, 1), rows)
    unit = ones_at(iota((HID, HID), 0) == iota((HID, HID), 1))
    turned = dot(unit, rows.astype(bf16), NT)
    b_one, b_two, w_three = turned[:, 0:1], turned[:, 1:2], turned[:, 2:3]
    bias = rest_ref[0, BIAS : BIAS + 1, 0:1]

    def unpacked(row, count):
        pieces = []
        for m in range(micro_count):
            low = pooled_ref[m, row : row + HALF, :LANES]
            high = pooled_ref[m, row : row + HALF, LANES:]
            pieces.append(jnp.concatenate([low, high], axis=0)[:count])
        return jnp.concatenate(pieces, axis=1)

    for d in range(EMB):
        embed_ref[d * FPAD : (d + 1) * FPAD, :] = unpacked(d * HALF, FPAD)
    linear = jnp.concatenate(
        [
            pooled_ref[m, EMB * HALF : EMB * HALF + 1, :LANES]
            + pooled_ref[m, EMB * HALF : EMB * HALF + 1, LANES:]
            for m in range(micro_count)
        ],
        axis=1,
    )

    def pair_row(i, carry):
        total = jnp.zeros((FPAD, width), f32)
        for d in range(EMB):
            own = embed_ref[pl.ds(d * FPAD + i, 1), :]
            product = (embed_ref[d * FPAD : (d + 1) * FPAD, :] * own).astype(jnp.bfloat16)
            total = total + product.astype(f32)
        total_ref[pl.ds(pl.multiple_of(i * FPAD, 8), FPAD), :] = total
        return carry

    lax.fori_loop(0, FIELDS, pair_row, 0, unroll=3)
    thirds = split_three(total_ref[...])
    map_sum = sum(dot(cin_w, third) for third in thirds)
    cin_logits = jnp.sum(map_sum * cin_u, axis=0, keepdims=True)

    flat = embed_ref[...].astype(jnp.bfloat16)
    pre_one = dot(w_one, flat, TN) + b_one
    hidden_one = jnp.maximum(pre_one, 0.0).astype(jnp.bfloat16)
    pre_two = dot(w_two, hidden_one, TN) + b_two
    active_two = jnp.maximum(pre_two, 0.0)
    deep_logits = jnp.sum(active_two * w_three, axis=0, keepdims=True)
    logits = cin_logits + deep_logits + linear + bias

    samples = weight_ref.shape[1]
    lane_ref[...] = jnp.zeros_like(lane_ref)
    for m in range(micro_count):
        span = slice(m * LANES, m * LANES + samples)
        lane_ref[0:1, span] = weight_ref[m : m + 1, :].astype(f32)
        lane_ref[1:2, span] = label_ref[m : m + 1, :].astype(f32)
    weight = lane_ref[0:1, :]
    label = lane_ref[1:2, :]
    soft = jnp.maximum(logits, 0.0) + jnp.log1p(jnp.exp(-jnp.abs(logits)))
    loss_ref[...] = jnp.broadcast_to(
        jnp.sum(weight * (soft - label * logits), axis=1, keepdims=True), loss_ref.shape
    )
    grad_logits = weight * (jax.nn.sigmoid(logits) - label) / stat_ref[0:1, 0:1]

    grad_maps = (grad_logits * cin_u).astype(jnp.bfloat16)
    grad_two = jnp.where(pre_two > 0, grad_logits * w_three, 0.0).astype(jnp.bfloat16)
    grad_hidden = dot(w_two, grad_two)
    grad_one = jnp.where(pre_one > 0, grad_hidden, 0.0).astype(jnp.bfloat16)
    grad_flat = dot(w_one, grad_one)

    grad_pairs = dot(cin_w, grad_maps, TN)
    for m in range(micro_count):
        pairs_ref[m, :PAIRS, :] = grad_pairs[:, m * LANES : (m + 1) * LANES]
        pairs_ref[m, PAIRS:, :] = jnp.zeros((FPAD * FPAD - PAIRS, LANES), f32)

    def mirror(j, carry):
        here = pl.ds(pl.multiple_of(j * FPAD, 8), FPAD)
        both = [
            pairs_ref[m, here, :] + pairs_ref[m, pl.ds(j, FPAD, stride=FPAD), :]
            for m in range(micro_count)
        ]
        sym_ref[here, :] = jnp.concatenate(both, axis=1)
        return carry

    lax.fori_loop(0, FIELDS, mirror, 0, unroll=3)
    empty = jnp.zeros((2 * HALF - FPAD, width), f32)

    for d in range(EMB):

        def add_row(j, total):
            here = pl.ds(pl.multiple_of(j * FPAD, 8), FPAD)
            return total + sym_ref[here, :] * embed_ref[pl.ds(d * FPAD + j, 1), :]

        grad_embed = lax.fori_loop(
            0, FIELDS, add_row, grad_flat[d * FPAD : (d + 1) * FPAD], unroll=13
        )
        grad_embed = jnp.concatenate([grad_embed, empty], axis=0)
        for m in range(micro_count):
            span = slice(m * LANES, (m + 1) * LANES)
            block = jnp.concatenate([grad_embed[:HALF, span], grad_embed[HALF:, span]], axis=1)
            bags_ref[m, d * HALF : (d + 1) * HALF, :] = block.astype(bf16)
    for m in range(micro_count):
        row = grad_logits[:, m * LANES : (m + 1) * LANES]
        row = jnp.concatenate([row, row], axis=1)
        bags_ref[m, EMB * HALF :, :] = jnp.broadcast_to(row, (8, WIDE)).astype(bf16)

    ones = jnp.ones((8, width), bf16)

    def row_sum(x):
        return sum(dot(ones, third, NT) for third in split_three(x))[:1]

    rest_ref[...] = jnp.zeros_like(rest_ref)

    def put(begin, count, value, stride=None):
        for l in range(groups):
            piece = value[:, l * LANES : min((l + 1) * LANES, HID)]
            lanes = slice(0, piece.shape[1])
            if stride is None:
                rest_ref[l, begin : begin + count, lanes] = piece
            else:
                piece = jnp.pad(piece, ((0, 0), (0, LANES - piece.shape[1])))
                rest_ref[l, pl.ds(begin, count, stride=stride), :] = piece

    g_w_one = dot(flat, grad_one, NT)
    for d in range(EMB):
        put(d, FIELDS, g_w_one[d * FPAD : d * FPAD + FIELDS], EMB)

    @pl.when(tower_ref[0] == 0)
    def _():
        cin_ref[...] = jnp.zeros_like(cin_ref)
        cin_ref[:MAPS, :] = sum(dot(grad_maps, third, NT) for third in thirds)
        g_cin_u = jnp.sum(map_sum * grad_logits, axis=1, keepdims=True)
        thirds_u = split_three(jnp.broadcast_to(g_cin_u, (MAPS, 8)))
        cin_ref[MAPS : MAPS + 1, :] = sum(dot(third, picks_u, TN) for third in thirds_u)[:1]
        for b, at in enumerate(windows.cin_at):
            g_cins_ref[windows.slots[b], : windows.cin_rows, :] = cin_ref[
                at : at + windows.cin_rows, :
            ]
        for e, at in enumerate(windows.extra_at):
            skip = max(0, -at)
            for l in range(groups):
                span = slice(l * LANES, (l + 1) * LANES)
                g_extras_ref[e, skip : windows.rest_rows, span] = rest_ref[
                    l, at + skip : at + windows.rest_rows, :
                ]

    @pl.when(tower_ref[0] != 0)
    def _():
        put(W_TWO, HID, dot(hidden_one, grad_two, NT))
        put(B_ONE, 1, dot(ones, grad_one, NT)[:1])
        put(B_TWO, 1, dot(ones, grad_two, NT)[:1])
        put(W_THREE, 1, row_sum(active_two * grad_logits))
        g_bias = jnp.sum(grad_logits, axis=1, keepdims=True)
        put(BIAS, 1, jnp.where(iota((1, HID), 1) == 0, g_bias, 0.0))
        for b, at in enumerate(windows.rest_at):
            for l in range(groups):
                span = slice(l * LANES, (l + 1) * LANES)
                g_rests_ref[windows.slots[b], : windows.rest_rows, span] = rest_ref[
                    l, at : at + windows.rest_rows, :
                ]


def dense_step(tower_at, stats, pooled, labels, weights, cins, rests, extras, windows):
    micro_count = pooled.shape[0]
    width = micro_count * LANES
    in_vmem = pl.BlockSpec(memory_space=pltpu.VMEM)
    in_smem = pl.BlockSpec(memory_space=pltpu.SMEM)
    f32 = jnp.float32
    shapes = [
        ((micro_count, BAG_ROWS, WIDE), jnp.bfloat16),
        ((8, LANES), f32),
        ((cins.shape[0], windows.cin_pad_wide, PAIRS), f32),
        ((rests.shape[0], windows.rest_pad_wide, HPAD), f32),
        ((extras.shape[0], windows.rest_pad_wide, HPAD), f32),
    ]
    return pl.pallas_call(
        partial(dense_kernel, micro_count, windows),
        in_specs=[in_smem] + [in_vmem] * 7,
        out_specs=[in_vmem] * len(shapes),
        out_shape=[jax.ShapeDtypeStruct(*shape) for shape in shapes],
        scratch_shapes=[
            pltpu.VMEM((EMB * FPAD, width), f32),
            pltpu.VMEM((PAIRS, width), f32),
            pltpu.VMEM((micro_count, FPAD * FPAD, LANES), f32),
            pltpu.VMEM((PAIRS, width), f32),
            pltpu.VMEM((windows.cin_total, PAIRS), f32),
            pltpu.VMEM((HPAD // LANES, windows.rest_total, LANES), f32),
            pltpu.VMEM((8, width), f32),
        ],
        compiler_params=pltpu.CompilerParams(vmem_limit_bytes=vmem_limit(windows.batch_count)),
        name="dense",
    )(tower_at.reshape(1), stats, pooled, labels, weights, cins, rests, extras)


def shards(
    shard_ids,
    local_rows,
    bag_counts,
    click_labels,
    sample_weights,
    embed_table,
    table_first,
    table_second,
    dense_params,
    dense_first,
    dense_second,
):
    tower_count = lax.axis_size("tower")
    batch_count = lax.axis_size("batch")
    tower_at = lax.axis_index("tower")
    micro_count, samples = shard_ids.shape[:2]
    columns, rows_dev = embed_table.shape
    capacity = 4 * samples * IDS_SAMP // (tower_count * batch_count)
    share = dense_params.shape[0]
    windows = Windows(share, batch_count)
    slots = Slots(micro_count, capacity)

    device = tower_at * batch_count + lax.axis_index("batch")
    cin_phase, rest_phase = windows.phases(device)
    low = dense_params.astype(jnp.bfloat16)

    def window(rows, row_size, phase):
        return lax.dynamic_update_slice(
            jnp.zeros((rows * row_size,), jnp.bfloat16), low, (phase,)
        )

    cin_window = window(windows.cin_rows, SQUARE, cin_phase).reshape(-1, FIELDS, FIELDS)
    cin_window = jnp.pad(
        cin_window,
        ((0, windows.cin_pad - windows.cin_rows), (0, 0), (0, FPAD - FIELDS)),
    ).reshape(windows.cin_pad, PAIRS)
    rest_window = jnp.pad(
        window(windows.rest_rows, HID, rest_phase).reshape(-1, HID),
        ((0, windows.rest_pad - windows.rest_rows), (0, HPAD - HID)),
    )

    def lanes_of(values):
        return jnp.moveaxis(values, 1, -1).reshape(micro_count, -1, samples)

    requests, codes, halves = route(
        lanes_of(shard_ids), lanes_of(local_rows), lanes_of(bag_counts), slots, batch_count
    )
    pooled, served, stats, cins, rests, extras = fetch(
        requests, codes, halves, embed_table, sample_weights, cin_window, rest_window, windows,
        slots,
    )
    grad_bags, loss, g_cins, g_rests, g_extras = dense_step(
        tower_at, stats, pooled, click_labels, sample_weights, cins, rests, extras, windows
    )
    table_grad, losses, g_cin, g_rest = return_grads(
        grad_bags, codes, halves, served, loss, g_cins, g_rests, g_extras, windows, slots, columns
    )
    g_cin = g_cin[: windows.cin_rows].reshape(-1, FIELDS, FPAD)[:, :, :FIELDS].reshape(-1)
    g_rest = g_rest[: windows.rest_rows, :HID].reshape(-1)
    is_cin = device * share + jnp.arange(share, dtype=jnp.int32) < CIN_SIZE
    own_grad = jnp.where(
        is_cin,
        lax.dynamic_slice(g_cin, (cin_phase,), (share,)),
        lax.dynamic_slice(g_rest, (rest_phase,), (share,)),
    )

    table_new, table_first_new, table_second_new = adam_update(
        embed_table, table_first, table_second, table_grad, rate_table
    )
    dense_new, dense_first_new, dense_second_new = adam_update(
        dense_params, dense_first, dense_second, own_grad, rate_dense
    )
    loss_sum = losses[0, 0] / stats[0, 0]
    return (
        table_new,
        table_first_new,
        table_second_new,
        table_new.astype(jnp.bfloat16),
        dense_new,
        dense_first_new,
        dense_second_new,
        dense_new.astype(jnp.bfloat16),
        loss_sum,
    )


def solution(mesh):
    rows = P(None, ("tower", "batch"))
    dense = P(("tower", "batch"))
    placed = (
        P(None, "batch", None, None),
        P(None, "batch", None, None),
        P(None, "batch", None),
        P(None, "batch"),
        P(None, "batch"),
        rows,
        rows,
        rows,
        dense,
        dense,
        dense,
    )
    return jax.shard_map(
        shards,
        mesh=mesh,
        in_specs=placed,
        out_specs=(rows, rows, rows, rows, dense, dense, dense, dense, P()),
        check_vma=False,
    )
```

```python
from functools import partial

import jax
import jax.numpy as jnp
from jax import lax
from jax.experimental import pallas as pl
from jax.experimental.pallas import tpu as pltpu
from jax.sharding import PartitionSpec as P

FIELDS = 39
EMB = 10
MAPS = 200
HID = 400
IDS_SAMP = 80

beta_one = 0.9
beta_two = 0.999
epsilon = 1e-08
decay_rate = 0.15
rate_table = 0.1
rate_dense = 0.05
step_count = 10

LANES = 128
WIDE = 256
BROAD = 512
TALL = 64
HALF = 24
BAG_ROWS = EMB * HALF + 8
FPAD = 40
PAIRS = FIELDS * FPAD
SQUARE = FIELDS * FIELDS
CIN_SIZE = MAPS * SQUARE + MAPS
FLAT = EMB * FIELDS
B_ONE, W_TWO, B_TWO, W_THREE, BIAS = FLAT, FLAT + 1, FLAT + HID + 1, FLAT + HID + 2, FLAT + HID + 3
HPAD = 512
PLANE = 4
NT = (((1,), (1,)), ((), ()))
TN = (((0,), (0,)), ((), ()))
NN = (((1,), (0,)), ((), ()))


def adam_update(weight, first_old, second_old, gradient, step_rate):
    first_new = beta_one * first_old + (1.0 - beta_one) * gradient
    second_new = beta_two * second_old + (1.0 - beta_two) * gradient * gradient
    first_hat = first_new / (1.0 - beta_one**step_count)
    second_hat = second_new / (1.0 - beta_two**step_count)
    weight_new = weight - step_rate * (
        first_hat / (jnp.sqrt(second_hat) + epsilon) + decay_rate * weight
    )
    return (weight_new, first_new, second_new)


def dot(a, b, dims=NN):
    return lax.dot_general(a, b, dims, preferred_element_type=jnp.float32)


def vmem_limit(batch_count):
    return (28 + batch_count // 4) << 20


def iota(shape, dim):
    return lax.broadcasted_iota(jnp.int32, shape, dim)


def ones_at(mask):
    return jnp.where(mask, 1.0, 0.0).astype(jnp.bfloat16)


class Slots:
    def __init__(self, micro_count, capacity):
        self.micro_count = micro_count
        self.first_rows = [m * capacity // WIDE for m in range(micro_count)]
        self.shifts = [m * capacity % WIDE for m in range(micro_count)]
        self.spans = [-(-(shift + capacity) // LANES) * LANES for shift in self.shifts]
        self.length = max(
            first * WIDE + span for first, span in zip(self.first_rows, self.spans)
        )
        self.rows = -(-self.length // WIDE)
        self.window = max(-(-span // WIDE) for span in self.spans)

    def width(self, row):
        return min(WIDE, self.length - row * WIDE)

    def micro_width(self, micro, row):
        inside = row - self.first_rows[micro]
        return max(0, min(WIDE, self.spans[micro] - inside * WIDE)) if inside >= 0 else 0


class Windows:
    def __init__(self, share, batch_count):
        self.share, self.batch_count = share, batch_count
        self.cin_rows = -(-(SQUARE - 1 + share) // SQUARE)
        self.rest_rows = -(-(HID - 1 + share) // HID)
        self.cin_pad = -(-self.cin_rows // 16) * 16
        self.rest_pad = -(-self.rest_rows // 16) * 16
        self.cin_pad_wide = -(-self.cin_rows // 8) * 8
        self.rest_pad_wide = -(-self.rest_rows // 8) * 8
        self.first_extra = CIN_SIZE // share
        self.extras = batch_count - self.first_extra
        self.cin_at = [b * share // SQUARE for b in range(batch_count)]
        self.rest_at = [
            ((batch_count + b) * share - CIN_SIZE) // HID for b in range(batch_count)
        ]
        self.extra_at = [
            (b * share - CIN_SIZE) // HID for b in range(self.first_extra, batch_count)
        ]
        depth = batch_count // PLANE
        self.slots = [b % PLANE * depth + b // PLANE for b in range(batch_count)]
        self.cin_total = -(-max(a + self.cin_rows for a in self.cin_at) // 8) * 8
        self.rest_total = -(-max(a + self.rest_rows for a in self.rest_at) // 8) * 8

    def phases(self, device):
        start = device * self.share
        return start % SQUARE, jnp.mod(start - CIN_SIZE, HID)


def coded(x):
    return jnp.where(x < 256, x + 1, 255 - x).astype(jnp.float32)


def decoded(x):
    return jnp.where(x > 0, x - 1, 255 - x)


def route_kernel(
    slots, batch_count, ids_ref, rows_ref, counts_ref, weight_ref,
    req_ref, code_ref, half_ref, part_ref, left_ref, right_ref,
):
    f32, bf16 = jnp.float32, jnp.bfloat16
    micro_count, window = slots.micro_count, slots.window
    micro = pl.program_id(0)
    id_rows, samples = ids_ref.shape[1:]
    chunk = 16
    tower = lax.axis_index("tower")

    @pl.when(micro == 0)
    def _():
        req_ref[...] = jnp.zeros_like(req_ref)
        code_ref[...] = jnp.zeros_like(code_ref)
        half_ref[...] = jnp.zeros_like(half_ref)
        part_ref[...] = jnp.zeros_like(part_ref)
        weight_sum = jnp.sum(weight_ref[...].astype(f32)).astype(jnp.int32)
        req_ref[:, slots.rows, :] = jnp.full((batch_count, WIDE), weight_sum)

    def widened(x, filler):
        part_ref[0, :, :samples] = x.astype(f32)
        inside = iota((id_rows, LANES), 1) < samples
        return jnp.where(inside, part_ref[0], filler)

    owner = ids_ref[0]
    target = widened(
        jnp.where(owner // batch_count == tower, owner % batch_count, batch_count), batch_count
    ).astype(jnp.int32)
    local = widened(rows_ref[0], 0.0).astype(jnp.int32)
    before = ones_at(iota((FIELDS, FIELDS), 1) <= iota((FIELDS, FIELDS), 0))
    ends = dot(before, counts_ref[0].astype(f32).astype(bf16)).astype(jnp.int32)
    field = jnp.zeros((id_rows, samples), jnp.int32)
    for f in range(FIELDS):
        field = field + jnp.where(iota((id_rows, samples), 0) >= ends[f : f + 1], 1, 0)
    bag = iota((id_rows, LANES), 1) * FIELDS + widened(field, 0.0).astype(jnp.int32)

    earlier_rows = ones_at(iota((id_rows, id_rows), 1) < iota((id_rows, id_rows), 0))
    upper = iota((2 * LANES, LANES), 0)
    mixing = ones_at((upper < iota((2 * LANES, LANES), 1)) | (upper >= LANES))
    rank = jnp.zeros((id_rows, LANES), f32)
    for begin in range(0, batch_count, chunk):
        hots = [ones_at(target == begin + d) for d in range(chunk)]
        above = dot(earlier_rows, jnp.concatenate(hots, axis=1)).astype(bf16)
        stacked = jnp.concatenate(
            [
                jnp.concatenate([hots[d], above[:, d * LANES : (d + 1) * LANES]], axis=1)
                for d in range(chunk)
            ],
            axis=0,
        )
        ranks = dot(stacked, mixing)
        for d in range(chunk):
            rank = rank + jnp.where(
                target == begin + d, ranks[d * id_rows : (d + 1) * id_rows], 0.0
            )
    shift = sum(jnp.where(micro == m, slots.shifts[m], 0) for m in range(micro_count))
    slot = rank.astype(jnp.int32) + shift
    place = jnp.where(target < batch_count, (slot // WIDE) * batch_count + target, -1)
    part_ref[0] = place.astype(f32)
    part_ref[1] = (slot % WIDE).astype(f32)
    part_ref[2] = coded(local // 64)
    part_ref[3] = coded((local % 64) * 8 + bag // 512)
    part_ref[4] = coded(bag % 512)
    places = window * batch_count

    def build(t, carry):
        span = pl.ds(pl.multiple_of(t * LANES, LANES), LANES)

        def row(k):
            return part_ref[k, pl.ds(t, 1), :]

        mask = iota((places, LANES), 0).astype(f32) == row(0)
        for v in range(3):
            left_ref[v * places : (v + 1) * places, span] = jnp.where(
                mask, row(2 + v), 0.0
            ).astype(bf16)
        right_ref[:, span] = ones_at(iota((WIDE, LANES), 0).astype(f32) == row(1))
        return carry

    lax.fori_loop(0, id_rows, build, 0, unroll=4)
    placed = dot(left_ref[...], right_ref[...], NT).astype(jnp.int32)

    def part(v, r):
        begin = (v * window + r) * batch_count
        return placed[begin : begin + batch_count]

    for m in range(micro_count):

        @pl.when(micro == m)
        def _():
            for r in range(window):
                at = slots.first_rows[m] + r
                if slots.micro_width(m, at) == 0:
                    continue
                middle = decoded(part(1, r))
                bag = middle % 8 * 512 + decoded(part(2, r))
                valid = part(2, r) != 0
                sample = ((bag.astype(f32) + 0.5) * (1.0 / FIELDS)).astype(jnp.int32)
                field = bag - sample * FIELDS
                late = jnp.where(field >= HALF, 1, 0)
                code = sample + late * LANES + (m * WIDE + 1)
                row = decoded(part(0, r)) * 64 + middle // 8
                req_ref[:, at, :] += jnp.where(valid, row, 0)
                code_ref[:, at, :] += jnp.where(valid, code, 0)
                half_ref[:, at, :] += jnp.where(valid, field - late * HALF, 0)


def in_hbm(x):
    return pltpu.with_memory_space_constraint(x, pltpu.HBM)


def route(ids, rows, counts, weights, slots, batch_count):
    micro_count, id_rows, samples = ids.shape
    places = slots.window * batch_count

    def block(x):
        return pl.BlockSpec((1,) + x.shape[1:], lambda m: (m, 0, 0))

    shapes = [(batch_count, slots.rows + k, WIDE) for k in (1, 0, 0)]
    return pl.pallas_call(
        partial(route_kernel, slots, batch_count),
        grid=(micro_count,),
        in_specs=[block(ids), block(rows), block(counts), pl.BlockSpec(weights.shape, lambda m: (0, 0))],
        out_specs=[pl.BlockSpec(shape, lambda m: (0, 0, 0)) for shape in shapes],
        out_shape=[jax.ShapeDtypeStruct(shape, jnp.int32) for shape in shapes],
        scratch_shapes=[
            pltpu.VMEM((5, id_rows, LANES), jnp.float32),
            pltpu.VMEM((3 * places, id_rows * LANES), jnp.bfloat16),
            pltpu.VMEM((WIDE, id_rows * LANES), jnp.bfloat16),
        ],
        compiler_params=pltpu.CompilerParams(vmem_limit_bytes=vmem_limit(batch_count)),
        name="route",
    )(in_hbm(ids), in_hbm(rows), in_hbm(counts), weights)


def peer_copy(src, dst, send_sem, recv_sem, peer):
    return pltpu.make_async_remote_copy(
        src_ref=src,
        dst_ref=dst,
        send_sem=send_sem,
        recv_sem=recv_sem,
        device_id={"batch": peer},
        device_id_type=pl.DeviceIdType.MESH,
    )


def greet(me, batch_count, other_tower=None):
    barrier = pltpu.get_barrier_semaphore()

    def signal(i, carry):
        pl.semaphore_signal(
            barrier,
            inc=1,
            device_id={"batch": lax.rem(me + i, batch_count)},
            device_id_type=pl.DeviceIdType.MESH,
        )
        return carry

    lax.fori_loop(1, batch_count, signal, 0)
    if other_tower is not None:
        pl.semaphore_signal(
            barrier,
            inc=1,
            device_id={"tower": other_tower},
            device_id_type=pl.DeviceIdType.MESH,
        )


def all_greeted(batch_count, pair):
    pl.semaphore_wait(pltpu.get_barrier_semaphore(), batch_count - 1 + (1 if pair else 0))


def message_rows(rows_msg, columns):
    return -(-(rows_msg * columns + 1) // 16) * 16


def each(count, action):
    def body(i, carry):
        action(i)
        return carry

    lax.fori_loop(1, count, body, 0)


def pick_rows(result, mask, depth, columns):
    width = result.shape[1]
    out = jnp.zeros((16, width), jnp.float32)
    for c in range(columns):
        row = jnp.sum(
            jnp.where(mask, result[c * depth : (c + 1) * depth], 0.0), axis=0, keepdims=True
        )
        out = jnp.where(iota((16, width), 0) == c, row, out)
    return out


def tile_table(table_ref, tiles_ref, stage_ref, columns):
    for c in range(columns):
        for q in range(TALL):
            stage_ref[q : q + 1, :] = table_ref[c : c + 1, q * BROAD : (q + 1) * BROAD]
        tiles_ref[c * TALL : (c + 1) * TALL, :] = stage_ref[...].astype(jnp.bfloat16)


def fetch_kernel(
    slots, windows, columns,
    req_ref, code_ref, half_ref, table_hbm_ref, cin_ref, rest_ref,
    out_ref, served_ref, stat_out_ref, cins_ref, rests_ref, extras_ref,
    table_ref, tiles_ref, stage_ref, first_ref, second_ref, ans_out_ref, ans_in_ref, left_ref, pooled_ref,
    other_ref,
    req_send, req_recv, ans_send, ans_recv, win_send, win_recv, plane_send,
    plane_recv, ext_send, ext_recv, pair_send, pair_recv, table_sem,
):
    rows_msg = slots.rows
    batch_count = windows.batch_count
    first_extra = windows.first_extra
    me = lax.axis_index("batch")
    tower = lax.axis_index("tower")
    other_tower = 1 - tower
    greet(me, batch_count, other_tower)
    load_table = pltpu.make_async_copy(table_hbm_ref, table_ref, table_sem)
    load_table.start()
    pooled_ref[...] = jnp.zeros_like(pooled_ref)
    first_ref[...] = jnp.zeros_like(first_ref)
    second_ref[...] = jnp.zeros_like(second_ref)

    def request_copy(peer, slot):
        return peer_copy(
            req_ref.at[peer], served_ref.at[slot], req_send.at[peer], req_recv.at[slot], peer
        )

    def answer_copy(peer, slot):
        return peer_copy(
            ans_out_ref.at[peer], ans_in_ref.at[slot], ans_send.at[peer], ans_recv.at[slot], peer
        )

    def own_copy():
        return pltpu.make_async_copy(ans_out_ref.at[me], ans_in_ref.at[me], ans_recv.at[me])

    all_greeted(batch_count, True)

    def send_requests(i, carry):
        peer = lax.rem(me + i, batch_count)
        request_copy(peer, me).start()
        return carry

    lax.fori_loop(1, batch_count, send_requests, 0)

    depth = batch_count // PLANE
    high, low = me // PLANE, lax.rem(me, PLANE)

    def others(action):
        each(batch_count, lambda i: action(lax.rem(me + i, batch_count)))

    def column(action):
        each(depth, lambda i: action(lax.rem(high + i, depth)))

    def plane(action):
        each(PLANE, lambda i: action(lax.rem(low + i, PLANE)))

    def column_copy(src, dst, to, source):
        return peer_copy(
            src, dst.at[low * depth + source], win_send.at[to], win_recv.at[source],
            to * PLANE + low,
        )

    def plane_copy(dst, to, source):
        block = dst.at[pl.ds(source * depth, depth)]
        return peer_copy(
            block, block, plane_send.at[to], plane_recv.at[source], high * PLANE + to
        )

    def extra_copy(peer, slot):
        return peer_copy(rest_ref, extras_ref.at[slot], ext_send.at[peer], ext_recv.at[slot], peer)

    def start_windows(src, dst):
        column(lambda to: column_copy(src, dst, to, high).start())
        dst[low * depth + high] = src[...]

    def pass_windows(src, dst):
        column(lambda source: column_copy(src, dst, source, source).wait_recv())
        plane(lambda to: plane_copy(dst, to, low).start())

    def sent_windows(src, dst):
        column(lambda to: column_copy(src, dst, to, high).wait_send())
        plane(lambda to: plane_copy(dst, to, low).wait_send())

    def split(action):
        @pl.when(tower == 0)
        def _():
            action(cin_ref, cins_ref)

        @pl.when(tower == 1)
        def _():
            action(rest_ref, rests_ref)

    served_ref[me] = req_ref[me]
    load_table.wait()
    tile_table(table_ref, tiles_ref, stage_ref, columns)

    sizes = ans_out_ref.shape[1]

    def look_up(first, second):
        for r in range(rows_msg):
            w = slots.width(r)
            row = jnp.concatenate(
                [served_ref[first, r : r + 1, :w], served_ref[second, r : r + 1, :w]], axis=1
            )
            hot = ones_at(iota((BROAD, 2 * w), 0) == row % BROAD)
            result = dot(tiles_ref[...], hot)
            mask = iota((TALL, 2 * w), 0) == row // BROAD
            block = pick_rows(result, mask, TALL, columns)
            first_ref[r * columns : r * columns + 16, :w] = block[:, :w]
            second_ref[r * columns : r * columns + 16, :w] = block[:, w:]
        ans_out_ref[first] = first_ref[:sizes, :].astype(jnp.bfloat16)
        ans_out_ref[second] = second_ref[:sizes, :].astype(jnp.bfloat16)

    def pool(owner, after=None):
        first_ref[:sizes, :] = ans_in_ref[owner].astype(jnp.float32)
        for r in range(rows_msg):
            w = slots.width(r)
            begin = r * columns
            values = [first_ref[begin + c : begin + c + 1, :w] for c in range(columns)]
            mask = iota((HALF, w), 0) == half_ref[owner, r : r + 1, :w]
            pieces = [jnp.where(mask, values[c], 0.0) for c in range(EMB)]
            pieces.append(jnp.where(iota((8, w), 0) == 0, values[EMB], 0.0))
            left_ref[:, r * WIDE : r * WIDE + w] = jnp.concatenate(pieces, axis=0).astype(
                jnp.bfloat16
            )
        for m in range(slots.micro_count):
            rights = []
            for r in range(slots.first_rows[m], rows_msg):
                w = slots.micro_width(m, r)
                if w:
                    lane = iota((WIDE, w), 0) + (m * WIDE + 1)
                    rights.append(ones_at(lane == code_ref[owner, r : r + 1, :w]))
            begin = slots.first_rows[m] * WIDE
            pooled_ref[m] += dot(
                left_ref[:, begin : begin + slots.spans[m]], jnp.concatenate(rights, axis=1), NT
            )
            if after is not None:
                after(m)

    def pair_copy(src, dst, k):
        return pltpu.make_async_remote_copy(
            src_ref=src,
            dst_ref=dst,
            send_sem=pair_send.at[k],
            recv_sem=pair_recv.at[k],
            device_id={"tower": other_tower},
            device_id_type=pl.DeviceIdType.MESH,
        )

    def swap_windows():
        @pl.when(tower == 0)
        def _():
            plane(lambda source: plane_copy(cins_ref, source, source).wait_recv())
            for e in range(windows.extras):

                @pl.when(me != first_extra + e)
                def _():
                    extra_copy(first_extra + e, e).wait_recv()

            pair_copy(cins_ref, cins_ref, 0).start()
            pair_copy(extras_ref, extras_ref, 1).start()

        @pl.when(tower == 1)
        def _():
            plane(lambda source: plane_copy(rests_ref, source, source).wait_recv())
            pair_copy(rests_ref, rests_ref, 0).start()

    pairs = batch_count // 2
    lag = 2

    def step(j, carry):
        @pl.when(j < pairs)
        def _():
            first = lax.rem(me + batch_count - (2 * j + 1), batch_count)
            second = lax.rem(me + 2 * batch_count - (2 * j + 2), batch_count)
            request_copy(first, first).wait_recv()

            @pl.when(j < pairs - 1)
            def _():
                request_copy(second, second).wait_recv()

            look_up(first, second)

            @pl.when(j == 0)
            def _():
                split(start_windows)

            @pl.when((j == 0) & (tower == 0) & (me >= first_extra))
            def _():
                others(lambda peer: extra_copy(peer, me - first_extra).start())
                extras_ref[me - first_extra] = rest_ref[...]

            @pl.when(j == 3)
            def _():
                split(pass_windows)

            @pl.when(j == pairs - 2)
            def _():
                swap_windows()

            answer_copy(first, me).start()

            @pl.when(j < pairs - 1)
            def _():
                answer_copy(second, me).start()

            @pl.when(j == pairs - 1)
            def _():
                own_copy().start()

        @pl.when(j >= lag)
        def _():
            first = lax.rem(me + 2 * (j - lag) + 1, batch_count)
            answer_copy(first, first).wait_recv()
            pool(first)

        @pl.when((j >= lag) & (j < pairs - 1 + lag))
        def _():
            second = lax.rem(me + 2 * (j - lag) + 2, batch_count)
            answer_copy(second, second).wait_recv()
            pool(second)

        return carry

    lax.fori_loop(0, pairs + lag, step, 0)

    def pooled_copy(m):
        return pair_copy(pooled_ref.at[m], other_ref.at[m], 2 + m)

    own_copy().wait()
    pool(me, lambda m: pooled_copy(m).start())

    def finish(i, carry):
        peer = lax.rem(me + i, batch_count)
        request_copy(peer, me).wait_send()
        answer_copy(peer, me).wait_send()
        return carry

    lax.fori_loop(1, batch_count, finish, 0)
    weight_sum = jnp.sum(served_ref[:, rows_msg, :LANES], axis=0, keepdims=True)
    stat_out_ref[...] = jnp.broadcast_to(weight_sum.astype(jnp.float32), stat_out_ref.shape)

    split(sent_windows)

    @pl.when(tower == 0)
    def _():
        @pl.when(me >= first_extra)
        def _():
            others(lambda peer: extra_copy(peer, me - first_extra).wait_send())

        pair_copy(cins_ref, cins_ref, 0).wait_send()
        pair_copy(extras_ref, extras_ref, 1).wait_send()
        pair_copy(rests_ref, rests_ref, 0).wait_recv()

    @pl.when(tower == 1)
    def _():
        pair_copy(rests_ref, rests_ref, 0).wait_send()
        pair_copy(cins_ref, cins_ref, 0).wait_recv()
        pair_copy(extras_ref, extras_ref, 1).wait_recv()

    for m in range(slots.micro_count):
        pooled_copy(m).wait()
        out_ref[m] = pooled_ref[m] + other_ref[m]


def fetch(
    requests, codes, halves, table, cin_window, rest_window, windows, slots
):
    batch_count, rows_msg, _ = codes.shape
    columns, rows_dev = table.shape
    sizes = message_rows(rows_msg, columns)
    in_vmem = pl.BlockSpec(memory_space=pltpu.VMEM)
    dma = pltpu.SemaphoreType.DMA
    bags = (slots.micro_count, BAG_ROWS, WIDE)
    return pl.pallas_call(
        partial(fetch_kernel, slots, windows, columns),
        in_specs=[in_vmem] * 3 + [pl.BlockSpec(memory_space=pltpu.HBM)] + [in_vmem] * 2,
        out_specs=[in_vmem] * 6,
        out_shape=[
            jax.ShapeDtypeStruct(bags, jnp.float32),
            jax.ShapeDtypeStruct(requests.shape, jnp.int32),
            jax.ShapeDtypeStruct((8, LANES), jnp.float32),
            jax.ShapeDtypeStruct((batch_count,) + cin_window.shape, jnp.bfloat16),
            jax.ShapeDtypeStruct((batch_count,) + rest_window.shape, jnp.bfloat16),
            jax.ShapeDtypeStruct((windows.extras,) + rest_window.shape, jnp.bfloat16),
        ],
        scratch_shapes=[
            pltpu.VMEM(table.shape, jnp.float32),
            pltpu.VMEM((columns * TALL, BROAD), jnp.bfloat16),
            pltpu.VMEM((TALL, BROAD), jnp.float32),
            pltpu.VMEM((sizes + 16, WIDE), jnp.float32),
            pltpu.VMEM((sizes + 16, WIDE), jnp.float32),
            pltpu.VMEM((batch_count, sizes, WIDE), jnp.bfloat16),
            pltpu.VMEM((batch_count, sizes, WIDE), jnp.bfloat16),
            pltpu.VMEM((BAG_ROWS, rows_msg * WIDE), jnp.bfloat16),
            pltpu.VMEM(bags, jnp.float32),
            pltpu.VMEM(bags, jnp.float32),
        ]
        + [dma((batch_count,))] * 9
        + [dma((windows.extras,)), dma((2 + slots.micro_count,)), dma((2 + slots.micro_count,)), dma],
        compiler_params=pltpu.CompilerParams(
            vmem_limit_bytes=vmem_limit(batch_count), collective_id=0, has_side_effects=True
        ),
        name="fetch",
    )(requests, codes, halves, in_hbm(table), cin_window, rest_window)


def return_kernel(
    slots, windows, columns,
    grad_ref, code_ref, half_ref, served_ref, stat_ref, cins_ref, rests_ref, extras_ref,
    out_ref, stat_out_ref, cin_ref, rest_ref,
    send_ref, recv_ref, first_ref, second_ref, left_ref, right_ref, total_ref,
    extra_in_ref, cin_near_ref, cin_sum_ref, cin_far_ref, rest_near_ref, rest_sum_ref, rest_far_ref,
    val_send, val_recv, win_send, win_recv, plane_send, plane_recv, ext_send,
    ext_recv,
):
    batch_count = windows.batch_count
    first_extra = windows.first_extra
    tower = lax.axis_index("tower")
    rows_msg = slots.rows
    me = lax.axis_index("batch")
    greet(me, batch_count)

    def value_copy(peer, slot):
        return peer_copy(
            send_ref.at[peer], recv_ref.at[slot], val_send.at[peer], val_recv.at[slot], peer
        )

    def own_copy():
        return pltpu.make_async_copy(send_ref.at[me], recv_ref.at[me], val_recv.at[me])

    depth = batch_count // PLANE
    high, low = me // PLANE, lax.rem(me, PLANE)

    def others(action):
        each(batch_count, lambda i: action(lax.rem(me + i, batch_count)))

    def column(action):
        each(depth, lambda i: action(lax.rem(high + i, depth)))

    def plane(action):
        each(PLANE, lambda i: action(lax.rem(low + i, PLANE)))

    def plane_copy(src, near, to, source):
        return peer_copy(
            src.at[pl.ds(to * depth, depth)], near.at[source], plane_send.at[to],
            plane_recv.at[source], high * PLANE + to,
        )

    def column_copy(total, far, to, source):
        return peer_copy(
            total.at[to], far.at[source], win_send.at[to], win_recv.at[source], to * PLANE + low
        )

    def start_windows(src, near, total, far, out):
        plane(lambda to: plane_copy(src, near, to, low).start())
        near[low] = src[pl.ds(low * depth, depth)]

    def pass_windows(src, near, total, far, out):
        plane(lambda source: plane_copy(src, near, source, source).wait_recv())
        total[...] = jnp.sum(near[...], axis=0)
        column(lambda to: column_copy(total, far, to, high).start())
        far[high] = total[high]

    def end_windows(src, near, total, far, out):
        column(lambda source: column_copy(total, far, source, source).wait_recv())
        out[...] = jnp.sum(far[...], axis=0)
        plane(lambda to: plane_copy(src, near, to, low).wait_send())
        column(lambda to: column_copy(total, far, to, high).wait_send())

    def split(action):
        @pl.when(tower == 0)
        def _():
            action(cins_ref, cin_near_ref, cin_sum_ref, cin_far_ref, cin_ref)

        @pl.when(tower == 1)
        def _():
            action(rests_ref, rest_near_ref, rest_sum_ref, rest_far_ref, rest_ref)

    def extra_copy(peer, slot):
        return peer_copy(
            extras_ref.at[peer - first_extra],
            extra_in_ref.at[slot],
            ext_send.at[peer],
            ext_recv.at[slot],
            peer,
        )

    first_ref[...] = jnp.zeros_like(first_ref)
    second_ref[...] = jnp.zeros_like(second_ref)
    spare = rows_msg * columns
    loss_parts = split_three(stat_ref[0:1, :])
    loss_row = sum(
        jnp.where(iota((1, LANES), 1) == k, part.astype(jnp.float32), 0.0)
        for k, part in enumerate(loss_parts)
    )
    stat_out_ref[...] = jnp.zeros_like(stat_out_ref)
    total_ref[...] = jnp.zeros_like(total_ref)

    sizes = send_ref.shape[1]

    def spread(first, second):
        def both(ref, r, w):
            return jnp.concatenate([ref[first, r : r + 1, :w], ref[second, r : r + 1, :w]], axis=1)

        for r in range(rows_msg):
            w = slots.width(r)
            result = None
            for m in range(slots.micro_count):
                inner = slots.micro_width(m, r)
                if inner == 0:
                    continue
                hot = ones_at(iota((WIDE, 2 * inner), 0) + (m * WIDE + 1) == both(code_ref, r, inner))
                found = dot(grad_ref[m], hot)
                if inner < w:
                    blank = jnp.zeros((BAG_ROWS, w - inner), jnp.float32)
                    found = jnp.concatenate(
                        [found[:, :inner], blank, found[:, inner:], blank], axis=1
                    )
                result = found if result is None else result + found
            mask = iota((HALF, 2 * w), 0) == both(half_ref, r, w)
            block = pick_rows(result, mask, HALF, EMB)
            linear = result[EMB * HALF : EMB * HALF + 1]
            block = jnp.where(iota((16, 2 * w), 0) == EMB, linear, block)
            first_ref[r * columns : r * columns + 16, :w] = block[:, :w]
            second_ref[r * columns : r * columns + 16, :w] = block[:, w:]
        first_ref[spare : spare + 1, :LANES] = loss_row
        second_ref[spare : spare + 1, :LANES] = loss_row
        send_ref[first] = first_ref[:sizes, :].astype(jnp.bfloat16)
        send_ref[second] = second_ref[:sizes, :].astype(jnp.bfloat16)

    def scatter(source):
        first_ref[:sizes, :] = recv_ref[source].astype(jnp.float32)
        stat_out_ref[0:1, :] += first_ref[spare : spare + 1, :LANES]
        for r in range(rows_msg):
            w = slots.width(r)
            span = slice(r * WIDE, r * WIDE + w)
            row = served_ref[source, r : r + 1, :w]
            mask = iota((TALL, w), 0) == row // BROAD
            for c in range(columns):
                left_ref[c * TALL : (c + 1) * TALL, span] = jnp.where(
                    mask, first_ref[r * columns + c : r * columns + c + 1, :w], 0.0
                ).astype(jnp.bfloat16)
            right_ref[:, span] = ones_at(iota((BROAD, w), 0) == row % BROAD)
        total_ref[...] += dot(
            left_ref[:, : slots.length], right_ref[:, : slots.length], NT
        )

    pairs = batch_count // 2
    lag = 2

    def step(j, carry):
        @pl.when(j < pairs)
        def _():
            first = lax.rem(me + 2 * j + 1, batch_count)
            second = lax.rem(me + 2 * j + 2, batch_count)
            spread(first, second)

            @pl.when(j == 0)
            def _():
                all_greeted(batch_count, False)

            value_copy(first, me).start()

            @pl.when(j == 1)
            def _():
                split(start_windows)

            @pl.when((j == 1) & (tower == 0))
            def _():
                for e in range(windows.extras):

                    @pl.when(me != first_extra + e)
                    def _():
                        extra_copy(first_extra + e, me).start()

            @pl.when(j < pairs - 1)
            def _():
                value_copy(second, me).start()

            @pl.when(j == pairs - 1)
            def _():
                own_copy().start()

        @pl.when(j == pairs - 1)
        def _():
            split(pass_windows)

        @pl.when(j >= lag)
        def _():
            first = lax.rem(me + batch_count - (2 * (j - lag) + 1), batch_count)
            value_copy(first, first).wait_recv()
            scatter(first)

        @pl.when((j >= lag) & (j < pairs - 1 + lag))
        def _():
            second = lax.rem(me + 2 * batch_count - (2 * (j - lag) + 2), batch_count)
            value_copy(second, second).wait_recv()
            scatter(second)

        return carry

    lax.fori_loop(0, pairs + lag, step, 0)
    own_copy().wait()
    scatter(me)

    split(end_windows)

    @pl.when(tower == 0)
    def _():
        for e in range(windows.extras):

            @pl.when(me != first_extra + e)
            def _():
                extra_copy(first_extra + e, me).wait_send()

        @pl.when(me >= first_extra)
        def _():
            extra_in_ref[me] = extras_ref[me - first_extra]
            others(lambda peer: extra_copy(me, peer).wait_recv())
            rest_ref[...] = jnp.sum(extra_in_ref[...], axis=0)

        @pl.when(me < first_extra)
        def _():
            rest_ref[...] = jnp.zeros_like(rest_ref)

    @pl.when(tower == 1)
    def _():
        cin_ref[...] = jnp.zeros_like(cin_ref)

    def finish(i, carry):
        peer = lax.rem(me + i, batch_count)
        value_copy(peer, me).wait_send()
        return carry

    lax.fori_loop(1, batch_count, finish, 0)
    losses = jnp.sum(stat_out_ref[0:1, :], axis=1, keepdims=True)
    stat_out_ref[...] = jnp.broadcast_to(losses, stat_out_ref.shape)
    for c in range(columns):
        for q in range(TALL):
            out_ref[c : c + 1, q * BROAD : (q + 1) * BROAD] = total_ref[
                c * TALL + q : c * TALL + q + 1, :
            ]


def return_grads(
    grad_bags, codes, halves, served, stat, cins, rests, extras, windows, slots, columns
):
    batch_count, rows_msg, _ = codes.shape
    long = rows_msg * WIDE
    sizes = message_rows(rows_msg, columns)
    depth = batch_count // PLANE
    in_vmem = pl.BlockSpec(memory_space=pltpu.VMEM)
    dma = pltpu.SemaphoreType.DMA
    return pl.pallas_call(
        partial(return_kernel, slots, windows, columns),
        in_specs=[in_vmem] * 8,
        out_specs=[in_vmem] * 4,
        out_shape=[
            jax.ShapeDtypeStruct((columns, TALL * BROAD), jnp.float32),
            jax.ShapeDtypeStruct(stat.shape, jnp.float32),
            jax.ShapeDtypeStruct(cins.shape[1:], jnp.float32),
            jax.ShapeDtypeStruct(rests.shape[1:], jnp.float32),
        ],
        scratch_shapes=[
            pltpu.VMEM((batch_count, sizes, WIDE), jnp.bfloat16),
            pltpu.VMEM((batch_count, sizes, WIDE), jnp.bfloat16),
            pltpu.VMEM((sizes + 16, WIDE), jnp.float32),
            pltpu.VMEM((sizes + 16, WIDE), jnp.float32),
            pltpu.VMEM((columns * TALL, long), jnp.bfloat16),
            pltpu.VMEM((BROAD, long), jnp.bfloat16),
            pltpu.VMEM((columns * TALL, BROAD), jnp.float32),
            pltpu.VMEM(rests.shape, jnp.float32),
        ]
        + [
            pltpu.VMEM(lead + x.shape[1:], jnp.float32)
            for x in (cins, rests)
            for lead in ((PLANE, depth), (depth,), (depth,))
        ]
        + [dma((batch_count,))] * 8,
        compiler_params=pltpu.CompilerParams(
            vmem_limit_bytes=vmem_limit(batch_count), collective_id=1, has_side_effects=True
        ),
        name="return_grads",
    )(grad_bags, codes, halves, served, stat, cins, rests, extras)


def split_three(x):
    high = x.astype(jnp.bfloat16)
    rest = x - high.astype(jnp.float32)
    middle = rest.astype(jnp.bfloat16)
    low = (rest - middle.astype(jnp.float32)).astype(jnp.bfloat16)
    return high, middle, low


def dense_kernel(
    micro_count, windows, tower_ref, stat_ref, pooled_ref, label_ref, weight_ref,
    cins_ref, rests_ref, extras_ref,
    bags_ref, loss_ref, g_cins_ref, g_rests_ref, g_extras_ref,
    embed_ref, total_ref, pairs_ref, sym_ref, cin_ref, rest_ref, lane_ref,
):
    f32 = jnp.float32
    bf16 = jnp.bfloat16
    width = micro_count * LANES
    groups = HPAD // LANES

    cin_ref[...] = jnp.zeros_like(cin_ref)
    for b, at in enumerate(windows.cin_at):
        block = cins_ref[windows.slots[b]].astype(f32)
        cin_ref[at : at + windows.cin_rows, :] += block[: windows.cin_rows]
    rest_ref[...] = jnp.zeros_like(rest_ref)
    pieces = [(rests_ref, windows.slots[b], at) for b, at in enumerate(windows.rest_at)]
    pieces += [(extras_ref, e, at) for e, at in enumerate(windows.extra_at)]
    for source, b, at in pieces:
        skip = max(0, -at)
        block = source[b].astype(f32)
        for l in range(groups):
            rest_ref[l, at + skip : at + windows.rest_rows, :] += block[
                skip : windows.rest_rows, l * LANES : (l + 1) * LANES
            ]

    def rest_rows(begin, count):
        return jnp.concatenate(
            [rest_ref[l, begin : begin + count, :] for l in range(groups)], axis=1
        )[:, :HID]

    cin_w = cin_ref[:MAPS, :].astype(bf16)
    place = iota((MAPS, PAIRS), 0)
    place = place // FIELDS * FPAD + place % FIELDS == iota((MAPS, PAIRS), 1)
    picks_u = ones_at(place)
    row_u = jnp.broadcast_to(cin_ref[MAPS : MAPS + 1, :], (8, PAIRS)).astype(bf16)
    cin_u = dot(picks_u, row_u, NT)[:, :1]
    w_one = jnp.concatenate(
        [
            jnp.concatenate(
                [rest_ref[l, pl.ds(d, FPAD, stride=EMB), :] for l in range(groups)], axis=1
            )[:, :HID]
            for d in range(EMB)
        ],
        axis=0,
    ).astype(bf16)
    w_two = rest_rows(W_TWO, HID).astype(bf16)
    rows = jnp.zeros((8, HID), f32)
    for k, at in enumerate((B_ONE, B_TWO, W_THREE)):
        rows = jnp.where(iota((8, HID), 0) == k, rest_rows(at, 1), rows)
    unit = ones_at(iota((HID, HID), 0) == iota((HID, HID), 1))
    turned = dot(unit, rows.astype(bf16), NT)
    b_one, b_two, w_three = turned[:, 0:1], turned[:, 1:2], turned[:, 2:3]
    bias = rest_ref[0, BIAS : BIAS + 1, 0:1]

    def unpacked(row, count):
        pieces = []
        for m in range(micro_count):
            low = pooled_ref[m, row : row + HALF, :LANES]
            high = pooled_ref[m, row : row + HALF, LANES:]
            pieces.append(jnp.concatenate([low, high], axis=0)[:count])
        return jnp.concatenate(pieces, axis=1)

    for d in range(EMB):
        embed_ref[d * FPAD : (d + 1) * FPAD, :] = unpacked(d * HALF, FPAD)
    linear = jnp.concatenate(
        [
            pooled_ref[m, EMB * HALF : EMB * HALF + 1, :LANES]
            + pooled_ref[m, EMB * HALF : EMB * HALF + 1, LANES:]
            for m in range(micro_count)
        ],
        axis=1,
    )

    def pair_row(i, carry):
        total = jnp.zeros((FPAD, width), f32)
        for d in range(EMB):
            own = embed_ref[pl.ds(d * FPAD + i, 1), :]
            product = (embed_ref[d * FPAD : (d + 1) * FPAD, :] * own).astype(jnp.bfloat16)
            total = total + product.astype(f32)
        total_ref[pl.ds(pl.multiple_of(i * FPAD, 8), FPAD), :] = total
        return carry

    lax.fori_loop(0, FIELDS, pair_row, 0, unroll=3)
    thirds = split_three(total_ref[...])
    map_sum = sum(dot(cin_w, third) for third in thirds)
    cin_logits = jnp.sum(map_sum * cin_u, axis=0, keepdims=True)

    flat = embed_ref[...].astype(jnp.bfloat16)
    pre_one = dot(w_one, flat, TN) + b_one
    hidden_one = jnp.maximum(pre_one, 0.0).astype(jnp.bfloat16)
    pre_two = dot(w_two, hidden_one, TN) + b_two
    active_two = jnp.maximum(pre_two, 0.0)
    deep_logits = jnp.sum(active_two * w_three, axis=0, keepdims=True)
    logits = cin_logits + deep_logits + linear + bias

    samples = weight_ref.shape[1]
    lane_ref[...] = jnp.zeros_like(lane_ref)
    for m in range(micro_count):
        span = slice(m * LANES, m * LANES + samples)
        lane_ref[0:1, span] = weight_ref[m : m + 1, :].astype(f32)
        lane_ref[1:2, span] = label_ref[m : m + 1, :].astype(f32)
    weight = lane_ref[0:1, :]
    label = lane_ref[1:2, :]
    soft = jnp.maximum(logits, 0.0) + jnp.log1p(jnp.exp(-jnp.abs(logits)))
    loss_ref[...] = jnp.broadcast_to(
        jnp.sum(weight * (soft - label * logits), axis=1, keepdims=True), loss_ref.shape
    )
    grad_logits = weight * (jax.nn.sigmoid(logits) - label) / stat_ref[0:1, 0:1]

    grad_maps = (grad_logits * cin_u).astype(jnp.bfloat16)
    grad_two = jnp.where(pre_two > 0, grad_logits * w_three, 0.0).astype(jnp.bfloat16)
    grad_hidden = dot(w_two, grad_two)
    grad_one = jnp.where(pre_one > 0, grad_hidden, 0.0).astype(jnp.bfloat16)
    grad_flat = dot(w_one, grad_one)

    grad_pairs = dot(cin_w, grad_maps, TN)
    for m in range(micro_count):
        pairs_ref[m, :PAIRS, :] = grad_pairs[:, m * LANES : (m + 1) * LANES]
        pairs_ref[m, PAIRS:, :] = jnp.zeros((FPAD * FPAD - PAIRS, LANES), f32)

    def mirror(j, carry):
        here = pl.ds(pl.multiple_of(j * FPAD, 8), FPAD)
        both = [
            pairs_ref[m, here, :] + pairs_ref[m, pl.ds(j, FPAD, stride=FPAD), :]
            for m in range(micro_count)
        ]
        sym_ref[here, :] = jnp.concatenate(both, axis=1)
        return carry

    lax.fori_loop(0, FIELDS, mirror, 0, unroll=3)
    empty = jnp.zeros((2 * HALF - FPAD, width), f32)

    for d in range(EMB):

        def add_row(j, total):
            here = pl.ds(pl.multiple_of(j * FPAD, 8), FPAD)
            return total + sym_ref[here, :] * embed_ref[pl.ds(d * FPAD + j, 1), :]

        grad_embed = lax.fori_loop(
            0, FIELDS, add_row, grad_flat[d * FPAD : (d + 1) * FPAD], unroll=13
        )
        grad_embed = jnp.concatenate([grad_embed, empty], axis=0)
        for m in range(micro_count):
            span = slice(m * LANES, (m + 1) * LANES)
            block = jnp.concatenate([grad_embed[:HALF, span], grad_embed[HALF:, span]], axis=1)
            bags_ref[m, d * HALF : (d + 1) * HALF, :] = block.astype(bf16)
    for m in range(micro_count):
        row = grad_logits[:, m * LANES : (m + 1) * LANES]
        row = jnp.concatenate([row, row], axis=1)
        bags_ref[m, EMB * HALF :, :] = jnp.broadcast_to(row, (8, WIDE)).astype(bf16)

    ones = jnp.ones((8, width), bf16)

    def row_sum(x):
        return sum(dot(ones, third, NT) for third in split_three(x))[:1]

    rest_ref[...] = jnp.zeros_like(rest_ref)

    def put(begin, count, value, stride=None):
        for l in range(groups):
            piece = value[:, l * LANES : min((l + 1) * LANES, HID)]
            lanes = slice(0, piece.shape[1])
            if stride is None:
                rest_ref[l, begin : begin + count, lanes] = piece
            else:
                piece = jnp.pad(piece, ((0, 0), (0, LANES - piece.shape[1])))
                rest_ref[l, pl.ds(begin, count, stride=stride), :] = piece

    g_w_one = dot(flat, grad_one, NT)
    for d in range(EMB):
        put(d, FIELDS, g_w_one[d * FPAD : d * FPAD + FIELDS], EMB)

    @pl.when(tower_ref[0] == 0)
    def _():
        cin_ref[...] = jnp.zeros_like(cin_ref)
        cin_ref[:MAPS, :] = sum(dot(grad_maps, third, NT) for third in thirds)
        g_cin_u = jnp.sum(map_sum * grad_logits, axis=1, keepdims=True)
        thirds_u = split_three(jnp.broadcast_to(g_cin_u, (MAPS, 8)))
        cin_ref[MAPS : MAPS + 1, :] = sum(dot(third, picks_u, TN) for third in thirds_u)[:1]
        for b, at in enumerate(windows.cin_at):
            g_cins_ref[windows.slots[b], : windows.cin_rows, :] = cin_ref[
                at : at + windows.cin_rows, :
            ]
        for e, at in enumerate(windows.extra_at):
            skip = max(0, -at)
            for l in range(groups):
                span = slice(l * LANES, (l + 1) * LANES)
                g_extras_ref[e, skip : windows.rest_rows, span] = rest_ref[
                    l, at + skip : at + windows.rest_rows, :
                ]

    @pl.when(tower_ref[0] != 0)
    def _():
        put(W_TWO, HID, dot(hidden_one, grad_two, NT))
        put(B_ONE, 1, dot(ones, grad_one, NT)[:1])
        put(B_TWO, 1, dot(ones, grad_two, NT)[:1])
        put(W_THREE, 1, row_sum(active_two * grad_logits))
        g_bias = jnp.sum(grad_logits, axis=1, keepdims=True)
        put(BIAS, 1, jnp.where(iota((1, HID), 1) == 0, g_bias, 0.0))
        for b, at in enumerate(windows.rest_at):
            for l in range(groups):
                span = slice(l * LANES, (l + 1) * LANES)
                g_rests_ref[windows.slots[b], : windows.rest_rows, span] = rest_ref[
                    l, at : at + windows.rest_rows, :
                ]


def dense_step(tower_at, stats, pooled, labels, weights, cins, rests, extras, windows):
    micro_count = pooled.shape[0]
    width = micro_count * LANES
    in_vmem = pl.BlockSpec(memory_space=pltpu.VMEM)
    in_smem = pl.BlockSpec(memory_space=pltpu.SMEM)
    f32 = jnp.float32
    shapes = [
        ((micro_count, BAG_ROWS, WIDE), jnp.bfloat16),
        ((8, LANES), f32),
        ((cins.shape[0], windows.cin_pad_wide, PAIRS), f32),
        ((rests.shape[0], windows.rest_pad_wide, HPAD), f32),
        ((extras.shape[0], windows.rest_pad_wide, HPAD), f32),
    ]
    return pl.pallas_call(
        partial(dense_kernel, micro_count, windows),
        in_specs=[in_smem] + [in_vmem] * 7,
        out_specs=[in_vmem] * len(shapes),
        out_shape=[jax.ShapeDtypeStruct(*shape) for shape in shapes],
        scratch_shapes=[
            pltpu.VMEM((EMB * FPAD, width), f32),
            pltpu.VMEM((PAIRS, width), f32),
            pltpu.VMEM((micro_count, FPAD * FPAD, LANES), f32),
            pltpu.VMEM((PAIRS, width), f32),
            pltpu.VMEM((windows.cin_total, PAIRS), f32),
            pltpu.VMEM((HPAD // LANES, windows.rest_total, LANES), f32),
            pltpu.VMEM((8, width), f32),
        ],
        compiler_params=pltpu.CompilerParams(vmem_limit_bytes=vmem_limit(windows.batch_count)),
        name="dense",
    )(tower_at.reshape(1), stats, pooled, labels, weights, cins, rests, extras)


def shards(
    shard_ids,
    local_rows,
    bag_counts,
    click_labels,
    sample_weights,
    embed_table,
    table_first,
    table_second,
    dense_params,
    dense_first,
    dense_second,
):
    tower_count = lax.axis_size("tower")
    batch_count = lax.axis_size("batch")
    tower_at = lax.axis_index("tower")
    micro_count, samples = shard_ids.shape[:2]
    columns, rows_dev = embed_table.shape
    capacity = 4 * samples * IDS_SAMP // (tower_count * batch_count)
    share = dense_params.shape[0]
    windows = Windows(share, batch_count)
    slots = Slots(micro_count, capacity)

    device = tower_at * batch_count + lax.axis_index("batch")
    cin_phase, rest_phase = windows.phases(device)
    low = dense_params.astype(jnp.bfloat16)

    def window(rows, row_size, phase):
        return lax.dynamic_update_slice(
            jnp.zeros((rows * row_size,), jnp.bfloat16), low, (phase,)
        )

    cin_window = window(windows.cin_rows, SQUARE, cin_phase).reshape(-1, FIELDS, FIELDS)
    cin_window = jnp.pad(
        cin_window,
        ((0, windows.cin_pad - windows.cin_rows), (0, 0), (0, FPAD - FIELDS)),
    ).reshape(windows.cin_pad, PAIRS)
    rest_window = jnp.pad(
        window(windows.rest_rows, HID, rest_phase).reshape(-1, HID),
        ((0, windows.rest_pad - windows.rest_rows), (0, HPAD - HID)),
    )

    def lanes_of(values):
        return jnp.moveaxis(values, 1, -1).reshape(micro_count, -1, samples)

    requests, codes, halves = route(
        lanes_of(shard_ids), lanes_of(local_rows), lanes_of(bag_counts), sample_weights,
        slots, batch_count,
    )
    pooled, served, stats, cins, rests, extras = fetch(
        requests, codes, halves, embed_table, cin_window, rest_window, windows, slots
    )
    grad_bags, loss, g_cins, g_rests, g_extras = dense_step(
        tower_at, stats, pooled, click_labels, sample_weights, cins, rests, extras, windows
    )
    table_grad, losses, g_cin, g_rest = return_grads(
        grad_bags, codes, halves, served, loss, g_cins, g_rests, g_extras, windows, slots, columns
    )
    g_cin = g_cin[: windows.cin_rows].reshape(-1, FIELDS, FPAD)[:, :, :FIELDS].reshape(-1)
    g_rest = g_rest[: windows.rest_rows, :HID].reshape(-1)
    is_cin = device * share + jnp.arange(share, dtype=jnp.int32) < CIN_SIZE
    own_grad = jnp.where(
        is_cin,
        lax.dynamic_slice(g_cin, (cin_phase,), (share,)),
        lax.dynamic_slice(g_rest, (rest_phase,), (share,)),
    )

    table_new, table_first_new, table_second_new = adam_update(
        embed_table, table_first, table_second, table_grad, rate_table
    )
    dense_new, dense_first_new, dense_second_new = adam_update(
        dense_params, dense_first, dense_second, own_grad, rate_dense
    )
    loss_sum = losses[0, 0] / stats[0, 0]
    return (
        table_new,
        table_first_new,
        table_second_new,
        table_new.astype(jnp.bfloat16),
        dense_new,
        dense_first_new,
        dense_second_new,
        dense_new.astype(jnp.bfloat16),
        loss_sum,
    )


def solution(mesh):
    rows = P(None, ("tower", "batch"))
    dense = P(("tower", "batch"))
    placed = (
        P(None, "batch", None, None),
        P(None, "batch", None, None),
        P(None, "batch", None),
        P(None, "batch"),
        P(None, "batch"),
        rows,
        rows,
        rows,
        dense,
        dense,
        dense,
    )
    return jax.shard_map(
        shards,
        mesh=mesh,
        in_specs=placed,
        out_specs=(rows, rows, rows, rows, dense, dense, dense, dense, P()),
        check_vma=False,
    )
```

```python
from functools import partial

import jax
import jax.numpy as jnp
from jax import lax
from jax.experimental import pallas as pl
from jax.experimental.pallas import tpu as pltpu
from jax.sharding import PartitionSpec as P

FIELDS = 39
EMB = 10
MAPS = 200
HID = 400
IDS_SAMP = 80

beta_one = 0.9
beta_two = 0.999
epsilon = 1e-08
decay_rate = 0.15
rate_table = 0.1
rate_dense = 0.05
step_count = 10

LANES = 128
WIDE = 256
BROAD = 512
TALL = 64
HALF = 24
BAG_ROWS = EMB * HALF + 8
FPAD = 40
PAIRS = FIELDS * FPAD
SQUARE = FIELDS * FIELDS
CIN_SIZE = MAPS * SQUARE + MAPS
FLAT = EMB * FIELDS
B_ONE, W_TWO, B_TWO, W_THREE, BIAS = FLAT, FLAT + 1, FLAT + HID + 1, FLAT + HID + 2, FLAT + HID + 3
HPAD = 512
PLANE = 4
NT = (((1,), (1,)), ((), ()))
TN = (((0,), (0,)), ((), ()))
NN = (((1,), (0,)), ((), ()))


def adam_update(weight, first_old, second_old, gradient, step_rate):
    first_new = beta_one * first_old + (1.0 - beta_one) * gradient
    second_new = beta_two * second_old + (1.0 - beta_two) * gradient * gradient
    first_hat = first_new / (1.0 - beta_one**step_count)
    second_hat = second_new / (1.0 - beta_two**step_count)
    weight_new = weight - step_rate * (
        first_hat / (jnp.sqrt(second_hat) + epsilon) + decay_rate * weight
    )
    return (weight_new, first_new, second_new)


def dot(a, b, dims=NN):
    return lax.dot_general(a, b, dims, preferred_element_type=jnp.float32)


def vmem_limit(batch_count):
    return (28 + batch_count // 4) << 20


def iota(shape, dim):
    return lax.broadcasted_iota(jnp.int32, shape, dim)


def ones_at(mask):
    return jnp.where(mask, 1.0, 0.0).astype(jnp.bfloat16)


class Slots:
    def __init__(self, micro_count, capacity):
        self.micro_count = micro_count
        self.first_rows = [m * capacity // WIDE for m in range(micro_count)]
        self.shifts = [m * capacity % WIDE for m in range(micro_count)]
        self.spans = [-(-(shift + capacity) // LANES) * LANES for shift in self.shifts]
        self.length = max(
            first * WIDE + span for first, span in zip(self.first_rows, self.spans)
        )
        self.rows = -(-self.length // WIDE)
        self.window = max(-(-span // WIDE) for span in self.spans)

    def width(self, row):
        return min(WIDE, self.length - row * WIDE)

    def micro_width(self, micro, row):
        inside = row - self.first_rows[micro]
        return max(0, min(WIDE, self.spans[micro] - inside * WIDE)) if inside >= 0 else 0


class Windows:
    def __init__(self, share, batch_count):
        self.share, self.batch_count = share, batch_count
        self.cin_rows = -(-(SQUARE - 1 + share) // SQUARE)
        self.rest_rows = -(-(HID - 1 + share) // HID)
        self.cin_pad = -(-self.cin_rows // 16) * 16
        self.rest_pad = -(-self.rest_rows // 16) * 16
        self.cin_pad_wide = -(-self.cin_rows // 8) * 8
        self.rest_pad_wide = -(-self.rest_rows // 8) * 8
        self.first_extra = CIN_SIZE // share
        self.extras = batch_count - self.first_extra
        self.cin_at = [b * share // SQUARE for b in range(batch_count)]
        self.rest_at = [
            ((batch_count + b) * share - CIN_SIZE) // HID for b in range(batch_count)
        ]
        self.extra_at = [
            (b * share - CIN_SIZE) // HID for b in range(self.first_extra, batch_count)
        ]
        depth = batch_count // PLANE
        self.slots = [b % PLANE * depth + b // PLANE for b in range(batch_count)]
        self.cin_total = -(-max(a + self.cin_rows for a in self.cin_at) // 8) * 8
        self.rest_total = -(-max(a + self.rest_rows for a in self.rest_at) // 8) * 8

    def phases(self, device):
        start = device * self.share
        return start % SQUARE, jnp.mod(start - CIN_SIZE, HID)


def coded(x):
    return jnp.where(x < 256, x + 1, 255 - x).astype(jnp.float32)


def decoded(x):
    return jnp.where(x > 0, x - 1, 255 - x)


def route_kernel(
    slots, batch_count, ids_ref, rows_ref, counts_ref, weight_ref,
    req_ref, code_ref, half_ref, part_ref, left_ref, right_ref,
):
    f32, bf16 = jnp.float32, jnp.bfloat16
    micro_count, window = slots.micro_count, slots.window
    micro = pl.program_id(0)
    id_rows, samples = ids_ref.shape[1:]
    chunk = 16
    tower = lax.axis_index("tower")

    @pl.when(micro == 0)
    def _():
        req_ref[...] = jnp.zeros_like(req_ref)
        code_ref[...] = jnp.zeros_like(code_ref)
        half_ref[...] = jnp.zeros_like(half_ref)
        part_ref[...] = jnp.zeros_like(part_ref)
        weight_sum = jnp.sum(weight_ref[...].astype(f32)).astype(jnp.int32)
        req_ref[:, slots.rows, :] = jnp.full((batch_count, WIDE), weight_sum)

    def widened(x, filler):
        part_ref[0, :, :samples] = x.astype(f32)
        inside = iota((id_rows, LANES), 1) < samples
        return jnp.where(inside, part_ref[0], filler)

    owner = ids_ref[0]
    target = widened(
        jnp.where(owner // batch_count == tower, owner % batch_count, batch_count), batch_count
    ).astype(jnp.int32)
    local = widened(rows_ref[0], 0.0).astype(jnp.int32)
    before = ones_at(iota((FIELDS, FIELDS), 1) <= iota((FIELDS, FIELDS), 0))
    ends = dot(before, counts_ref[0].astype(f32).astype(bf16)).astype(jnp.int32)
    field = jnp.zeros((id_rows, samples), jnp.int32)
    for f in range(FIELDS):
        field = field + jnp.where(iota((id_rows, samples), 0) >= ends[f : f + 1], 1, 0)
    bag = iota((id_rows, LANES), 1) * FIELDS + widened(field, 0.0).astype(jnp.int32)

    earlier_rows = ones_at(iota((id_rows, id_rows), 1) < iota((id_rows, id_rows), 0))
    upper = iota((2 * LANES, LANES), 0)
    mixing = ones_at((upper < iota((2 * LANES, LANES), 1)) | (upper >= LANES))
    rank = jnp.zeros((id_rows, LANES), f32)
    for begin in range(0, batch_count, chunk):
        hots = [ones_at(target == begin + d) for d in range(chunk)]
        above = dot(earlier_rows, jnp.concatenate(hots, axis=1)).astype(bf16)
        stacked = jnp.concatenate(
            [
                jnp.concatenate([hots[d], above[:, d * LANES : (d + 1) * LANES]], axis=1)
                for d in range(chunk)
            ],
            axis=0,
        )
        ranks = dot(stacked, mixing)
        for d in range(chunk):
            rank = rank + jnp.where(
                target == begin + d, ranks[d * id_rows : (d + 1) * id_rows], 0.0
            )
    shift = sum(jnp.where(micro == m, slots.shifts[m], 0) for m in range(micro_count))
    slot = rank.astype(jnp.int32) + shift
    place = jnp.where(target < batch_count, (slot // WIDE) * batch_count + target, -1)
    part_ref[0] = place.astype(f32)
    part_ref[1] = (slot % WIDE).astype(f32)
    part_ref[2] = coded(local // 64)
    part_ref[3] = coded((local % 64) * 8 + bag // 512)
    part_ref[4] = coded(bag % 512)
    places = window * batch_count

    def build(t, carry):
        span = pl.ds(pl.multiple_of(t * LANES, LANES), LANES)

        def row(k):
            return part_ref[k, pl.ds(t, 1), :]

        mask = iota((places, LANES), 0).astype(f32) == row(0)
        for v in range(3):
            left_ref[v * places : (v + 1) * places, span] = jnp.where(
                mask, row(2 + v), 0.0
            ).astype(bf16)
        right_ref[:, span] = ones_at(iota((WIDE, LANES), 0).astype(f32) == row(1))
        return carry

    lax.fori_loop(0, id_rows, build, 0, unroll=4)
    placed = dot(left_ref[...], right_ref[...], NT).astype(jnp.int32)

    def part(v, r):
        begin = (v * window + r) * batch_count
        return placed[begin : begin + batch_count]

    for m in range(micro_count):

        @pl.when(micro == m)
        def _():
            for r in range(window):
                at = slots.first_rows[m] + r
                if slots.micro_width(m, at) == 0:
                    continue
                middle = decoded(part(1, r))
                bag = middle % 8 * 512 + decoded(part(2, r))
                valid = part(2, r) != 0
                sample = ((bag.astype(f32) + 0.5) * (1.0 / FIELDS)).astype(jnp.int32)
                field = bag - sample * FIELDS
                late = jnp.where(field >= HALF, 1, 0)
                code = sample + late * LANES + (m * WIDE + 1)
                row = decoded(part(0, r)) * 64 + middle // 8
                req_ref[:, at, :] += jnp.where(valid, row, 0)
                code_ref[:, at, :] += jnp.where(valid, code, 0)
                half_ref[:, at, :] += jnp.where(valid, field - late * HALF, 0)


def in_hbm(x):
    return pltpu.with_memory_space_constraint(x, pltpu.HBM)


def route(ids, rows, counts, weights, slots, batch_count):
    micro_count, id_rows, samples = ids.shape
    places = slots.window * batch_count

    def block(x):
        return pl.BlockSpec((1,) + x.shape[1:], lambda m: (m, 0, 0))

    shapes = [(batch_count, slots.rows + k, WIDE) for k in (1, 0, 0)]
    return pl.pallas_call(
        partial(route_kernel, slots, batch_count),
        grid=(micro_count,),
        in_specs=[block(ids), block(rows), block(counts), pl.BlockSpec(weights.shape, lambda m: (0, 0))],
        out_specs=[pl.BlockSpec(shape, lambda m: (0, 0, 0)) for shape in shapes],
        out_shape=[jax.ShapeDtypeStruct(shape, jnp.int32) for shape in shapes],
        scratch_shapes=[
            pltpu.VMEM((5, id_rows, LANES), jnp.float32),
            pltpu.VMEM((3 * places, id_rows * LANES), jnp.bfloat16),
            pltpu.VMEM((WIDE, id_rows * LANES), jnp.bfloat16),
        ],
        compiler_params=pltpu.CompilerParams(vmem_limit_bytes=vmem_limit(batch_count)),
        name="route",
    )(in_hbm(ids), in_hbm(rows), in_hbm(counts), weights)


def peer_copy(src, dst, send_sem, recv_sem, peer):
    return pltpu.make_async_remote_copy(
        src_ref=src,
        dst_ref=dst,
        send_sem=send_sem,
        recv_sem=recv_sem,
        device_id={"batch": peer},
        device_id_type=pl.DeviceIdType.MESH,
    )


def greet(me, batch_count, other_tower=None):
    barrier = pltpu.get_barrier_semaphore()

    def signal(i, carry):
        pl.semaphore_signal(
            barrier,
            inc=1,
            device_id={"batch": lax.rem(me + i, batch_count)},
            device_id_type=pl.DeviceIdType.MESH,
        )
        return carry

    lax.fori_loop(1, batch_count, signal, 0)
    if other_tower is not None:
        pl.semaphore_signal(
            barrier,
            inc=1,
            device_id={"tower": other_tower},
            device_id_type=pl.DeviceIdType.MESH,
        )


def all_greeted(batch_count, pair):
    pl.semaphore_wait(pltpu.get_barrier_semaphore(), batch_count - 1 + (1 if pair else 0))


def message_rows(rows_msg, columns):
    return -(-(rows_msg * columns + 1) // 16) * 16


def each(count, action):
    def body(i, carry):
        action(i)
        return carry

    lax.fori_loop(1, count, body, 0)


def pick_rows(result, mask, depth, columns):
    width = result.shape[1]
    out = jnp.zeros((16, width), jnp.float32)
    for c in range(columns):
        row = jnp.sum(
            jnp.where(mask, result[c * depth : (c + 1) * depth], 0.0), axis=0, keepdims=True
        )
        out = jnp.where(iota((16, width), 0) == c, row, out)
    return out


def tile_table(table_ref, tiles_ref, stage_ref, columns):
    for c in range(columns):
        for q in range(TALL):
            stage_ref[q : q + 1, :] = table_ref[c : c + 1, q * BROAD : (q + 1) * BROAD]
        tiles_ref[c * TALL : (c + 1) * TALL, :] = stage_ref[...].astype(jnp.bfloat16)


def fetch_kernel(
    slots, windows, columns,
    req_ref, code_ref, half_ref, table_hbm_ref, cin_ref, rest_ref,
    out_ref, served_ref, stat_out_ref, cin_full_ref, rest_full_ref,
    cins_ref, rests_ref, extras_ref, table_ref, tiles_ref, stage_ref, first_ref, second_ref, ans_out_ref, ans_in_ref, left_ref, pooled_ref,
    other_ref,
    req_send, req_recv, ans_send, ans_recv, win_send, win_recv, plane_send,
    plane_recv, ext_send, ext_recv, pair_send, pair_recv, table_sem,
):
    rows_msg = slots.rows
    batch_count = windows.batch_count
    first_extra = windows.first_extra
    me = lax.axis_index("batch")
    tower = lax.axis_index("tower")
    other_tower = 1 - tower
    greet(me, batch_count, other_tower)
    load_table = pltpu.make_async_copy(table_hbm_ref, table_ref, table_sem)
    load_table.start()
    pooled_ref[...] = jnp.zeros_like(pooled_ref)
    first_ref[...] = jnp.zeros_like(first_ref)
    second_ref[...] = jnp.zeros_like(second_ref)

    def request_copy(peer, slot):
        return peer_copy(
            req_ref.at[peer], served_ref.at[slot], req_send.at[peer], req_recv.at[slot], peer
        )

    def answer_copy(peer, slot):
        return peer_copy(
            ans_out_ref.at[peer], ans_in_ref.at[slot], ans_send.at[peer], ans_recv.at[slot], peer
        )

    all_greeted(batch_count, True)

    def send_requests(i, carry):
        peer = lax.rem(me + i, batch_count)
        request_copy(peer, me).start()
        return carry

    lax.fori_loop(1, batch_count, send_requests, 0)

    depth = batch_count // PLANE
    high, low = me // PLANE, lax.rem(me, PLANE)

    def others(action):
        each(batch_count, lambda i: action(lax.rem(me + i, batch_count)))

    def column(action):
        each(depth, lambda i: action(lax.rem(high + i, depth)))

    def plane(action):
        each(PLANE, lambda i: action(lax.rem(low + i, PLANE)))

    def column_copy(src, dst, to, source):
        return peer_copy(
            src, dst.at[low * depth + source], win_send.at[to], win_recv.at[source],
            to * PLANE + low,
        )

    def plane_copy(dst, to, source):
        block = dst.at[pl.ds(source * depth, depth)]
        return peer_copy(
            block, block, plane_send.at[to], plane_recv.at[source], high * PLANE + to
        )

    def extra_copy(peer, slot):
        return peer_copy(rest_ref, extras_ref.at[slot], ext_send.at[peer], ext_recv.at[slot], peer)

    def start_windows(src, dst):
        column(lambda to: column_copy(src, dst, to, high).start())
        dst[low * depth + high] = src[...]

    def pass_windows(src, dst):
        column(lambda source: column_copy(src, dst, source, source).wait_recv())
        plane(lambda to: plane_copy(dst, to, low).start())

    def sent_windows(src, dst):
        column(lambda to: column_copy(src, dst, to, high).wait_send())
        plane(lambda to: plane_copy(dst, to, low).wait_send())

    def split(action):
        @pl.when(tower == 0)
        def _():
            action(cin_ref, cins_ref)

        @pl.when(tower == 1)
        def _():
            action(rest_ref, rests_ref)

    served_ref[me] = req_ref[me]
    load_table.wait()
    tile_table(table_ref, tiles_ref, stage_ref, columns)

    sizes = ans_out_ref.shape[1]

    def look_up(first, second):
        for r in range(rows_msg):
            w = slots.width(r)
            row = jnp.concatenate(
                [served_ref[first, r : r + 1, :w], served_ref[second, r : r + 1, :w]], axis=1
            )
            hot = ones_at(iota((BROAD, 2 * w), 0) == row % BROAD)
            result = dot(tiles_ref[...], hot)
            mask = iota((TALL, 2 * w), 0) == row // BROAD
            block = pick_rows(result, mask, TALL, columns)
            first_ref[r * columns : r * columns + 16, :w] = block[:, :w]
            second_ref[r * columns : r * columns + 16, :w] = block[:, w:]
        ans_out_ref[first] = first_ref[:sizes, :].astype(jnp.bfloat16)
        ans_out_ref[second] = second_ref[:sizes, :].astype(jnp.bfloat16)

    def look_up_one(source):
        half = rows_msg // 2
        for r in range(half + rows_msg % 2):
            both = [r, r + half] if r < half else [rows_msg - 1]
            widths = [slots.width(x) for x in both]
            row = jnp.concatenate(
                [served_ref[source, x : x + 1, :w] for x, w in zip(both, widths)], axis=1
            )
            hot = ones_at(iota((BROAD, row.shape[1]), 0) == row % BROAD)
            result = dot(tiles_ref[...], hot)
            mask = iota((TALL, row.shape[1]), 0) == row // BROAD
            block = pick_rows(result, mask, TALL, columns)
            for at, x, w in zip((0, WIDE), both, widths):
                first_ref[x * columns : (x + 1) * columns, :w] = block[:columns, at : at + w]

    def pool(owner, after=None):
        first_ref[:sizes, :] = ans_in_ref[owner].astype(jnp.float32)
        for r in range(rows_msg):
            w = slots.width(r)
            begin = r * columns
            values = [first_ref[begin + c : begin + c + 1, :w] for c in range(columns)]
            mask = iota((HALF, w), 0) == half_ref[owner, r : r + 1, :w]
            pieces = [jnp.where(mask, values[c], 0.0) for c in range(EMB)]
            pieces.append(jnp.where(iota((8, w), 0) == 0, values[EMB], 0.0))
            left_ref[:, r * WIDE : r * WIDE + w] = jnp.concatenate(pieces, axis=0).astype(
                jnp.bfloat16
            )
        for m in range(slots.micro_count):
            rights = []
            for r in range(slots.first_rows[m], rows_msg):
                w = slots.micro_width(m, r)
                if w:
                    lane = iota((WIDE, w), 0) + (m * WIDE + 1)
                    rights.append(ones_at(lane == code_ref[owner, r : r + 1, :w]))
            begin = slots.first_rows[m] * WIDE
            pooled_ref[m] += dot(
                left_ref[:, begin : begin + slots.spans[m]], jnp.concatenate(rights, axis=1), NT
            )
            if after is not None:
                after(m)

    def pair_copy(src, dst, k):
        return pltpu.make_async_remote_copy(
            src_ref=src,
            dst_ref=dst,
            send_sem=pair_send.at[k],
            recv_sem=pair_recv.at[k],
            device_id={"tower": other_tower},
            device_id_type=pl.DeviceIdType.MESH,
        )

    def swap_windows():
        @pl.when(tower == 0)
        def _():
            plane(lambda source: plane_copy(cins_ref, source, source).wait_recv())
            for e in range(windows.extras):

                @pl.when(me != first_extra + e)
                def _():
                    extra_copy(first_extra + e, e).wait_recv()

            pair_copy(cins_ref, cins_ref, 0).start()
            pair_copy(extras_ref, extras_ref, 1).start()

        @pl.when(tower == 1)
        def _():
            plane(lambda source: plane_copy(rests_ref, source, source).wait_recv())
            pair_copy(rests_ref, rests_ref, 0).start()

    pairs = batch_count // 2
    lag = 2

    last = lax.rem(me + 1, batch_count)

    def step(j, carry):
        @pl.when((j == 0) | (j == pairs))
        def _():
            @pl.when(j == pairs)
            def _():
                request_copy(last, last).wait_recv()

            look_up_one(jnp.where(j == 0, me, last))

            @pl.when(j == 0)
            def _():
                ans_in_ref[me] = first_ref[:sizes, :].astype(jnp.bfloat16)
                split(start_windows)

            @pl.when(j == pairs)
            def _():
                ans_out_ref[last] = first_ref[:sizes, :].astype(jnp.bfloat16)
                answer_copy(last, me).start()

        @pl.when((j == 0) & (tower == 0) & (me >= first_extra))
        def _():
            others(lambda peer: extra_copy(peer, me - first_extra).start())
            extras_ref[me - first_extra] = rest_ref[...]

        @pl.when((j > 0) & (j < pairs))
        def _():
            first = lax.rem(me + batch_count - (2 * j - 1), batch_count)
            second = lax.rem(me + batch_count - 2 * j, batch_count)
            request_copy(first, first).wait_recv()
            request_copy(second, second).wait_recv()
            look_up(first, second)
            answer_copy(first, me).start()
            answer_copy(second, me).start()

        @pl.when(j == 3)
        def _():
            split(pass_windows)

        @pl.when(j == pairs - 2)
        def _():
            swap_windows()

        ready = j - lag

        @pl.when((ready >= 0) & (ready < pairs))
        def _():
            first = lax.rem(me + batch_count + 2 * ready - 1, batch_count)

            @pl.when(ready > 0)
            def _():
                answer_copy(first, first).wait_recv()

            pool(jnp.where(ready == 0, me, first))

        @pl.when((ready > 0) & (ready < pairs))
        def _():
            second = lax.rem(me + 2 * ready, batch_count)
            answer_copy(second, second).wait_recv()
            pool(second)

        return carry

    lax.fori_loop(0, pairs + lag, step, 0)

    def pooled_copy(m):
        return pair_copy(pooled_ref.at[m], other_ref.at[m], 2 + m)

    final = lax.rem(me + batch_count - 1, batch_count)
    answer_copy(final, final).wait_recv()
    pool(final, lambda m: pooled_copy(m).start())

    def finish(i, carry):
        peer = lax.rem(me + i, batch_count)
        request_copy(peer, me).wait_send()
        answer_copy(peer, me).wait_send()
        return carry

    lax.fori_loop(1, batch_count, finish, 0)
    weight_sum = jnp.sum(served_ref[:, rows_msg, :LANES], axis=0, keepdims=True)
    stat_out_ref[...] = jnp.broadcast_to(weight_sum.astype(jnp.float32), stat_out_ref.shape)

    split(sent_windows)

    @pl.when(tower == 0)
    def _():
        @pl.when(me >= first_extra)
        def _():
            others(lambda peer: extra_copy(peer, me - first_extra).wait_send())

        pair_copy(cins_ref, cins_ref, 0).wait_send()
        pair_copy(extras_ref, extras_ref, 1).wait_send()
        pair_copy(rests_ref, rests_ref, 0).wait_recv()

    @pl.when(tower == 1)
    def _():
        pair_copy(rests_ref, rests_ref, 0).wait_send()
        pair_copy(cins_ref, cins_ref, 0).wait_recv()
        pair_copy(extras_ref, extras_ref, 1).wait_recv()

    cin_full_ref[...] = jnp.zeros_like(cin_full_ref)
    for b, at in enumerate(windows.cin_at):
        block = cins_ref[windows.slots[b]].astype(jnp.float32)
        cin_full_ref[at : at + windows.cin_rows, :] += block[: windows.cin_rows]
    rest_full_ref[...] = jnp.zeros_like(rest_full_ref)
    pieces = [(rests_ref, windows.slots[b], at) for b, at in enumerate(windows.rest_at)]
    pieces += [(extras_ref, e, at) for e, at in enumerate(windows.extra_at)]
    for source, b, at in pieces:
        skip = max(0, -at)
        block = source[b].astype(jnp.float32)
        for l in range(HPAD // LANES):
            rest_full_ref[l, at + skip : at + windows.rest_rows, :] += block[
                skip : windows.rest_rows, l * LANES : (l + 1) * LANES
            ]
    for m in range(slots.micro_count):
        pooled_copy(m).wait()
        out_ref[m] = pooled_ref[m] + other_ref[m]


def fetch(
    requests, codes, halves, table, cin_window, rest_window, windows, slots
):
    batch_count, rows_msg, _ = codes.shape
    columns, rows_dev = table.shape
    sizes = message_rows(rows_msg, columns)
    in_vmem = pl.BlockSpec(memory_space=pltpu.VMEM)
    dma = pltpu.SemaphoreType.DMA
    bags = (slots.micro_count, BAG_ROWS, WIDE)
    return pl.pallas_call(
        partial(fetch_kernel, slots, windows, columns),
        in_specs=[in_vmem] * 3 + [pl.BlockSpec(memory_space=pltpu.HBM)] + [in_vmem] * 2,
        out_specs=[in_vmem] * 5,
        out_shape=[
            jax.ShapeDtypeStruct(bags, jnp.float32),
            jax.ShapeDtypeStruct(requests.shape, jnp.int32),
            jax.ShapeDtypeStruct((8, LANES), jnp.float32),
            jax.ShapeDtypeStruct((windows.cin_total, PAIRS), jnp.float32),
            jax.ShapeDtypeStruct((HPAD // LANES, windows.rest_total, LANES), jnp.float32),
        ],
        scratch_shapes=[
            pltpu.VMEM((batch_count,) + cin_window.shape, jnp.bfloat16),
            pltpu.VMEM((batch_count,) + rest_window.shape, jnp.bfloat16),
            pltpu.VMEM((windows.extras,) + rest_window.shape, jnp.bfloat16),
            pltpu.VMEM(table.shape, jnp.float32),
            pltpu.VMEM((columns * TALL, BROAD), jnp.bfloat16),
            pltpu.VMEM((TALL, BROAD), jnp.float32),
            pltpu.VMEM((sizes + 16, WIDE), jnp.float32),
            pltpu.VMEM((sizes + 16, WIDE), jnp.float32),
            pltpu.VMEM((batch_count, sizes, WIDE), jnp.bfloat16),
            pltpu.VMEM((batch_count, sizes, WIDE), jnp.bfloat16),
            pltpu.VMEM((BAG_ROWS, rows_msg * WIDE), jnp.bfloat16),
            pltpu.VMEM(bags, jnp.float32),
            pltpu.VMEM(bags, jnp.float32),
        ]
        + [dma((batch_count,))] * 9
        + [dma((windows.extras,)), dma((2 + slots.micro_count,)), dma((2 + slots.micro_count,)), dma],
        compiler_params=pltpu.CompilerParams(
            vmem_limit_bytes=vmem_limit(batch_count), collective_id=0, has_side_effects=True
        ),
        name="fetch",
    )(requests, codes, halves, in_hbm(table), cin_window, rest_window)


def return_kernel(
    slots, windows, columns,
    grad_ref, code_ref, half_ref, served_ref, stat_ref, cins_ref, rests_ref, extras_ref,
    out_ref, stat_out_ref, cin_ref, rest_ref,
    send_ref, recv_ref, first_ref, second_ref, left_ref, right_ref, total_ref,
    extra_in_ref, cin_near_ref, cin_sum_ref, cin_far_ref, rest_near_ref, rest_sum_ref, rest_far_ref,
    val_send, val_recv, win_send, win_recv, plane_send, plane_recv, ext_send,
    ext_recv,
):
    batch_count = windows.batch_count
    first_extra = windows.first_extra
    tower = lax.axis_index("tower")
    rows_msg = slots.rows
    me = lax.axis_index("batch")
    greet(me, batch_count)

    def value_copy(peer, slot):
        return peer_copy(
            send_ref.at[peer], recv_ref.at[slot], val_send.at[peer], val_recv.at[slot], peer
        )

    def own_copy():
        return pltpu.make_async_copy(send_ref.at[me], recv_ref.at[me], val_recv.at[me])

    depth = batch_count // PLANE
    high, low = me // PLANE, lax.rem(me, PLANE)

    def others(action):
        each(batch_count, lambda i: action(lax.rem(me + i, batch_count)))

    def column(action):
        each(depth, lambda i: action(lax.rem(high + i, depth)))

    def plane(action):
        each(PLANE, lambda i: action(lax.rem(low + i, PLANE)))

    def plane_copy(src, near, to, source):
        return peer_copy(
            src.at[pl.ds(to * depth, depth)], near.at[source], plane_send.at[to],
            plane_recv.at[source], high * PLANE + to,
        )

    def column_copy(total, far, to, source):
        return peer_copy(
            total.at[to], far.at[source], win_send.at[to], win_recv.at[source], to * PLANE + low
        )

    def start_windows(src, near, total, far, out):
        plane(lambda to: plane_copy(src, near, to, low).start())
        near[low] = src[pl.ds(low * depth, depth)]

    def pass_windows(src, near, total, far, out):
        plane(lambda source: plane_copy(src, near, source, source).wait_recv())
        total[...] = jnp.sum(near[...], axis=0)
        column(lambda to: column_copy(total, far, to, high).start())
        far[high] = total[high]

    def end_windows(src, near, total, far, out):
        column(lambda source: column_copy(total, far, source, source).wait_recv())
        out[...] = jnp.sum(far[...], axis=0)
        plane(lambda to: plane_copy(src, near, to, low).wait_send())
        column(lambda to: column_copy(total, far, to, high).wait_send())

    def split(action):
        @pl.when(tower == 0)
        def _():
            action(cins_ref, cin_near_ref, cin_sum_ref, cin_far_ref, cin_ref)

        @pl.when(tower == 1)
        def _():
            action(rests_ref, rest_near_ref, rest_sum_ref, rest_far_ref, rest_ref)

    def extra_copy(peer, slot):
        return peer_copy(
            extras_ref.at[peer - first_extra],
            extra_in_ref.at[slot],
            ext_send.at[peer],
            ext_recv.at[slot],
            peer,
        )

    first_ref[...] = jnp.zeros_like(first_ref)
    second_ref[...] = jnp.zeros_like(second_ref)
    spare = rows_msg * columns
    loss_parts = split_three(stat_ref[0:1, :])
    loss_row = sum(
        jnp.where(iota((1, LANES), 1) == k, part.astype(jnp.float32), 0.0)
        for k, part in enumerate(loss_parts)
    )
    stat_out_ref[...] = jnp.zeros_like(stat_out_ref)
    total_ref[...] = jnp.zeros_like(total_ref)

    sizes = send_ref.shape[1]

    def spread(first, second):
        def both(ref, r, w):
            return jnp.concatenate([ref[first, r : r + 1, :w], ref[second, r : r + 1, :w]], axis=1)

        for r in range(rows_msg):
            w = slots.width(r)
            result = None
            for m in range(slots.micro_count):
                inner = slots.micro_width(m, r)
                if inner == 0:
                    continue
                hot = ones_at(iota((WIDE, 2 * inner), 0) + (m * WIDE + 1) == both(code_ref, r, inner))
                found = dot(grad_ref[m], hot)
                if inner < w:
                    blank = jnp.zeros((BAG_ROWS, w - inner), jnp.float32)
                    found = jnp.concatenate(
                        [found[:, :inner], blank, found[:, inner:], blank], axis=1
                    )
                result = found if result is None else result + found
            mask = iota((HALF, 2 * w), 0) == both(half_ref, r, w)
            block = pick_rows(result, mask, HALF, EMB)
            linear = result[EMB * HALF : EMB * HALF + 1]
            block = jnp.where(iota((16, 2 * w), 0) == EMB, linear, block)
            first_ref[r * columns : r * columns + 16, :w] = block[:, :w]
            second_ref[r * columns : r * columns + 16, :w] = block[:, w:]
        first_ref[spare : spare + 1, :LANES] = loss_row
        second_ref[spare : spare + 1, :LANES] = loss_row
        send_ref[first] = first_ref[:sizes, :].astype(jnp.bfloat16)
        send_ref[second] = second_ref[:sizes, :].astype(jnp.bfloat16)

    def scatter(source):
        first_ref[:sizes, :] = recv_ref[source].astype(jnp.float32)
        stat_out_ref[0:1, :] += first_ref[spare : spare + 1, :LANES]
        for r in range(rows_msg):
            w = slots.width(r)
            span = slice(r * WIDE, r * WIDE + w)
            row = served_ref[source, r : r + 1, :w]
            mask = iota((TALL, w), 0) == row // BROAD
            for c in range(columns):
                left_ref[c * TALL : (c + 1) * TALL, span] = jnp.where(
                    mask, first_ref[r * columns + c : r * columns + c + 1, :w], 0.0
                ).astype(jnp.bfloat16)
            right_ref[:, span] = ones_at(iota((BROAD, w), 0) == row % BROAD)
        total_ref[...] += dot(
            left_ref[:, : slots.length], right_ref[:, : slots.length], NT
        )

    pairs = batch_count // 2
    lag = 2

    def step(j, carry):
        @pl.when(j < pairs)
        def _():
            first = lax.rem(me + 2 * j + 1, batch_count)
            second = lax.rem(me + 2 * j + 2, batch_count)
            spread(first, second)

            @pl.when(j == 0)
            def _():
                all_greeted(batch_count, False)

            value_copy(first, me).start()

            @pl.when(j == 1)
            def _():
                split(start_windows)

            @pl.when((j == 1) & (tower == 0))
            def _():
                for e in range(windows.extras):

                    @pl.when(me != first_extra + e)
                    def _():
                        extra_copy(first_extra + e, me).start()

            @pl.when(j < pairs - 1)
            def _():
                value_copy(second, me).start()

            @pl.when(j == pairs - 1)
            def _():
                own_copy().start()

        @pl.when(j == pairs - 1)
        def _():
            split(pass_windows)

        @pl.when(j >= lag)
        def _():
            first = lax.rem(me + batch_count - (2 * (j - lag) + 1), batch_count)
            value_copy(first, first).wait_recv()
            scatter(first)

        @pl.when((j >= lag) & (j < pairs - 1 + lag))
        def _():
            second = lax.rem(me + 2 * batch_count - (2 * (j - lag) + 2), batch_count)
            value_copy(second, second).wait_recv()
            scatter(second)

        return carry

    lax.fori_loop(0, pairs + lag, step, 0)
    own_copy().wait()
    scatter(me)

    split(end_windows)

    @pl.when(tower == 0)
    def _():
        for e in range(windows.extras):

            @pl.when(me != first_extra + e)
            def _():
                extra_copy(first_extra + e, me).wait_send()

        @pl.when(me >= first_extra)
        def _():
            extra_in_ref[me] = extras_ref[me - first_extra]
            others(lambda peer: extra_copy(me, peer).wait_recv())
            rest_ref[...] = jnp.sum(extra_in_ref[...], axis=0)

        @pl.when(me < first_extra)
        def _():
            rest_ref[...] = jnp.zeros_like(rest_ref)

    @pl.when(tower == 1)
    def _():
        cin_ref[...] = jnp.zeros_like(cin_ref)

    def finish(i, carry):
        peer = lax.rem(me + i, batch_count)
        value_copy(peer, me).wait_send()
        return carry

    lax.fori_loop(1, batch_count, finish, 0)
    losses = jnp.sum(stat_out_ref[0:1, :], axis=1, keepdims=True)
    stat_out_ref[...] = jnp.broadcast_to(losses, stat_out_ref.shape)
    for c in range(columns):
        for q in range(TALL):
            out_ref[c : c + 1, q * BROAD : (q + 1) * BROAD] = total_ref[
                c * TALL + q : c * TALL + q + 1, :
            ]


def return_grads(
    grad_bags, codes, halves, served, stat, cins, rests, extras, windows, slots, columns
):
    batch_count, rows_msg, _ = codes.shape
    long = rows_msg * WIDE
    sizes = message_rows(rows_msg, columns)
    depth = batch_count // PLANE
    in_vmem = pl.BlockSpec(memory_space=pltpu.VMEM)
    dma = pltpu.SemaphoreType.DMA
    return pl.pallas_call(
        partial(return_kernel, slots, windows, columns),
        in_specs=[in_vmem] * 8,
        out_specs=[in_vmem] * 4,
        out_shape=[
            jax.ShapeDtypeStruct((columns, TALL * BROAD), jnp.float32),
            jax.ShapeDtypeStruct(stat.shape, jnp.float32),
            jax.ShapeDtypeStruct(cins.shape[1:], jnp.float32),
            jax.ShapeDtypeStruct(rests.shape[1:], jnp.float32),
        ],
        scratch_shapes=[
            pltpu.VMEM((batch_count, sizes, WIDE), jnp.bfloat16),
            pltpu.VMEM((batch_count, sizes, WIDE), jnp.bfloat16),
            pltpu.VMEM((sizes + 16, WIDE), jnp.float32),
            pltpu.VMEM((sizes + 16, WIDE), jnp.float32),
            pltpu.VMEM((columns * TALL, long), jnp.bfloat16),
            pltpu.VMEM((BROAD, long), jnp.bfloat16),
            pltpu.VMEM((columns * TALL, BROAD), jnp.float32),
            pltpu.VMEM(rests.shape, jnp.float32),
        ]
        + [
            pltpu.VMEM(lead + x.shape[1:], jnp.float32)
            for x in (cins, rests)
            for lead in ((PLANE, depth), (depth,), (depth,))
        ]
        + [dma((batch_count,))] * 8,
        compiler_params=pltpu.CompilerParams(
            vmem_limit_bytes=vmem_limit(batch_count), collective_id=1, has_side_effects=True
        ),
        name="return_grads",
    )(grad_bags, codes, halves, served, stat, cins, rests, extras)


def split_three(x):
    high = x.astype(jnp.bfloat16)
    rest = x - high.astype(jnp.float32)
    middle = rest.astype(jnp.bfloat16)
    low = (rest - middle.astype(jnp.float32)).astype(jnp.bfloat16)
    return high, middle, low


def dense_kernel(
    micro_count, windows, tower_ref, stat_ref, pooled_ref, label_ref, weight_ref,
    cin_ref, rest_ref,
    bags_ref, loss_ref, g_cins_ref, g_rests_ref, g_extras_ref,
    embed_ref, total_ref, pairs_ref, sym_ref, g_cin_ref, g_rest_ref, lane_ref,
):
    f32 = jnp.float32
    bf16 = jnp.bfloat16
    width = micro_count * LANES
    groups = HPAD // LANES

    def rest_rows(begin, count):
        return jnp.concatenate(
            [rest_ref[l, begin : begin + count, :] for l in range(groups)], axis=1
        )[:, :HID]

    cin_w = cin_ref[:MAPS, :].astype(bf16)
    place = iota((MAPS, PAIRS), 0)
    place = place // FIELDS * FPAD + place % FIELDS == iota((MAPS, PAIRS), 1)
    picks_u = ones_at(place)
    row_u = jnp.broadcast_to(cin_ref[MAPS : MAPS + 1, :], (8, PAIRS)).astype(bf16)
    cin_u = dot(picks_u, row_u, NT)[:, :1]
    w_one = jnp.concatenate(
        [
            jnp.concatenate(
                [rest_ref[l, pl.ds(d, FPAD, stride=EMB), :] for l in range(groups)], axis=1
            )[:, :HID]
            for d in range(EMB)
        ],
        axis=0,
    ).astype(bf16)
    w_two = rest_rows(W_TWO, HID).astype(bf16)
    rows = jnp.zeros((8, HID), f32)
    for k, at in enumerate((B_ONE, B_TWO, W_THREE)):
        rows = jnp.where(iota((8, HID), 0) == k, rest_rows(at, 1), rows)
    unit = ones_at(iota((HID, HID), 0) == iota((HID, HID), 1))
    turned = dot(unit, rows.astype(bf16), NT)
    b_one, b_two, w_three = turned[:, 0:1], turned[:, 1:2], turned[:, 2:3]
    bias = rest_ref[0, BIAS : BIAS + 1, 0:1]

    def unpacked(row, count):
        pieces = []
        for m in range(micro_count):
            low = pooled_ref[m, row : row + HALF, :LANES]
            high = pooled_ref[m, row : row + HALF, LANES:]
            pieces.append(jnp.concatenate([low, high], axis=0)[:count])
        return jnp.concatenate(pieces, axis=1)

    for d in range(EMB):
        embed_ref[d * FPAD : (d + 1) * FPAD, :] = unpacked(d * HALF, FPAD)
    linear = jnp.concatenate(
        [
            pooled_ref[m, EMB * HALF : EMB * HALF + 1, :LANES]
            + pooled_ref[m, EMB * HALF : EMB * HALF + 1, LANES:]
            for m in range(micro_count)
        ],
        axis=1,
    )

    def pair_row(i, carry):
        total = jnp.zeros((FPAD, width), f32)
        for d in range(EMB):
            own = embed_ref[pl.ds(d * FPAD + i, 1), :]
            product = (embed_ref[d * FPAD : (d + 1) * FPAD, :] * own).astype(jnp.bfloat16)
            total = total + product.astype(f32)
        total_ref[pl.ds(pl.multiple_of(i * FPAD, 8), FPAD), :] = total
        return carry

    lax.fori_loop(0, FIELDS, pair_row, 0, unroll=3)
    thirds = split_three(total_ref[...])
    map_sum = sum(dot(cin_w, third) for third in thirds)
    cin_logits = jnp.sum(map_sum * cin_u, axis=0, keepdims=True)

    flat = embed_ref[...].astype(jnp.bfloat16)
    pre_one = dot(w_one, flat, TN) + b_one
    hidden_one = jnp.maximum(pre_one, 0.0).astype(jnp.bfloat16)
    pre_two = dot(w_two, hidden_one, TN) + b_two
    active_two = jnp.maximum(pre_two, 0.0)
    deep_logits = jnp.sum(active_two * w_three, axis=0, keepdims=True)
    logits = cin_logits + deep_logits + linear + bias

    samples = weight_ref.shape[1]
    lane_ref[...] = jnp.zeros_like(lane_ref)
    for m in range(micro_count):
        span = slice(m * LANES, m * LANES + samples)
        lane_ref[0:1, span] = weight_ref[m : m + 1, :].astype(f32)
        lane_ref[1:2, span] = label_ref[m : m + 1, :].astype(f32)
    weight = lane_ref[0:1, :]
    label = lane_ref[1:2, :]
    soft = jnp.maximum(logits, 0.0) + jnp.log1p(jnp.exp(-jnp.abs(logits)))
    loss_ref[...] = jnp.broadcast_to(
        jnp.sum(weight * (soft - label * logits), axis=1, keepdims=True), loss_ref.shape
    )
    grad_logits = weight * (jax.nn.sigmoid(logits) - label) / stat_ref[0:1, 0:1]

    grad_maps = (grad_logits * cin_u).astype(jnp.bfloat16)
    grad_two = jnp.where(pre_two > 0, grad_logits * w_three, 0.0).astype(jnp.bfloat16)
    grad_hidden = dot(w_two, grad_two)
    grad_one = jnp.where(pre_one > 0, grad_hidden, 0.0).astype(jnp.bfloat16)
    grad_flat = dot(w_one, grad_one)

    grad_pairs = dot(cin_w, grad_maps, TN)
    for m in range(micro_count):
        pairs_ref[m, :PAIRS, :] = grad_pairs[:, m * LANES : (m + 1) * LANES]
        pairs_ref[m, PAIRS:, :] = jnp.zeros((FPAD * FPAD - PAIRS, LANES), f32)

    def mirror(j, carry):
        here = pl.ds(pl.multiple_of(j * FPAD, 8), FPAD)
        both = [
            pairs_ref[m, here, :] + pairs_ref[m, pl.ds(j, FPAD, stride=FPAD), :]
            for m in range(micro_count)
        ]
        sym_ref[here, :] = jnp.concatenate(both, axis=1)
        return carry

    lax.fori_loop(0, FIELDS, mirror, 0, unroll=3)
    empty = jnp.zeros((2 * HALF - FPAD, width), f32)

    for d in range(EMB):

        def add_row(j, total):
            here = pl.ds(pl.multiple_of(j * FPAD, 8), FPAD)
            return total + sym_ref[here, :] * embed_ref[pl.ds(d * FPAD + j, 1), :]

        grad_embed = lax.fori_loop(
            0, FIELDS, add_row, grad_flat[d * FPAD : (d + 1) * FPAD], unroll=13
        )
        grad_embed = jnp.concatenate([grad_embed, empty], axis=0)
        for m in range(micro_count):
            span = slice(m * LANES, (m + 1) * LANES)
            block = jnp.concatenate([grad_embed[:HALF, span], grad_embed[HALF:, span]], axis=1)
            bags_ref[m, d * HALF : (d + 1) * HALF, :] = block.astype(bf16)
    for m in range(micro_count):
        row = grad_logits[:, m * LANES : (m + 1) * LANES]
        row = jnp.concatenate([row, row], axis=1)
        bags_ref[m, EMB * HALF :, :] = jnp.broadcast_to(row, (8, WIDE)).astype(bf16)

    ones = jnp.ones((8, width), bf16)

    def row_sum(x):
        return sum(dot(ones, third, NT) for third in split_three(x))[:1]

    g_rest_ref[...] = jnp.zeros_like(g_rest_ref)

    def put(begin, count, value, stride=None):
        for l in range(groups):
            piece = value[:, l * LANES : min((l + 1) * LANES, HID)]
            lanes = slice(0, piece.shape[1])
            if stride is None:
                g_rest_ref[l, begin : begin + count, lanes] = piece
            else:
                piece = jnp.pad(piece, ((0, 0), (0, LANES - piece.shape[1])))
                g_rest_ref[l, pl.ds(begin, count, stride=stride), :] = piece

    g_w_one = dot(flat, grad_one, NT)
    for d in range(EMB):
        put(d, FIELDS, g_w_one[d * FPAD : d * FPAD + FIELDS], EMB)

    @pl.when(tower_ref[0] == 0)
    def _():
        g_cin_ref[...] = jnp.zeros_like(g_cin_ref)
        g_cin_ref[:MAPS, :] = sum(dot(grad_maps, third, NT) for third in thirds)
        g_cin_u = jnp.sum(map_sum * grad_logits, axis=1, keepdims=True)
        thirds_u = split_three(jnp.broadcast_to(g_cin_u, (MAPS, 8)))
        g_cin_ref[MAPS : MAPS + 1, :] = sum(dot(third, picks_u, TN) for third in thirds_u)[:1]
        for b, at in enumerate(windows.cin_at):
            g_cins_ref[windows.slots[b], : windows.cin_rows, :] = g_cin_ref[
                at : at + windows.cin_rows, :
            ]
        for e, at in enumerate(windows.extra_at):
            skip = max(0, -at)
            for l in range(groups):
                span = slice(l * LANES, (l + 1) * LANES)
                g_extras_ref[e, skip : windows.rest_rows, span] = g_rest_ref[
                    l, at + skip : at + windows.rest_rows, :
                ]

    @pl.when(tower_ref[0] != 0)
    def _():
        put(W_TWO, HID, dot(hidden_one, grad_two, NT))
        put(B_ONE, 1, dot(ones, grad_one, NT)[:1])
        put(B_TWO, 1, dot(ones, grad_two, NT)[:1])
        put(W_THREE, 1, row_sum(active_two * grad_logits))
        g_bias = jnp.sum(grad_logits, axis=1, keepdims=True)
        put(BIAS, 1, jnp.where(iota((1, HID), 1) == 0, g_bias, 0.0))
        for b, at in enumerate(windows.rest_at):
            for l in range(groups):
                span = slice(l * LANES, (l + 1) * LANES)
                g_rests_ref[windows.slots[b], : windows.rest_rows, span] = g_rest_ref[
                    l, at : at + windows.rest_rows, :
                ]


def dense_step(tower_at, stats, pooled, labels, weights, cin_full, rest_full, windows):
    micro_count = pooled.shape[0]
    width = micro_count * LANES
    in_vmem = pl.BlockSpec(memory_space=pltpu.VMEM)
    in_smem = pl.BlockSpec(memory_space=pltpu.SMEM)
    f32 = jnp.float32
    shapes = [
        ((micro_count, BAG_ROWS, WIDE), jnp.bfloat16),
        ((8, LANES), f32),
        ((windows.batch_count, windows.cin_pad_wide, PAIRS), f32),
        ((windows.batch_count, windows.rest_pad_wide, HPAD), f32),
        ((windows.extras, windows.rest_pad_wide, HPAD), f32),
    ]
    return pl.pallas_call(
        partial(dense_kernel, micro_count, windows),
        in_specs=[in_smem] + [in_vmem] * 6,
        out_specs=[in_vmem] * len(shapes),
        out_shape=[jax.ShapeDtypeStruct(*shape) for shape in shapes],
        scratch_shapes=[
            pltpu.VMEM((EMB * FPAD, width), f32),
            pltpu.VMEM((PAIRS, width), f32),
            pltpu.VMEM((micro_count, FPAD * FPAD, LANES), f32),
            pltpu.VMEM((PAIRS, width), f32),
            pltpu.VMEM((windows.cin_total, PAIRS), f32),
            pltpu.VMEM((HPAD // LANES, windows.rest_total, LANES), f32),
            pltpu.VMEM((8, width), f32),
        ],
        compiler_params=pltpu.CompilerParams(vmem_limit_bytes=vmem_limit(windows.batch_count)),
        name="dense",
    )(tower_at.reshape(1), stats, pooled, labels, weights, cin_full, rest_full)


def shards(
    shard_ids,
    local_rows,
    bag_counts,
    click_labels,
    sample_weights,
    embed_table,
    table_first,
    table_second,
    dense_params,
    dense_first,
    dense_second,
):
    tower_count = lax.axis_size("tower")
    batch_count = lax.axis_size("batch")
    tower_at = lax.axis_index("tower")
    micro_count, samples = shard_ids.shape[:2]
    columns, rows_dev = embed_table.shape
    capacity = 4 * samples * IDS_SAMP // (tower_count * batch_count)
    share = dense_params.shape[0]
    windows = Windows(share, batch_count)
    slots = Slots(micro_count, capacity)

    device = tower_at * batch_count + lax.axis_index("batch")
    cin_phase, rest_phase = windows.phases(device)
    low = dense_params.astype(jnp.bfloat16)

    def window(rows, row_size, phase):
        return lax.dynamic_update_slice(
            jnp.zeros((rows * row_size,), jnp.bfloat16), low, (phase,)
        )

    cin_window = window(windows.cin_rows, SQUARE, cin_phase).reshape(-1, FIELDS, FIELDS)
    cin_window = jnp.pad(
        cin_window,
        ((0, windows.cin_pad - windows.cin_rows), (0, 0), (0, FPAD - FIELDS)),
    ).reshape(windows.cin_pad, PAIRS)
    rest_window = jnp.pad(
        window(windows.rest_rows, HID, rest_phase).reshape(-1, HID),
        ((0, windows.rest_pad - windows.rest_rows), (0, HPAD - HID)),
    )

    def lanes_of(values):
        return jnp.moveaxis(values, 1, -1).reshape(micro_count, -1, samples)

    requests, codes, halves = route(
        lanes_of(shard_ids), lanes_of(local_rows), lanes_of(bag_counts), sample_weights,
        slots, batch_count,
    )
    pooled, served, stats, cin_full, rest_full = fetch(
        requests, codes, halves, embed_table, cin_window, rest_window, windows, slots
    )
    grad_bags, loss, g_cins, g_rests, g_extras = dense_step(
        tower_at, stats, pooled, click_labels, sample_weights, cin_full, rest_full, windows
    )
    table_grad, losses, g_cin, g_rest = return_grads(
        grad_bags, codes, halves, served, loss, g_cins, g_rests, g_extras, windows, slots, columns
    )
    g_cin = g_cin[: windows.cin_rows].reshape(-1, FIELDS, FPAD)[:, :, :FIELDS].reshape(-1)
    g_rest = g_rest[: windows.rest_rows, :HID].reshape(-1)
    is_cin = device * share + jnp.arange(share, dtype=jnp.int32) < CIN_SIZE
    own_grad = jnp.where(
        is_cin,
        lax.dynamic_slice(g_cin, (cin_phase,), (share,)),
        lax.dynamic_slice(g_rest, (rest_phase,), (share,)),
    )

    table_new, table_first_new, table_second_new = adam_update(
        embed_table, table_first, table_second, table_grad, rate_table
    )
    dense_new, dense_first_new, dense_second_new = adam_update(
        dense_params, dense_first, dense_second, own_grad, rate_dense
    )
    loss_sum = losses[0, 0] / stats[0, 0]
    return (
        table_new,
        table_first_new,
        table_second_new,
        table_new.astype(jnp.bfloat16),
        dense_new,
        dense_first_new,
        dense_second_new,
        dense_new.astype(jnp.bfloat16),
        loss_sum,
    )


def solution(mesh):
    rows = P(None, ("tower", "batch"))
    dense = P(("tower", "batch"))
    placed = (
        P(None, "batch", None, None),
        P(None, "batch", None, None),
        P(None, "batch", None),
        P(None, "batch"),
        P(None, "batch"),
        rows,
        rows,
        rows,
        dense,
        dense,
        dense,
    )
    return jax.shard_map(
        shards,
        mesh=mesh,
        in_specs=placed,
        out_specs=(rows, rows, rows, rows, dense, dense, dense, dense, P()),
        check_vma=False,
    )
```

```python
from functools import partial

import jax
import jax.numpy as jnp
from jax import lax
from jax.experimental import pallas as pl
from jax.experimental.pallas import tpu as pltpu
from jax.sharding import PartitionSpec as P

FIELDS = 39
EMB = 10
MAPS = 200
HID = 400
IDS_SAMP = 80

beta_one = 0.9
beta_two = 0.999
epsilon = 1e-08
decay_rate = 0.15
rate_table = 0.1
rate_dense = 0.05
step_count = 10

LANES = 128
WIDE = 256
BROAD = 512
TALL = 64
HALF = 24
BAG_ROWS = EMB * HALF + 8
FPAD = 40
PAIRS = FIELDS * FPAD
PAIRS_PAD = -(-PAIRS // LANES) * LANES
SQUARE = FIELDS * FIELDS
CIN_SIZE = MAPS * SQUARE + MAPS
FLAT = EMB * FIELDS
B_ONE, W_TWO, B_TWO, W_THREE, BIAS = FLAT, FLAT + 1, FLAT + HID + 1, FLAT + HID + 2, FLAT + HID + 3
HPAD = 512
PLANE = 4
NT = (((1,), (1,)), ((), ()))
TN = (((0,), (0,)), ((), ()))
NN = (((1,), (0,)), ((), ()))


def adam_update(weight, first_old, second_old, gradient, step_rate):
    first_new = beta_one * first_old + (1.0 - beta_one) * gradient
    second_new = beta_two * second_old + (1.0 - beta_two) * gradient * gradient
    first_hat = first_new / (1.0 - beta_one**step_count)
    second_hat = second_new / (1.0 - beta_two**step_count)
    weight_new = weight - step_rate * (
        first_hat / (jnp.sqrt(second_hat) + epsilon) + decay_rate * weight
    )
    return (weight_new, first_new, second_new)


def dot(a, b, dims=NN):
    return lax.dot_general(a, b, dims, preferred_element_type=jnp.float32)


def vmem_limit(batch_count):
    return (28 + batch_count // 4) << 20


def iota(shape, dim):
    return lax.broadcasted_iota(jnp.int32, shape, dim)


def ones_at(mask):
    return jnp.where(mask, 1.0, 0.0).astype(jnp.bfloat16)


class Slots:
    def __init__(self, micro_count, capacity):
        self.micro_count = micro_count
        self.first_rows = [m * capacity // WIDE for m in range(micro_count)]
        self.shifts = [m * capacity % WIDE for m in range(micro_count)]
        self.spans = [-(-(shift + capacity) // LANES) * LANES for shift in self.shifts]
        self.length = max(
            first * WIDE + span for first, span in zip(self.first_rows, self.spans)
        )
        self.rows = -(-self.length // WIDE)
        self.window = max(-(-span // WIDE) for span in self.spans)

    def width(self, row):
        return min(WIDE, self.length - row * WIDE)

    def micro_width(self, micro, row):
        inside = row - self.first_rows[micro]
        return max(0, min(WIDE, self.spans[micro] - inside * WIDE)) if inside >= 0 else 0


class Windows:
    def __init__(self, share, batch_count):
        self.share, self.batch_count = share, batch_count
        self.cin_rows = -(-(SQUARE - 1 + share) // SQUARE)
        self.rest_rows = -(-(HID - 1 + share) // HID)
        self.cin_pad = -(-self.cin_rows // 16) * 16
        self.rest_pad = -(-self.rest_rows // 16) * 16
        self.cin_pad_wide = -(-self.cin_rows // 8) * 8
        self.rest_pad_wide = -(-self.rest_rows // 8) * 8
        self.first_extra = CIN_SIZE // share
        self.extras = batch_count - self.first_extra
        self.cin_at = [b * share // SQUARE for b in range(batch_count)]
        self.rest_at = [
            ((batch_count + b) * share - CIN_SIZE) // HID for b in range(batch_count)
        ]
        self.extra_at = [
            (b * share - CIN_SIZE) // HID for b in range(self.first_extra, batch_count)
        ]
        depth = batch_count // PLANE
        self.slots = [b % PLANE * depth + b // PLANE for b in range(batch_count)]
        self.extra_skip = [max(0, -at) for at in self.extra_at]
        longest = max(self.rest_rows - skip for skip in self.extra_skip)
        self.extra_pad_wide = -(-longest // 8) * 8
        self.cin_total = -(-max(a + self.cin_rows for a in self.cin_at) // 8) * 8
        self.rest_total = -(-max(a + self.rest_rows for a in self.rest_at) // 8) * 8

    def phases(self, device):
        start = device * self.share
        return start % SQUARE, jnp.mod(start - CIN_SIZE, HID)


def coded(x):
    return jnp.where(x < 256, x + 1, 255 - x).astype(jnp.float32)


def decoded(x):
    return jnp.where(x > 0, x - 1, 255 - x)


def route_kernel(
    slots, batch_count, ids_ref, rows_ref, counts_ref, weight_ref,
    req_ref, code_ref, half_ref, part_ref, left_ref, right_ref,
):
    f32, bf16 = jnp.float32, jnp.bfloat16
    micro_count, window = slots.micro_count, slots.window
    micro = pl.program_id(0)
    id_rows, samples = ids_ref.shape[1:]
    chunk = 16
    tower = lax.axis_index("tower")

    @pl.when(micro == 0)
    def _():
        req_ref[...] = jnp.zeros_like(req_ref)
        code_ref[...] = jnp.zeros_like(code_ref)
        half_ref[...] = jnp.zeros_like(half_ref)
        part_ref[...] = jnp.zeros_like(part_ref)
        weight_sum = jnp.sum(weight_ref[...].astype(f32)).astype(jnp.int32)
        req_ref[:, slots.rows, :] = jnp.full((batch_count, WIDE), weight_sum)

    def widened(x, filler):
        part_ref[0, :, :samples] = x.astype(f32)
        inside = iota((id_rows, LANES), 1) < samples
        return jnp.where(inside, part_ref[0], filler)

    owner = ids_ref[0]
    target = widened(
        jnp.where(owner // batch_count == tower, owner % batch_count, batch_count), batch_count
    ).astype(jnp.int32)
    local = widened(rows_ref[0], 0.0).astype(jnp.int32)
    before = ones_at(iota((FIELDS, FIELDS), 1) <= iota((FIELDS, FIELDS), 0))
    ends = dot(before, counts_ref[0].astype(f32).astype(bf16)).astype(jnp.int32)
    field = jnp.zeros((id_rows, samples), jnp.int32)
    for f in range(FIELDS):
        field = field + jnp.where(iota((id_rows, samples), 0) >= ends[f : f + 1], 1, 0)
    bag = iota((id_rows, LANES), 1) * FIELDS + widened(field, 0.0).astype(jnp.int32)

    earlier_rows = ones_at(iota((id_rows, id_rows), 1) < iota((id_rows, id_rows), 0))
    upper = iota((2 * LANES, LANES), 0)
    mixing = ones_at((upper < iota((2 * LANES, LANES), 1)) | (upper >= LANES))
    rank = jnp.zeros((id_rows, LANES), f32)
    for begin in range(0, batch_count, chunk):
        hots = [ones_at(target == begin + d) for d in range(chunk)]
        above = dot(earlier_rows, jnp.concatenate(hots, axis=1)).astype(bf16)
        stacked = jnp.concatenate(
            [
                jnp.concatenate([hots[d], above[:, d * LANES : (d + 1) * LANES]], axis=1)
                for d in range(chunk)
            ],
            axis=0,
        )
        ranks = dot(stacked, mixing)
        for d in range(chunk):
            rank = rank + jnp.where(
                target == begin + d, ranks[d * id_rows : (d + 1) * id_rows], 0.0
            )
    shift = sum(jnp.where(micro == m, slots.shifts[m], 0) for m in range(micro_count))
    slot = rank.astype(jnp.int32) + shift
    place = jnp.where(target < batch_count, (slot // WIDE) * batch_count + target, -1)
    part_ref[0] = place.astype(f32)
    part_ref[1] = (slot % WIDE).astype(f32)
    part_ref[2] = coded(local // 64)
    part_ref[3] = coded((local % 64) * 8 + bag // 512)
    part_ref[4] = coded(bag % 512)
    places = window * batch_count

    def build(t, carry):
        span = pl.ds(pl.multiple_of(t * LANES, LANES), LANES)

        def row(k):
            return part_ref[k, pl.ds(t, 1), :]

        mask = iota((places, LANES), 0).astype(f32) == row(0)
        for v in range(3):
            left_ref[v * places : (v + 1) * places, span] = jnp.where(
                mask, row(2 + v), 0.0
            ).astype(bf16)
        right_ref[:, span] = ones_at(iota((WIDE, LANES), 0).astype(f32) == row(1))
        return carry

    lax.fori_loop(0, id_rows, build, 0, unroll=2)
    placed = dot(left_ref[...], right_ref[...], NT).astype(jnp.int32)

    def part(v, r):
        begin = (v * window + r) * batch_count
        return placed[begin : begin + batch_count]

    for m in range(micro_count):

        @pl.when(micro == m)
        def _():
            for r in range(window):
                at = slots.first_rows[m] + r
                if slots.micro_width(m, at) == 0:
                    continue
                middle = decoded(part(1, r))
                bag = middle % 8 * 512 + decoded(part(2, r))
                valid = part(2, r) != 0
                sample = ((bag.astype(f32) + 0.5) * (1.0 / FIELDS)).astype(jnp.int32)
                field = bag - sample * FIELDS
                late = jnp.where(field >= HALF, 1, 0)
                code = sample + late * LANES + (m * WIDE + 1)
                row = decoded(part(0, r)) * 64 + middle // 8
                req_ref[:, at, :] += jnp.where(valid, row, 0)
                code_ref[:, at, :] += jnp.where(valid, code, 0)
                half_ref[:, at, :] += jnp.where(valid, field - late * HALF, 0)


def in_hbm(x):
    return pltpu.with_memory_space_constraint(x, pltpu.HBM)


def route(ids, rows, counts, weights, slots, batch_count):
    micro_count, id_rows, samples = ids.shape
    places = slots.window * batch_count

    def block(x):
        return pl.BlockSpec((1,) + x.shape[1:], lambda m: (m, 0, 0))

    shapes = [(batch_count, slots.rows + k, WIDE) for k in (1, 0, 0)]
    return pl.pallas_call(
        partial(route_kernel, slots, batch_count),
        grid=(micro_count,),
        in_specs=[block(ids), block(rows), block(counts), pl.BlockSpec(weights.shape, lambda m: (0, 0))],
        out_specs=[pl.BlockSpec(shape, lambda m: (0, 0, 0)) for shape in shapes],
        out_shape=[jax.ShapeDtypeStruct(shape, jnp.int32) for shape in shapes],
        scratch_shapes=[
            pltpu.VMEM((5, id_rows, LANES), jnp.float32),
            pltpu.VMEM((3 * places, id_rows * LANES), jnp.bfloat16),
            pltpu.VMEM((WIDE, id_rows * LANES), jnp.bfloat16),
        ],
        compiler_params=pltpu.CompilerParams(vmem_limit_bytes=vmem_limit(batch_count)),
        name="route",
    )(in_hbm(ids), in_hbm(rows), in_hbm(counts), in_hbm(weights))


def peer_copy(src, dst, send_sem, recv_sem, peer):
    return pltpu.make_async_remote_copy(
        src_ref=src,
        dst_ref=dst,
        send_sem=send_sem,
        recv_sem=recv_sem,
        device_id={"batch": peer},
        device_id_type=pl.DeviceIdType.MESH,
    )


def greet(me, batch_count, other_tower=None):
    barrier = pltpu.get_barrier_semaphore()

    def signal(i, carry):
        pl.semaphore_signal(
            barrier,
            inc=1,
            device_id={"batch": lax.rem(me + i, batch_count)},
            device_id_type=pl.DeviceIdType.MESH,
        )
        return carry

    lax.fori_loop(1, batch_count, signal, 0)
    if other_tower is not None:
        pl.semaphore_signal(
            barrier,
            inc=1,
            device_id={"tower": other_tower},
            device_id_type=pl.DeviceIdType.MESH,
        )


def all_greeted(batch_count, pair):
    pl.semaphore_wait(pltpu.get_barrier_semaphore(), batch_count - 1 + (1 if pair else 0))


def message_rows(rows_msg, columns):
    return -(-(rows_msg * columns + 1) // 16) * 16


def each(count, action):
    def body(i, carry):
        action(i)
        return carry

    lax.fori_loop(1, count, body, 0)


def pick_rows(result, mask, depth, columns):
    width = result.shape[1]
    out = jnp.zeros((16, width), jnp.float32)
    for c in range(columns):
        row = jnp.sum(
            jnp.where(mask, result[c * depth : (c + 1) * depth], 0.0), axis=0, keepdims=True
        )
        out = jnp.where(iota((16, width), 0) == c, row, out)
    return out


def tile_table(table_ref, tiles_ref, stage_ref, columns):
    for c in range(columns):
        for q in range(TALL):
            stage_ref[q : q + 1, :] = table_ref[c : c + 1, q * BROAD : (q + 1) * BROAD]
        tiles_ref[c * TALL : (c + 1) * TALL, :] = stage_ref[...].astype(jnp.bfloat16)


def fetch_kernel(
    slots, windows, columns,
    req_ref, code_ref, half_ref, table_hbm_ref, cin_ref, rest_ref,
    out_ref, served_ref, stat_out_ref, cin_full_ref, rest_full_ref,
    cins_ref, rests_ref, extras_ref, table_ref, tiles_ref, stage_ref, first_ref, second_ref, ans_out_ref, ans_in_ref, left_ref, pooled_ref,
    other_ref,
    req_send, req_recv, ans_send, ans_recv, win_send, win_recv, plane_send,
    plane_recv, ext_send, ext_recv, pair_send, pair_recv, table_sem,
):
    rows_msg = slots.rows
    batch_count = windows.batch_count
    first_extra = windows.first_extra
    me = lax.axis_index("batch")
    tower = lax.axis_index("tower")
    other_tower = 1 - tower
    greet(me, batch_count, other_tower)
    load_table = pltpu.make_async_copy(table_hbm_ref, table_ref, table_sem)
    load_table.start()
    pooled_ref[...] = jnp.zeros_like(pooled_ref)
    first_ref[...] = jnp.zeros_like(first_ref)
    second_ref[...] = jnp.zeros_like(second_ref)

    def request_copy(peer, slot):
        return peer_copy(
            req_ref.at[peer], served_ref.at[slot], req_send.at[peer], req_recv.at[slot], peer
        )

    def answer_copy(peer, slot):
        return peer_copy(
            ans_out_ref.at[peer], ans_in_ref.at[slot], ans_send.at[peer], ans_recv.at[slot], peer
        )

    all_greeted(batch_count, True)

    def send_requests(i, carry):
        peer = lax.rem(me + i, batch_count)
        request_copy(peer, me).start()
        return carry

    lax.fori_loop(1, batch_count, send_requests, 0)

    depth = batch_count // PLANE
    high, low = me // PLANE, lax.rem(me, PLANE)

    def others(action):
        each(batch_count, lambda i: action(lax.rem(me + i, batch_count)))

    def column(action):
        each(depth, lambda i: action(lax.rem(high + i, depth)))

    def plane(action):
        each(PLANE, lambda i: action(lax.rem(low + i, PLANE)))

    def column_copy(src, dst, to, source):
        return peer_copy(
            src, dst.at[low * depth + source], win_send.at[to], win_recv.at[source],
            to * PLANE + low,
        )

    def plane_copy(dst, to, source):
        block = dst.at[pl.ds(source * depth, depth)]
        return peer_copy(
            block, block, plane_send.at[to], plane_recv.at[source], high * PLANE + to
        )

    def extra_copy(peer, slot):
        return peer_copy(rest_ref, extras_ref.at[slot], ext_send.at[peer], ext_recv.at[slot], peer)

    def start_windows(src, dst):
        column(lambda to: column_copy(src, dst, to, high).start())
        dst[low * depth + high] = src[...]

    def pass_windows(src, dst):
        column(lambda source: column_copy(src, dst, source, source).wait_recv())
        plane(lambda to: plane_copy(dst, to, low).start())

    def sent_windows(src, dst):
        column(lambda to: column_copy(src, dst, to, high).wait_send())
        plane(lambda to: plane_copy(dst, to, low).wait_send())

    def split(action):
        @pl.when(tower == 0)
        def _():
            action(cin_ref, cins_ref)

        @pl.when(tower == 1)
        def _():
            action(rest_ref, rests_ref)

    served_ref[me] = req_ref[me]
    load_table.wait()
    tile_table(table_ref, tiles_ref, stage_ref, columns)

    sizes = ans_out_ref.shape[1]

    def look_up(first, second):
        for r in range(rows_msg):
            w = slots.width(r)
            row = jnp.concatenate(
                [served_ref[first, r : r + 1, :w], served_ref[second, r : r + 1, :w]], axis=1
            )
            hot = ones_at(iota((BROAD, 2 * w), 0) == row % BROAD)
            result = dot(tiles_ref[...], hot)
            mask = iota((TALL, 2 * w), 0) == row // BROAD
            block = pick_rows(result, mask, TALL, columns)
            first_ref[r * columns : r * columns + 16, :w] = block[:, :w]
            second_ref[r * columns : r * columns + 16, :w] = block[:, w:]
        ans_out_ref[first] = first_ref[:sizes, :].astype(jnp.bfloat16)
        ans_out_ref[second] = second_ref[:sizes, :].astype(jnp.bfloat16)

    def look_up_one(source):
        half = rows_msg // 2
        for r in range(half + rows_msg % 2):
            both = [r, r + half] if r < half else [rows_msg - 1]
            widths = [slots.width(x) for x in both]
            row = jnp.concatenate(
                [served_ref[source, x : x + 1, :w] for x, w in zip(both, widths)], axis=1
            )
            hot = ones_at(iota((BROAD, row.shape[1]), 0) == row % BROAD)
            result = dot(tiles_ref[...], hot)
            mask = iota((TALL, row.shape[1]), 0) == row // BROAD
            block = pick_rows(result, mask, TALL, columns)
            for at, x, w in zip((0, WIDE), both, widths):
                first_ref[x * columns : (x + 1) * columns, :w] = block[:columns, at : at + w]

    def pool(owner, after=None):
        first_ref[:sizes, :] = ans_in_ref[owner].astype(jnp.float32)
        for r in range(rows_msg):
            w = slots.width(r)
            begin = r * columns
            values = [first_ref[begin + c : begin + c + 1, :w] for c in range(columns)]
            mask = iota((HALF, w), 0) == half_ref[owner, r : r + 1, :w]
            pieces = [jnp.where(mask, values[c], 0.0) for c in range(EMB)]
            pieces.append(jnp.where(iota((8, w), 0) == 0, values[EMB], 0.0))
            left_ref[:, r * WIDE : r * WIDE + w] = jnp.concatenate(pieces, axis=0).astype(
                jnp.bfloat16
            )
        for m in range(slots.micro_count):
            rights = []
            for r in range(slots.first_rows[m], rows_msg):
                w = slots.micro_width(m, r)
                if w:
                    lane = iota((WIDE, w), 0) + (m * WIDE + 1)
                    rights.append(ones_at(lane == code_ref[owner, r : r + 1, :w]))
            begin = slots.first_rows[m] * WIDE
            pooled_ref[m] += dot(
                left_ref[:, begin : begin + slots.spans[m]], jnp.concatenate(rights, axis=1), NT
            )
            if after is not None:
                after(m)

    def pair_copy(src, dst, k):
        return pltpu.make_async_remote_copy(
            src_ref=src,
            dst_ref=dst,
            send_sem=pair_send.at[k],
            recv_sem=pair_recv.at[k],
            device_id={"tower": other_tower},
            device_id_type=pl.DeviceIdType.MESH,
        )

    def swap_windows():
        @pl.when(tower == 0)
        def _():
            plane(lambda source: plane_copy(cins_ref, source, source).wait_recv())
            for e in range(windows.extras):

                @pl.when(me != first_extra + e)
                def _():
                    extra_copy(first_extra + e, e).wait_recv()

            pair_copy(cins_ref, cins_ref, 0).start()
            pair_copy(extras_ref, extras_ref, 1).start()

        @pl.when(tower == 1)
        def _():
            plane(lambda source: plane_copy(rests_ref, source, source).wait_recv())
            pair_copy(rests_ref, rests_ref, 0).start()

    pairs = batch_count // 2
    lag = 2

    last = lax.rem(me + 1, batch_count)

    def step(j, carry):
        @pl.when((j == 0) | (j == pairs))
        def _():
            @pl.when(j == pairs)
            def _():
                request_copy(last, last).wait_recv()

            look_up_one(jnp.where(j == 0, me, last))

            @pl.when(j == 0)
            def _():
                ans_in_ref[me] = first_ref[:sizes, :].astype(jnp.bfloat16)
                split(start_windows)

            @pl.when(j == pairs)
            def _():
                ans_out_ref[last] = first_ref[:sizes, :].astype(jnp.bfloat16)
                answer_copy(last, me).start()

        @pl.when((j == 0) & (tower == 0) & (me >= first_extra))
        def _():
            others(lambda peer: extra_copy(peer, me - first_extra).start())
            extras_ref[me - first_extra] = rest_ref[...]

        @pl.when((j > 0) & (j < pairs))
        def _():
            first = lax.rem(me + batch_count - (2 * j - 1), batch_count)
            second = lax.rem(me + batch_count - 2 * j, batch_count)
            request_copy(first, first).wait_recv()
            request_copy(second, second).wait_recv()
            look_up(first, second)
            answer_copy(first, me).start()
            answer_copy(second, me).start()

        @pl.when(j == 3)
        def _():
            split(pass_windows)

        @pl.when(j == pairs - 2)
        def _():
            swap_windows()

        ready = j - lag

        @pl.when((ready >= 0) & (ready < pairs))
        def _():
            first = lax.rem(me + batch_count + 2 * ready - 1, batch_count)

            @pl.when(ready > 0)
            def _():
                answer_copy(first, first).wait_recv()

            pool(jnp.where(ready == 0, me, first))

        @pl.when((ready > 0) & (ready < pairs))
        def _():
            second = lax.rem(me + 2 * ready, batch_count)
            answer_copy(second, second).wait_recv()
            pool(second)

        return carry

    lax.fori_loop(0, pairs + lag, step, 0)

    def pooled_copy(m):
        return pair_copy(pooled_ref.at[m], other_ref.at[m], 2 + m)

    final = lax.rem(me + batch_count - 1, batch_count)
    answer_copy(final, final).wait_recv()
    pool(final, lambda m: pooled_copy(m).start())

    def finish(i, carry):
        peer = lax.rem(me + i, batch_count)
        request_copy(peer, me).wait_send()
        answer_copy(peer, me).wait_send()
        return carry

    lax.fori_loop(1, batch_count, finish, 0)
    weight_sum = jnp.sum(served_ref[:, rows_msg, :LANES], axis=0, keepdims=True)
    stat_out_ref[...] = jnp.broadcast_to(weight_sum.astype(jnp.float32), stat_out_ref.shape)

    split(sent_windows)

    @pl.when(tower == 0)
    def _():
        @pl.when(me >= first_extra)
        def _():
            others(lambda peer: extra_copy(peer, me - first_extra).wait_send())

        pair_copy(cins_ref, cins_ref, 0).wait_send()
        pair_copy(extras_ref, extras_ref, 1).wait_send()
        pair_copy(rests_ref, rests_ref, 0).wait_recv()

    @pl.when(tower == 1)
    def _():
        pair_copy(rests_ref, rests_ref, 0).wait_send()
        pair_copy(cins_ref, cins_ref, 0).wait_recv()
        pair_copy(extras_ref, extras_ref, 1).wait_recv()

    cin_full_ref[...] = jnp.zeros_like(cin_full_ref)
    for b, at in enumerate(windows.cin_at):
        block = cins_ref[windows.slots[b]].astype(jnp.float32)
        cin_full_ref[at : at + windows.cin_rows, :] += block[: windows.cin_rows, :PAIRS]
    rest_full_ref[...] = jnp.zeros_like(rest_full_ref)
    pieces = [(rests_ref, windows.slots[b], at) for b, at in enumerate(windows.rest_at)]
    pieces += [(extras_ref, e, at) for e, at in enumerate(windows.extra_at)]
    for source, b, at in pieces:
        skip = max(0, -at)
        block = source[b].astype(jnp.float32)
        for l in range(HPAD // LANES):
            rest_full_ref[l, at + skip : at + windows.rest_rows, :] += block[
                skip : windows.rest_rows, l * LANES : (l + 1) * LANES
            ]
    for m in range(slots.micro_count):
        pooled_copy(m).wait()
        out_ref[m] = pooled_ref[m] + other_ref[m]


def fetch(
    requests, codes, halves, table, cin_window, rest_window, windows, slots
):
    batch_count, rows_msg, _ = codes.shape
    columns, rows_dev = table.shape
    sizes = message_rows(rows_msg, columns)
    in_vmem = pl.BlockSpec(memory_space=pltpu.VMEM)
    dma = pltpu.SemaphoreType.DMA
    bags = (slots.micro_count, BAG_ROWS, WIDE)
    return pl.pallas_call(
        partial(fetch_kernel, slots, windows, columns),
        in_specs=[in_vmem] * 3 + [pl.BlockSpec(memory_space=pltpu.HBM)] + [in_vmem] * 2,
        out_specs=[in_vmem] * 5,
        out_shape=[
            jax.ShapeDtypeStruct(bags, jnp.float32),
            jax.ShapeDtypeStruct(requests.shape, jnp.int32),
            jax.ShapeDtypeStruct((8, LANES), jnp.float32),
            jax.ShapeDtypeStruct((windows.cin_total, PAIRS), jnp.float32),
            jax.ShapeDtypeStruct((HPAD // LANES, windows.rest_total, LANES), jnp.float32),
        ],
        scratch_shapes=[
            pltpu.VMEM((batch_count,) + cin_window.shape, jnp.bfloat16),
            pltpu.VMEM((batch_count,) + rest_window.shape, jnp.bfloat16),
            pltpu.VMEM((windows.extras,) + rest_window.shape, jnp.bfloat16),
            pltpu.VMEM(table.shape, jnp.float32),
            pltpu.VMEM((columns * TALL, BROAD), jnp.bfloat16),
            pltpu.VMEM((TALL, BROAD), jnp.float32),
            pltpu.VMEM((sizes + 16, WIDE), jnp.float32),
            pltpu.VMEM((sizes + 16, WIDE), jnp.float32),
            pltpu.VMEM((batch_count, sizes, WIDE), jnp.bfloat16),
            pltpu.VMEM((batch_count, sizes, WIDE), jnp.bfloat16),
            pltpu.VMEM((BAG_ROWS, rows_msg * WIDE), jnp.bfloat16),
            pltpu.VMEM(bags, jnp.float32),
            pltpu.VMEM(bags, jnp.float32),
        ]
        + [dma((batch_count,))] * 9
        + [dma((windows.extras,)), dma((2 + slots.micro_count,)), dma((2 + slots.micro_count,)), dma],
        compiler_params=pltpu.CompilerParams(
            vmem_limit_bytes=vmem_limit(batch_count), collective_id=0, has_side_effects=True
        ),
        name="fetch",
    )(requests, codes, halves, in_hbm(table), cin_window, rest_window)


def return_kernel(
    slots, windows, columns,
    grad_ref, code_ref, half_ref, served_ref, stat_ref, cins_ref, rests_ref, extras_ref,
    out_ref, stat_out_ref, cin_ref, rest_ref,
    send_ref, recv_ref, first_ref, second_ref, left_ref, right_ref, total_ref,
    extra_in_ref, cin_near_ref, cin_sum_ref, cin_far_ref, rest_near_ref, rest_sum_ref, rest_far_ref,
    val_send, val_recv, win_send, win_recv, plane_send, plane_recv, ext_send,
    ext_recv,
):
    batch_count = windows.batch_count
    first_extra = windows.first_extra
    tower = lax.axis_index("tower")
    rows_msg = slots.rows
    me = lax.axis_index("batch")
    greet(me, batch_count)

    def value_copy(peer, slot):
        return peer_copy(
            send_ref.at[peer], recv_ref.at[slot], val_send.at[peer], val_recv.at[slot], peer
        )

    def own_copy():
        return pltpu.make_async_copy(send_ref.at[me], recv_ref.at[me], val_recv.at[me])

    depth = batch_count // PLANE
    high, low = me // PLANE, lax.rem(me, PLANE)

    def others(action):
        each(batch_count, lambda i: action(lax.rem(me + i, batch_count)))

    def column(action):
        each(depth, lambda i: action(lax.rem(high + i, depth)))

    def plane(action):
        each(PLANE, lambda i: action(lax.rem(low + i, PLANE)))

    def plane_copy(src, near, to, source):
        return peer_copy(
            src.at[pl.ds(to * depth, depth)], near.at[source], plane_send.at[to],
            plane_recv.at[source], high * PLANE + to,
        )

    def column_copy(total, far, to, source):
        return peer_copy(
            total.at[to], far.at[source], win_send.at[to], win_recv.at[source], to * PLANE + low
        )

    def start_windows(src, near, total, far, out):
        plane(lambda to: plane_copy(src, near, to, low).start())
        near[low] = src[pl.ds(low * depth, depth)]

    def pass_windows(src, near, total, far, out):
        plane(lambda source: plane_copy(src, near, source, source).wait_recv())
        total[...] = jnp.sum(near[...], axis=0)
        column(lambda to: column_copy(total, far, to, high).start())
        far[high] = total[high]

    def end_windows(src, near, total, far, out):
        column(lambda source: column_copy(total, far, source, source).wait_recv())
        out[...] = jnp.sum(far[...], axis=0)
        plane(lambda to: plane_copy(src, near, to, low).wait_send())
        column(lambda to: column_copy(total, far, to, high).wait_send())

    def split(action):
        @pl.when(tower == 0)
        def _():
            action(cins_ref, cin_near_ref, cin_sum_ref, cin_far_ref, cin_ref)

        @pl.when(tower == 1)
        def _():
            action(rests_ref, rest_near_ref, rest_sum_ref, rest_far_ref, rest_ref)

    def extra_copy(peer, slot):
        return peer_copy(
            extras_ref.at[peer - first_extra],
            extra_in_ref.at[slot],
            ext_send.at[peer],
            ext_recv.at[slot],
            peer,
        )

    first_ref[...] = jnp.zeros_like(first_ref)
    second_ref[...] = jnp.zeros_like(second_ref)
    spare = rows_msg * columns
    loss_parts = split_three(stat_ref[0:1, :])
    loss_row = sum(
        jnp.where(iota((1, LANES), 1) == k, part.astype(jnp.float32), 0.0)
        for k, part in enumerate(loss_parts)
    )
    stat_out_ref[...] = jnp.zeros_like(stat_out_ref)
    total_ref[...] = jnp.zeros_like(total_ref)

    sizes = send_ref.shape[1]

    def spread(first, second):
        def both(ref, r, w):
            return jnp.concatenate([ref[first, r : r + 1, :w], ref[second, r : r + 1, :w]], axis=1)

        for r in range(rows_msg):
            w = slots.width(r)
            result = None
            for m in range(slots.micro_count):
                inner = slots.micro_width(m, r)
                if inner == 0:
                    continue
                hot = ones_at(iota((WIDE, 2 * inner), 0) + (m * WIDE + 1) == both(code_ref, r, inner))
                found = dot(grad_ref[m], hot)
                if inner < w:
                    blank = jnp.zeros((BAG_ROWS, w - inner), jnp.float32)
                    found = jnp.concatenate(
                        [found[:, :inner], blank, found[:, inner:], blank], axis=1
                    )
                result = found if result is None else result + found
            mask = iota((HALF, 2 * w), 0) == both(half_ref, r, w)
            block = pick_rows(result, mask, HALF, EMB)
            linear = result[EMB * HALF : EMB * HALF + 1]
            block = jnp.where(iota((16, 2 * w), 0) == EMB, linear, block)
            first_ref[r * columns : r * columns + 16, :w] = block[:, :w]
            second_ref[r * columns : r * columns + 16, :w] = block[:, w:]
        first_ref[spare : spare + 1, :LANES] = loss_row
        second_ref[spare : spare + 1, :LANES] = loss_row
        send_ref[first] = first_ref[:sizes, :].astype(jnp.bfloat16)
        send_ref[second] = second_ref[:sizes, :].astype(jnp.bfloat16)

    def scatter(source):
        first_ref[:sizes, :] = recv_ref[source].astype(jnp.float32)
        stat_out_ref[0:1, :] += first_ref[spare : spare + 1, :LANES]
        for r in range(rows_msg):
            w = slots.width(r)
            span = slice(r * WIDE, r * WIDE + w)
            row = served_ref[source, r : r + 1, :w]
            mask = iota((TALL, w), 0) == row // BROAD
            for c in range(columns):
                left_ref[c * TALL : (c + 1) * TALL, span] = jnp.where(
                    mask, first_ref[r * columns + c : r * columns + c + 1, :w], 0.0
                ).astype(jnp.bfloat16)
            right_ref[:, span] = ones_at(iota((BROAD, w), 0) == row % BROAD)
        total_ref[...] += dot(
            left_ref[:, : slots.length], right_ref[:, : slots.length], NT
        )

    pairs = batch_count // 2
    lag = 2

    def step(j, carry):
        @pl.when(j < pairs)
        def _():
            first = lax.rem(me + 2 * j + 1, batch_count)
            second = lax.rem(me + 2 * j + 2, batch_count)
            spread(first, second)

            @pl.when(j == 0)
            def _():
                all_greeted(batch_count, False)

            value_copy(first, me).start()

            @pl.when(j == 1)
            def _():
                split(start_windows)

            @pl.when((j == 3) & (tower == 0))
            def _():
                for e in range(windows.extras):

                    @pl.when(me != first_extra + e)
                    def _():
                        extra_copy(first_extra + e, me).start()

            @pl.when(j < pairs - 1)
            def _():
                value_copy(second, me).start()

            @pl.when(j == pairs - 1)
            def _():
                own_copy().start()

        @pl.when(j == pairs - 1)
        def _():
            split(pass_windows)

        @pl.when(j >= lag)
        def _():
            first = lax.rem(me + batch_count - (2 * (j - lag) + 1), batch_count)
            value_copy(first, first).wait_recv()
            scatter(first)

        @pl.when((j >= lag) & (j < pairs - 1 + lag))
        def _():
            second = lax.rem(me + 2 * batch_count - (2 * (j - lag) + 2), batch_count)
            value_copy(second, second).wait_recv()
            scatter(second)

        return carry

    lax.fori_loop(0, pairs + lag, step, 0)
    own_copy().wait()
    scatter(me)

    split(end_windows)

    @pl.when(tower == 0)
    def _():
        rest_ref[...] = jnp.zeros_like(rest_ref)
        for e in range(windows.extras):

            @pl.when(me != first_extra + e)
            def _():
                extra_copy(first_extra + e, me).wait_send()

        @pl.when(me >= first_extra)
        def _():
            extra_in_ref[me] = extras_ref[me - first_extra]
            others(lambda peer: extra_copy(me, peer).wait_recv())
            total = jnp.sum(extra_in_ref[...], axis=0)
            for e, skip in enumerate(windows.extra_skip):

                @pl.when(me == first_extra + e)
                def _():
                    rest_ref[skip : windows.rest_rows, :] = total[: windows.rest_rows - skip]

    @pl.when(tower == 1)
    def _():
        cin_ref[...] = jnp.zeros_like(cin_ref)

    def finish(i, carry):
        peer = lax.rem(me + i, batch_count)
        value_copy(peer, me).wait_send()
        return carry

    lax.fori_loop(1, batch_count, finish, 0)
    losses = jnp.sum(stat_out_ref[0:1, :], axis=1, keepdims=True)
    stat_out_ref[...] = jnp.broadcast_to(losses, stat_out_ref.shape)
    for c in range(columns):
        for q in range(TALL):
            out_ref[c : c + 1, q * BROAD : (q + 1) * BROAD] = total_ref[
                c * TALL + q : c * TALL + q + 1, :
            ]


def return_grads(
    grad_bags, codes, halves, served, stat, cins, rests, extras, windows, slots, columns
):
    batch_count, rows_msg, _ = codes.shape
    long = rows_msg * WIDE
    sizes = message_rows(rows_msg, columns)
    depth = batch_count // PLANE
    in_vmem = pl.BlockSpec(memory_space=pltpu.VMEM)
    dma = pltpu.SemaphoreType.DMA
    return pl.pallas_call(
        partial(return_kernel, slots, windows, columns),
        in_specs=[in_vmem] * 8,
        out_specs=[in_vmem] * 4,
        out_shape=[
            jax.ShapeDtypeStruct((columns, TALL * BROAD), jnp.float32),
            jax.ShapeDtypeStruct(stat.shape, jnp.float32),
            jax.ShapeDtypeStruct(cins.shape[1:], jnp.float32),
            jax.ShapeDtypeStruct(rests.shape[1:], jnp.float32),
        ],
        scratch_shapes=[
            pltpu.VMEM((batch_count, sizes, WIDE), jnp.bfloat16),
            pltpu.VMEM((batch_count, sizes, WIDE), jnp.bfloat16),
            pltpu.VMEM((sizes + 16, WIDE), jnp.float32),
            pltpu.VMEM((sizes + 16, WIDE), jnp.float32),
            pltpu.VMEM((columns * TALL, long), jnp.bfloat16),
            pltpu.VMEM((BROAD, long), jnp.bfloat16),
            pltpu.VMEM((columns * TALL, BROAD), jnp.float32),
            pltpu.VMEM((batch_count,) + extras.shape[1:], jnp.float32),
        ]
        + [
            pltpu.VMEM(lead + x.shape[1:], jnp.float32)
            for x in (cins, rests)
            for lead in ((PLANE, depth), (depth,), (depth,))
        ]
        + [dma((batch_count,))] * 8,
        compiler_params=pltpu.CompilerParams(
            vmem_limit_bytes=vmem_limit(batch_count), collective_id=1, has_side_effects=True
        ),
        name="return_grads",
    )(grad_bags, codes, halves, served, stat, cins, rests, extras)


def split_three(x):
    high = x.astype(jnp.bfloat16)
    rest = x - high.astype(jnp.float32)
    middle = rest.astype(jnp.bfloat16)
    low = (rest - middle.astype(jnp.float32)).astype(jnp.bfloat16)
    return high, middle, low


def dense_kernel(
    micro_count, windows, tower_ref, stat_ref, pooled_ref, label_ref, weight_ref,
    cin_ref, rest_ref,
    bags_ref, loss_ref, g_cins_ref, g_rests_ref, g_extras_ref,
    embed_ref, total_ref, pairs_ref, sym_ref, g_cin_ref, g_rest_ref, lane_ref,
):
    f32 = jnp.float32
    bf16 = jnp.bfloat16
    width = micro_count * LANES
    groups = HPAD // LANES

    def rest_rows(begin, count):
        return jnp.concatenate(
            [rest_ref[l, begin : begin + count, :] for l in range(groups)], axis=1
        )[:, :HID]

    cin_w = cin_ref[:MAPS, :].astype(bf16)
    place = iota((MAPS, PAIRS), 0)
    place = place // FIELDS * FPAD + place % FIELDS == iota((MAPS, PAIRS), 1)
    picks_u = ones_at(place)
    row_u = jnp.broadcast_to(cin_ref[MAPS : MAPS + 1, :], (8, PAIRS)).astype(bf16)
    cin_u = dot(picks_u, row_u, NT)[:, :1]
    w_one = jnp.concatenate(
        [
            jnp.concatenate(
                [rest_ref[l, pl.ds(d, FPAD, stride=EMB), :] for l in range(groups)], axis=1
            )[:, :HID]
            for d in range(EMB)
        ],
        axis=0,
    ).astype(bf16)
    w_two = rest_rows(W_TWO, HID).astype(bf16)
    rows = jnp.zeros((8, HID), f32)
    for k, at in enumerate((B_ONE, B_TWO, W_THREE)):
        rows = jnp.where(iota((8, HID), 0) == k, rest_rows(at, 1), rows)
    unit = ones_at(iota((HID, HID), 0) == iota((HID, HID), 1))
    turned = dot(unit, rows.astype(bf16), NT)
    b_one, b_two, w_three = turned[:, 0:1], turned[:, 1:2], turned[:, 2:3]
    bias = rest_ref[0, BIAS : BIAS + 1, 0:1]

    def unpacked(row, count):
        pieces = []
        for m in range(micro_count):
            low = pooled_ref[m, row : row + HALF, :LANES]
            high = pooled_ref[m, row : row + HALF, LANES:]
            pieces.append(jnp.concatenate([low, high], axis=0)[:count])
        return jnp.concatenate(pieces, axis=1)

    for d in range(EMB):
        embed_ref[d * FPAD : (d + 1) * FPAD, :] = unpacked(d * HALF, FPAD)
    linear = jnp.concatenate(
        [
            pooled_ref[m, EMB * HALF : EMB * HALF + 1, :LANES]
            + pooled_ref[m, EMB * HALF : EMB * HALF + 1, LANES:]
            for m in range(micro_count)
        ],
        axis=1,
    )

    def pair_row(i, carry):
        total = jnp.zeros((FPAD, width), f32)
        for d in range(EMB):
            own = embed_ref[pl.ds(d * FPAD + i, 1), :]
            product = (embed_ref[d * FPAD : (d + 1) * FPAD, :] * own).astype(jnp.bfloat16)
            total = total + product.astype(f32)
        total_ref[pl.ds(pl.multiple_of(i * FPAD, 8), FPAD), :] = total
        return carry

    lax.fori_loop(0, FIELDS, pair_row, 0, unroll=3)
    thirds = split_three(total_ref[...])
    map_sum = sum(dot(cin_w, third) for third in thirds)
    cin_logits = jnp.sum(map_sum * cin_u, axis=0, keepdims=True)

    flat = embed_ref[...].astype(jnp.bfloat16)
    pre_one = dot(w_one, flat, TN) + b_one
    hidden_one = jnp.maximum(pre_one, 0.0).astype(jnp.bfloat16)
    pre_two = dot(w_two, hidden_one, TN) + b_two
    active_two = jnp.maximum(pre_two, 0.0)
    deep_logits = jnp.sum(active_two * w_three, axis=0, keepdims=True)
    logits = cin_logits + deep_logits + linear + bias

    samples = weight_ref.shape[1]
    lane_ref[...] = jnp.zeros_like(lane_ref)
    for m in range(micro_count):
        span = slice(m * LANES, m * LANES + samples)
        lane_ref[0:1, span] = weight_ref[m : m + 1, :].astype(f32)
        lane_ref[1:2, span] = label_ref[m : m + 1, :].astype(f32)
    weight = lane_ref[0:1, :]
    label = lane_ref[1:2, :]
    soft = jnp.maximum(logits, 0.0) + jnp.log1p(jnp.exp(-jnp.abs(logits)))
    loss_ref[...] = jnp.broadcast_to(
        jnp.sum(weight * (soft - label * logits), axis=1, keepdims=True), loss_ref.shape
    )
    grad_logits = weight * (jax.nn.sigmoid(logits) - label) / stat_ref[0:1, 0:1]

    grad_maps = (grad_logits * cin_u).astype(jnp.bfloat16)
    grad_two = jnp.where(pre_two > 0, grad_logits * w_three, 0.0).astype(jnp.bfloat16)
    grad_hidden = dot(w_two, grad_two)
    grad_one = jnp.where(pre_one > 0, grad_hidden, 0.0).astype(jnp.bfloat16)
    grad_flat = dot(w_one, grad_one)

    grad_pairs = dot(cin_w, grad_maps, TN)
    for m in range(micro_count):
        pairs_ref[m, :PAIRS, :] = grad_pairs[:, m * LANES : (m + 1) * LANES]
        pairs_ref[m, PAIRS:, :] = jnp.zeros((FPAD * FPAD - PAIRS, LANES), f32)

    def mirror(j, carry):
        here = pl.ds(pl.multiple_of(j * FPAD, 8), FPAD)
        both = [
            pairs_ref[m, here, :] + pairs_ref[m, pl.ds(j, FPAD, stride=FPAD), :]
            for m in range(micro_count)
        ]
        sym_ref[here, :] = jnp.concatenate(both, axis=1)
        return carry

    lax.fori_loop(0, FIELDS, mirror, 0, unroll=3)
    empty = jnp.zeros((2 * HALF - FPAD, width), f32)

    for d in range(EMB):

        def add_row(j, total):
            here = pl.ds(pl.multiple_of(j * FPAD, 8), FPAD)
            return total + sym_ref[here, :] * embed_ref[pl.ds(d * FPAD + j, 1), :]

        grad_embed = lax.fori_loop(
            0, FIELDS, add_row, grad_flat[d * FPAD : (d + 1) * FPAD], unroll=39
        )
        grad_embed = jnp.concatenate([grad_embed, empty], axis=0)
        for m in range(micro_count):
            span = slice(m * LANES, (m + 1) * LANES)
            block = jnp.concatenate([grad_embed[:HALF, span], grad_embed[HALF:, span]], axis=1)
            bags_ref[m, d * HALF : (d + 1) * HALF, :] = block.astype(bf16)
    for m in range(micro_count):
        row = grad_logits[:, m * LANES : (m + 1) * LANES]
        row = jnp.concatenate([row, row], axis=1)
        bags_ref[m, EMB * HALF :, :] = jnp.broadcast_to(row, (8, WIDE)).astype(bf16)

    ones = jnp.ones((8, width), bf16)

    def row_sum(x):
        return sum(dot(ones, third, NT) for third in split_three(x))[:1]

    g_rest_ref[...] = jnp.zeros_like(g_rest_ref)

    def put(begin, count, value, stride=None):
        for l in range(groups):
            piece = value[:, l * LANES : min((l + 1) * LANES, HID)]
            lanes = slice(0, piece.shape[1])
            if stride is None:
                g_rest_ref[l, begin : begin + count, lanes] = piece
            else:
                piece = jnp.pad(piece, ((0, 0), (0, LANES - piece.shape[1])))
                g_rest_ref[l, pl.ds(begin, count, stride=stride), :] = piece

    g_w_one = dot(flat, grad_one, NT)
    for d in range(EMB):
        put(d, FIELDS, g_w_one[d * FPAD : d * FPAD + FIELDS], EMB)

    @pl.when(tower_ref[0] == 0)
    def _():
        g_cin_ref[...] = jnp.zeros_like(g_cin_ref)
        g_cin_ref[:MAPS, :] = sum(dot(grad_maps, third, NT) for third in thirds)
        g_cin_u = jnp.sum(map_sum * grad_logits, axis=1, keepdims=True)
        thirds_u = split_three(jnp.broadcast_to(g_cin_u, (MAPS, 8)))
        g_cin_ref[MAPS : MAPS + 1, :] = sum(dot(third, picks_u, TN) for third in thirds_u)[:1]
        for b, at in enumerate(windows.cin_at):
            g_cins_ref[windows.slots[b], : windows.cin_rows, :PAIRS] = g_cin_ref[
                at : at + windows.cin_rows, :
            ]
        for e, at in enumerate(windows.extra_at):
            skip = max(0, -at)
            for l in range(groups):
                span = slice(l * LANES, (l + 1) * LANES)
                g_extras_ref[e, : windows.rest_rows - skip, span] = g_rest_ref[
                    l, at + skip : at + windows.rest_rows, :
                ]

    @pl.when(tower_ref[0] != 0)
    def _():
        put(W_TWO, HID, dot(hidden_one, grad_two, NT))
        put(B_ONE, 1, dot(ones, grad_one, NT)[:1])
        put(B_TWO, 1, dot(ones, grad_two, NT)[:1])
        put(W_THREE, 1, row_sum(active_two * grad_logits))
        g_bias = jnp.sum(grad_logits, axis=1, keepdims=True)
        put(BIAS, 1, jnp.where(iota((1, HID), 1) == 0, g_bias, 0.0))
        for b, at in enumerate(windows.rest_at):
            for l in range(groups):
                span = slice(l * LANES, (l + 1) * LANES)
                g_rests_ref[windows.slots[b], : windows.rest_rows, span] = g_rest_ref[
                    l, at : at + windows.rest_rows, :
                ]


def dense_step(tower_at, stats, pooled, labels, weights, cin_full, rest_full, windows):
    micro_count = pooled.shape[0]
    width = micro_count * LANES
    in_vmem = pl.BlockSpec(memory_space=pltpu.VMEM)
    in_smem = pl.BlockSpec(memory_space=pltpu.SMEM)
    f32 = jnp.float32
    shapes = [
        ((micro_count, BAG_ROWS, WIDE), jnp.bfloat16),
        ((8, LANES), f32),
        ((windows.batch_count, windows.cin_pad_wide, PAIRS_PAD), f32),
        ((windows.batch_count, windows.rest_pad_wide, HPAD), f32),
        ((windows.extras, windows.extra_pad_wide, HPAD), f32),
    ]
    return pl.pallas_call(
        partial(dense_kernel, micro_count, windows),
        in_specs=[in_smem] + [in_vmem] * 6,
        out_specs=[in_vmem] * len(shapes),
        out_shape=[jax.ShapeDtypeStruct(*shape) for shape in shapes],
        scratch_shapes=[
            pltpu.VMEM((EMB * FPAD, width), f32),
            pltpu.VMEM((PAIRS, width), f32),
            pltpu.VMEM((micro_count, FPAD * FPAD, LANES), f32),
            pltpu.VMEM((PAIRS, width), f32),
            pltpu.VMEM((windows.cin_total, PAIRS), f32),
            pltpu.VMEM((HPAD // LANES, windows.rest_total, LANES), f32),
            pltpu.VMEM((8, width), f32),
        ],
        compiler_params=pltpu.CompilerParams(vmem_limit_bytes=vmem_limit(windows.batch_count)),
        name="dense",
    )(tower_at.reshape(1), stats, pooled, labels, weights, cin_full, rest_full)


def shards(
    shard_ids,
    local_rows,
    bag_counts,
    click_labels,
    sample_weights,
    embed_table,
    table_first,
    table_second,
    dense_params,
    dense_first,
    dense_second,
):
    tower_count = lax.axis_size("tower")
    batch_count = lax.axis_size("batch")
    tower_at = lax.axis_index("tower")
    micro_count, samples = shard_ids.shape[:2]
    columns, rows_dev = embed_table.shape
    capacity = 4 * samples * IDS_SAMP // (tower_count * batch_count)
    share = dense_params.shape[0]
    windows = Windows(share, batch_count)
    slots = Slots(micro_count, capacity)

    device = tower_at * batch_count + lax.axis_index("batch")
    cin_phase, rest_phase = windows.phases(device)
    low = dense_params.astype(jnp.bfloat16)

    def window(rows, row_size, phase):
        return lax.dynamic_update_slice(
            jnp.zeros((rows * row_size,), jnp.bfloat16), low, (phase,)
        )

    cin_window = window(windows.cin_rows, SQUARE, cin_phase).reshape(-1, FIELDS, FIELDS)
    cin_window = jnp.pad(
        cin_window,
        ((0, windows.cin_pad - windows.cin_rows), (0, 0), (0, FPAD - FIELDS)),
    ).reshape(windows.cin_pad, PAIRS)
    cin_window = jnp.pad(cin_window, ((0, 0), (0, PAIRS_PAD - PAIRS)))
    rest_window = jnp.pad(
        window(windows.rest_rows, HID, rest_phase).reshape(-1, HID),
        ((0, windows.rest_pad - windows.rest_rows), (0, HPAD - HID)),
    )

    def lanes_of(values):
        return jnp.moveaxis(values, 1, -1).reshape(micro_count, -1, samples)

    requests, codes, halves = route(
        lanes_of(shard_ids), lanes_of(local_rows), lanes_of(bag_counts), sample_weights,
        slots, batch_count,
    )
    pooled, served, stats, cin_full, rest_full = fetch(
        requests, codes, halves, embed_table, cin_window, rest_window, windows, slots
    )
    grad_bags, loss, g_cins, g_rests, g_extras = dense_step(
        tower_at, stats, pooled, click_labels, sample_weights, cin_full, rest_full, windows
    )
    table_grad, losses, g_cin, g_rest = return_grads(
        grad_bags, codes, halves, served, loss, g_cins, g_rests, g_extras, windows, slots, columns
    )
    g_cin = g_cin[: windows.cin_rows, :PAIRS].reshape(-1, FIELDS, FPAD)[:, :, :FIELDS].reshape(-1)
    g_rest = g_rest[: windows.rest_rows, :HID].reshape(-1)
    is_cin = device * share + jnp.arange(share, dtype=jnp.int32) < CIN_SIZE
    own_grad = jnp.where(
        is_cin,
        lax.dynamic_slice(g_cin, (cin_phase,), (share,)),
        lax.dynamic_slice(g_rest, (rest_phase,), (share,)),
    )

    table_new, table_first_new, table_second_new = adam_update(
        embed_table, table_first, table_second, table_grad, rate_table
    )
    dense_new, dense_first_new, dense_second_new = adam_update(
        dense_params, dense_first, dense_second, own_grad, rate_dense
    )
    loss_sum = losses[0, 0] / stats[0, 0]
    return (
        table_new,
        table_first_new,
        table_second_new,
        table_new.astype(jnp.bfloat16),
        dense_new,
        dense_first_new,
        dense_second_new,
        dense_new.astype(jnp.bfloat16),
        loss_sum,
    )


def solution(mesh):
    rows = P(None, ("tower", "batch"))
    dense = P(("tower", "batch"))
    placed = (
        P(None, "batch", None, None),
        P(None, "batch", None, None),
        P(None, "batch", None),
        P(None, "batch"),
        P(None, "batch"),
        rows,
        rows,
        rows,
        dense,
        dense,
        dense,
    )
    return jax.shard_map(
        shards,
        mesh=mesh,
        in_specs=placed,
        out_specs=(rows, rows, rows, rows, dense, dense, dense, dense, P()),
        check_vma=False,
    )
```

```python
from functools import partial

import jax
import jax.numpy as jnp
from jax import lax
from jax.experimental import pallas as pl
from jax.experimental.pallas import tpu as pltpu
from jax.sharding import PartitionSpec as P

FIELDS = 39
EMB = 10
MAPS = 200
HID = 400
IDS_SAMP = 80

beta_one = 0.9
beta_two = 0.999
epsilon = 1e-08
decay_rate = 0.15
rate_table = 0.1
rate_dense = 0.05
step_count = 10

LANES = 128
WIDE = 256
BROAD = 512
TALL = 64
HALF = 24
BAG_ROWS = EMB * HALF + 8
FPAD = 40
PAIRS = FIELDS * FPAD
PAIRS_PAD = -(-PAIRS // LANES) * LANES
SQUARE = FIELDS * FIELDS
CIN_SIZE = MAPS * SQUARE + MAPS
FLAT = EMB * FIELDS
B_ONE, W_TWO, B_TWO, W_THREE, BIAS = FLAT, FLAT + 1, FLAT + HID + 1, FLAT + HID + 2, FLAT + HID + 3
HPAD = 512
PLANE = 4
NT = (((1,), (1,)), ((), ()))
TN = (((0,), (0,)), ((), ()))
NN = (((1,), (0,)), ((), ()))


def adam_update(weight, first_old, second_old, gradient, step_rate):
    first_new = beta_one * first_old + (1.0 - beta_one) * gradient
    second_new = beta_two * second_old + (1.0 - beta_two) * gradient * gradient
    first_hat = first_new / (1.0 - beta_one**step_count)
    second_hat = second_new / (1.0 - beta_two**step_count)
    weight_new = weight - step_rate * (
        first_hat / (jnp.sqrt(second_hat) + epsilon) + decay_rate * weight
    )
    return (weight_new, first_new, second_new)


def dot(a, b, dims=NN):
    return lax.dot_general(a, b, dims, preferred_element_type=jnp.float32)


def vmem_limit(batch_count):
    return (28 + batch_count // 4) << 20


def iota(shape, dim):
    return lax.broadcasted_iota(jnp.int32, shape, dim)


def ones_at(mask):
    return jnp.where(mask, 1.0, 0.0).astype(jnp.bfloat16)


class Slots:
    def __init__(self, micro_count, capacity):
        self.micro_count = micro_count
        self.first_rows = [m * capacity // WIDE for m in range(micro_count)]
        self.shifts = [m * capacity % WIDE for m in range(micro_count)]
        self.spans = [-(-(shift + capacity) // LANES) * LANES for shift in self.shifts]
        self.length = max(
            first * WIDE + span for first, span in zip(self.first_rows, self.spans)
        )
        self.rows = -(-self.length // WIDE)
        self.window = max(-(-span // WIDE) for span in self.spans)

    def width(self, row):
        return min(WIDE, self.length - row * WIDE)

    def micro_width(self, micro, row):
        inside = row - self.first_rows[micro]
        return max(0, min(WIDE, self.spans[micro] - inside * WIDE)) if inside >= 0 else 0


class Windows:
    def __init__(self, share, batch_count):
        self.share, self.batch_count = share, batch_count
        self.cin_rows = -(-(SQUARE - 1 + share) // SQUARE)
        self.rest_rows = -(-(HID - 1 + share) // HID)
        self.cin_pad = -(-self.cin_rows // 16) * 16
        self.rest_pad = -(-self.rest_rows // 16) * 16
        self.cin_pad_wide = -(-self.cin_rows // 8) * 8
        self.rest_pad_wide = -(-self.rest_rows // 8) * 8
        self.first_extra = CIN_SIZE // share
        self.extras = batch_count - self.first_extra
        self.cin_at = [b * share // SQUARE for b in range(batch_count)]
        self.rest_at = [
            ((batch_count + b) * share - CIN_SIZE) // HID for b in range(batch_count)
        ]
        self.extra_at = [
            (b * share - CIN_SIZE) // HID for b in range(self.first_extra, batch_count)
        ]
        depth = batch_count // PLANE
        self.slots = [b % PLANE * depth + b // PLANE for b in range(batch_count)]
        self.extra_skip = [max(0, -at) for at in self.extra_at]
        longest = max(self.rest_rows - skip for skip in self.extra_skip)
        self.extra_pad_wide = -(-longest // 8) * 8
        self.cin_total = -(-max(a + self.cin_rows for a in self.cin_at) // 8) * 8
        self.rest_total = -(-max(a + self.rest_rows for a in self.rest_at) // 8) * 8

    def phases(self, device):
        start = device * self.share
        return start % SQUARE, jnp.mod(start - CIN_SIZE, HID)


def coded(x):
    return jnp.where(x < 256, x + 1, 255 - x).astype(jnp.float32)


def decoded(x):
    return jnp.where(x > 0, x - 1, 255 - x)


def route_kernel(
    slots, batch_count, ids_ref, rows_ref, counts_ref, weight_ref,
    req_ref, code_ref, half_ref, part_ref, left_ref, right_ref,
):
    f32, bf16 = jnp.float32, jnp.bfloat16
    micro_count, window = slots.micro_count, slots.window
    micro = pl.program_id(0)
    id_rows, samples = ids_ref.shape[1:]
    chunk = 16
    tower = lax.axis_index("tower")

    @pl.when(micro == 0)
    def _():
        req_ref[...] = jnp.zeros_like(req_ref)
        code_ref[...] = jnp.zeros_like(code_ref)
        half_ref[...] = jnp.zeros_like(half_ref)
        part_ref[...] = jnp.zeros_like(part_ref)
        weight_sum = jnp.sum(weight_ref[...].astype(f32)).astype(jnp.int32)
        req_ref[:, slots.rows, :] = jnp.full((batch_count, WIDE), weight_sum)

    def widened(x, filler):
        part_ref[0, :, :samples] = x.astype(f32)
        inside = iota((id_rows, LANES), 1) < samples
        return jnp.where(inside, part_ref[0], filler)

    owner = ids_ref[0]
    target = widened(
        jnp.where(owner // batch_count == tower, owner % batch_count, batch_count), batch_count
    ).astype(jnp.int32)
    local = widened(rows_ref[0], 0.0).astype(jnp.int32)
    before = ones_at(iota((FIELDS, FIELDS), 1) <= iota((FIELDS, FIELDS), 0))
    ends = dot(before, counts_ref[0].astype(f32).astype(bf16)).astype(jnp.int32)
    field = jnp.zeros((id_rows, samples), jnp.int32)
    for f in range(FIELDS):
        field = field + jnp.where(iota((id_rows, samples), 0) >= ends[f : f + 1], 1, 0)
    bag = iota((id_rows, LANES), 1) * FIELDS + widened(field, 0.0).astype(jnp.int32)

    earlier_rows = ones_at(iota((id_rows, id_rows), 1) < iota((id_rows, id_rows), 0))
    upper = iota((2 * LANES, LANES), 0)
    mixing = ones_at((upper < iota((2 * LANES, LANES), 1)) | (upper >= LANES))
    rank = jnp.zeros((id_rows, LANES), f32)
    for begin in range(0, batch_count, chunk):
        hots = [ones_at(target == begin + d) for d in range(chunk)]
        above = dot(earlier_rows, jnp.concatenate(hots, axis=1)).astype(bf16)
        stacked = jnp.concatenate(
            [
                jnp.concatenate([hots[d], above[:, d * LANES : (d + 1) * LANES]], axis=1)
                for d in range(chunk)
            ],
            axis=0,
        )
        ranks = dot(stacked, mixing)
        for d in range(chunk):
            rank = rank + jnp.where(
                target == begin + d, ranks[d * id_rows : (d + 1) * id_rows], 0.0
            )
    shift = sum(jnp.where(micro == m, slots.shifts[m], 0) for m in range(micro_count))
    slot = rank.astype(jnp.int32) + shift
    place = jnp.where(target < batch_count, (slot // WIDE) * batch_count + target, -1)
    part_ref[0] = place.astype(f32)
    part_ref[1] = (slot % WIDE).astype(f32)
    part_ref[2] = coded(local // 64)
    part_ref[3] = coded((local % 64) * 8 + bag // 512)
    part_ref[4] = coded(bag % 512)
    places = window * batch_count

    def build(t, carry):
        span = pl.ds(pl.multiple_of(t * LANES, LANES), LANES)

        def row(k):
            return part_ref[k, pl.ds(t, 1), :]

        mask = iota((places, LANES), 0).astype(f32) == row(0)
        for v in range(3):
            left_ref[v * places : (v + 1) * places, span] = jnp.where(
                mask, row(2 + v), 0.0
            ).astype(bf16)
        right_ref[:, span] = ones_at(iota((WIDE, LANES), 0).astype(f32) == row(1))
        return carry

    lax.fori_loop(0, id_rows, build, 0, unroll=2)
    placed = dot(left_ref[...], right_ref[...], NT).astype(jnp.int32)

    def part(v, r):
        begin = (v * window + r) * batch_count
        return placed[begin : begin + batch_count]

    for m in range(micro_count):

        @pl.when(micro == m)
        def _():
            for r in range(window):
                at = slots.first_rows[m] + r
                if slots.micro_width(m, at) == 0:
                    continue
                middle = decoded(part(1, r))
                bag = middle % 8 * 512 + decoded(part(2, r))
                valid = part(2, r) != 0
                sample = ((bag.astype(f32) + 0.5) * (1.0 / FIELDS)).astype(jnp.int32)
                field = bag - sample * FIELDS
                late = jnp.where(field >= HALF, 1, 0)
                code = sample + late * LANES + (m * WIDE + 1)
                row = decoded(part(0, r)) * 64 + middle // 8
                req_ref[:, at, :] += jnp.where(valid, row, 0)
                code_ref[:, at, :] += jnp.where(valid, code, 0)
                half_ref[:, at, :] += jnp.where(valid, field - late * HALF, 0)


def in_hbm(x):
    return pltpu.with_memory_space_constraint(x, pltpu.HBM)


def route(ids, rows, counts, weights, slots, batch_count):
    micro_count, id_rows, samples = ids.shape
    places = slots.window * batch_count

    def block(x):
        return pl.BlockSpec((1,) + x.shape[1:], lambda m: (m, 0, 0))

    shapes = [(batch_count, slots.rows + k, WIDE) for k in (1, 0, 0)]
    return pl.pallas_call(
        partial(route_kernel, slots, batch_count),
        grid=(micro_count,),
        in_specs=[block(ids), block(rows), block(counts), pl.BlockSpec(weights.shape, lambda m: (0, 0))],
        out_specs=[pl.BlockSpec(shape, lambda m: (0, 0, 0)) for shape in shapes],
        out_shape=[jax.ShapeDtypeStruct(shape, jnp.int32) for shape in shapes],
        scratch_shapes=[
            pltpu.VMEM((5, id_rows, LANES), jnp.float32),
            pltpu.VMEM((3 * places, id_rows * LANES), jnp.bfloat16),
            pltpu.VMEM((WIDE, id_rows * LANES), jnp.bfloat16),
        ],
        compiler_params=pltpu.CompilerParams(vmem_limit_bytes=vmem_limit(batch_count)),
        name="route",
    )(in_hbm(ids), in_hbm(rows), in_hbm(counts), in_hbm(weights))


def peer_copy(src, dst, send_sem, recv_sem, peer):
    return pltpu.make_async_remote_copy(
        src_ref=src,
        dst_ref=dst,
        send_sem=send_sem,
        recv_sem=recv_sem,
        device_id={"batch": peer},
        device_id_type=pl.DeviceIdType.MESH,
    )


def greet(me, batch_count, other_tower=None):
    barrier = pltpu.get_barrier_semaphore()

    def signal(i, carry):
        pl.semaphore_signal(
            barrier,
            inc=1,
            device_id={"batch": lax.rem(me + i, batch_count)},
            device_id_type=pl.DeviceIdType.MESH,
        )
        return carry

    lax.fori_loop(1, batch_count, signal, 0)
    if other_tower is not None:
        pl.semaphore_signal(
            barrier,
            inc=1,
            device_id={"tower": other_tower},
            device_id_type=pl.DeviceIdType.MESH,
        )


def all_greeted(batch_count, pair):
    pl.semaphore_wait(pltpu.get_barrier_semaphore(), batch_count - 1 + (1 if pair else 0))


def message_rows(rows_msg, columns):
    return -(-(rows_msg * columns + 1) // 16) * 16


def each(count, action):
    def body(i, carry):
        action(i)
        return carry

    lax.fori_loop(1, count, body, 0)


def pick_rows(result, mask, depth, columns):
    width = result.shape[1]
    out = jnp.zeros((16, width), jnp.float32)
    for c in range(columns):
        row = jnp.sum(
            jnp.where(mask, result[c * depth : (c + 1) * depth], 0.0), axis=0, keepdims=True
        )
        out = jnp.where(iota((16, width), 0) == c, row, out)
    return out


def tile_table(table_ref, tiles_ref, stage_ref, columns):
    for c in range(columns):
        for q in range(TALL):
            stage_ref[q : q + 1, :] = table_ref[c : c + 1, q * BROAD : (q + 1) * BROAD]
        tiles_ref[c * TALL : (c + 1) * TALL, :] = stage_ref[...].astype(jnp.bfloat16)


def fetch_kernel(
    slots, windows, columns,
    req_ref, code_ref, half_ref, table_hbm_ref, cin_ref, rest_ref,
    out_ref, served_ref, stat_out_ref, cin_full_ref, rest_full_ref,
    cins_ref, rests_ref, extras_ref, table_ref, tiles_ref, stage_ref, first_ref, second_ref, ans_out_ref, ans_in_ref, left_ref, pooled_ref,
    other_ref,
    req_send, req_recv, ans_send, ans_recv, win_send, win_recv, plane_send,
    plane_recv, ext_send, ext_recv, pair_send, pair_recv, table_sem,
):
    rows_msg = slots.rows
    batch_count = windows.batch_count
    first_extra = windows.first_extra
    me = lax.axis_index("batch")
    tower = lax.axis_index("tower")
    other_tower = 1 - tower
    greet(me, batch_count, other_tower)
    load_table = pltpu.make_async_copy(table_hbm_ref, table_ref, table_sem)
    load_table.start()
    pooled_ref[...] = jnp.zeros_like(pooled_ref)
    first_ref[...] = jnp.zeros_like(first_ref)
    second_ref[...] = jnp.zeros_like(second_ref)

    def request_copy(peer, slot):
        return peer_copy(
            req_ref.at[peer], served_ref.at[slot], req_send.at[peer], req_recv.at[slot], peer
        )

    def answer_copy(peer, slot):
        return peer_copy(
            ans_out_ref.at[peer], ans_in_ref.at[slot], ans_send.at[peer], ans_recv.at[slot], peer
        )

    all_greeted(batch_count, True)

    def send_requests(i, carry):
        peer = lax.rem(me + i, batch_count)
        request_copy(peer, me).start()
        return carry

    lax.fori_loop(1, batch_count, send_requests, 0)

    depth = batch_count // PLANE
    high, low = me // PLANE, lax.rem(me, PLANE)

    def others(action):
        each(batch_count, lambda i: action(lax.rem(me + i, batch_count)))

    def column(action):
        each(depth, lambda i: action(lax.rem(high + i, depth)))

    def plane(action):
        each(PLANE, lambda i: action(lax.rem(low + i, PLANE)))

    def column_copy(src, dst, to, source):
        return peer_copy(
            src, dst.at[low * depth + source], win_send.at[to], win_recv.at[source],
            to * PLANE + low,
        )

    def plane_copy(dst, to, source):
        block = dst.at[pl.ds(source * depth, depth)]
        return peer_copy(
            block, block, plane_send.at[to], plane_recv.at[source], high * PLANE + to
        )

    def extra_copy(peer, slot):
        return peer_copy(rest_ref, extras_ref.at[slot], ext_send.at[peer], ext_recv.at[slot], peer)

    def start_windows(src, dst):
        column(lambda to: column_copy(src, dst, to, high).start())
        dst[low * depth + high] = src[...]

    def pass_windows(src, dst):
        column(lambda source: column_copy(src, dst, source, source).wait_recv())
        plane(lambda to: plane_copy(dst, to, low).start())

    def sent_windows(src, dst):
        column(lambda to: column_copy(src, dst, to, high).wait_send())
        plane(lambda to: plane_copy(dst, to, low).wait_send())

    def split(action):
        @pl.when(tower == 0)
        def _():
            action(cin_ref, cins_ref)

        @pl.when(tower == 1)
        def _():
            action(rest_ref, rests_ref)

    served_ref[me] = req_ref[me]
    load_table.wait()
    tile_table(table_ref, tiles_ref, stage_ref, columns)

    sizes = ans_out_ref.shape[1]

    def look_up(first, second):
        for r in range(rows_msg):
            w = slots.width(r)
            row = jnp.concatenate(
                [served_ref[first, r : r + 1, :w], served_ref[second, r : r + 1, :w]], axis=1
            )
            hot = ones_at(iota((BROAD, 2 * w), 0) == row % BROAD)
            result = dot(tiles_ref[...], hot)
            mask = iota((TALL, 2 * w), 0) == row // BROAD
            block = pick_rows(result, mask, TALL, columns)
            first_ref[r * columns : r * columns + 16, :w] = block[:, :w]
            second_ref[r * columns : r * columns + 16, :w] = block[:, w:]
        ans_out_ref[first] = first_ref[:sizes, :].astype(jnp.bfloat16)
        ans_out_ref[second] = second_ref[:sizes, :].astype(jnp.bfloat16)

    def look_up_one(source):
        half = rows_msg // 2
        for r in range(half + rows_msg % 2):
            both = [r, r + half] if r < half else [rows_msg - 1]
            widths = [slots.width(x) for x in both]
            row = jnp.concatenate(
                [served_ref[source, x : x + 1, :w] for x, w in zip(both, widths)], axis=1
            )
            hot = ones_at(iota((BROAD, row.shape[1]), 0) == row % BROAD)
            result = dot(tiles_ref[...], hot)
            mask = iota((TALL, row.shape[1]), 0) == row // BROAD
            block = pick_rows(result, mask, TALL, columns)
            for at, x, w in zip((0, WIDE), both, widths):
                first_ref[x * columns : (x + 1) * columns, :w] = block[:columns, at : at + w]

    def pool(owner, after=None):
        first_ref[:sizes, :] = ans_in_ref[owner].astype(jnp.float32)
        for r in range(rows_msg):
            w = slots.width(r)
            begin = r * columns
            values = [first_ref[begin + c : begin + c + 1, :w] for c in range(columns)]
            mask = iota((HALF, w), 0) == half_ref[owner, r : r + 1, :w]
            pieces = [jnp.where(mask, values[c], 0.0) for c in range(EMB)]
            pieces.append(jnp.where(iota((8, w), 0) == 0, values[EMB], 0.0))
            left_ref[:, r * WIDE : r * WIDE + w] = jnp.concatenate(pieces, axis=0).astype(
                jnp.bfloat16
            )
        for m in range(slots.micro_count):
            rights = []
            for r in range(slots.first_rows[m], rows_msg):
                w = slots.micro_width(m, r)
                if w:
                    lane = iota((WIDE, w), 0) + (m * WIDE + 1)
                    rights.append(ones_at(lane == code_ref[owner, r : r + 1, :w]))
            begin = slots.first_rows[m] * WIDE
            pooled_ref[m] += dot(
                left_ref[:, begin : begin + slots.spans[m]], jnp.concatenate(rights, axis=1), NT
            )
            if after is not None:
                after(m)

    def pair_copy(src, dst, k):
        return pltpu.make_async_remote_copy(
            src_ref=src,
            dst_ref=dst,
            send_sem=pair_send.at[k],
            recv_sem=pair_recv.at[k],
            device_id={"tower": other_tower},
            device_id_type=pl.DeviceIdType.MESH,
        )

    def swap_windows():
        @pl.when(tower == 0)
        def _():
            plane(lambda source: plane_copy(cins_ref, source, source).wait_recv())
            for e in range(windows.extras):

                @pl.when(me != first_extra + e)
                def _():
                    extra_copy(first_extra + e, e).wait_recv()

            pair_copy(cins_ref, cins_ref, 0).start()
            pair_copy(extras_ref, extras_ref, 1).start()

        @pl.when(tower == 1)
        def _():
            plane(lambda source: plane_copy(rests_ref, source, source).wait_recv())
            pair_copy(rests_ref, rests_ref, 0).start()

    pairs = batch_count // 2
    lag = 3

    last = lax.rem(me + 1, batch_count)

    def step(j, carry):
        @pl.when((j == 0) | (j == pairs))
        def _():
            @pl.when(j == pairs)
            def _():
                request_copy(last, last).wait_recv()

            look_up_one(jnp.where(j == 0, me, last))

            @pl.when(j == 0)
            def _():
                ans_in_ref[me] = first_ref[:sizes, :].astype(jnp.bfloat16)
                split(start_windows)

            @pl.when(j == pairs)
            def _():
                ans_out_ref[last] = first_ref[:sizes, :].astype(jnp.bfloat16)
                answer_copy(last, me).start()

        @pl.when((j == 0) & (tower == 0) & (me >= first_extra))
        def _():
            others(lambda peer: extra_copy(peer, me - first_extra).start())
            extras_ref[me - first_extra] = rest_ref[...]

        @pl.when((j > 0) & (j < pairs))
        def _():
            first = lax.rem(me + batch_count - (2 * j - 1), batch_count)
            second = lax.rem(me + batch_count - 2 * j, batch_count)
            request_copy(first, first).wait_recv()
            request_copy(second, second).wait_recv()
            look_up(first, second)
            answer_copy(first, me).start()
            answer_copy(second, me).start()

        @pl.when(j == 3)
        def _():
            split(pass_windows)

        @pl.when(j == pairs - 2)
        def _():
            swap_windows()

        ready = j - lag

        @pl.when((ready >= 0) & (ready < pairs))
        def _():
            first = lax.rem(me + batch_count + 2 * ready - 1, batch_count)

            @pl.when(ready > 0)
            def _():
                answer_copy(first, first).wait_recv()

            pool(jnp.where(ready == 0, me, first))

        @pl.when((ready > 0) & (ready < pairs))
        def _():
            second = lax.rem(me + 2 * ready, batch_count)
            answer_copy(second, second).wait_recv()
            pool(second)

        return carry

    lax.fori_loop(0, pairs + lag, step, 0)

    def pooled_copy(m):
        return pair_copy(pooled_ref.at[m], other_ref.at[m], 2 + m)

    final = lax.rem(me + batch_count - 1, batch_count)
    answer_copy(final, final).wait_recv()
    pool(final, lambda m: pooled_copy(m).start())

    def finish(i, carry):
        peer = lax.rem(me + i, batch_count)
        request_copy(peer, me).wait_send()
        answer_copy(peer, me).wait_send()
        return carry

    lax.fori_loop(1, batch_count, finish, 0)
    weight_sum = jnp.sum(served_ref[:, rows_msg, :LANES], axis=0, keepdims=True)
    stat_out_ref[...] = jnp.broadcast_to(weight_sum.astype(jnp.float32), stat_out_ref.shape)

    split(sent_windows)

    @pl.when(tower == 0)
    def _():
        @pl.when(me >= first_extra)
        def _():
            others(lambda peer: extra_copy(peer, me - first_extra).wait_send())

        pair_copy(cins_ref, cins_ref, 0).wait_send()
        pair_copy(extras_ref, extras_ref, 1).wait_send()
        pair_copy(rests_ref, rests_ref, 0).wait_recv()

    @pl.when(tower == 1)
    def _():
        pair_copy(rests_ref, rests_ref, 0).wait_send()
        pair_copy(cins_ref, cins_ref, 0).wait_recv()
        pair_copy(extras_ref, extras_ref, 1).wait_recv()

    cin_full_ref[...] = jnp.zeros_like(cin_full_ref)
    for b, at in enumerate(windows.cin_at):
        block = cins_ref[windows.slots[b]].astype(jnp.float32)
        cin_full_ref[at : at + windows.cin_rows, :] += block[: windows.cin_rows, :PAIRS]
    rest_full_ref[...] = jnp.zeros_like(rest_full_ref)
    pieces = [(rests_ref, windows.slots[b], at) for b, at in enumerate(windows.rest_at)]
    pieces += [(extras_ref, e, at) for e, at in enumerate(windows.extra_at)]
    for source, b, at in pieces:
        skip = max(0, -at)
        block = source[b].astype(jnp.float32)
        for l in range(HPAD // LANES):
            rest_full_ref[l, at + skip : at + windows.rest_rows, :] += block[
                skip : windows.rest_rows, l * LANES : (l + 1) * LANES
            ]
    for m in range(slots.micro_count):
        pooled_copy(m).wait()
        out_ref[m] = pooled_ref[m] + other_ref[m]


def fetch(
    requests, codes, halves, table, cin_window, rest_window, windows, slots
):
    batch_count, rows_msg, _ = codes.shape
    columns, rows_dev = table.shape
    sizes = message_rows(rows_msg, columns)
    in_vmem = pl.BlockSpec(memory_space=pltpu.VMEM)
    dma = pltpu.SemaphoreType.DMA
    bags = (slots.micro_count, BAG_ROWS, WIDE)
    return pl.pallas_call(
        partial(fetch_kernel, slots, windows, columns),
        in_specs=[in_vmem] * 3 + [pl.BlockSpec(memory_space=pltpu.HBM)] + [in_vmem] * 2,
        out_specs=[in_vmem] * 5,
        out_shape=[
            jax.ShapeDtypeStruct(bags, jnp.float32),
            jax.ShapeDtypeStruct(requests.shape, jnp.int32),
            jax.ShapeDtypeStruct((8, LANES), jnp.float32),
            jax.ShapeDtypeStruct((windows.cin_total, PAIRS), jnp.float32),
            jax.ShapeDtypeStruct((HPAD // LANES, windows.rest_total, LANES), jnp.float32),
        ],
        scratch_shapes=[
            pltpu.VMEM((batch_count,) + cin_window.shape, jnp.bfloat16),
            pltpu.VMEM((batch_count,) + rest_window.shape, jnp.bfloat16),
            pltpu.VMEM((windows.extras,) + rest_window.shape, jnp.bfloat16),
            pltpu.VMEM(table.shape, jnp.float32),
            pltpu.VMEM((columns * TALL, BROAD), jnp.bfloat16),
            pltpu.VMEM((TALL, BROAD), jnp.float32),
            pltpu.VMEM((sizes + 16, WIDE), jnp.float32),
            pltpu.VMEM((sizes + 16, WIDE), jnp.float32),
            pltpu.VMEM((batch_count, sizes, WIDE), jnp.bfloat16),
            pltpu.VMEM((batch_count, sizes, WIDE), jnp.bfloat16),
            pltpu.VMEM((BAG_ROWS, rows_msg * WIDE), jnp.bfloat16),
            pltpu.VMEM(bags, jnp.float32),
            pltpu.VMEM(bags, jnp.float32),
        ]
        + [dma((batch_count,))] * 9
        + [dma((windows.extras,)), dma((2 + slots.micro_count,)), dma((2 + slots.micro_count,)), dma],
        compiler_params=pltpu.CompilerParams(
            vmem_limit_bytes=vmem_limit(batch_count), collective_id=0, has_side_effects=True
        ),
        name="fetch",
    )(requests, codes, halves, in_hbm(table), cin_window, rest_window)


def return_kernel(
    slots, windows, columns,
    grad_ref, code_ref, half_ref, served_ref, stat_ref, cins_ref, rests_ref, extras_ref,
    out_ref, stat_out_ref, cin_ref, rest_ref,
    send_ref, recv_ref, first_ref, second_ref, left_ref, right_ref, total_ref,
    extra_in_ref, cin_near_ref, cin_sum_ref, cin_far_ref, rest_near_ref, rest_sum_ref, rest_far_ref,
    val_send, val_recv, win_send, win_recv, plane_send, plane_recv, ext_send,
    ext_recv,
):
    batch_count = windows.batch_count
    first_extra = windows.first_extra
    tower = lax.axis_index("tower")
    rows_msg = slots.rows
    me = lax.axis_index("batch")
    greet(me, batch_count)

    def value_copy(peer, slot):
        return peer_copy(
            send_ref.at[peer], recv_ref.at[slot], val_send.at[peer], val_recv.at[slot], peer
        )

    def own_copy():
        return pltpu.make_async_copy(send_ref.at[me], recv_ref.at[me], val_recv.at[me])

    depth = batch_count // PLANE
    high, low = me // PLANE, lax.rem(me, PLANE)

    def others(action):
        each(batch_count, lambda i: action(lax.rem(me + i, batch_count)))

    def column(action):
        each(depth, lambda i: action(lax.rem(high + i, depth)))

    def plane(action):
        each(PLANE, lambda i: action(lax.rem(low + i, PLANE)))

    def plane_copy(src, near, to, source):
        return peer_copy(
            src.at[pl.ds(to * depth, depth)], near.at[source], plane_send.at[to],
            plane_recv.at[source], high * PLANE + to,
        )

    def column_copy(total, far, to, source):
        return peer_copy(
            total.at[to], far.at[source], win_send.at[to], win_recv.at[source], to * PLANE + low
        )

    def start_windows(src, near, total, far, out):
        plane(lambda to: plane_copy(src, near, to, low).start())
        near[low] = src[pl.ds(low * depth, depth)]

    def pass_windows(src, near, total, far, out):
        plane(lambda source: plane_copy(src, near, source, source).wait_recv())
        total[...] = jnp.sum(near[...], axis=0)
        column(lambda to: column_copy(total, far, to, high).start())
        far[high] = total[high]

    def end_windows(src, near, total, far, out):
        column(lambda source: column_copy(total, far, source, source).wait_recv())
        out[...] = jnp.sum(far[...], axis=0)
        plane(lambda to: plane_copy(src, near, to, low).wait_send())
        column(lambda to: column_copy(total, far, to, high).wait_send())

    def split(action):
        @pl.when(tower == 0)
        def _():
            action(cins_ref, cin_near_ref, cin_sum_ref, cin_far_ref, cin_ref)

        @pl.when(tower == 1)
        def _():
            action(rests_ref, rest_near_ref, rest_sum_ref, rest_far_ref, rest_ref)

    def extra_copy(peer, slot):
        return peer_copy(
            extras_ref.at[peer - first_extra],
            extra_in_ref.at[slot],
            ext_send.at[peer],
            ext_recv.at[slot],
            peer,
        )

    first_ref[...] = jnp.zeros_like(first_ref)
    second_ref[...] = jnp.zeros_like(second_ref)
    spare = rows_msg * columns
    loss_parts = split_three(stat_ref[0:1, :])
    loss_row = sum(
        jnp.where(iota((1, LANES), 1) == k, part.astype(jnp.float32), 0.0)
        for k, part in enumerate(loss_parts)
    )
    stat_out_ref[...] = jnp.zeros_like(stat_out_ref)
    total_ref[...] = jnp.zeros_like(total_ref)

    sizes = send_ref.shape[1]

    def spread(first, second):
        def both(ref, r, w):
            return jnp.concatenate([ref[first, r : r + 1, :w], ref[second, r : r + 1, :w]], axis=1)

        for r in range(rows_msg):
            w = slots.width(r)
            result = None
            for m in range(slots.micro_count):
                inner = slots.micro_width(m, r)
                if inner == 0:
                    continue
                hot = ones_at(iota((WIDE, 2 * inner), 0) + (m * WIDE + 1) == both(code_ref, r, inner))
                found = dot(grad_ref[m], hot)
                if inner < w:
                    blank = jnp.zeros((BAG_ROWS, w - inner), jnp.float32)
                    found = jnp.concatenate(
                        [found[:, :inner], blank, found[:, inner:], blank], axis=1
                    )
                result = found if result is None else result + found
            mask = iota((HALF, 2 * w), 0) == both(half_ref, r, w)
            block = pick_rows(result, mask, HALF, EMB)
            linear = result[EMB * HALF : EMB * HALF + 1]
            block = jnp.where(iota((16, 2 * w), 0) == EMB, linear, block)
            first_ref[r * columns : r * columns + 16, :w] = block[:, :w]
            second_ref[r * columns : r * columns + 16, :w] = block[:, w:]
        first_ref[spare : spare + 1, :LANES] = loss_row
        second_ref[spare : spare + 1, :LANES] = loss_row
        send_ref[first] = first_ref[:sizes, :].astype(jnp.bfloat16)
        send_ref[second] = second_ref[:sizes, :].astype(jnp.bfloat16)

    def scatter(source):
        first_ref[:sizes, :] = recv_ref[source].astype(jnp.float32)
        stat_out_ref[0:1, :] += first_ref[spare : spare + 1, :LANES]
        for r in range(rows_msg):
            w = slots.width(r)
            span = slice(r * WIDE, r * WIDE + w)
            row = served_ref[source, r : r + 1, :w]
            mask = iota((TALL, w), 0) == row // BROAD
            for c in range(columns):
                left_ref[c * TALL : (c + 1) * TALL, span] = jnp.where(
                    mask, first_ref[r * columns + c : r * columns + c + 1, :w], 0.0
                ).astype(jnp.bfloat16)
            right_ref[:, span] = ones_at(iota((BROAD, w), 0) == row % BROAD)
        total_ref[...] += dot(
            left_ref[:, : slots.length], right_ref[:, : slots.length], NT
        )

    pairs = batch_count // 2
    lag = 2

    def step(j, carry):
        @pl.when(j < pairs)
        def _():
            first = lax.rem(me + 2 * j + 1, batch_count)
            second = lax.rem(me + 2 * j + 2, batch_count)
            spread(first, second)

            @pl.when(j == 0)
            def _():
                all_greeted(batch_count, False)

            value_copy(first, me).start()

            @pl.when(j == 1)
            def _():
                split(start_windows)

            @pl.when((j == 3) & (tower == 0))
            def _():
                for e in range(windows.extras):

                    @pl.when(me != first_extra + e)
                    def _():
                        extra_copy(first_extra + e, me).start()

            @pl.when(j < pairs - 1)
            def _():
                value_copy(second, me).start()

            @pl.when(j == pairs - 1)
            def _():
                own_copy().start()

        @pl.when(j == pairs - 1)
        def _():
            split(pass_windows)

        @pl.when(j >= lag)
        def _():
            first = lax.rem(me + batch_count - (2 * (j - lag) + 1), batch_count)
            value_copy(first, first).wait_recv()
            scatter(first)

        @pl.when((j >= lag) & (j < pairs - 1 + lag))
        def _():
            second = lax.rem(me + 2 * batch_count - (2 * (j - lag) + 2), batch_count)
            value_copy(second, second).wait_recv()
            scatter(second)

        return carry

    lax.fori_loop(0, pairs + lag, step, 0)
    own_copy().wait()
    scatter(me)

    split(end_windows)

    @pl.when(tower == 0)
    def _():
        rest_ref[...] = jnp.zeros_like(rest_ref)
        for e in range(windows.extras):

            @pl.when(me != first_extra + e)
            def _():
                extra_copy(first_extra + e, me).wait_send()

        @pl.when(me >= first_extra)
        def _():
            extra_in_ref[me] = extras_ref[me - first_extra]
            others(lambda peer: extra_copy(me, peer).wait_recv())
            total = jnp.sum(extra_in_ref[...], axis=0)
            for e, skip in enumerate(windows.extra_skip):

                @pl.when(me == first_extra + e)
                def _():
                    rest_ref[skip : windows.rest_rows, :] = total[: windows.rest_rows - skip]

    @pl.when(tower == 1)
    def _():
        cin_ref[...] = jnp.zeros_like(cin_ref)

    def finish(i, carry):
        peer = lax.rem(me + i, batch_count)
        value_copy(peer, me).wait_send()
        return carry

    lax.fori_loop(1, batch_count, finish, 0)
    losses = jnp.sum(stat_out_ref[0:1, :], axis=1, keepdims=True)
    stat_out_ref[...] = jnp.broadcast_to(losses, stat_out_ref.shape)
    for c in range(columns):
        for q in range(TALL):
            out_ref[c : c + 1, q * BROAD : (q + 1) * BROAD] = total_ref[
                c * TALL + q : c * TALL + q + 1, :
            ]


def return_grads(
    grad_bags, codes, halves, served, stat, cins, rests, extras, windows, slots, columns
):
    batch_count, rows_msg, _ = codes.shape
    long = rows_msg * WIDE
    sizes = message_rows(rows_msg, columns)
    depth = batch_count // PLANE
    in_vmem = pl.BlockSpec(memory_space=pltpu.VMEM)
    dma = pltpu.SemaphoreType.DMA
    return pl.pallas_call(
        partial(return_kernel, slots, windows, columns),
        in_specs=[in_vmem] * 8,
        out_specs=[in_vmem] * 4,
        out_shape=[
            jax.ShapeDtypeStruct((columns, TALL * BROAD), jnp.float32),
            jax.ShapeDtypeStruct(stat.shape, jnp.float32),
            jax.ShapeDtypeStruct(cins.shape[1:], jnp.float32),
            jax.ShapeDtypeStruct(rests.shape[1:], jnp.float32),
        ],
        scratch_shapes=[
            pltpu.VMEM((batch_count, sizes, WIDE), jnp.bfloat16),
            pltpu.VMEM((batch_count, sizes, WIDE), jnp.bfloat16),
            pltpu.VMEM((sizes + 16, WIDE), jnp.float32),
            pltpu.VMEM((sizes + 16, WIDE), jnp.float32),
            pltpu.VMEM((columns * TALL, long), jnp.bfloat16),
            pltpu.VMEM((BROAD, long), jnp.bfloat16),
            pltpu.VMEM((columns * TALL, BROAD), jnp.float32),
            pltpu.VMEM((batch_count,) + extras.shape[1:], jnp.float32),
        ]
        + [
            pltpu.VMEM(lead + x.shape[1:], jnp.float32)
            for x in (cins, rests)
            for lead in ((PLANE, depth), (depth,), (depth,))
        ]
        + [dma((batch_count,))] * 8,
        compiler_params=pltpu.CompilerParams(
            vmem_limit_bytes=vmem_limit(batch_count), collective_id=1, has_side_effects=True
        ),
        name="return_grads",
    )(grad_bags, codes, halves, served, stat, cins, rests, extras)


def split_three(x):
    high = x.astype(jnp.bfloat16)
    rest = x - high.astype(jnp.float32)
    middle = rest.astype(jnp.bfloat16)
    low = (rest - middle.astype(jnp.float32)).astype(jnp.bfloat16)
    return high, middle, low


def dense_kernel(
    micro_count, windows, tower_ref, stat_ref, pooled_ref, label_ref, weight_ref,
    cin_ref, rest_ref,
    bags_ref, loss_ref, g_cins_ref, g_rests_ref, g_extras_ref,
    embed_ref, total_ref, pairs_ref, sym_ref, g_cin_ref, g_rest_ref, lane_ref,
):
    f32 = jnp.float32
    bf16 = jnp.bfloat16
    width = micro_count * LANES
    groups = HPAD // LANES

    def rest_rows(begin, count):
        return jnp.concatenate(
            [rest_ref[l, begin : begin + count, :] for l in range(groups)], axis=1
        )[:, :HID]

    cin_w = cin_ref[:MAPS, :].astype(bf16)
    place = iota((MAPS, PAIRS), 0)
    place = place // FIELDS * FPAD + place % FIELDS == iota((MAPS, PAIRS), 1)
    picks_u = ones_at(place)
    row_u = jnp.broadcast_to(cin_ref[MAPS : MAPS + 1, :], (8, PAIRS)).astype(bf16)
    cin_u = dot(picks_u, row_u, NT)[:, :1]
    w_one = jnp.concatenate(
        [
            jnp.concatenate(
                [rest_ref[l, pl.ds(d, FPAD, stride=EMB), :] for l in range(groups)], axis=1
            )[:, :HID]
            for d in range(EMB)
        ],
        axis=0,
    ).astype(bf16)
    w_two = rest_rows(W_TWO, HID).astype(bf16)
    rows = jnp.zeros((8, HID), f32)
    for k, at in enumerate((B_ONE, B_TWO, W_THREE)):
        rows = jnp.where(iota((8, HID), 0) == k, rest_rows(at, 1), rows)
    unit = ones_at(iota((HID, HID), 0) == iota((HID, HID), 1))
    turned = dot(unit, rows.astype(bf16), NT)
    b_one, b_two, w_three = turned[:, 0:1], turned[:, 1:2], turned[:, 2:3]
    bias = rest_ref[0, BIAS : BIAS + 1, 0:1]

    def unpacked(row, count):
        pieces = []
        for m in range(micro_count):
            low = pooled_ref[m, row : row + HALF, :LANES]
            high = pooled_ref[m, row : row + HALF, LANES:]
            pieces.append(jnp.concatenate([low, high], axis=0)[:count])
        return jnp.concatenate(pieces, axis=1)

    for d in range(EMB):
        embed_ref[d * FPAD : (d + 1) * FPAD, :] = unpacked(d * HALF, FPAD)
    linear = jnp.concatenate(
        [
            pooled_ref[m, EMB * HALF : EMB * HALF + 1, :LANES]
            + pooled_ref[m, EMB * HALF : EMB * HALF + 1, LANES:]
            for m in range(micro_count)
        ],
        axis=1,
    )

    def pair_row(i, carry):
        total = jnp.zeros((FPAD, width), f32)
        for d in range(EMB):
            own = embed_ref[pl.ds(d * FPAD + i, 1), :]
            product = (embed_ref[d * FPAD : (d + 1) * FPAD, :] * own).astype(jnp.bfloat16)
            total = total + product.astype(f32)
        total_ref[pl.ds(pl.multiple_of(i * FPAD, 8), FPAD), :] = total
        return carry

    lax.fori_loop(0, FIELDS, pair_row, 0, unroll=3)
    thirds = split_three(total_ref[...])
    map_sum = sum(dot(cin_w, third) for third in thirds)
    cin_logits = jnp.sum(map_sum * cin_u, axis=0, keepdims=True)

    flat = embed_ref[...].astype(jnp.bfloat16)
    pre_one = dot(w_one, flat, TN) + b_one
    hidden_one = jnp.maximum(pre_one, 0.0).astype(jnp.bfloat16)
    pre_two = dot(w_two, hidden_one, TN) + b_two
    active_two = jnp.maximum(pre_two, 0.0)
    deep_logits = jnp.sum(active_two * w_three, axis=0, keepdims=True)
    logits = cin_logits + deep_logits + linear + bias

    samples = weight_ref.shape[1]
    lane_ref[...] = jnp.zeros_like(lane_ref)
    for m in range(micro_count):
        span = slice(m * LANES, m * LANES + samples)
        lane_ref[0:1, span] = weight_ref[m : m + 1, :].astype(f32)
        lane_ref[1:2, span] = label_ref[m : m + 1, :].astype(f32)
    weight = lane_ref[0:1, :]
    label = lane_ref[1:2, :]
    soft = jnp.maximum(logits, 0.0) + jnp.log1p(jnp.exp(-jnp.abs(logits)))
    loss_ref[...] = jnp.broadcast_to(
        jnp.sum(weight * (soft - label * logits), axis=1, keepdims=True), loss_ref.shape
    )
    grad_logits = weight * (jax.nn.sigmoid(logits) - label) / stat_ref[0:1, 0:1]

    grad_maps = (grad_logits * cin_u).astype(jnp.bfloat16)
    grad_two = jnp.where(pre_two > 0, grad_logits * w_three, 0.0).astype(jnp.bfloat16)
    grad_hidden = dot(w_two, grad_two)
    grad_one = jnp.where(pre_one > 0, grad_hidden, 0.0).astype(jnp.bfloat16)
    grad_flat = dot(w_one, grad_one)

    grad_pairs = dot(cin_w, grad_maps, TN)
    for m in range(micro_count):
        pairs_ref[m, :PAIRS, :] = grad_pairs[:, m * LANES : (m + 1) * LANES]
        pairs_ref[m, PAIRS:, :] = jnp.zeros((FPAD * FPAD - PAIRS, LANES), f32)

    def mirror(j, carry):
        here = pl.ds(pl.multiple_of(j * FPAD, 8), FPAD)
        both = [
            pairs_ref[m, here, :] + pairs_ref[m, pl.ds(j, FPAD, stride=FPAD), :]
            for m in range(micro_count)
        ]
        sym_ref[here, :] = jnp.concatenate(both, axis=1)
        return carry

    lax.fori_loop(0, FIELDS, mirror, 0, unroll=13)
    empty = jnp.zeros((2 * HALF - FPAD, width), f32)

    for d in range(EMB):

        def add_row(j, total):
            here = pl.ds(pl.multiple_of(j * FPAD, 8), FPAD)
            return total + sym_ref[here, :] * embed_ref[pl.ds(d * FPAD + j, 1), :]

        grad_embed = lax.fori_loop(
            0, FIELDS, add_row, grad_flat[d * FPAD : (d + 1) * FPAD], unroll=39
        )
        grad_embed = jnp.concatenate([grad_embed, empty], axis=0)
        for m in range(micro_count):
            span = slice(m * LANES, (m + 1) * LANES)
            block = jnp.concatenate([grad_embed[:HALF, span], grad_embed[HALF:, span]], axis=1)
            bags_ref[m, d * HALF : (d + 1) * HALF, :] = block.astype(bf16)
    for m in range(micro_count):
        row = grad_logits[:, m * LANES : (m + 1) * LANES]
        row = jnp.concatenate([row, row], axis=1)
        bags_ref[m, EMB * HALF :, :] = jnp.broadcast_to(row, (8, WIDE)).astype(bf16)

    ones = jnp.ones((8, width), bf16)

    def row_sum(x):
        return sum(dot(ones, third, NT) for third in split_three(x))[:1]

    g_rest_ref[...] = jnp.zeros_like(g_rest_ref)

    def put(begin, count, value, stride=None):
        for l in range(groups):
            piece = value[:, l * LANES : min((l + 1) * LANES, HID)]
            lanes = slice(0, piece.shape[1])
            if stride is None:
                g_rest_ref[l, begin : begin + count, lanes] = piece
            else:
                piece = jnp.pad(piece, ((0, 0), (0, LANES - piece.shape[1])))
                g_rest_ref[l, pl.ds(begin, count, stride=stride), :] = piece

    g_w_one = dot(flat, grad_one, NT)
    for d in range(EMB):
        put(d, FIELDS, g_w_one[d * FPAD : d * FPAD + FIELDS], EMB)

    @pl.when(tower_ref[0] == 0)
    def _():
        g_cin_ref[...] = jnp.zeros_like(g_cin_ref)
        g_cin_ref[:MAPS, :] = sum(dot(grad_maps, third, NT) for third in thirds)
        g_cin_u = jnp.sum(map_sum * grad_logits, axis=1, keepdims=True)
        thirds_u = split_three(jnp.broadcast_to(g_cin_u, (MAPS, 8)))
        g_cin_ref[MAPS : MAPS + 1, :] = sum(dot(third, picks_u, TN) for third in thirds_u)[:1]
        for b, at in enumerate(windows.cin_at):
            g_cins_ref[windows.slots[b], : windows.cin_rows, :PAIRS] = g_cin_ref[
                at : at + windows.cin_rows, :
            ]
        for e, at in enumerate(windows.extra_at):
            skip = max(0, -at)
            for l in range(groups):
                span = slice(l * LANES, (l + 1) * LANES)
                g_extras_ref[e, : windows.rest_rows - skip, span] = g_rest_ref[
                    l, at + skip : at + windows.rest_rows, :
                ]

    @pl.when(tower_ref[0] != 0)
    def _():
        put(W_TWO, HID, dot(hidden_one, grad_two, NT))
        put(B_ONE, 1, dot(ones, grad_one, NT)[:1])
        put(B_TWO, 1, dot(ones, grad_two, NT)[:1])
        put(W_THREE, 1, row_sum(active_two * grad_logits))
        g_bias = jnp.sum(grad_logits, axis=1, keepdims=True)
        put(BIAS, 1, jnp.where(iota((1, HID), 1) == 0, g_bias, 0.0))
        for b, at in enumerate(windows.rest_at):
            for l in range(groups):
                span = slice(l * LANES, (l + 1) * LANES)
                g_rests_ref[windows.slots[b], : windows.rest_rows, span] = g_rest_ref[
                    l, at : at + windows.rest_rows, :
                ]


def dense_step(tower_at, stats, pooled, labels, weights, cin_full, rest_full, windows):
    micro_count = pooled.shape[0]
    width = micro_count * LANES
    in_vmem = pl.BlockSpec(memory_space=pltpu.VMEM)
    in_smem = pl.BlockSpec(memory_space=pltpu.SMEM)
    f32 = jnp.float32
    shapes = [
        ((micro_count, BAG_ROWS, WIDE), jnp.bfloat16),
        ((8, LANES), f32),
        ((windows.batch_count, windows.cin_pad_wide, PAIRS_PAD), f32),
        ((windows.batch_count, windows.rest_pad_wide, HPAD), f32),
        ((windows.extras, windows.extra_pad_wide, HPAD), f32),
    ]
    return pl.pallas_call(
        partial(dense_kernel, micro_count, windows),
        in_specs=[in_smem] + [in_vmem] * 6,
        out_specs=[in_vmem] * len(shapes),
        out_shape=[jax.ShapeDtypeStruct(*shape) for shape in shapes],
        scratch_shapes=[
            pltpu.VMEM((EMB * FPAD, width), f32),
            pltpu.VMEM((PAIRS, width), f32),
            pltpu.VMEM((micro_count, FPAD * FPAD, LANES), f32),
            pltpu.VMEM((PAIRS, width), f32),
            pltpu.VMEM((windows.cin_total, PAIRS), f32),
            pltpu.VMEM((HPAD // LANES, windows.rest_total, LANES), f32),
            pltpu.VMEM((8, width), f32),
        ],
        compiler_params=pltpu.CompilerParams(vmem_limit_bytes=vmem_limit(windows.batch_count)),
        name="dense",
    )(tower_at.reshape(1), stats, pooled, labels, weights, cin_full, rest_full)


def shards(
    shard_ids,
    local_rows,
    bag_counts,
    click_labels,
    sample_weights,
    embed_table,
    table_first,
    table_second,
    dense_params,
    dense_first,
    dense_second,
):
    tower_count = lax.axis_size("tower")
    batch_count = lax.axis_size("batch")
    tower_at = lax.axis_index("tower")
    micro_count, samples = shard_ids.shape[:2]
    columns, rows_dev = embed_table.shape
    capacity = 4 * samples * IDS_SAMP // (tower_count * batch_count)
    share = dense_params.shape[0]
    windows = Windows(share, batch_count)
    slots = Slots(micro_count, capacity)

    device = tower_at * batch_count + lax.axis_index("batch")
    cin_phase, rest_phase = windows.phases(device)
    low = dense_params.astype(jnp.bfloat16)

    def window(rows, row_size, phase):
        return lax.dynamic_update_slice(
            jnp.zeros((rows * row_size,), jnp.bfloat16), low, (phase,)
        )

    cin_window = window(windows.cin_rows, SQUARE, cin_phase).reshape(-1, FIELDS, FIELDS)
    cin_window = jnp.pad(
        cin_window,
        ((0, windows.cin_pad - windows.cin_rows), (0, 0), (0, FPAD - FIELDS)),
    ).reshape(windows.cin_pad, PAIRS)
    cin_window = jnp.pad(cin_window, ((0, 0), (0, PAIRS_PAD - PAIRS)))
    rest_window = jnp.pad(
        window(windows.rest_rows, HID, rest_phase).reshape(-1, HID),
        ((0, windows.rest_pad - windows.rest_rows), (0, HPAD - HID)),
    )

    def lanes_of(values):
        return jnp.moveaxis(values, 1, -1).reshape(micro_count, -1, samples)

    requests, codes, halves = route(
        lanes_of(shard_ids), lanes_of(local_rows), lanes_of(bag_counts), sample_weights,
        slots, batch_count,
    )
    pooled, served, stats, cin_full, rest_full = fetch(
        requests, codes, halves, embed_table, cin_window, rest_window, windows, slots
    )
    grad_bags, loss, g_cins, g_rests, g_extras = dense_step(
        tower_at, stats, pooled, click_labels, sample_weights, cin_full, rest_full, windows
    )
    table_grad, losses, g_cin, g_rest = return_grads(
        grad_bags, codes, halves, served, loss, g_cins, g_rests, g_extras, windows, slots, columns
    )
    g_cin = g_cin[: windows.cin_rows, :PAIRS].reshape(-1, FIELDS, FPAD)[:, :, :FIELDS].reshape(-1)
    g_rest = g_rest[: windows.rest_rows, :HID].reshape(-1)
    is_cin = device * share + jnp.arange(share, dtype=jnp.int32) < CIN_SIZE
    own_grad = jnp.where(
        is_cin,
        lax.dynamic_slice(g_cin, (cin_phase,), (share,)),
        lax.dynamic_slice(g_rest, (rest_phase,), (share,)),
    )

    table_new, table_first_new, table_second_new = adam_update(
        embed_table, table_first, table_second, table_grad, rate_table
    )
    dense_new, dense_first_new, dense_second_new = adam_update(
        dense_params, dense_first, dense_second, own_grad, rate_dense
    )
    loss_sum = losses[0, 0] / stats[0, 0]
    return (
        table_new,
        table_first_new,
        table_second_new,
        table_new.astype(jnp.bfloat16),
        dense_new,
        dense_first_new,
        dense_second_new,
        dense_new.astype(jnp.bfloat16),
        loss_sum,
    )


def solution(mesh):
    rows = P(None, ("tower", "batch"))
    dense = P(("tower", "batch"))
    placed = (
        P(None, "batch", None, None),
        P(None, "batch", None, None),
        P(None, "batch", None),
        P(None, "batch"),
        P(None, "batch"),
        rows,
        rows,
        rows,
        dense,
        dense,
        dense,
    )
    return jax.shard_map(
        shards,
        mesh=mesh,
        in_specs=placed,
        out_specs=(rows, rows, rows, rows, dense, dense, dense, dense, P()),
        check_vma=False,
    )
```
